32 devices in a mesh: seq: 4 (over x, core), fsdp: 8 (over z, y).
Axes of the slice: x: 2, y: 2, z: 4, core: 2. Of those that a mesh axis runs over, the one named last changes fastest.
Arguments:
- hidden_in: bfloat16 [8, 512, 1024], P('fsdp', 'seq'), may hold values from -6 to 6
- grad_out: bfloat16 [8, 512, 1024], P('fsdp', 'seq'), may hold values from -6 to 6
- segments: int32 [8, 512], P('fsdp'), may hold values from 0 to 1, as said below
- norm_gain: bfloat16 [1024], P('fsdp'), may hold values from 0.5 to 1.5
- mamba_in: bfloat16 [1024, 3328], P('fsdp'), may hold values from -0.1875 to 0.1875
- step_in: bfloat16 [1024, 24], P('fsdp'), may hold values from -0.1875 to 0.1875
- attn_in: bfloat16 [1024, 768], P('fsdp'), may hold values from -0.1875 to 0.1875
- conv_taps: float32 [4, 1792], replicated, may hold values from -3 to 3
- conv_bias: float32 [1792], replicated, may hold values from -1.75 to 1.75
- step_bias: float32 [24], replicated, may hold values from -2 to 0.5
- log_decay: float32 [24], replicated, may hold values from -7 to -2.5
- skip_gain: float32 [24], replicated, may hold values from 0.5 to 1.5
- gated_gain: bfloat16 [1536], P('fsdp'), may hold values from 0.5 to 1.5
- mamba_out: bfloat16 [1536, 1024], P('fsdp'), may hold values from -0.15625 to 0.15625
- attn_out: bfloat16 [512, 1024], P('fsdp'), may hold values from -0.75 to 0.75
- ffn_gain: bfloat16 [1024], P('fsdp'), may hold values from 0.5 to 1.5
- gate_up: bfloat16 [1024, 4096], P('fsdp'), may hold values from -0.1875 to 0.1875
- down_proj: bfloat16 [2048, 1024], P('fsdp'), may hold values from -0.125 to 0.125
Outputs:
- hidden_out: bfloat16 [8, 512, 1024], P('fsdp', 'seq')
- grad_in: float32 [8, 512, 1024], P('fsdp', 'seq')
- grad_norm_gain: float32 [1024], P('fsdp')
- grad_mamba_in: float32 [1024, 3328], P('fsdp')
- grad_step_in: float32 [1024, 24], P('fsdp')
- grad_attn_in: float32 [1024, 768], P('fsdp')
- grad_conv_taps: float32 [4, 1792], replicated
- grad_conv_bias: float32 [1792], replicated
- grad_step_bias: float32 [24], replicated
- grad_log_decay: float32 [24], replicated
- grad_skip_gain: float32 [24], replicated
- grad_gated_gain: float32 [1536], P('fsdp')
- grad_mamba_out: float32 [1536, 1024], P('fsdp')
- grad_attn_out: float32 [512, 1024], P('fsdp')
- grad_ffn_gain: float32 [1024], P('fsdp')
- grad_gate_up: float32 [1024, 4096], P('fsdp')
- grad_down_proj: float32 [2048, 1024], P('fsdp')
The draws below stay inside these ranges and needn't reach their ends.
Inputs may be any that keep to these rules, and one draw needn't show every extreme that they name: `segments`: in each pack the ids are 0 up to some position and 1 from there on: a pack holds one sequence or two, the first at least 128 tokens long.
All inputs are finite; a program needn't handle non-finite values.
Results may differ from the reference program's by a relative error of at most 0.015.
Values may be sent and summed in bfloat16 or wider, within the bound.
A program may use at most 192 MiB of HBM per device.

```python
import math
from functools import partial
import jax
import jax.numpy as jnp
from jax import lax

D = 1024
MH = 24
HD = 64
NST = 128
KC = 4
QH = 8
KVH = 2
FF = 2048
SPAN = 128
DI = 1536
LEN = 512
NPACK = 8
CONV_CH = 1792
N_SEQ = 4


def draw_segments(key, part):
    cut_at = jax.random.randint(key, (NPACK, 1), LEN // 4, LEN + LEN // 4)
    places = jnp.arange(LEN, dtype=jnp.int32)[None, :]
    return (places >= cut_at).astype(jnp.int32)


def steps_of(stream_key, shape, cuts, low, largest):
    factor_of = 1.0
    for axis_at, blocks in cuts:
        steps = jax.random.uniform(jax.random.fold_in(jax.random.fold_in(stream_key, 6), axis_at), (blocks,), jnp.float32, low / len(cuts), largest / len(cuts))
        factor_of = factor_of * jnp.repeat(jnp.exp(steps), shape[axis_at] // blocks).reshape((-1,) + (1,) * (len(shape) - 1 - axis_at))
    return factor_of


def scatter_about(rng, extent, deviation, reach, pieces=(), held_as=jnp.bfloat16):
    factor_of = steps_of(rng, extent, pieces, -0.22, 0.18) if pieces else 1.0
    result = jax.random.normal(rng, extent, jnp.float32) * deviation * factor_of
    return jnp.minimum(jnp.maximum(result, -reach), reach).astype(held_as)


def setup_inputs(seed: int = 0) -> dict:
    key_of = jax.random.split(jax.random.key(seed), 19)
    return {
        "hidden_in": scatter_about(key_of[0], (NPACK, LEN, D), 1.0, 6.0, ((0, 8), (1, 4))),
        "grad_out": scatter_about(key_of[1], (NPACK, LEN, D), 1.0, 6.0, ((0, 8), (1, 4))),
        "segments": draw_segments(jax.random.fold_in(key_of[18], 71), 0),
        "norm_gain": jnp.clip(1.0 + 0.1 * jax.random.normal(key_of[3], (D,), jnp.float32), 0.5, 1.5).astype(jnp.bfloat16),
        "mamba_in": scatter_about(key_of[4], (D, 2 * DI + 2 * NST), D ** -0.5, 0.1875, ((0, 8),)),
        "step_in": scatter_about(key_of[5], (D, MH), D ** -0.5, 0.1875, ((0, 8),)),
        "attn_in": scatter_about(key_of[6], (D, (QH + 2 * KVH) * HD), D ** -0.5, 0.1875, ((0, 8),)),
        "conv_taps": scatter_about(key_of[7], (KC, CONV_CH), 0.5, 3.0, (), jnp.float32),
        "conv_bias": scatter_about(key_of[8], (CONV_CH,), 0.3, 1.75, (), jnp.float32),
        "step_bias": jnp.clip(jax.random.uniform(key_of[9], (MH,), jnp.float32, -2.0, 0.5), -2.0, 0.5),
        "log_decay": jnp.clip(jax.random.uniform(key_of[10], (MH,), jnp.float32, -7.0, -2.5), -7.0, -2.5),
        "skip_gain": jnp.clip(jax.random.uniform(key_of[11], (MH,), jnp.float32, 0.5, 1.5), 0.5, 1.5),
        "gated_gain": jnp.clip(1.0 + 0.1 * jax.random.normal(key_of[12], (DI,), jnp.float32), 0.5, 1.5).astype(jnp.bfloat16),
        "mamba_out": scatter_about(key_of[13], (DI, D), DI ** -0.5, 0.15625, ((0, 8),)),
        "attn_out": scatter_about(key_of[14], (QH * HD, D), HD ** -0.5, 0.75, ((0, 8),)),
        "ffn_gain": jnp.clip(1.0 + 0.1 * jax.random.normal(key_of[15], (D,), jnp.float32), 0.5, 1.5).astype(jnp.bfloat16),
        "gate_up": scatter_about(key_of[16], (D, 2 * FF), D ** -0.5, 0.1875, ((0, 8),)),
        "down_proj": scatter_about(key_of[17], (FF, D), FF ** -0.5, 0.125, ((0, 8),)),
    }


EPS = 1e-05
ROPE_THETA = 10000.0

def rms_scale(values):
    return lax.rsqrt(lax.optimization_barrier(jnp.mean(values * values, axis=-1, keepdims=True)) + EPS)

def swish_slope(values):
    sigma = jax.nn.sigmoid(values)
    return sigma * (1.0 + values * (1.0 - sigma))

def scan_blocks(x_heads, b_mat, c_mat, step, log_step, seg_ids):
    row_count, head_count, width = x_heads.shape
    state = b_mat.shape[1]
    block_count = row_count // SPAN
    highest = lax.Precision.HIGHEST
    spots = jnp.arange(SPAN, dtype=jnp.int32)
    causal = spots[:, None] >= spots[None, :]

    def one_block(carry, items):
        state_in, prev_seg = carry
        x_blk, b_blk, c_blk, step_blk, log_blk, seg_blk = items
        local = jnp.cumsum(log_blk, axis=0)
        inside = causal & (seg_blk[:, None] == seg_blk[None, :])
        inner = jnp.dot(c_blk, b_blk.T, precision=highest)
        local_t = local.T
        expo = jnp.where(inside[None], local_t[:, :, None] - local_t[:, None, :], -1e+30)
        mixing = inner[None] * jnp.exp(expo) * step_blk.T[:, None, :]
        intra = jnp.einsum('htp,phd->thd', mixing, x_blk, precision=highest)
        carried = jnp.einsum('tn,hnd->thd', c_blk, state_in, precision=highest)
        lead = jnp.where((seg_blk == prev_seg)[:, None], jnp.exp(local), 0.0)
        out_blk = intra + lead[:, :, None] * carried
        last_seg = seg_blk[SPAN - 1]
        tail = jnp.where((seg_blk == last_seg)[:, None], jnp.exp(local[SPAN - 1][None, :] - local) * step_blk, 0.0)
        fresh = jnp.einsum('ph,pn,phd->hnd', tail, b_blk, x_blk, precision=highest)
        keep = jnp.where(prev_seg == last_seg, jnp.exp(local[SPAN - 1]), 0.0)
        state_out = keep[:, None, None] * state_in + fresh
        return ((state_out, last_seg), out_blk)
    start = (jnp.zeros((head_count, state, width), x_heads.dtype), jnp.int32(-1))
    items = (x_heads.reshape(block_count, SPAN, head_count, width), b_mat.reshape(block_count, SPAN, state), c_mat.reshape(block_count, SPAN, state), step.reshape(block_count, SPAN, head_count), log_step.reshape(block_count, SPAN, head_count), seg_ids.reshape(block_count, SPAN))
    final, outputs = lax.scan(one_block, start, items)
    return outputs.reshape(row_count, head_count, width)

def mixer_core(xs_in, bc_in, step_raw, query_in, kv_in, seg_ids, taps, tap_bias, step_bias, log_decay, skip_gain):
    row_count = xs_in.shape[0]
    head_count = step_raw.shape[1]
    width = xs_in.shape[1] // head_count
    state = bc_in.shape[1] // 2
    highest = lax.Precision.HIGHEST
    pre_conv = jnp.concatenate([xs_in, bc_in], axis=1)
    tap_count = taps.shape[0]
    accum = tap_bias[None, :] + taps[tap_count - 1][None, :] * pre_conv
    for lag_step in range(1, tap_count):
        moved = jnp.concatenate([jnp.zeros((lag_step, pre_conv.shape[1]), pre_conv.dtype), pre_conv[:row_count - lag_step]], axis=0)
        prior = jnp.concatenate([jnp.full((lag_step,), -1, jnp.int32), seg_ids[:row_count - lag_step]])
        same_seq = (prior == seg_ids)[:, None]
        accum = accum + taps[tap_count - 1 - lag_step][None, :] * jnp.where(same_seq, moved, 0.0)
    activated = jax.nn.silu(accum)
    x_heads = activated[:, :head_count * width].reshape(row_count, head_count, width)
    b_mat = activated[:, head_count * width:head_count * width + state]
    c_mat = activated[:, head_count * width + state:]
    step = jax.nn.softplus(step_raw + step_bias[None, :])
    log_step = -jnp.exp(log_decay)[None, :] * step
    ssm_out = scan_blocks(x_heads, b_mat, c_mat, step, log_step, seg_ids) + skip_gain[None, :, None] * x_heads
    positions = jnp.arange(row_count, dtype=jnp.int32)
    mask = (positions[:, None] >= positions[None, :]) & (seg_ids[:, None] == seg_ids[None, :])
    query_count = query_in.shape[1] // width
    kv_count = kv_in.shape[1] // (2 * width)
    group_size = query_count // kv_count
    place = (lax.optimization_barrier(jnp.sum(mask.astype(jnp.int32), axis=1)) - 1).astype(xs_in.dtype)
    half = width // 2
    freqs = jnp.exp(-math.log(ROPE_THETA) * 2.0 * jnp.arange(half, dtype=xs_in.dtype) / width)
    angles = place[:, None] * freqs[None, :]
    cosine = jnp.cos(angles)[:, None, :]
    sine = jnp.sin(angles)[:, None, :]

    def rotate(tensor):
        first_half = tensor[..., :half]
        second_half = tensor[..., half:]
        return jnp.concatenate([first_half * cosine - second_half * sine, second_half * cosine + first_half * sine], axis=-1)
    queries = rotate(query_in.reshape(row_count, query_count, width)).reshape(row_count, kv_count, group_size, width)
    kv_pair = kv_in.reshape(row_count, kv_count, 2, width)
    keys = rotate(kv_pair[:, :, 0])
    values = kv_pair[:, :, 1]
    scores = jnp.einsum('ikgp,jkp->kgij', queries, keys, precision=highest) * (1.0 / math.sqrt(width))
    scores = jnp.where(mask[None, None], scores, -1e+30)
    weights = jnp.exp(scores)
    weights = weights / lax.optimization_barrier(jnp.sum(weights, axis=-1, keepdims=True))
    attended = jnp.einsum('kgij,jkp->ikgp', weights, values, precision=highest)
    return (ssm_out.reshape(row_count, head_count * width), attended.reshape(row_count, query_count * width))

def core_apply(seg_ids, inputs, params):
    return mixer_core(*inputs, seg_ids, *params)

def reference(hidden_in, grad_out, segments, norm_gain, mamba_in, step_in, attn_in, conv_taps, conv_bias, step_bias, log_decay, skip_gain, gated_gain, mamba_out, attn_out, ffn_gain, gate_up, down_proj):
    x_width = DI // N_SEQ
    head_share = MH // N_SEQ
    query_share = QH * HD // N_SEQ
    owners = [group * KVH // N_SEQ for group in range(N_SEQ)]
    first_gain = norm_gain.astype(jnp.float32)
    mixer_gain = gated_gain.astype(jnp.float32)
    second_gain = ffn_gain.astype(jnp.float32)
    bf_type = jnp.bfloat16
    fl_type = jnp.float32

    def one_pack(totals, data):
        tok_in, cot_in, seg_ids = data
        residual = tok_in.astype(fl_type)
        first_scale = rms_scale(residual)
        first_norm = residual * first_scale
        normed = (first_norm * first_gain).astype(bf_type)
        projected = jnp.dot(normed, mamba_in, preferred_element_type=fl_type)
        gate_raw = projected[:, :DI]
        conv_in = projected[:, DI:].astype(bf_type)
        step_raw = jnp.dot(normed, step_in, preferred_element_type=fl_type).astype(bf_type)
        qkv_out = jnp.dot(normed, attn_in, preferred_element_type=fl_type).astype(bf_type)
        query_all = qkv_out[:, :QH * HD]
        key_part = qkv_out[:, QH * HD:(QH + KVH) * HD].reshape(LEN, KVH, HD)
        value_part = qkv_out[:, (QH + KVH) * HD:].reshape(LEN, KVH, HD)
        kv_pairs = jnp.concatenate([key_part, value_part], axis=2)
        ssm_parts, attn_parts, pullers = ([], [], [])
        for group in range(N_SEQ):
            x_cols = slice(group * x_width, (group + 1) * x_width)
            head_cols = slice(group * head_share, (group + 1) * head_share)
            taps = jnp.concatenate([conv_taps[:, x_cols], conv_taps[:, DI:]], axis=1)
            tap_bias = jnp.concatenate([conv_bias[x_cols], conv_bias[DI:]])
            inputs = (conv_in[:, x_cols].astype(fl_type), conv_in[:, DI:].astype(fl_type), step_raw[:, head_cols].astype(fl_type), query_all[:, group * query_share:(group + 1) * query_share].astype(fl_type), kv_pairs[:, owners[group]].astype(fl_type))
            params = (taps, tap_bias, step_bias[head_cols], log_decay[head_cols], skip_gain[head_cols])
            (ssm_group, attn_group), pull_back = jax.vjp(partial(core_apply, seg_ids), inputs, params)
            ssm_parts.append(ssm_group.astype(bf_type))
            attn_parts.append(attn_group.astype(bf_type))
            pullers.append(pull_back)
        scan_out = jnp.concatenate(ssm_parts, axis=1)
        attn_mix = jnp.concatenate(attn_parts, axis=1)
        scan_float = scan_out.astype(fl_type)
        gate_act = jax.nn.silu(gate_raw)
        gated = scan_float * gate_act
        gated_scale = rms_scale(gated)
        gated_norm = gated * gated_scale
        gated_b = (gated_norm * mixer_gain).astype(bf_type)
        mixed = residual + jnp.dot(gated_b, mamba_out, preferred_element_type=fl_type) + jnp.dot(attn_mix, attn_out, preferred_element_type=fl_type)
        second_scale = rms_scale(mixed)
        second_norm = mixed * second_scale
        ffn_in = (second_norm * second_gain).astype(bf_type)
        gate_vals = jnp.dot(ffn_in, gate_up, preferred_element_type=fl_type)
        gate_lin = gate_vals[:, :FF]
        up_lin = gate_vals[:, FF:]
        ffn_act = (jax.nn.silu(gate_lin) * up_lin).astype(bf_type)
        layer_out = (mixed + jnp.dot(ffn_act, down_proj, preferred_element_type=fl_type)).astype(bf_type)
        cot_float = cot_in.astype(fl_type)
        g_down = jnp.dot(ffn_act.T, cot_in, preferred_element_type=fl_type)
        d_act = jnp.dot(cot_in, down_proj.T, preferred_element_type=fl_type)
        d_ffn = jnp.concatenate([d_act * up_lin * swish_slope(gate_lin), d_act * jax.nn.silu(gate_lin)], axis=1).astype(bf_type)
        g_gate_up = jnp.dot(ffn_in.T, d_ffn, preferred_element_type=fl_type)
        d_ffn_in = jnp.dot(d_ffn, gate_up.T, preferred_element_type=fl_type)
        g_ffn_gain = lax.optimization_barrier(jnp.sum(d_ffn_in * second_norm, axis=0))
        d_second = d_ffn_in * second_gain
        d_mixed = cot_float + second_scale * (d_second - second_norm * lax.optimization_barrier(jnp.mean(d_second * second_norm, axis=-1, keepdims=True)))
        d_mixed_b = d_mixed.astype(bf_type)
        g_attn_out = jnp.dot(attn_mix.T, d_mixed_b, preferred_element_type=fl_type)
        d_attn_mix = jnp.dot(d_mixed_b, attn_out.T, preferred_element_type=fl_type).astype(bf_type)
        g_mamba_out = jnp.dot(gated_b.T, d_mixed_b, preferred_element_type=fl_type)
        d_gated_b = jnp.dot(d_mixed_b, mamba_out.T, preferred_element_type=fl_type)
        g_gated_gain = lax.optimization_barrier(jnp.sum(d_gated_b * gated_norm, axis=0))
        d_gnorm = d_gated_b * mixer_gain
        d_gated = gated_scale * (d_gnorm - gated_norm * lax.optimization_barrier(jnp.mean(d_gnorm * gated_norm, axis=-1, keepdims=True)))
        d_scan = (d_gated * gate_act).astype(bf_type)
        d_gate_raw = d_gated * scan_float * swish_slope(gate_raw)
        x_grads, step_grads, query_grads = ([], [], [])
        bc_total = jnp.zeros((LEN, 2 * NST), fl_type)
        kv_totals = [jnp.zeros((LEN, 2 * HD), fl_type) for kv_head in range(KVH)]
        taps_total = jnp.zeros((KC, CONV_CH), fl_type)
        bias_total = jnp.zeros((CONV_CH,), fl_type)
        step_total = jnp.zeros((MH,), fl_type)
        decay_total = jnp.zeros((MH,), fl_type)
        skip_total = jnp.zeros((MH,), fl_type)
        for group in range(N_SEQ):
            x_cols = slice(group * x_width, (group + 1) * x_width)
            head_cols = slice(group * head_share, (group + 1) * head_share)
            cot_pair = (d_scan[:, x_cols].astype(fl_type), d_attn_mix[:, group * query_share:(group + 1) * query_share].astype(fl_type))
            grad_inputs, grad_params = pullers[group](cot_pair)
            x_grads.append(grad_inputs[0].astype(bf_type))
            bc_total = bc_total + lax.optimization_barrier(grad_inputs[1].astype(bf_type)).astype(fl_type)
            step_grads.append(grad_inputs[2].astype(bf_type))
            query_grads.append(grad_inputs[3].astype(bf_type))
            kv_totals[owners[group]] = kv_totals[owners[group]] + lax.optimization_barrier(grad_inputs[4].astype(bf_type)).astype(fl_type)
            taps_total = taps_total.at[:, x_cols].add(grad_params[0][:, :x_width])
            taps_total = taps_total.at[:, DI:].add(grad_params[0][:, x_width:])
            bias_total = bias_total.at[x_cols].add(grad_params[1][:x_width])
            bias_total = bias_total.at[DI:].add(grad_params[1][x_width:])
            step_total = step_total.at[head_cols].add(grad_params[2])
            decay_total = decay_total.at[head_cols].add(grad_params[3])
            skip_total = skip_total.at[head_cols].add(grad_params[4])
        d_proj = jnp.concatenate([d_gate_raw.astype(bf_type)] + x_grads + [bc_total.astype(bf_type)], axis=1)
        d_step = jnp.concatenate(step_grads, axis=1)
        key_grads = [kv_totals[kv_head][:, :HD] for kv_head in range(KVH)]
        value_grads = [kv_totals[kv_head][:, HD:] for kv_head in range(KVH)]
        d_qkv = jnp.concatenate(query_grads + [jnp.concatenate(key_grads, axis=1).astype(bf_type), jnp.concatenate(value_grads, axis=1).astype(bf_type)], axis=1)
        g_mamba_in = jnp.dot(normed.T, d_proj, preferred_element_type=fl_type)
        g_step_in = jnp.dot(normed.T, d_step, preferred_element_type=fl_type)
        g_attn_in = jnp.dot(normed.T, d_qkv, preferred_element_type=fl_type)
        d_normed = jnp.dot(d_proj, mamba_in.T, preferred_element_type=fl_type) + jnp.dot(d_step, step_in.T, preferred_element_type=fl_type) + jnp.dot(d_qkv, attn_in.T, preferred_element_type=fl_type)
        g_norm_gain = lax.optimization_barrier(jnp.sum(d_normed * first_norm, axis=0))
        d_first = d_normed * first_gain
        grad_tok = d_mixed + first_scale * (d_first - first_norm * lax.optimization_barrier(jnp.mean(d_first * first_norm, axis=-1, keepdims=True)))
        terms = (g_norm_gain, g_mamba_in, g_step_in, g_attn_in, taps_total, bias_total, step_total, decay_total, skip_total, g_gated_gain, g_mamba_out, g_attn_out, g_ffn_gain, g_gate_up, g_down)
        totals = jax.tree.map(lambda acc_val, term: acc_val + term, totals, terms)
        return (totals, (layer_out, grad_tok))
    zeros = (jnp.zeros((D,), fl_type), jnp.zeros((D, 2 * DI + 2 * NST), fl_type), jnp.zeros((D, MH), fl_type), jnp.zeros((D, (QH + 2 * KVH) * HD), fl_type), jnp.zeros((KC, CONV_CH), fl_type), jnp.zeros((CONV_CH,), fl_type), jnp.zeros((MH,), fl_type), jnp.zeros((MH,), fl_type), jnp.zeros((MH,), fl_type), jnp.zeros((DI,), fl_type), jnp.zeros((DI, D), fl_type), jnp.zeros((QH * HD, D), fl_type), jnp.zeros((D,), fl_type), jnp.zeros((D, 2 * FF), fl_type), jnp.zeros((FF, D), fl_type))
    totals, stacked = lax.scan(one_pack, zeros, (hidden_in, grad_out, segments))
    return (stacked[0], stacked[1], totals[0], totals[1], totals[2], totals[3], totals[4], totals[5], totals[6], totals[7], totals[8], totals[9], totals[10], totals[11], totals[12], totals[13], totals[14])
```

```python
from functools import partial
import math

import jax
import jax.numpy as jnp
from jax import lax
from jax.experimental import pallas as pl
from jax.experimental.pallas import tpu as pltpu
from jax.sharding import PartitionSpec as P

MH = 24
HD = 64
NST = 128
KC = 4
QH = 8
KVH = 2
FF = 2048
DI = 1536


EPS = 1e-05
ROPE_THETA = 10000.0

MESH = pl.DeviceIdType.MESH
VMEM_LIMIT = 56 * 2**20
HIGHEST = lax.Precision.HIGHEST


def rcopy(src, dst, send, recv, device):
    return pltpu.make_async_remote_copy(
        src_ref=src,
        dst_ref=dst,
        send_sem=send,
        recv_sem=recv,
        device_id=device,
        device_id_type=MESH,
    )


class Place:
    def __init__(self, seq_count, fsdp_count):
        self.s = lax.axis_index("seq")
        self.f = lax.axis_index("fsdp")
        self.count = fsdp_count
        self.L = fsdp_count // 2
        self.z = self.f // 2
        self.y = self.f % 2
        self.has_right = self.z < self.L - 1
        self.has_left = self.z > 0
        self.right = (self.s, jnp.minimum(self.f + 2, fsdp_count - 1))
        self.left = (self.s, jnp.maximum(self.f - 2, 0))
        self.pair = (self.s, self.f + 1 - 2 * self.y)
        self.s1 = self.s + 1 - 2 * (self.s % 2)
        self.s2 = (self.s + 2) % 4
        self.s3 = 3 - self.s
        self.sib = (self.s1, self.f)
        self.across = (self.s2, self.f)
        self.diag = (self.s3, self.f)

    def greet(self, line=True, pair=True, diag=False):
        barrier = pltpu.get_barrier_semaphore()

        def hello(device):
            pl.semaphore_signal(barrier, inc=1, device_id=device, device_id_type=MESH)

        amount = 2
        hello(self.sib)
        hello(self.across)
        if diag:
            hello(self.diag)
            amount = amount + 1
        if pair:
            hello(self.pair)
            amount = amount + 1
        if line:

            @pl.when(self.has_right)
            def _():
                hello(self.right)

            @pl.when(self.has_left)
            def _():
                hello(self.left)

            amount = amount + jnp.where(self.has_right, 1, 0) + jnp.where(self.has_left, 1, 0)
        pl.semaphore_wait(barrier, amount)


class SeqGather:
    def __init__(self, place, src, out, send, recv):
        p = place
        self.own_sib = rcopy(src, out.at[p.s], send.at[0], recv.at[0], p.sib)
        self.own_across = rcopy(src, out.at[p.s], send.at[1], recv.at[1], p.across)
        self.forward_copy = rcopy(out.at[p.s2], out.at[p.s2], send.at[2], recv.at[2], p.sib)
        self.got_sib = rcopy(src, out.at[p.s1], send.at[0], recv.at[0], p.sib)
        self.got_across = rcopy(src, out.at[p.s2], send.at[1], recv.at[1], p.across)
        self.got_diag = rcopy(src, out.at[p.s3], send.at[2], recv.at[2], p.sib)

    def start(self):
        self.own_across.start()
        self.own_sib.start()

    def wait_sib(self):
        self.got_sib.wait_recv()

    def forward(self):
        self.got_across.wait_recv()
        self.forward_copy.start()

    def wait_diag(self):
        self.got_diag.wait_recv()

    def wait_sends(self):
        self.own_sib.wait_send()
        self.own_across.wait_send()
        self.forward_copy.wait_send()

    def finish(self):
        self.wait_sib()
        self.wait_diag()
        self.wait_sends()


class SeqReduce:
    def __init__(self, place, stage, got, send, recv):
        p = place
        self.stage, self.got = stage, got
        self.copies = [
            rcopy(stage.at[0], got.at[0], send.at[0], recv.at[0], p.sib),
            rcopy(stage.at[1], got.at[1], send.at[1], recv.at[1], p.sib),
            rcopy(stage.at[2], got.at[2], send.at[2], recv.at[2], p.across),
        ]

    def send_diag(self, value):
        self.stage[0] = value.astype(self.stage.dtype)
        self.copies[0].start()

    def send_sib(self, value):
        self.stage[1] = value.astype(self.stage.dtype)
        self.copies[1].start()

    def send_across(self, value):
        self.copies[0].wait_recv()
        self.stage[2] = (value + self.got[0].astype(jnp.float32)).astype(self.stage.dtype)
        self.copies[2].start()

    def total(self, value):
        self.copies[1].wait_recv()
        self.copies[2].wait_recv()
        return value + self.got[1].astype(jnp.float32) + self.got[2].astype(jnp.float32)

    def wait_sends(self):
        for copy in self.copies:
            copy.wait_send()


class LineGather:
    def __init__(self, place, out, send, recv, pair=True):
        self.p, self.out, self.send, self.recv, self.pair = place, out, send, recv, pair

    def at(self, b, other=0):
        p = self.p
        if not self.pair:
            return b
        return 2 * b + (1 - p.y if other else p.y)

    def copy(self, b, way):
        p = self.p
        ref = self.out.at[self.at(b)]
        device = (p.right, p.left, p.pair)[way]
        return rcopy(ref, ref, self.send.at[way, b], self.recv.at[self.at(b)], device)

    def push(self, b, right, left):
        if right:

            @pl.when(self.p.has_right)
            def _():
                self.copy(b, 0).start()

        if left:

            @pl.when(self.p.has_left)
            def _():
                self.copy(b, 1).start()

        if self.pair:
            self.copy(b, 2).start()

    def start(self):
        self.push(self.p.z, True, True)

    def step(self, d):
        p = self.p

        @pl.when(p.z - d >= 0)
        def _():
            self.copy(p.z - d, 0).wait_recv()
            self.push(p.z - d, True, False)

        @pl.when(p.z + d <= p.L - 1)
        def _():
            self.copy(p.z + d, 0).wait_recv()
            self.push(p.z + d, False, True)

    def finish(self):
        p = self.p

        def each(b, carry):
            if self.pair:
                ref = self.out.at[self.at(b, 1)]
                rcopy(ref, ref, self.send.at[2, b], self.recv.at[self.at(b, 1)], p.pair).wait_recv()
                self.copy(b, 2).wait_send()

            @pl.when(p.has_right & (b <= p.z))
            def _():
                self.copy(b, 0).wait_send()

            @pl.when(p.has_left & (b >= p.z))
            def _():
                self.copy(b, 1).wait_send()

            return carry

        lax.fori_loop(0, p.L, each, 0)


def loop(count, body):
    def step(index, carry):
        body(index)
        return carry

    lax.fori_loop(0, count, step, 0)


def add_rows(target, *parts):
    def some(index):
        at = pl.ds(pl.multiple_of(index * 16, 16), 16)
        total = parts[0][at].astype(jnp.float32)
        for part in parts[1:]:
            total = total + part[at].astype(jnp.float32)
        target[at] = total.astype(target.dtype)

    loop(target.shape[0] // 16, some)


CHUNKS = 4


def gather_kernel(
    seq_count,
    fsdp_count,
    x_width,
    query_width,
    ff_width,
    hidden,
    cot,
    mamba_in,
    attn_in,
    small,
    gate_up,
    out_pack,
    w_in,
    w_gu,
    w_out,
    hidden_all,
    cot_all,
    local,
    in_send,
    in_recv,
    gu_send,
    gu_recv,
    out_send,
    out_recv,
    hid_send,
    hid_recv,
    cot_send,
    cot_recv,
):
    p = Place(seq_count, fsdp_count)
    s, f, z, y, L = p.s, p.f, p.z, p.y, p.L
    per = fsdp_count // seq_count
    half = per // 2

    def part(ref, start, size, unit):
        return ref.at[:, pl.ds(pl.multiple_of(start, unit), size)]

    bc = mamba_in.shape[1] - 2 * DI
    copies = []

    def bring(src, dst):
        copy = pltpu.make_async_copy(src, dst, local.at[len(copies)])
        copy.start()
        copies.append(copy)

    own = w_in.at[f]
    c0 = 0
    bring(part(mamba_in, s * x_width, x_width, 128), own.at[:, pl.ds(c0, x_width)])
    c0 += x_width
    bring(part(mamba_in, DI + s * x_width, x_width, 128), own.at[:, pl.ds(c0, x_width)])
    c0 += x_width
    bring(mamba_in.at[:, pl.ds(2 * DI, bc)], own.at[:, pl.ds(c0, bc)])
    c0 += bc
    bring(part(attn_in, s * query_width, query_width, 128), own.at[:, pl.ds(c0, query_width)])
    c0 += query_width
    bring(small, own.at[:, pl.ds(c0, small.shape[1])])
    own = w_gu.at[f]
    bring(part(gate_up, s * ff_width, ff_width, 128), own.at[:, pl.ds(0, ff_width)])
    bring(part(gate_up, FF + s * ff_width, ff_width, 128), own.at[:, pl.ds(ff_width, ff_width)])
    bring(hidden, hidden_all.at[s])
    bring(cot, cot_all.at[s])
    holder = f // per == s
    chunk = w_out.shape[1] // CHUNKS
    out_local = local.at[len(copies)]

    @pl.when(holder)
    def _():
        pltpu.make_async_copy(out_pack, w_out.at[f - s * per], out_local).start()

    p.greet()
    hid = SeqGather(p, hidden, hidden_all, hid_send, hid_recv)
    cots = SeqGather(p, cot, cot_all, cot_send, cot_recv)
    hid.start()
    cots.start()
    for copy in copies:
        copy.wait()

    @pl.when(holder)
    def _():
        pltpu.make_async_copy(out_pack, w_out.at[f - s * per], out_local).wait()

    ins = LineGather(p, w_in, in_send, in_recv)
    gus = LineGather(p, w_gu, gu_send, gu_recv)
    ins.start()
    gus.start()
    hid.forward()
    cots.forward()

    def hop(d):
        ins.step(d + 1)
        gus.step(d + 1)

    loop(L - 1, hop)

    def out_copy(i, c, other, way):
        ref = w_out.at[2 * i + (1 - y if other else y), pl.ds(pl.multiple_of(c * chunk, 16), chunk)]
        device = (p.right, p.left, p.pair)[way]
        return rcopy(ref, ref, out_send.at[way, i, c], out_recv.at[way // 2, i, c], device)

    def spread(index):
        i, c = index // CHUNKS, index % CHUNKS
        zs = s * half + i

        @pl.when(z != zs)
        def _():
            out_copy(i, c, 0, 0).wait_recv()

        @pl.when((z >= zs) & p.has_right)
        def _():
            out_copy(i, c, 0, 0).start()

        @pl.when((z <= zs) & p.has_left)
        def _():
            out_copy(i, c, 0, 1).start()

        out_copy(i, c, 0, 2).start()

    loop(half * CHUNKS, spread)

    def spread_end(index):
        i, c = index // CHUNKS, index % CHUNKS
        zs = s * half + i
        out_copy(i, c, 1, 2).wait_recv()
        out_copy(i, c, 0, 2).wait_send()

        @pl.when((z >= zs) & p.has_right)
        def _():
            out_copy(i, c, 0, 0).wait_send()

        @pl.when((z <= zs) & p.has_left)
        def _():
            out_copy(i, c, 0, 1).wait_send()

    loop(half * CHUNKS, spread_end)
    ins.finish()
    gus.finish()
    hid.finish()
    cots.finish()


def dma(*shape):
    return pltpu.SemaphoreType.DMA(shape)


def gather_all(seq_count, fsdp_count, widths, arrays):
    hidden, cot, mamba_in, attn_in, small, gate_up, out_pack = arrays
    x_width, query_width, ff_width = widths
    own_rows = mamba_in.shape[0]
    per = fsdp_count // seq_count
    bc = mamba_in.shape[1] - 2 * DI
    in_width = 2 * x_width + bc + query_width + small.shape[1]
    bf = jnp.bfloat16
    L = fsdp_count // 2
    return pl.pallas_call(
        partial(gather_kernel, seq_count, fsdp_count, x_width, query_width, ff_width),
        out_shape=[
            jax.ShapeDtypeStruct((fsdp_count, own_rows, in_width), bf),
            jax.ShapeDtypeStruct((fsdp_count, own_rows, 2 * ff_width), bf),
            jax.ShapeDtypeStruct((per,) + out_pack.shape, bf),
            jax.ShapeDtypeStruct((seq_count,) + hidden.shape, bf),
            jax.ShapeDtypeStruct((seq_count,) + cot.shape, bf),
        ],
        in_specs=[pl.BlockSpec(memory_space=pl.ANY)] * 7,
        out_specs=[pl.BlockSpec(memory_space=pl.ANY)] * 5,
        scratch_shapes=[
            dma(10),
            dma(3, L),
            dma(fsdp_count),
            dma(3, L),
            dma(fsdp_count),
            dma(3, per // 2, CHUNKS),
            dma(2, per // 2, CHUNKS),
            dma(3),
            dma(3),
            dma(3),
            dma(3),
        ],
        compiler_params=pltpu.CompilerParams(collective_id=0, has_side_effects=True),
        name="gather_weights",
    )(*arrays)


def mid_kernel(
    seq_count,
    fsdp_count,
    gated,
    attn_mix,
    w_mo,
    w_ao,
    w_dn,
    w_gu,
    hidden,
    cot_own,
    cot_all,
    mixer_gain,
    ffn_gain,
    layer_out,
    d_mixed,
    ffn_in,
    ffn_act,
    d_ffn,
    d_mixed_all,
    gated_b,
    d_gated,
    d_attn,
    g_ffn_gain,
    g_gated_gain,
    part_mix,
    gate_vals,
    d_act,
    d_gn,
    mixed,
    norm2,
    sq_buf,
    mean_buf,
    stage,
    got,
    seq_send,
    seq_recv,
):
    p = Place(seq_count, fsdp_count)
    s = p.s
    fl, bf = jnp.float32, jnp.bfloat16
    rows = cot_own.shape[0]
    model = cot_own.shape[1]
    ff = w_dn.shape[0]
    peers = (p.sib, p.across, p.diag)
    peer_at = (p.s1, p.s2, p.s3)

    def dot(a, b):
        return jnp.dot(a, b, preferred_element_type=fl)

    def dot_t(a, b):
        return lax.dot_general(a, b, (((1,), (1,)), ((), ())), preferred_element_type=fl)

    def row_sums(values):
        ones = jnp.ones((8, values.shape[1]), fl)
        return lax.dot_general(
            ones, values, (((1,), (1,)), ((), ())), preferred_element_type=fl, precision=HIGHEST
        )

    def exchange(buf, at):
        copies = []
        for k in range(3):
            copy = rcopy(buf.at[s], buf.at[s], seq_send.at[at, k], seq_recv.at[at, k], peers[k])
            copy.start()
            got_it = rcopy(
                buf.at[peer_at[k]], buf.at[peer_at[k]], seq_send.at[at, k], seq_recv.at[at, k], peers[k]
            )
            copies.append((copy, got_it))

        def end():
            for copy, got_it in copies:
                got_it.wait_recv()
                copy.wait_send()
            total = buf[0] + buf[1] + buf[2] + buf[3]
            return total

        return end

    for r in range(4):
        values = gated[r]
        sq_buf[s, :, r * rows : (r + 1) * rows] = row_sums(values * values)
    p.greet(line=False, pair=False, diag=True)
    sq_end = exchange(sq_buf, 0)
    gain = mixer_gain[...]
    for r in range(4):
        part_mix[r] = dot((gated[r] * gain).astype(bf), w_mo[...])
    sq_total = sq_end()
    scale_cols = lax.rsqrt(sq_total / DI + EPS).T

    for r in range(4):
        scale = scale_cols[r * rows : (r + 1) * rows, 0:1]
        part_mix[r] = part_mix[r] * scale + dot(attn_mix[r], w_ao[...])
        gated_norm = gated[r] * scale
        gated_b[r] = (gated_norm * gain).astype(bf)

    def reducer(at):
        return SeqReduce(p, stage.at[at], got.at[at], seq_send.at[at + 1], seq_recv.at[at + 1])

    mix = reducer(0)
    mix.send_diag(part_mix[p.s3])
    mix.send_sib(part_mix[p.s1])
    mix.send_across(part_mix[p.s2])
    d_act[0] = dot_t(cot_all[0], w_dn[...])
    d_act[1] = dot_t(cot_all[1], w_dn[...])
    residual = hidden[...].astype(fl)
    mixed[...] = residual + mix.total(part_mix[s])
    scale2 = lax.rsqrt(jnp.mean(mixed[...] * mixed[...], axis=-1, keepdims=True) + EPS)
    norm2[...] = mixed[...] * scale2
    ffn_in[s] = (norm2[...] * ffn_gain[...]).astype(bf)
    ffn_all = SeqGather(p, ffn_in.at[s], ffn_in, seq_send.at[4], seq_recv.at[4])
    ffn_all.start()

    def ffn_block(r):
        gate_vals[r] = dot(ffn_in[r], w_gu[...])

    def act_block(r):
        gate_lin = gate_vals[r, :, :ff]
        up_lin = gate_vals[r, :, ff:]
        sigma = jax.nn.sigmoid(gate_lin)
        act = gate_lin * sigma
        ffn_act[r] = (act * up_lin).astype(bf)
        slope = sigma * (1.0 + gate_lin * (1.0 - sigma))
        da = d_act[r]
        d_ffn[r, :, :ff] = (da * up_lin * slope).astype(bf)
        d_ffn[r, :, ff:] = (da * act).astype(bf)

    d_act[2] = dot_t(cot_all[2], w_dn[...])
    d_act[3] = dot_t(cot_all[3], w_dn[...])
    ffn_block(s)
    act_block(s)
    ffn_all.wait_sib()
    ffn_block(p.s1)
    ffn_all.forward()
    act_block(p.s1)
    ffn_block(p.s2)
    act_block(p.s2)
    ffn_all.wait_diag()
    ffn_block(p.s3)
    act_block(p.s3)
    back = reducer(1)
    back.send_diag(dot_t(d_ffn[p.s3], w_gu[...]))
    back.send_sib(dot_t(d_ffn[p.s1], w_gu[...]))
    back.send_across(dot_t(d_ffn[p.s2], w_gu[...]))
    out = reducer(2)
    d_ffn_own = dot_t(d_ffn[s], w_gu[...])
    d_ffn_in = back.total(d_ffn_own)
    g_ffn_gain[...] = jnp.sum(d_ffn_in * norm2[...], axis=0, keepdims=True)
    d_second = d_ffn_in * ffn_gain[...]
    d_mixed[...] = cot_own[...].astype(fl) + scale2 * (
        d_second - norm2[...] * jnp.mean(d_second * norm2[...], axis=-1, keepdims=True)
    )
    d_mixed_all[s] = d_mixed[...].astype(bf)
    back_all = SeqGather(p, d_mixed_all.at[s], d_mixed_all, seq_send.at[5], seq_recv.at[5])
    back_all.start()
    out.send_diag(dot(ffn_act[p.s3], w_dn[...]))
    out.send_sib(dot(ffn_act[p.s1], w_dn[...]))

    def mixer_block(r):
        block = d_mixed_all[r]
        d_gated_b = dot_t(block, w_mo[...])
        d_gn[r] = d_gated_b
        d_attn[r] = dot_t(block, w_ao[...]).astype(bf)

    mixer_block(s)
    back_all.wait_sib()
    mixer_block(p.s1)
    out.send_across(dot(ffn_act[p.s2], w_dn[...]))
    back_all.forward()
    mixer_block(p.s2)
    back_all.wait_diag()
    mixer_block(p.s3)
    for r in range(4):
        scale = scale_cols[r * rows : (r + 1) * rows, 0:1]
        values = d_gn[r] * gain * (gated[r] * scale)
        mean_buf[s, :, r * rows : (r + 1) * rows] = row_sums(values)
    mean_end = exchange(mean_buf, 6)
    layer_out[...] = (mixed[...] + out.total(dot(ffn_act[s], w_dn[...]))).astype(bf)
    gain_total = jnp.zeros_like(g_gated_gain[...])
    for r in range(4):
        scale = scale_cols[r * rows : (r + 1) * rows, 0:1]
        gain_total = gain_total + jnp.sum(d_gn[r] * (gated[r] * scale), axis=0, keepdims=True)
    g_gated_gain[...] = gain_total
    means = (mean_end() / DI).T
    for r in range(4):
        scale = scale_cols[r * rows : (r + 1) * rows, 0:1]
        mean = means[r * rows : (r + 1) * rows, 0:1]
        d_gated[r] = scale * (d_gn[r] * gain - (gated[r] * scale) * mean)
    mix.wait_sends()
    back.wait_sends()
    out.wait_sends()
    ffn_all.wait_sends()
    back_all.wait_sends()


def middle(seq_count, fsdp_count, arrays):
    gated, attn_mix, w_mo, w_ao, w_dn, w_gu, hidden = arrays[:7]
    fl, bf = jnp.float32, jnp.bfloat16
    rows, model = hidden.shape
    ff = w_dn.shape[0]
    n = seq_count
    total = n * rows

    def sds(*shape, dtype=bf):
        return jax.ShapeDtypeStruct(shape, dtype)

    return pl.pallas_call(
        partial(mid_kernel, seq_count, fsdp_count),
        out_shape=[
            sds(rows, model),
            sds(rows, model, dtype=fl),
            sds(n, rows, model),
            sds(n, rows, ff),
            sds(n, rows, 2 * ff),
            sds(n, rows, model),
            sds(*gated.shape),
            sds(*gated.shape, dtype=fl),
            sds(*attn_mix.shape),
            sds(1, model, dtype=fl),
            sds(1, gated.shape[2], dtype=fl),
        ],
        in_specs=[pl.BlockSpec(memory_space=pltpu.VMEM)] * len(arrays),
        out_specs=[pl.BlockSpec(memory_space=pltpu.VMEM)] * 11,
        scratch_shapes=[
            pltpu.VMEM((n, rows, model), fl),
            pltpu.VMEM((n, rows, 2 * ff), fl),
            pltpu.VMEM((n, rows, ff), fl),
            pltpu.VMEM(gated.shape, fl),
            pltpu.VMEM((rows, model), fl),
            pltpu.VMEM((rows, model), fl),
            pltpu.VMEM((n, 8, total), fl),
            pltpu.VMEM((n, 8, total), fl),
            pltpu.VMEM((3, 3, rows, model), bf),
            pltpu.VMEM((3, 3, rows, model), bf),
            dma(7, 3),
            dma(7, 3),
        ],
        compiler_params=pltpu.CompilerParams(
            collective_id=1, has_side_effects=True, vmem_limit_bytes=VMEM_LIMIT
        ),
        name="ffn_middle",
    )(*arrays)


class LineReduce:
    def __init__(self, place, g, pair_got, side_got, acc, send, recv):
        self.p, self.g, self.pair_got, self.side_got, self.acc = place, g, pair_got, side_got, acc
        self.send, self.recv = send, recv

    def pair_copy(self, b):
        p = self.p
        return rcopy(
            self.g.at[2 * b + 1 - p.y],
            self.pair_got.at[b],
            self.send.at[0, b],
            self.recv.at[0, b],
            p.pair,
        )

    def each_from_far(self, body):
        p = self.p

        def step(k):
            d = p.L - 1 - k

            @pl.when(p.z + d <= p.L - 1)
            def _():
                body(p.z + d)

            @pl.when((d > 0) & (p.z - d >= 0))
            def _():
                body(p.z - d)

        loop(p.L, step)

    def start(self):
        self.each_from_far(lambda b: self.pair_copy(b).start())

    def got_from(self, b, right):
        p = self.p
        slot = b if right else b + p.L
        ref = self.side_got.at[slot]
        rcopy(ref, ref, self.send.at[1, b], self.recv.at[1, slot], p.right).wait_recv()
        return ref

    def pass_on(self, b, right):
        p = self.p
        self.pair_copy(b).wait_recv()
        mine, other = self.g.at[2 * b + p.y], self.pair_got.at[b]
        inner = p.has_left if right else p.has_right

        @pl.when(inner)
        def _():
            add_rows(other, mine, other, self.got_from(b, right))

        @pl.when(jnp.logical_not(inner))
        def _():
            add_rows(other, mine, other)

        slot = b if right else b + p.L
        rcopy(
            other,
            self.side_got.at[slot],
            self.send.at[1, b],
            self.recv.at[1, slot],
            p.right if right else p.left,
        ).start()

    def step(self, k):
        p = self.p
        d = p.L - 1 - k

        @pl.when(p.z + d <= p.L - 1)
        def _():
            self.pass_on(p.z + d, True)

        @pl.when(p.z - d >= 0)
        def _():
            self.pass_on(p.z - d, False)

    def total(self, target):
        p = self.p
        b = p.z
        self.pair_copy(b).wait_recv()
        add_rows(self.acc, self.g.at[2 * b + p.y], self.pair_got.at[b])

        @pl.when(p.has_left)
        def _():
            add_rows(self.acc, self.acc, self.got_from(b, True))

        @pl.when(p.has_right)
        def _():
            add_rows(self.acc, self.acc, self.got_from(b, False))

        add_rows(target, self.acc)

    def wait_sends(self):
        p = self.p

        def each(b):
            self.pair_copy(b).wait_send()

            @pl.when(b != p.z)
            def _():
                ref = self.pair_got.at[b]
                rcopy(ref, ref, self.send.at[1, b], self.recv.at[1, b], p.right).wait_send()

        loop(p.L, each)


def reduce_kernel(
    seq_count,
    fsdp_count,
    g_in,
    g_gu,
    g_out,
    small,
    d_norm,
    in_got,
    gu_got,
    out_got,
    small_got,
    d_norm_sum,
    in_pair,
    in_side,
    in_acc,
    gu_pair,
    gu_side,
    gu_acc,
    out_pair,
    out_side,
    out_acc,
    small_pair,
    small_line,
    stage,
    got,
    in_send,
    in_recv,
    gu_send,
    gu_recv,
    out_send,
    out_recv,
    cast_send,
    cast_recv,
    small_send,
    small_recv,
    sp_send,
    sp_recv,
    seq_send,
    seq_recv,
):
    p = Place(seq_count, fsdp_count)
    s, f, z, y, L = p.s, p.f, p.z, p.y, p.L
    per = fsdp_count // seq_count
    half = per // 2
    fl = jnp.float32
    chunk = g_out.shape[1] // CHUNKS
    p.greet()
    pair_small = rcopy(small, small_pair, sp_send.at[0], sp_recv.at[0], p.pair)
    pair_small.start()

    def rows_of(c):
        return pl.ds(pl.multiple_of(c * chunk, 16), chunk)

    def out_pair_copy(i, c):
        return rcopy(
            g_out.at[2 * i + 1 - y, rows_of(c)],
            out_pair.at[i, rows_of(c)],
            out_send.at[0, i, c],
            out_recv.at[0, i, c],
            p.pair,
        )

    def side_copy(i, c, right):
        at = 0 if right else 1
        return rcopy(
            out_pair.at[i, rows_of(c)],
            out_side.at[at, i, rows_of(c)],
            out_send.at[1, i, c],
            out_recv.at[1 + at, i, c],
            p.right if right else p.left,
        )

    ins = LineReduce(p, g_in, in_pair, in_side, in_acc, in_send, in_recv)
    gus = LineReduce(p, g_gu, gu_pair, gu_side, gu_acc, gu_send, gu_recv)
    d_sum = SeqReduce(p, stage, got, seq_send.at[0], seq_recv.at[0])
    loop(half * CHUNKS, lambda index: out_pair_copy(index // CHUNKS, index % CHUNKS).start())
    gus.start()
    ins.start()
    d_sum.send_diag(d_norm[p.s3])
    d_sum.send_sib(d_norm[p.s1])
    d_sum.send_across(d_norm[p.s2].astype(fl))
    pair_small.wait_recv()
    small_line[z] = small[...] + small_pair[...]
    smalls = LineGather(p, small_line, small_send, small_recv, pair=False)
    smalls.start()
    loop(L - 1, lambda d: smalls.step(d + 1))
    smalls.finish()
    pair_small.wait_send()
    small_sum = small_line[0]
    for b in range(1, L):
        small_sum = small_sum + small_line[b]
    small_got[s] = small_sum
    small_all = SeqGather(p, small_got.at[s], small_got, seq_send.at[1], seq_recv.at[1])
    small_all.start()
    d_norm_sum[...] = d_sum.total(d_norm[s].astype(fl))

    def cast(c, way):
        ref = out_got.at[rows_of(c)]
        return rcopy(ref, ref, cast_send.at[way, c], cast_recv.at[c], p.across if way else p.sib)

    def out_step(index):
        i, c = index // CHUNKS, index % CHUNKS
        zs = s * half + i
        out_pair_copy(i, c).wait_recv()
        mine = g_out.at[2 * i + y, rows_of(c)]
        other = out_pair.at[i, rows_of(c)]
        add_rows(out_acc, mine, other)

        @pl.when(p.has_left & (z <= zs))
        def _():
            side_copy(i, c, True).wait_recv()
            add_rows(out_acc, out_acc, out_side.at[0, i, rows_of(c)])

        @pl.when(p.has_right & (z >= zs))
        def _():
            side_copy(i, c, False).wait_recv()
            add_rows(out_acc, out_acc, out_side.at[1, i, rows_of(c)])

        @pl.when(z == zs)
        def _():
            add_rows(out_got.at[rows_of(c)], out_acc)
            cast(c, 1).start()
            cast(c, 0).start()

        @pl.when(z < zs)
        def _():
            add_rows(other, out_acc)
            side_copy(i, c, True).start()

        @pl.when(z > zs)
        def _():
            add_rows(other, out_acc)
            side_copy(i, c, False).start()

    loop(half * CHUNKS, out_step)
    small_all.forward()
    loop(L - 1, gus.step)
    gus.total(gu_got.at[s])
    gu_all = SeqGather(p, gu_got.at[s], gu_got, seq_send.at[2], seq_recv.at[2])
    gu_all.start()
    holder = f // per
    moved = (s + 4 - holder) % 4
    is_across = moved == 2

    @pl.when(is_across)
    def _():
        def pass_cast(c):
            cast(c, 0).wait_recv()
            cast(c, 0).start()

        loop(CHUNKS, pass_cast)

    loop(L - 1, ins.step)
    gu_all.forward()
    ins.total(in_got.at[s])
    in_all = SeqGather(p, in_got.at[s], in_got, seq_send.at[3], seq_recv.at[3])
    in_all.start()

    @pl.when((s != holder) & jnp.logical_not(is_across))
    def _():
        loop(CHUNKS, lambda c: cast(c, 0).wait_recv())

    @pl.when(s == holder)
    def _():
        def sent(c):
            cast(c, 0).wait_send()
            cast(c, 1).wait_send()

        loop(CHUNKS, sent)

    @pl.when(is_across)
    def _():
        loop(CHUNKS, lambda c: cast(c, 0).wait_send())

    def out_sent(index):
        i, c = index // CHUNKS, index % CHUNKS
        out_pair_copy(i, c).wait_send()

        @pl.when(z != s * half + i)
        def _():
            side_copy(i, c, True).wait_send()

    loop(half * CHUNKS, out_sent)
    gus.wait_sends()
    ins.wait_sends()
    d_sum.wait_sends()
    small_all.finish()
    gu_all.finish()
    in_all.forward()
    in_all.finish()


def reduce_all(seq_count, fsdp_count, arrays):
    g_in, g_gu, g_out, small, d_norm = arrays
    fl, bf = jnp.float32, jnp.bfloat16
    L = fsdp_count // 2
    per = fsdp_count // seq_count
    n = seq_count
    own, in_w = g_in.shape[1:]
    gu_w = g_gu.shape[2]
    out_rows, model = g_out.shape[1:]
    rows = d_norm.shape[1]
    v = pltpu.VMEM
    return pl.pallas_call(
        partial(reduce_kernel, seq_count, fsdp_count),
        out_shape=[
            jax.ShapeDtypeStruct((n, own, in_w), bf),
            jax.ShapeDtypeStruct((n, own, gu_w), bf),
            jax.ShapeDtypeStruct((out_rows, model), bf),
            jax.ShapeDtypeStruct((n,) + small.shape, fl),
            jax.ShapeDtypeStruct((rows, model), fl),
        ],
        in_specs=[pl.BlockSpec(memory_space=v)] * 5,
        out_specs=[pl.BlockSpec(memory_space=v)] * 5,
        scratch_shapes=[
            v((L, own, in_w), bf),
            v((2 * L, own, in_w), bf),
            v((own, in_w), fl),
            v((L, own, gu_w), bf),
            v((2 * L, own, gu_w), bf),
            v((own, gu_w), fl),
            v((per // 2, out_rows, model), bf),
            v((2, per // 2, out_rows, model), bf),
            v((out_rows // CHUNKS, model), fl),
            v(small.shape, fl),
            v((L,) + small.shape, fl),
            v((3, rows, model), bf),
            v((3, rows, model), bf),
            dma(2, L),
            dma(2, 2 * L),
            dma(2, L),
            dma(2, 2 * L),
            dma(2, per // 2, CHUNKS),
            dma(3, per // 2, CHUNKS),
            dma(2, CHUNKS),
            dma(CHUNKS),
            dma(3, L),
            dma(L),
            dma(1),
            dma(1),
            dma(4, 3),
            dma(4, 3),
        ],
        compiler_params=pltpu.CompilerParams(
            collective_id=2, has_side_effects=True, vmem_limit_bytes=VMEM_LIMIT
        ),
        name="reduce_grads",
    )(*arrays)


def rms_scale(values):
    return lax.rsqrt(jnp.mean(values * values, axis=-1, keepdims=True) + EPS)


def swish_slope(values):
    sigma = jax.nn.sigmoid(values)
    return sigma * (1.0 + values * (1.0 - sigma))


def core_inputs(seg_ids, inputs, params):
    pre_conv, step_raw, query_in, key_in = inputs
    taps, tap_bias, step_bias, log_decay = params
    row_count = pre_conv.shape[0]
    tap_count = taps.shape[0]
    accum = tap_bias[None, :] + taps[tap_count - 1][None, :] * pre_conv
    for lag_step in range(1, tap_count):
        moved = jnp.concatenate(
            [
                jnp.zeros((lag_step, pre_conv.shape[1]), pre_conv.dtype),
                pre_conv[: row_count - lag_step],
            ],
            axis=0,
        )
        prior = jnp.concatenate(
            [jnp.full((lag_step,), -1, jnp.int32), seg_ids[: row_count - lag_step]]
        )
        same_seq = (prior == seg_ids)[:, None]
        accum = accum + taps[tap_count - 1 - lag_step][None, :] * jnp.where(same_seq, moved, 0.0)
    activated = jax.nn.silu(accum)
    step = jax.nn.softplus(step_raw + step_bias[None, :])
    log_step = -jnp.exp(log_decay)[None, :] * step
    positions = jnp.arange(row_count, dtype=jnp.int32)
    first_count = jnp.sum((seg_ids == 0).astype(jnp.int32))
    place = (positions - jnp.where(seg_ids == 0, 0, first_count)).astype(jnp.float32)
    half = HD // 2
    freqs = jnp.exp(-math.log(ROPE_THETA) * 2.0 * jnp.arange(half, dtype=jnp.float32) / HD)
    angles = place[:, None] * freqs[None, :]
    cosine = jnp.cos(angles)[:, None, :]
    sine = jnp.sin(angles)[:, None, :]

    def rotate(tensor):
        heads = tensor.reshape(row_count, -1, HD)
        first_half = heads[..., :half]
        second_half = heads[..., half:]
        return jnp.concatenate(
            [first_half * cosine - second_half * sine, second_half * cosine + first_half * sine],
            axis=-1,
        ).reshape(tensor.shape)

    return activated, step, log_step, rotate(query_in), rotate(key_in)


def shards(
    hidden_in,
    grad_out,
    segments,
    norm_gain,
    mamba_in,
    step_in,
    attn_in,
    conv_taps,
    conv_bias,
    step_bias,
    log_decay,
    skip_gain,
    gated_gain,
    mamba_out,
    attn_out,
    ffn_gain,
    gate_up,
    down_proj,
):
    bf_type = jnp.bfloat16
    fl_type = jnp.float32
    seq_count = lax.axis_size("seq")
    seq_index = lax.axis_index("seq")
    fsdp_count = lax.axis_size("fsdp")
    block_rows = hidden_in.shape[1]
    model = hidden_in.shape[2]
    rows = block_rows * seq_count
    own_rows = model // fsdp_count
    x_width = DI // seq_count
    head_share = MH // seq_count
    query_width = QH * HD // seq_count
    query_share = QH // seq_count
    ff_width = FF // seq_count
    owners = [group * KVH // seq_count for group in range(seq_count)]
    owner = seq_index * KVH // seq_count
    gain_own = DI // fsdp_count
    gain_cols = -(-gain_own // own_rows)

    def cols(array, start, size):
        return lax.dynamic_slice_in_dim(array, start, size, 1)

    gain_pad = jnp.pad(gated_gain, (0, gain_cols * own_rows - gain_own))
    main_width = 2 * x_width + 2 * NST + query_width + 2 * HD
    pad_width = 128 - head_share - 2 - gain_cols
    small_pack = jnp.concatenate(
        [
            cols(attn_in, QH * HD + owner * HD, HD),
            cols(attn_in, (QH + KVH) * HD + owner * HD, HD),
            cols(step_in, seq_index * head_share, head_share),
            norm_gain[:, None],
            ffn_gain[:, None],
            gain_pad.reshape(gain_cols, own_rows).T,
            jnp.zeros((own_rows, pad_width), bf_type),
        ],
        axis=1,
    )
    out_pack = jnp.concatenate([mamba_out, attn_out, down_proj], axis=0)
    w_in, w_gate_up, w_out, hidden_all, cot_all = gather_all(
        seq_count,
        fsdp_count,
        (x_width, query_width, ff_width),
        (hidden_in[0], grad_out[0], mamba_in, attn_in, small_pack, gate_up, out_pack),
    )
    per = fsdp_count // seq_count
    in_all = w_in.reshape(model, -1)
    w_gate_up = w_gate_up.reshape(model, -1)
    hidden_all = hidden_all.reshape(rows, model)
    attn_own = QH * HD // fsdp_count
    ff_own = FF // fsdp_count
    w_mamba_out = w_out[:, :gain_own].reshape(x_width, model)
    w_attn_out = w_out[:, gain_own : gain_own + attn_own].reshape(query_width, model)
    w_down = w_out[:, gain_own + attn_own :].reshape(ff_width, model)
    gain_at = main_width + head_share
    first_gain = in_all[:, gain_at].astype(fl_type)
    second_gain = in_all[:, gain_at + 1].astype(fl_type)
    gated_gains = (
        in_all[:, gain_at + 2 : gain_at + 2 + gain_cols]
        .reshape(fsdp_count, own_rows, gain_cols)
        .transpose(0, 2, 1)
        .reshape(fsdp_count, gain_cols * own_rows)[:, :gain_own]
        .reshape(DI)
    )
    mixer_gain = lax.dynamic_slice_in_dim(gated_gains, seq_index * x_width, x_width, 0).astype(
        fl_type
    )

    res_all = hidden_all.astype(fl_type)
    normed = (res_all * rms_scale(res_all) * first_gain).astype(bf_type)
    projected = jnp.dot(normed, in_all, preferred_element_type=fl_type)
    gate_raw = projected[:, :x_width]
    inputs_b = projected[:, x_width:].astype(bf_type).astype(fl_type)
    conv_width = x_width + 2 * NST
    conv_in = inputs_b[:, :conv_width]
    query_in = inputs_b[:, conv_width : conv_width + query_width]
    key_in = inputs_b[:, conv_width + query_width : conv_width + query_width + HD]
    value_b = inputs_b[:, conv_width + query_width + HD : conv_width + query_width + 2 * HD].astype(
        bf_type
    )
    step_at = conv_width + query_width + 2 * HD
    step_raw = inputs_b[:, step_at : step_at + head_share]
    seg_ids = segments[0]
    taps = jnp.concatenate(
        [cols(conv_taps, seq_index * x_width, x_width), conv_taps[:, DI:]], axis=1
    )
    tap_bias = jnp.concatenate(
        [lax.dynamic_slice_in_dim(conv_bias, seq_index * x_width, x_width, 0), conv_bias[DI:]]
    )
    params = (
        taps,
        tap_bias,
        lax.dynamic_slice_in_dim(step_bias, seq_index * head_share, head_share, 0),
        lax.dynamic_slice_in_dim(log_decay, seq_index * head_share, head_share, 0),
    )
    skip = lax.dynamic_slice_in_dim(skip_gain, seq_index * head_share, head_share, 0)
    (activated, step, log_step, queries, keys), pull_back = jax.vjp(
        partial(core_inputs, seg_ids), (conv_in, step_raw, query_in, key_in), params
    )
    positions = jnp.arange(rows, dtype=jnp.int32)
    causal = positions[:, None] >= positions[None, :]
    mask = causal & (seg_ids[:, None] == seg_ids[None, :])
    highest = lax.Precision.HIGHEST
    x_all = activated[:, :x_width]
    b_mat = activated[:, x_width : x_width + NST].astype(bf_type)
    c_mat = activated[:, x_width + NST :].astype(bf_type)
    x_heads = x_all.reshape(rows, head_share, HD).transpose(1, 0, 2)
    step_t = step.T
    cum_t = jnp.dot(log_step.T, causal.T.astype(fl_type), precision=highest)
    inner = jnp.einsum("tn,pn->tp", c_mat, b_mat, preferred_element_type=fl_type)
    decay = jnp.exp(jnp.where(mask[None], cum_t[:, :, None] - cum_t[:, None, :], -1e30))
    kernel_b = (inner[None] * decay).astype(bf_type)
    x_step = (x_heads * step_t[:, :, None]).astype(bf_type)
    scan_y = jnp.einsum("htp,hpd->htd", kernel_b, x_step, preferred_element_type=fl_type)
    ssm = scan_y + skip[:, None, None] * x_heads
    scan_float = (
        ssm.astype(bf_type).transpose(1, 0, 2).reshape(rows, x_width).astype(fl_type)
    )
    key_b = keys.astype(bf_type)
    q_heads = queries.reshape(rows, query_share, HD).transpose(1, 0, 2)
    scores = jnp.einsum("hid,jd->hij", q_heads, keys, precision=highest) * (1.0 / math.sqrt(HD))
    weights = jnp.exp(jnp.where(mask[None], scores, -1e30))
    weights = weights / jnp.sum(weights, axis=-1, keepdims=True)
    weights_b = weights.astype(bf_type)
    attended = jnp.einsum("hij,jd->hid", weights_b, value_b, preferred_element_type=fl_type)
    attn_mix = attended.astype(bf_type).transpose(1, 0, 2).reshape(rows, query_width)

    gate_act = jax.nn.silu(gate_raw)
    gated = scan_float * gate_act
    (
        layer_out,
        d_mixed,
        ffn_in,
        ffn_act,
        d_ffn,
        d_mixed_b,
        gated_b,
        d_gated,
        d_attn,
        g_ffn_gain,
        g_gated_gain,
    ) = middle(
        seq_count,
        fsdp_count,
        (
            gated.reshape(seq_count, block_rows, x_width),
            attn_mix.reshape(seq_count, block_rows, query_width),
            w_mamba_out,
            w_attn_out,
            w_down,
            w_gate_up,
            hidden_in[0],
            grad_out[0],
            cot_all,
            mixer_gain[None],
            second_gain[None],
        ),
    )
    ffn_in = ffn_in.reshape(rows, model)
    ffn_act = ffn_act.reshape(rows, ff_width)
    d_ffn = d_ffn.reshape(rows, 2 * ff_width)
    d_mixed_b = d_mixed_b.reshape(rows, model)
    gated_b = gated_b.reshape(rows, x_width)
    d_gated = d_gated.reshape(rows, x_width)
    d_attn = d_attn.reshape(rows, query_width)
    cot_rows = cot_all.reshape(rows, model)
    g_down = jnp.einsum("tf,td->fd", ffn_act, cot_rows, preferred_element_type=fl_type)
    g_gate_up = jnp.einsum("td,tf->df", ffn_in, d_ffn, preferred_element_type=fl_type)
    g_attn_out = jnp.einsum("tq,td->qd", attn_mix, d_mixed_b, preferred_element_type=fl_type)
    g_mamba_out = jnp.einsum("ti,td->id", gated_b, d_mixed_b, preferred_element_type=fl_type)
    d_scan = (d_gated * gate_act).astype(bf_type)
    d_gate_raw = d_gated * scan_float * swish_slope(gate_raw)
    g_out = jnp.concatenate(
        [
            g_mamba_out.astype(bf_type).reshape(per, gain_own, model),
            g_attn_out.astype(bf_type).reshape(per, attn_own, model),
            g_down.astype(bf_type).reshape(per, ff_own, model),
        ],
        axis=1,
    )

    d_att = d_attn.astype(bf_type).reshape(rows, query_share, HD).transpose(1, 0, 2)
    d_weights = jnp.einsum("hid,jd->hij", d_att, value_b, preferred_element_type=fl_type)
    inner_sum = jnp.sum(d_att.astype(fl_type) * attended, axis=-1, keepdims=True)
    d_scores = (weights * (d_weights - inner_sum) * (1.0 / math.sqrt(HD))).astype(bf_type)
    d_queries = jnp.einsum("hij,jd->hid", d_scores, key_b, preferred_element_type=fl_type)
    d_keys = jnp.einsum(
        "hij,hid->jd", d_scores, q_heads.astype(bf_type), preferred_element_type=fl_type
    )
    d_value = jnp.einsum("hij,hid->jd", weights_b, d_att, preferred_element_type=fl_type)
    d_y = d_scan.reshape(rows, head_share, HD).transpose(1, 0, 2)
    d_y_float = d_y.astype(fl_type)
    d_kernel = jnp.einsum("htd,hpd->htp", d_y, x_step, preferred_element_type=fl_type)
    d_inner = jnp.sum(d_kernel * decay, axis=0).astype(bf_type)
    d_x_step = jnp.einsum("htp,htd->hpd", kernel_b, d_y, preferred_element_type=fl_type)
    d_c = jnp.dot(d_inner, b_mat, preferred_element_type=fl_type)
    d_b = jnp.einsum("tp,tn->pn", d_inner, c_mat, preferred_element_type=fl_type)
    d_x = step_t[:, :, None] * d_x_step + skip[:, None, None] * d_y_float
    g_skip = jnp.sum(d_y_float * x_heads, axis=(1, 2))
    d_step_direct = jnp.sum(x_heads * d_x_step, axis=-1)
    d_cum = jnp.sum(d_y_float * scan_y, axis=-1) - jnp.sum(
        x_step.astype(fl_type) * d_x_step, axis=-1
    )
    d_log_step = jnp.dot(d_cum, causal.astype(fl_type), precision=highest)
    (d_conv, d_step, d_query, d_key), grad_params = pull_back(
        (
            jnp.concatenate([d_x.transpose(1, 0, 2).reshape(rows, x_width), d_b, d_c], axis=1),
            d_step_direct.T,
            d_log_step.T,
            d_queries.transpose(1, 0, 2).reshape(rows, query_width),
            d_keys,
        )
    )
    d_in = jnp.concatenate(
        [
            d_gate_raw,
            d_conv,
            d_query,
            d_key,
            d_value,
            d_step,
            jnp.zeros((rows, 128 - head_share), fl_type),
        ],
        axis=1,
    ).astype(bf_type)
    g_in = jnp.einsum("td,tc->dc", normed, d_in, preferred_element_type=fl_type)
    d_normed_part = jnp.einsum("tc,dc->td", d_in, in_all, preferred_element_type=fl_type)
    first_norm_all = res_all * rms_scale(res_all)
    g_norm_gain = jnp.sum(d_normed_part * first_norm_all, axis=0)
    taps_bias = jnp.concatenate([grad_params[0], grad_params[1][None]], axis=0)
    small_parts = [
        taps_bias.reshape(-1),
        g_gated_gain.reshape(-1),
        g_norm_gain,
        g_ffn_gain.reshape(-1),
        grad_params[2],
        grad_params[3],
        g_skip,
    ]
    small_size = sum(part.shape[0] for part in small_parts)
    small_rows = -(-small_size // 1024) * 8
    small = jnp.concatenate(
        small_parts + [jnp.zeros((small_rows * 128 - small_size,), fl_type)]
    ).reshape(small_rows, 128)
    in_grads, gu_grads, out_grads, small_all, d_normed = reduce_all(
        seq_count,
        fsdp_count,
        (
            g_in.astype(bf_type).reshape(fsdp_count, own_rows, -1),
            g_gate_up.astype(bf_type).reshape(fsdp_count, own_rows, -1),
            g_out,
            small,
            d_normed_part.astype(bf_type).reshape(seq_count, block_rows, model),
        ),
    )
    in_grads = in_grads.astype(fl_type)
    gu_grads = gu_grads.astype(fl_type)
    out_grads = out_grads.astype(fl_type)
    residual = hidden_in[0].astype(fl_type)
    first_scale = rms_scale(residual)
    first_norm = residual * first_scale
    d_first = d_normed * first_gain
    grad_tok = d_mixed + first_scale * (
        d_first - first_norm * jnp.mean(d_first * first_norm, axis=-1, keepdims=True)
    )

    conv_width = x_width + 2 * NST
    small_all = small_all.reshape(seq_count, -1)
    at = (KC + 1) * conv_width
    taps_all = small_all[:, :at].reshape(seq_count, KC + 1, conv_width)
    taps_sum = jnp.concatenate(
        [taps_all[group, :, :x_width] for group in range(seq_count)]
        + [jnp.sum(taps_all[:, :, x_width:], axis=0)],
        axis=1,
    )
    fsdp_index = lax.axis_index("fsdp")
    gated_sum = lax.dynamic_slice_in_dim(
        small_all[:, at : at + x_width].reshape(-1), fsdp_index * gain_own, gain_own, 0
    )
    at = at + x_width
    gains_sum = jnp.sum(small_all[:, at : at + 2 * model], axis=0)
    norm_sum = lax.dynamic_slice_in_dim(gains_sum, fsdp_index * own_rows, own_rows, 0)
    ffn_gain_sum = lax.dynamic_slice_in_dim(gains_sum, model + fsdp_index * own_rows, own_rows, 0)
    at = at + 2 * model
    heads_sum = (
        small_all[:, at : at + 3 * head_share]
        .reshape(seq_count, 3, head_share)
        .transpose(1, 0, 2)
        .reshape(3, MH)
    )

    def side(array):
        return jnp.concatenate([array[group] for group in range(seq_count)], axis=1)

    def owned(start):
        slots = []
        for kv_head in range(KVH):
            users = [group for group in range(seq_count) if owners[group] == kv_head]
            total = in_grads[users[0]][:, start : start + HD]
            for group in users[1:]:
                total = total + in_grads[group][:, start : start + HD]
            slots.append(total)
        return slots

    q_at = 2 * x_width + 2 * NST
    grad_mamba_in = jnp.concatenate(
        [
            side(in_grads[:, :, :x_width]),
            side(in_grads[:, :, x_width : 2 * x_width]),
            jnp.sum(in_grads[:, :, 2 * x_width : q_at], axis=0),
        ],
        axis=1,
    )
    k_at = q_at + query_width
    grad_attn_in = jnp.concatenate(
        [side(in_grads[:, :, q_at:k_at])] + owned(k_at) + owned(k_at + HD), axis=1
    )
    grad_step_in = side(in_grads[:, :, main_width : main_width + head_share])
    grad_gate_up = jnp.concatenate(
        [side(gu_grads[:, :, :ff_width]), side(gu_grads[:, :, ff_width:])], axis=1
    )
    return (
        layer_out[None],
        grad_tok[None],
        norm_sum,
        grad_mamba_in,
        grad_step_in,
        grad_attn_in,
        taps_sum[:KC],
        taps_sum[KC],
        heads_sum[0],
        heads_sum[1],
        heads_sum[2],
        gated_sum,
        out_grads[:gain_own],
        out_grads[gain_own : gain_own + attn_own],
        ffn_gain_sum,
        grad_gate_up,
        out_grads[gain_own + attn_own :],
    )


def solution(mesh):
    placed = (
        P("fsdp", "seq", None),
        P("fsdp", "seq", None),
        P("fsdp", None),
        P("fsdp"),
        P("fsdp", None),
        P("fsdp", None),
        P("fsdp", None),
        P(),
        P(),
        P(),
        P(),
        P(),
        P("fsdp"),
        P("fsdp", None),
        P("fsdp", None),
        P("fsdp"),
        P("fsdp", None),
        P("fsdp", None),
    )
    return jax.shard_map(
        shards,
        mesh=mesh,
        in_specs=placed,
        out_specs=(
            P("fsdp", "seq", None),
            P("fsdp", "seq", None),
            P("fsdp"),
            P("fsdp", None),
            P("fsdp", None),
            P("fsdp", None),
            P(),
            P(),
            P(),
            P(),
            P(),
            P("fsdp"),
            P("fsdp", None),
            P("fsdp", None),
            P("fsdp"),
            P("fsdp", None),
            P("fsdp", None),
        ),
        check_vma=False,
    )
```

```python
from functools import partial
import math

import jax
import jax.numpy as jnp
from jax import lax
from jax.experimental import pallas as pl
from jax.experimental.pallas import tpu as pltpu
from jax.sharding import PartitionSpec as P

MH = 24
HD = 64
NST = 128
KC = 4
QH = 8
KVH = 2
FF = 2048
DI = 1536


EPS = 1e-05
ROPE_THETA = 10000.0

MESH = pl.DeviceIdType.MESH
VMEM_LIMIT = 62 * 2**20
HIGHEST = lax.Precision.HIGHEST


def rcopy(src, dst, send, recv, device):
    return pltpu.make_async_remote_copy(
        src_ref=src,
        dst_ref=dst,
        send_sem=send,
        recv_sem=recv,
        device_id=device,
        device_id_type=MESH,
    )


class Place:
    def __init__(self, seq_count, fsdp_count):
        self.s = lax.axis_index("seq")
        self.f = lax.axis_index("fsdp")
        self.count = fsdp_count
        self.L = fsdp_count // 2
        self.z = self.f // 2
        self.y = self.f % 2
        self.has_right = self.z < self.L - 1
        self.has_left = self.z > 0
        self.right = (self.s, jnp.minimum(self.f + 2, fsdp_count - 1))
        self.left = (self.s, jnp.maximum(self.f - 2, 0))
        self.pair = (self.s, self.f + 1 - 2 * self.y)
        self.s1 = self.s + 1 - 2 * (self.s % 2)
        self.s2 = (self.s + 2) % 4
        self.s3 = 3 - self.s
        self.sib = (self.s1, self.f)
        self.across = (self.s2, self.f)
        self.diag = (self.s3, self.f)

    def greet(self, line=True, pair=True, diag=False):
        barrier = pltpu.get_barrier_semaphore()

        def hello(device):
            pl.semaphore_signal(barrier, inc=1, device_id=device, device_id_type=MESH)

        amount = 2
        hello(self.sib)
        hello(self.across)
        if diag:
            hello(self.diag)
            amount = amount + 1
        if pair:
            hello(self.pair)
            amount = amount + 1
        if line:

            @pl.when(self.has_right)
            def _():
                hello(self.right)

            @pl.when(self.has_left)
            def _():
                hello(self.left)

            amount = amount + jnp.where(self.has_right, 1, 0) + jnp.where(self.has_left, 1, 0)
        pl.semaphore_wait(barrier, amount)


class SeqGather:
    def __init__(self, place, src, out, send, recv):
        p = place
        self.own_sib = rcopy(src, out.at[p.s], send.at[0], recv.at[0], p.sib)
        self.own_across = rcopy(src, out.at[p.s], send.at[1], recv.at[1], p.across)
        self.forward_copy = rcopy(out.at[p.s2], out.at[p.s2], send.at[2], recv.at[2], p.sib)
        self.got_sib = rcopy(src, out.at[p.s1], send.at[0], recv.at[0], p.sib)
        self.got_across = rcopy(src, out.at[p.s2], send.at[1], recv.at[1], p.across)
        self.got_diag = rcopy(src, out.at[p.s3], send.at[2], recv.at[2], p.sib)

    def start(self):
        self.own_across.start()
        self.own_sib.start()

    def wait_sib(self):
        self.got_sib.wait_recv()

    def forward(self):
        self.got_across.wait_recv()
        self.forward_copy.start()

    def wait_diag(self):
        self.got_diag.wait_recv()

    def wait_sends(self):
        self.own_sib.wait_send()
        self.own_across.wait_send()
        self.forward_copy.wait_send()

    def finish(self):
        self.wait_sib()
        self.wait_diag()
        self.wait_sends()


class SeqReduce:
    def __init__(self, place, stage, got, send, recv):
        p = place
        self.stage, self.got = stage, got
        self.copies = [
            rcopy(stage.at[0], got.at[0], send.at[0], recv.at[0], p.sib),
            rcopy(stage.at[1], got.at[1], send.at[1], recv.at[1], p.sib),
            rcopy(stage.at[2], got.at[2], send.at[2], recv.at[2], p.across),
        ]

    def send_diag(self, value):
        self.stage[0] = value.astype(self.stage.dtype)
        self.copies[0].start()

    def send_sib(self, value):
        self.stage[1] = value.astype(self.stage.dtype)
        self.copies[1].start()

    def send_across(self, value):
        self.copies[0].wait_recv()
        self.stage[2] = (value + self.got[0].astype(jnp.float32)).astype(self.stage.dtype)
        self.copies[2].start()

    def total(self, value):
        self.copies[1].wait_recv()
        self.copies[2].wait_recv()
        return value + self.got[1].astype(jnp.float32) + self.got[2].astype(jnp.float32)

    def wait_sends(self):
        for copy in self.copies:
            copy.wait_send()


class LineGather:
    def __init__(self, place, out, send, recv, pair=True, size=0):
        self.p, self.out, self.send, self.recv, self.pair = place, out, send, recv, pair
        self.size = size

    def block(self, index):
        if self.size:
            return self.out.at[pl.ds(pl.multiple_of(index * self.size, self.size), self.size)]
        return self.out.at[index]

    def at(self, b, other=0):
        p = self.p
        if not self.pair:
            return b
        return 2 * b + (1 - p.y if other else p.y)

    def copy(self, b, way):
        p = self.p
        ref = self.block(self.at(b))
        device = (p.right, p.left, p.pair)[way]
        return rcopy(ref, ref, self.send.at[way, b], self.recv.at[self.at(b)], device)

    def push(self, b, right, left):
        if right:

            @pl.when(self.p.has_right)
            def _():
                self.copy(b, 0).start()

        if left:

            @pl.when(self.p.has_left)
            def _():
                self.copy(b, 1).start()

        if self.pair:
            self.copy(b, 2).start()

    def start(self):
        self.push(self.p.z, True, True)

    def step(self, d):
        p = self.p

        @pl.when(p.z - d >= 0)
        def _():
            self.copy(p.z - d, 0).wait_recv()
            self.push(p.z - d, True, False)

        @pl.when(p.z + d <= p.L - 1)
        def _():
            self.copy(p.z + d, 0).wait_recv()
            self.push(p.z + d, False, True)

    def finish(self):
        p = self.p

        def each(b, carry):
            if self.pair:
                ref = self.block(self.at(b, 1))
                rcopy(ref, ref, self.send.at[2, b], self.recv.at[self.at(b, 1)], p.pair).wait_recv()
                self.copy(b, 2).wait_send()

            @pl.when(p.has_right & (b <= p.z))
            def _():
                self.copy(b, 0).wait_send()

            @pl.when(p.has_left & (b >= p.z))
            def _():
                self.copy(b, 1).wait_send()

            return carry

        lax.fori_loop(0, p.L, each, 0)


def loop(count, body):
    def step(index, carry):
        body(index)
        return carry

    lax.fori_loop(0, count, step, 0)


def add_rows(target, *parts):
    def some(index):
        at = pl.ds(pl.multiple_of(index * 16, 16), 16)
        total = parts[0][at].astype(jnp.float32)
        for part in parts[1:]:
            total = total + part[at].astype(jnp.float32)
        target[at] = total.astype(target.dtype)

    loop(target.shape[0] // 16, some)


CHUNKS = 4


def gather_kernel(
    seq_count,
    fsdp_count,
    x_width,
    query_width,
    ff_width,
    hidden,
    cot,
    mamba_in,
    attn_in,
    small,
    gate_up,
    out_pack,
    w_in,
    w_gu,
    w_out,
    hidden_all,
    cot_all,
    local,
    in_send,
    in_recv,
    gu_send,
    gu_recv,
    out_send,
    out_recv,
    hid_send,
    hid_recv,
    cot_send,
    cot_recv,
):
    p = Place(seq_count, fsdp_count)
    s, f, z, y, L = p.s, p.f, p.z, p.y, p.L
    per = fsdp_count // seq_count
    half = per // 2

    def part(ref, start, size, unit):
        return ref.at[:, pl.ds(pl.multiple_of(start, unit), size)]

    bc = mamba_in.shape[1] - 2 * DI
    copies = []

    def bring(src, dst):
        copy = pltpu.make_async_copy(src, dst, local.at[len(copies)])
        copy.start()
        copies.append(copy)

    own = w_in.at[f]
    c0 = 0
    bring(part(mamba_in, s * x_width, x_width, 128), own.at[:, pl.ds(c0, x_width)])
    c0 += x_width
    bring(part(mamba_in, DI + s * x_width, x_width, 128), own.at[:, pl.ds(c0, x_width)])
    c0 += x_width
    bring(mamba_in.at[:, pl.ds(2 * DI, bc)], own.at[:, pl.ds(c0, bc)])
    c0 += bc
    bring(part(attn_in, s * query_width, query_width, 128), own.at[:, pl.ds(c0, query_width)])
    c0 += query_width
    bring(small, own.at[:, pl.ds(c0, small.shape[1])])
    own = w_gu.at[f]
    bring(part(gate_up, s * ff_width, ff_width, 128), own.at[:, pl.ds(0, ff_width)])
    bring(part(gate_up, FF + s * ff_width, ff_width, 128), own.at[:, pl.ds(ff_width, ff_width)])
    bring(hidden, hidden_all.at[s])
    bring(cot, cot_all.at[s])
    holder = f // per == s
    chunk = w_out.shape[1] // CHUNKS
    out_local = local.at[len(copies)]

    @pl.when(holder)
    def _():
        pltpu.make_async_copy(out_pack, w_out.at[f - s * per], out_local).start()

    p.greet()
    hid = SeqGather(p, hidden, hidden_all, hid_send, hid_recv)
    cots = SeqGather(p, cot, cot_all, cot_send, cot_recv)
    hid.start()
    cots.start()
    for copy in copies:
        copy.wait()

    @pl.when(holder)
    def _():
        pltpu.make_async_copy(out_pack, w_out.at[f - s * per], out_local).wait()

    ins = LineGather(p, w_in, in_send, in_recv)
    gus = LineGather(p, w_gu, gu_send, gu_recv)
    ins.start()
    gus.start()
    hid.forward()
    cots.forward()

    def hop(d):
        ins.step(d + 1)
        gus.step(d + 1)

    loop(L - 1, hop)

    def out_copy(i, c, other, way):
        ref = w_out.at[2 * i + (1 - y if other else y), pl.ds(pl.multiple_of(c * chunk, 16), chunk)]
        device = (p.right, p.left, p.pair)[way]
        return rcopy(ref, ref, out_send.at[way, i, c], out_recv.at[way // 2, i, c], device)

    def spread(index):
        i, c = index // CHUNKS, index % CHUNKS
        zs = s * half + i

        @pl.when(z != zs)
        def _():
            out_copy(i, c, 0, 0).wait_recv()

        @pl.when((z >= zs) & p.has_right)
        def _():
            out_copy(i, c, 0, 0).start()

        @pl.when((z <= zs) & p.has_left)
        def _():
            out_copy(i, c, 0, 1).start()

        out_copy(i, c, 0, 2).start()

    loop(half * CHUNKS, spread)

    def spread_end(index):
        i, c = index // CHUNKS, index % CHUNKS
        zs = s * half + i
        out_copy(i, c, 1, 2).wait_recv()
        out_copy(i, c, 0, 2).wait_send()

        @pl.when((z >= zs) & p.has_right)
        def _():
            out_copy(i, c, 0, 0).wait_send()

        @pl.when((z <= zs) & p.has_left)
        def _():
            out_copy(i, c, 0, 1).wait_send()

    loop(half * CHUNKS, spread_end)
    ins.finish()
    gus.finish()
    hid.finish()
    cots.finish()


def dma(*shape):
    return pltpu.SemaphoreType.DMA(shape)


def gather_all(seq_count, fsdp_count, widths, arrays):
    hidden, cot, mamba_in, attn_in, small, gate_up, out_pack = arrays
    x_width, query_width, ff_width = widths
    own_rows = mamba_in.shape[0]
    per = fsdp_count // seq_count
    bc = mamba_in.shape[1] - 2 * DI
    in_width = 2 * x_width + bc + query_width + small.shape[1]
    bf = jnp.bfloat16
    L = fsdp_count // 2
    return pl.pallas_call(
        partial(gather_kernel, seq_count, fsdp_count, x_width, query_width, ff_width),
        out_shape=[
            jax.ShapeDtypeStruct((fsdp_count, own_rows, in_width), bf),
            jax.ShapeDtypeStruct((fsdp_count, own_rows, 2 * ff_width), bf),
            jax.ShapeDtypeStruct((per,) + out_pack.shape, bf),
            jax.ShapeDtypeStruct((seq_count,) + hidden.shape, bf),
            jax.ShapeDtypeStruct((seq_count,) + cot.shape, bf),
        ],
        in_specs=[pl.BlockSpec(memory_space=pl.ANY)] * 7,
        out_specs=[pl.BlockSpec(memory_space=pl.ANY)] * 5,
        scratch_shapes=[
            dma(10),
            dma(3, L),
            dma(fsdp_count),
            dma(3, L),
            dma(fsdp_count),
            dma(3, per // 2, CHUNKS),
            dma(2, per // 2, CHUNKS),
            dma(3),
            dma(3),
            dma(3),
            dma(3),
        ],
        compiler_params=pltpu.CompilerParams(collective_id=0, has_side_effects=True),
        name="gather_weights",
    )(*arrays)


def mid_kernel(
    seq_count,
    fsdp_count,
    gated,
    attn_mix,
    w_mo,
    w_ao,
    w_dn,
    w_gu,
    hidden,
    cot_own,
    cot_all,
    mixer_gain,
    ffn_gain,
    layer_out,
    d_mixed,
    ffn_in,
    ffn_act,
    d_ffn,
    d_mixed_all,
    gated_b,
    d_gated,
    d_attn,
    g_ffn_gain,
    g_gated_gain,
    part_mix,
    gate_vals,
    d_act,
    d_gn,
    mixed,
    norm2,
    sq_buf,
    mean_buf,
    stage,
    got,
    seq_send,
    seq_recv,
):
    p = Place(seq_count, fsdp_count)
    s = p.s
    fl, bf = jnp.float32, jnp.bfloat16
    rows = cot_own.shape[0]
    model = cot_own.shape[1]
    ff = w_dn.shape[0]
    peers = (p.sib, p.across, p.diag)
    peer_at = (p.s1, p.s2, p.s3)

    def dot(a, b):
        return jnp.dot(a, b, preferred_element_type=fl)

    def dot_t(a, b):
        return lax.dot_general(a, b, (((1,), (1,)), ((), ())), preferred_element_type=fl)

    def row_sums(values):
        ones = jnp.ones((8, values.shape[1]), fl)
        return lax.dot_general(
            ones, values, (((1,), (1,)), ((), ())), preferred_element_type=fl, precision=HIGHEST
        )

    def exchange(buf, at):
        copies = []
        for k in range(3):
            copy = rcopy(buf.at[s], buf.at[s], seq_send.at[at, k], seq_recv.at[at, k], peers[k])
            copy.start()
            got_it = rcopy(
                buf.at[peer_at[k]], buf.at[peer_at[k]], seq_send.at[at, k], seq_recv.at[at, k], peers[k]
            )
            copies.append((copy, got_it))

        def end():
            for copy, got_it in copies:
                got_it.wait_recv()
                copy.wait_send()
            total = buf[0] + buf[1] + buf[2] + buf[3]
            return total

        return end

    for r in range(4):
        values = gated[r]
        sq_buf[s, :, r * rows : (r + 1) * rows] = row_sums(values * values)
    p.greet(line=False, pair=False, diag=True)
    sq_end = exchange(sq_buf, 0)
    gain = mixer_gain[...]
    for r in range(4):
        part_mix[r] = dot((gated[r] * gain).astype(bf), w_mo[...])
    sq_total = sq_end()
    scale_cols = lax.rsqrt(sq_total / DI + EPS).T

    for r in range(4):
        scale = scale_cols[r * rows : (r + 1) * rows, 0:1]
        part_mix[r] = part_mix[r] * scale + dot(attn_mix[r], w_ao[...])
        gated_norm = gated[r] * scale
        gated_b[r] = (gated_norm * gain).astype(bf)

    def reducer(at):
        return SeqReduce(p, stage.at[at], got.at[at], seq_send.at[at + 1], seq_recv.at[at + 1])

    mix = reducer(0)
    mix.send_diag(part_mix[p.s3])
    mix.send_sib(part_mix[p.s1])
    mix.send_across(part_mix[p.s2])
    d_act[0] = dot_t(cot_all[0], w_dn[...])
    d_act[1] = dot_t(cot_all[1], w_dn[...])
    residual = hidden[...].astype(fl)
    mixed[...] = residual + mix.total(part_mix[s])
    scale2 = lax.rsqrt(jnp.mean(mixed[...] * mixed[...], axis=-1, keepdims=True) + EPS)
    norm2[...] = mixed[...] * scale2
    ffn_in[s] = (norm2[...] * ffn_gain[...]).astype(bf)
    ffn_all = SeqGather(p, ffn_in.at[s], ffn_in, seq_send.at[4], seq_recv.at[4])
    ffn_all.start()

    def ffn_block(r):
        gate_vals[r] = dot(ffn_in[r], w_gu[...])

    def act_block(r):
        gate_lin = gate_vals[r, :, :ff]
        up_lin = gate_vals[r, :, ff:]
        sigma = jax.nn.sigmoid(gate_lin)
        act = gate_lin * sigma
        ffn_act[r] = (act * up_lin).astype(bf)
        slope = sigma * (1.0 + gate_lin * (1.0 - sigma))
        da = d_act[r]
        d_ffn[r, :, :ff] = (da * up_lin * slope).astype(bf)
        d_ffn[r, :, ff:] = (da * act).astype(bf)

    d_act[2] = dot_t(cot_all[2], w_dn[...])
    d_act[3] = dot_t(cot_all[3], w_dn[...])
    ffn_block(s)
    act_block(s)
    ffn_all.wait_sib()
    ffn_block(p.s1)
    ffn_all.forward()
    act_block(p.s1)
    ffn_block(p.s2)
    act_block(p.s2)
    ffn_all.wait_diag()
    ffn_block(p.s3)
    act_block(p.s3)
    back = reducer(1)
    back.send_diag(dot_t(d_ffn[p.s3], w_gu[...]))
    back.send_sib(dot_t(d_ffn[p.s1], w_gu[...]))
    back.send_across(dot_t(d_ffn[p.s2], w_gu[...]))
    out = reducer(2)
    d_ffn_own = dot_t(d_ffn[s], w_gu[...])
    d_ffn_in = back.total(d_ffn_own)
    g_ffn_gain[...] = jnp.sum(d_ffn_in * norm2[...], axis=0, keepdims=True)
    d_second = d_ffn_in * ffn_gain[...]
    d_mixed[...] = cot_own[...].astype(fl) + scale2 * (
        d_second - norm2[...] * jnp.mean(d_second * norm2[...], axis=-1, keepdims=True)
    )
    d_mixed_all[s] = d_mixed[...].astype(bf)
    back_all = SeqGather(p, d_mixed_all.at[s], d_mixed_all, seq_send.at[5], seq_recv.at[5])
    back_all.start()
    out.send_diag(dot(ffn_act[p.s3], w_dn[...]))
    out.send_sib(dot(ffn_act[p.s1], w_dn[...]))

    def mixer_block(r):
        block = d_mixed_all[r]
        d_gated_b = dot_t(block, w_mo[...])
        d_gn[r] = d_gated_b
        d_attn[r] = dot_t(block, w_ao[...]).astype(bf)

    mixer_block(s)
    back_all.wait_sib()
    mixer_block(p.s1)
    out.send_across(dot(ffn_act[p.s2], w_dn[...]))
    back_all.forward()
    mixer_block(p.s2)
    back_all.wait_diag()
    mixer_block(p.s3)
    for r in range(4):
        scale = scale_cols[r * rows : (r + 1) * rows, 0:1]
        values = d_gn[r] * gain * (gated[r] * scale)
        mean_buf[s, :, r * rows : (r + 1) * rows] = row_sums(values)
    mean_end = exchange(mean_buf, 6)
    layer_out[...] = (mixed[...] + out.total(dot(ffn_act[s], w_dn[...]))).astype(bf)
    gain_total = jnp.zeros_like(g_gated_gain[...])
    for r in range(4):
        scale = scale_cols[r * rows : (r + 1) * rows, 0:1]
        gain_total = gain_total + jnp.sum(d_gn[r] * (gated[r] * scale), axis=0, keepdims=True)
    g_gated_gain[...] = gain_total
    means = (mean_end() / DI).T
    for r in range(4):
        scale = scale_cols[r * rows : (r + 1) * rows, 0:1]
        mean = means[r * rows : (r + 1) * rows, 0:1]
        d_gated[r] = scale * (d_gn[r] * gain - (gated[r] * scale) * mean)
    mix.wait_sends()
    back.wait_sends()
    out.wait_sends()
    ffn_all.wait_sends()
    back_all.wait_sends()


def middle(seq_count, fsdp_count, arrays):
    gated, attn_mix, w_mo, w_ao, w_dn, w_gu, hidden = arrays[:7]
    fl, bf = jnp.float32, jnp.bfloat16
    rows, model = hidden.shape
    ff = w_dn.shape[0]
    n = seq_count
    total = n * rows

    def sds(*shape, dtype=bf):
        return jax.ShapeDtypeStruct(shape, dtype)

    return pl.pallas_call(
        partial(mid_kernel, seq_count, fsdp_count),
        out_shape=[
            sds(rows, model),
            sds(rows, model, dtype=fl),
            sds(n, rows, model),
            sds(n, rows, ff),
            sds(n, rows, 2 * ff),
            sds(n, rows, model),
            sds(*gated.shape),
            sds(*gated.shape, dtype=fl),
            sds(*attn_mix.shape),
            sds(1, model, dtype=fl),
            sds(1, gated.shape[2], dtype=fl),
        ],
        in_specs=[pl.BlockSpec(memory_space=pltpu.VMEM)] * len(arrays),
        out_specs=[pl.BlockSpec(memory_space=pltpu.VMEM)] * 11,
        scratch_shapes=[
            pltpu.VMEM((n, rows, model), fl),
            pltpu.VMEM((n, rows, 2 * ff), fl),
            pltpu.VMEM((n, rows, ff), fl),
            pltpu.VMEM(gated.shape, fl),
            pltpu.VMEM((rows, model), fl),
            pltpu.VMEM((rows, model), fl),
            pltpu.VMEM((n, 8, total), fl),
            pltpu.VMEM((n, 8, total), fl),
            pltpu.VMEM((3, 3, rows, model), bf),
            pltpu.VMEM((3, 3, rows, model), bf),
            dma(7, 3),
            dma(7, 3),
        ],
        compiler_params=pltpu.CompilerParams(
            collective_id=1, has_side_effects=True, vmem_limit_bytes=VMEM_LIMIT
        ),
        name="ffn_middle",
    )(*arrays)


class LineReduce:
    def __init__(self, place, g, pair_got, side_got, acc, send, recv):
        self.p, self.g, self.pair_got, self.side_got, self.acc = place, g, pair_got, side_got, acc
        self.send, self.recv = send, recv

    def pair_copy(self, b):
        p = self.p
        return rcopy(
            self.g.at[2 * b + 1 - p.y],
            self.pair_got.at[b],
            self.send.at[0, b],
            self.recv.at[0, b],
            p.pair,
        )

    def each_from_far(self, body):
        p = self.p

        def step(k):
            d = p.L - 1 - k

            @pl.when(p.z + d <= p.L - 1)
            def _():
                body(p.z + d)

            @pl.when((d > 0) & (p.z - d >= 0))
            def _():
                body(p.z - d)

        loop(p.L, step)

    def start(self):
        self.each_from_far(lambda b: self.pair_copy(b).start())

    def got_from(self, b, right):
        p = self.p
        slot = b if right else b + p.L
        ref = self.side_got.at[slot]
        rcopy(ref, ref, self.send.at[1, b], self.recv.at[1, slot], p.right).wait_recv()
        return ref

    def pass_on(self, b, right):
        p = self.p
        self.pair_copy(b).wait_recv()
        mine, other = self.g.at[2 * b + p.y], self.pair_got.at[b]
        inner = p.has_left if right else p.has_right

        @pl.when(inner)
        def _():
            add_rows(other, mine, other, self.got_from(b, right))

        @pl.when(jnp.logical_not(inner))
        def _():
            add_rows(other, mine, other)

        slot = b if right else b + p.L
        rcopy(
            other,
            self.side_got.at[slot],
            self.send.at[1, b],
            self.recv.at[1, slot],
            p.right if right else p.left,
        ).start()

    def step(self, k):
        p = self.p
        d = p.L - 1 - k

        @pl.when(p.z + d <= p.L - 1)
        def _():
            self.pass_on(p.z + d, True)

        @pl.when(p.z - d >= 0)
        def _():
            self.pass_on(p.z - d, False)

    def total(self, target):
        p = self.p
        b = p.z
        self.pair_copy(b).wait_recv()
        add_rows(self.acc, self.g.at[2 * b + p.y], self.pair_got.at[b])

        @pl.when(p.has_left)
        def _():
            add_rows(self.acc, self.acc, self.got_from(b, True))

        @pl.when(p.has_right)
        def _():
            add_rows(self.acc, self.acc, self.got_from(b, False))

        add_rows(target, self.acc)

    def wait_sends(self):
        p = self.p

        def each(b):
            self.pair_copy(b).wait_send()

            @pl.when(b != p.z)
            def _():
                ref = self.pair_got.at[b]
                rcopy(ref, ref, self.send.at[1, b], self.recv.at[1, b], p.right).wait_send()

        loop(p.L, each)


def reduce_kernel(
    seq_count,
    fsdp_count,
    g_in,
    g_gu,
    g_out,
    small,
    d_norm,
    in_got,
    gu_got,
    out_got,
    small_got,
    d_norm_sum,
    in_pair,
    in_side,
    in_acc,
    gu_pair,
    gu_side,
    gu_acc,
    out_pair,
    out_side,
    out_acc,
    small_pair,
    small_line,
    stage,
    got,
    in_send,
    in_recv,
    gu_send,
    gu_recv,
    out_send,
    out_recv,
    cast_send,
    cast_recv,
    small_send,
    small_recv,
    sp_send,
    sp_recv,
    seq_send,
    seq_recv,
):
    p = Place(seq_count, fsdp_count)
    s, f, z, y, L = p.s, p.f, p.z, p.y, p.L
    per = fsdp_count // seq_count
    half = per // 2
    fl = jnp.float32
    chunk = g_out.shape[1] // CHUNKS
    p.greet()
    pair_small = rcopy(small, small_pair, sp_send.at[0], sp_recv.at[0], p.pair)
    pair_small.start()

    def rows_of(c):
        return pl.ds(pl.multiple_of(c * chunk, 16), chunk)

    def out_pair_copy(i, c):
        return rcopy(
            g_out.at[2 * i + 1 - y, rows_of(c)],
            out_pair.at[i, rows_of(c)],
            out_send.at[0, i, c],
            out_recv.at[0, i, c],
            p.pair,
        )

    def side_copy(i, c, right):
        at = 0 if right else 1
        return rcopy(
            out_pair.at[i, rows_of(c)],
            out_side.at[at, i, rows_of(c)],
            out_send.at[1, i, c],
            out_recv.at[1 + at, i, c],
            p.right if right else p.left,
        )

    ins = LineReduce(p, g_in, in_pair, in_side, in_acc, in_send, in_recv)
    gus = LineReduce(p, g_gu, gu_pair, gu_side, gu_acc, gu_send, gu_recv)
    d_sum = SeqReduce(p, stage, got, seq_send.at[0], seq_recv.at[0])
    loop(half * CHUNKS, lambda index: out_pair_copy(index // CHUNKS, index % CHUNKS).start())
    gus.start()
    ins.start()
    d_sum.send_diag(d_norm[p.s3])
    d_sum.send_sib(d_norm[p.s1])
    d_sum.send_across(d_norm[p.s2].astype(fl))
    pair_small.wait_recv()
    small_line[z] = small[...] + small_pair[...]
    smalls = LineGather(p, small_line, small_send, small_recv, pair=False)
    smalls.start()
    loop(L - 1, lambda d: smalls.step(d + 1))
    smalls.finish()
    pair_small.wait_send()
    small_sum = small_line[0]
    for b in range(1, L):
        small_sum = small_sum + small_line[b]
    small_got[s] = small_sum
    small_all = SeqGather(p, small_got.at[s], small_got, seq_send.at[1], seq_recv.at[1])
    small_all.start()
    d_norm_sum[...] = d_sum.total(d_norm[s].astype(fl))

    def cast(c, way):
        ref = out_got.at[rows_of(c)]
        return rcopy(ref, ref, cast_send.at[way, c], cast_recv.at[c], p.across if way else p.sib)

    def out_step(index):
        i, c = index // CHUNKS, index % CHUNKS
        zs = s * half + i
        out_pair_copy(i, c).wait_recv()
        mine = g_out.at[2 * i + y, rows_of(c)]
        other = out_pair.at[i, rows_of(c)]
        add_rows(out_acc, mine, other)

        @pl.when(p.has_left & (z <= zs))
        def _():
            side_copy(i, c, True).wait_recv()
            add_rows(out_acc, out_acc, out_side.at[0, i, rows_of(c)])

        @pl.when(p.has_right & (z >= zs))
        def _():
            side_copy(i, c, False).wait_recv()
            add_rows(out_acc, out_acc, out_side.at[1, i, rows_of(c)])

        @pl.when(z == zs)
        def _():
            add_rows(out_got.at[rows_of(c)], out_acc)
            cast(c, 1).start()
            cast(c, 0).start()

        @pl.when(z < zs)
        def _():
            add_rows(other, out_acc)
            side_copy(i, c, True).start()

        @pl.when(z > zs)
        def _():
            add_rows(other, out_acc)
            side_copy(i, c, False).start()

    loop(half * CHUNKS, out_step)
    small_all.forward()
    loop(L - 1, gus.step)
    gus.total(gu_got.at[s])
    gu_all = SeqGather(p, gu_got.at[s], gu_got, seq_send.at[2], seq_recv.at[2])
    gu_all.start()
    holder = f // per
    moved = (s + 4 - holder) % 4
    is_across = moved == 2

    @pl.when(is_across)
    def _():
        def pass_cast(c):
            cast(c, 0).wait_recv()
            cast(c, 0).start()

        loop(CHUNKS, pass_cast)

    loop(L - 1, ins.step)
    gu_all.forward()
    ins.total(in_got.at[s])
    in_all = SeqGather(p, in_got.at[s], in_got, seq_send.at[3], seq_recv.at[3])
    in_all.start()

    @pl.when((s != holder) & jnp.logical_not(is_across))
    def _():
        loop(CHUNKS, lambda c: cast(c, 0).wait_recv())

    @pl.when(s == holder)
    def _():
        def sent(c):
            cast(c, 0).wait_send()
            cast(c, 1).wait_send()

        loop(CHUNKS, sent)

    @pl.when(is_across)
    def _():
        loop(CHUNKS, lambda c: cast(c, 0).wait_send())

    def out_sent(index):
        i, c = index // CHUNKS, index % CHUNKS
        out_pair_copy(i, c).wait_send()

        @pl.when(z != s * half + i)
        def _():
            side_copy(i, c, True).wait_send()

    loop(half * CHUNKS, out_sent)
    gus.wait_sends()
    ins.wait_sends()
    d_sum.wait_sends()
    small_all.finish()
    gu_all.finish()
    in_all.forward()
    in_all.finish()


def reduce_all(seq_count, fsdp_count, arrays):
    g_in, g_gu, g_out, small, d_norm = arrays
    fl, bf = jnp.float32, jnp.bfloat16
    L = fsdp_count // 2
    per = fsdp_count // seq_count
    n = seq_count
    own, in_w = g_in.shape[1:]
    gu_w = g_gu.shape[2]
    out_rows, model = g_out.shape[1:]
    rows = d_norm.shape[1]
    v = pltpu.VMEM
    return pl.pallas_call(
        partial(reduce_kernel, seq_count, fsdp_count),
        out_shape=[
            jax.ShapeDtypeStruct((n, own, in_w), bf),
            jax.ShapeDtypeStruct((n, own, gu_w), bf),
            jax.ShapeDtypeStruct((out_rows, model), bf),
            jax.ShapeDtypeStruct((n,) + small.shape, fl),
            jax.ShapeDtypeStruct((rows, model), fl),
        ],
        in_specs=[pl.BlockSpec(memory_space=v)] * 5,
        out_specs=[pl.BlockSpec(memory_space=v)] * 5,
        scratch_shapes=[
            v((L, own, in_w), bf),
            v((2 * L, own, in_w), bf),
            v((own, in_w), fl),
            v((L, own, gu_w), bf),
            v((2 * L, own, gu_w), bf),
            v((own, gu_w), fl),
            v((per // 2, out_rows, model), bf),
            v((2, per // 2, out_rows, model), bf),
            v((out_rows // CHUNKS, model), fl),
            v(small.shape, fl),
            v((L,) + small.shape, fl),
            v((3, rows, model), bf),
            v((3, rows, model), bf),
            dma(2, L),
            dma(2, 2 * L),
            dma(2, L),
            dma(2, 2 * L),
            dma(2, per // 2, CHUNKS),
            dma(3, per // 2, CHUNKS),
            dma(2, CHUNKS),
            dma(CHUNKS),
            dma(3, L),
            dma(L),
            dma(1),
            dma(1),
            dma(4, 3),
            dma(4, 3),
        ],
        compiler_params=pltpu.CompilerParams(
            collective_id=2, has_side_effects=True, vmem_limit_bytes=VMEM_LIMIT
        ),
        name="reduce_grads",
    )(*arrays)


def rms_scale(values):
    return lax.rsqrt(jnp.mean(values * values, axis=-1, keepdims=True) + EPS)


def swish_slope(values):
    sigma = jax.nn.sigmoid(values)
    return sigma * (1.0 + values * (1.0 - sigma))


def silu_slope(values):
    sigma = jax.nn.sigmoid(values)
    return values * sigma, sigma * (1.0 + values * (1.0 - sigma))


def rows_at(r, size=128):
    return pl.ds(pl.multiple_of(r * size, size), size)


def dot(a, b, **kw):
    return jnp.dot(a, b, preferred_element_type=jnp.float32, **kw)


def dot_t(a, b, **kw):
    return lax.dot_general(a, b, (((1,), (1,)), ((), ())), preferred_element_type=jnp.float32, **kw)


def t_dot(a, b, **kw):
    return lax.dot_general(a, b, (((0,), (0,)), ((), ())), preferred_element_type=jnp.float32, **kw)


def row_sums(values):
    ones = jnp.ones((8, values.shape[1]), jnp.float32)
    return dot_t(ones, values, precision=HIGHEST)


def iota2(shape, axis):
    return lax.broadcasted_iota(jnp.int32, shape, axis)


def head_matrix(width):
    return (iota2((width, 128), 0) // HD == iota2((width, 128), 1)).astype(jnp.float32)


def partner(values):
    lane = iota2(values.shape, 1)
    return jnp.where(lane % HD < HD // 2, pltpu.roll(values, 96, 1), pltpu.roll(values, 32, 1))


def fill_mask(bias, seg_col, seg_row, transposed):
    total = bias.shape[0]

    def some(r):
        t = iota2((128, total), 0) + r * 128
        other = iota2((128, total), 1)
        order = t <= other if transposed else t >= other
        same = seg_col[rows_at(r)] == seg_row[0:1, :]
        bias[rows_at(r)] = jnp.where(order & same, 0.0, -1e30)

    loop(total // 128, some)


def forward_kernel(
    seq_count,
    fsdp_count,
    hidden,
    cot,
    mamba_in,
    attn_in,
    small,
    gate_up,
    mamba_out,
    attn_out,
    down_proj,
    gain_in,
    seg_col,
    seg_row,
    place,
    cosine,
    sine,
    taps,
    heads,
    layer_out,
    d_mixed,
    ffn_in,
    ffn_act,
    d_ffn,
    d_mixed_all,
    gated_b,
    d_gated,
    d_attn,
    g_ffn_gain,
    g_gated_gain,
    cot_all,
    in_all,
    normed,
    gate_raw,
    inputs_b,
    accum_out,
    scan_bf,
    scan_y,
    steps,
    cum,
    attn_mix,
    gain_rows,
    hid_all,
    w_gu,
    w_mo,
    w_ao,
    w_dn,
    w_gg,
    pre_pad,
    x_act,
    b_mat,
    c_mat,
    x_step,
    inner,
    bias,
    gated,
    part_mix,
    gate_vals,
    d_act,
    d_gn,
    mixed,
    norm2,
    sq_buf,
    mean_buf,
    stage,
    got,
    local,
    in_send,
    in_recv,
    gu_send,
    gu_recv,
    out_send,
    out_recv,
    seq_send,
    seq_recv,
):
    p = Place(seq_count, fsdp_count)
    s, f, z, y, L = p.s, p.f, p.z, p.y, p.L
    fl, bf = jnp.float32, jnp.bfloat16
    per = fsdp_count // seq_count
    half = per // 2
    own_rows = mamba_in.shape[0]
    x_width = gate_raw.shape[1]
    query_width = attn_mix.shape[2]
    ff = w_dn.shape[0]
    rows = hidden.shape[0]
    total = seq_count * rows
    head_share = x_width // HD
    bc = mamba_in.shape[1] - 2 * DI
    conv_width = x_width + bc

    copies = []

    def bring(src, dst):
        copy = pltpu.make_async_copy(src, dst, local.at[len(copies)])
        copy.start()
        copies.append(copy)

    def part(ref, start, size):
        return ref.at[:, pl.ds(pl.multiple_of(start, 128), size)]

    def own_cols(ref, start, size):
        return ref.at[rows_at(f, own_rows), pl.ds(start, size)]

    c0 = 0
    for src, start, size in (
        (mamba_in, s * x_width, x_width),
        (mamba_in, DI + s * x_width, x_width),
        (mamba_in, 2 * DI, bc),
        (attn_in, s * query_width, query_width),
        (small, 0, small.shape[1]),
    ):
        bring(part(src, start, size), own_cols(in_all, c0, size))
        c0 += size
    in_copies = len(copies)
    bring(hidden, hid_all.at[s])
    bring(cot, cot_all.at[s])
    bring(part(gate_up, s * ff, ff), own_cols(w_gu, 0, ff))
    bring(part(gate_up, FF + s * ff, ff), own_cols(w_gu, ff, ff))
    holder = f // per == s
    spread_arrays = ((gain_in, w_gg, 1), (mamba_out, w_mo, 2), (attn_out, w_ao, 1), (down_proj, w_dn, 2))

    def own_spread(act):
        @pl.when(holder)
        def _():
            for k, (src, dst, _) in enumerate(spread_arrays):
                size = src.shape[0]
                act(pltpu.make_async_copy(src, dst.at[rows_at(f - s * per, size)], local.at[12 + k]))

    own_spread(lambda copy: copy.start())
    p.greet(diag=True)
    for copy in copies[:in_copies]:
        copy.wait()
    ins = LineGather(p, in_all, in_send, in_recv, size=own_rows)
    gus = LineGather(p, w_gu, gu_send, gu_recv, size=own_rows)
    hid = SeqGather(p, hidden, hid_all, seq_send.at[7], seq_recv.at[7])
    cots = SeqGather(p, cot, cot_all, seq_send.at[8], seq_recv.at[8])
    hid.start()
    ins.start()
    fill_mask(bias, seg_col, seg_row, False)
    hid.forward()
    loop(L - 1, lambda d: ins.step(d + 1))
    cots.start()
    for copy in copies[in_copies:]:
        copy.wait()
    own_spread(lambda copy: copy.wait())

    pieces = []
    for k, (src, dst, count) in enumerate(spread_arrays):
        size = src.shape[0]
        for c in range(count):
            pieces.append((dst, size, c * (size // count), size // count))

    def piece_copy(i, k, way, other=0):
        dst, size, offset, count = pieces[k]
        j = 2 * i + (1 - y if other else y)
        ref = dst.at[pl.ds(pl.multiple_of(j * size + offset, 16), count)]
        device = (p.right, p.left, p.pair)[way]
        return rcopy(ref, ref, out_send.at[way, i, k], out_recv.at[way // 2, i, k], device)

    def push_piece(i, k):
        zs = s * half + i

        @pl.when((z >= zs) & p.has_right)
        def _():
            piece_copy(i, k, 0).start()

        @pl.when((z <= zs) & p.has_left)
        def _():
            piece_copy(i, k, 1).start()

        piece_copy(i, k, 2).start()

    def hold_piece(k):
        for i in range(half):

            @pl.when(z == s * half + i)
            def _():
                push_piece(i, k)

    def pass_piece(k):
        for i in range(half):

            @pl.when(z != s * half + i)
            def _():
                piece_copy(i, k, 0).wait_recv()
                push_piece(i, k)

    def end_piece(k):
        for i in range(half):
            piece_copy(i, k, 2, 1).wait_recv()

    def sent_piece(k):
        for i in range(half):
            zs = s * half + i
            piece_copy(i, k, 2).wait_send()

            @pl.when((z >= zs) & p.has_right)
            def _():
                piece_copy(i, k, 0).wait_send()

            @pl.when((z <= zs) & p.has_left)
            def _():
                piece_copy(i, k, 1).wait_send()

    early = range(4)
    late = range(4, len(pieces))
    for k in early:
        hold_piece(k)
    gus.start()
    for k in late:
        hold_piece(k)
    ins.finish()
    hid.finish()
    cots.forward()

    gain_t = in_all[:, in_all.shape[1] - 128 :].astype(fl).T
    gain_rows[...] = gain_t[0:16]
    first_gain = gain_rows[head_share : head_share + 1, :]

    def norm_block(r):
        values = hid_all[r].astype(fl)
        scale = lax.rsqrt(jnp.mean(values * values, axis=-1, keepdims=True) + EPS)
        normed[rows_at(r)] = (values * scale * first_gain).astype(bf)

    loop(seq_count, norm_block)
    pass_piece(0)
    gate_raw[...] = dot(normed[...], in_all[:, :x_width])
    inputs_b[:, :conv_width] = dot(normed[...], in_all[:, x_width : x_width + conv_width]).astype(bf)
    inputs_b[:, conv_width:] = dot(normed[...], in_all[:, x_width + conv_width :]).astype(bf)
    pass_piece(1)
    pre_pad[0:8] = jnp.zeros((8, conv_width), fl)
    pre_pad[8 : 8 + total] = inputs_b[:, :conv_width].astype(fl)
    for r in range(seq_count):
        at = slice(r * rows, (r + 1) * rows)
        accum = taps[KC : KC + 1, :] + taps[KC - 1 : KC, :] * pre_pad[8 + r * rows : 8 + (r + 1) * rows]
        for lag in range(1, KC):
            moved = pre_pad[8 + r * rows - lag : 8 + (r + 1) * rows - lag]
            accum = accum + taps[KC - 1 - lag : KC - lag, :] * jnp.where(
                place[at] >= lag, moved, 0.0
            )
        accum_out[at] = accum
        acts = accum * jax.nn.sigmoid(accum)
        x_act[at] = acts[:, :x_width]
        b_mat[at] = acts[:, x_width : x_width + NST].astype(bf)
        c_mat[at] = acts[:, x_width + NST :].astype(bf)
    pass_piece(2)
    raw = inputs_b[:, conv_width + query_width + 2 * HD :].astype(fl) + heads[0:1, :128]
    steps[...] = jnp.maximum(raw, 0.0) + jnp.log1p(jnp.exp(-jnp.abs(raw)))
    causal = (iota2((total, total), 0) >= iota2((total, total), 1)).astype(fl)
    cum[...] = dot(causal, heads[1:2, :128] * steps[...], precision=HIGHEST)
    cum_t = cum[...].T
    spread_heads = head_matrix(x_width)
    x_step[...] = (x_act[...] * dot_t(steps[...], spread_heads, precision=HIGHEST)).astype(bf)
    inner[...] = dot_t(c_mat[...], b_mat[...])
    pass_piece(3)
    pumps = {0: lambda: gus.step(1), 2: lambda: gus.step(2), 4: lambda: gus.step(3)}
    for h in range(head_share):
        hs = slice(h * HD, (h + 1) * HD)
        for r in range(seq_count):
            at = slice(r * rows, (r + 1) * rows)
            K = (r + 1) * rows
            decay = jnp.exp(cum[at, h : h + 1] - cum_t[h : h + 1, :K] + bias[at, :K])
            kernel_b = (inner[at, :K] * decay).astype(bf)
            scan_y[at, hs] = dot(kernel_b, x_step[:K, hs])
        if h in pumps and L == 4:
            pumps[h]()
    for r in range(seq_count):
        at = slice(r * rows, (r + 1) * rows)
        scan = (scan_y[at] + heads[2:3, :x_width] * x_act[at]).astype(bf)
        scan_bf[at] = scan
        gate = gate_raw[at]
        gated[r] = scan.astype(fl) * (gate * jax.nn.sigmoid(gate))
    for r in range(seq_count):
        values = gated[r]
        sq_buf[s, :, r * rows : (r + 1) * rows] = row_sums(values * values)
    peers = (p.sib, p.across, p.diag)
    peer_at = (p.s1, p.s2, p.s3)

    def exchange(buf, at):
        pairs = []
        for k in range(3):
            copy = rcopy(buf.at[s], buf.at[s], seq_send.at[at, k], seq_recv.at[at, k], peers[k])
            copy.start()
            other = buf.at[peer_at[k]]
            pairs.append((copy, rcopy(other, other, seq_send.at[at, k], seq_recv.at[at, k], peers[k])))

        def end():
            for copy, arrived in pairs:
                arrived.wait_recv()
                copy.wait_send()
            return buf[0] + buf[1] + buf[2] + buf[3]

        return end

    sq_end = exchange(sq_buf, 0)
    q_in = inputs_b[:, conv_width : conv_width + query_width].astype(fl)
    kv_in = inputs_b[:, conv_width + query_width : conv_width + query_width + 2 * HD].astype(fl)
    q_rot = q_in * cosine[...] + partner(q_in) * sine[...]
    k_rot = (kv_in * cosine[...] + partner(kv_in) * sine[...])[:, :HD]
    v_b = inputs_b[:, conv_width + query_width + HD : conv_width + query_width + 2 * HD]
    for r in range(seq_count):
        at = slice(r * rows, (r + 1) * rows)
        K = (r + 1) * rows
        for h in range(query_width // HD):
            hs = slice(h * HD, (h + 1) * HD)
            scores = dot_t(q_rot[at, hs], k_rot[:K], precision=HIGHEST) * (1.0 / math.sqrt(HD))
            weights = jnp.exp(scores + bias[at, :K])
            weights = weights / jnp.sum(weights, axis=-1, keepdims=True)
            attn_mix[r, :, hs] = dot(weights.astype(bf), v_b[:K]).astype(bf)
    cots.finish()
    for k in early:
        end_piece(k)
    gain = w_gg[...].astype(fl).T[0:1, :]
    for r in range(seq_count):
        part_mix[r] = dot((gated[r] * gain).astype(bf), w_mo[...])
    scale_cols = lax.rsqrt(sq_end() / DI + EPS).T
    for r in range(seq_count):
        scale = scale_cols[r * rows : (r + 1) * rows, 0:1]
        part_mix[r] = part_mix[r] * scale + dot(attn_mix[r], w_ao[...])
        gated_b[r] = (gated[r] * scale * gain).astype(bf)

    def reducer(at):
        return SeqReduce(p, stage.at[at], got.at[at], seq_send.at[at + 1], seq_recv.at[at + 1])

    mix = reducer(0)
    mix.send_diag(part_mix[p.s3])
    mix.send_sib(part_mix[p.s1])
    mix.send_across(part_mix[p.s2])
    for k in late:
        pass_piece(k)
    second_gain = gain_rows[head_share + 1 : head_share + 2, :]
    residual = hid_all[s].astype(fl)
    mixed[...] = residual + mix.total(part_mix[s])
    scale2 = lax.rsqrt(jnp.mean(mixed[...] * mixed[...], axis=-1, keepdims=True) + EPS)
    norm2[...] = mixed[...] * scale2
    ffn_in[s] = (norm2[...] * second_gain).astype(bf)
    ffn_all = SeqGather(p, ffn_in.at[s], ffn_in, seq_send.at[4], seq_recv.at[4])
    ffn_all.start()
    if L != 4:
        loop(L - 1, lambda d: gus.step(d + 1))
    for k in late:
        end_piece(k)
    gus.finish()

    def ffn_block(r):
        d_act[r] = dot_t(cot_all[r], w_dn[...])
        gate_vals[r] = dot(ffn_in[r], w_gu[...])

    def act_block(r):
        gate_lin = gate_vals[r, :, :ff]
        up_lin = gate_vals[r, :, ff:]
        act, slope = silu_slope(gate_lin)
        ffn_act[r] = (act * up_lin).astype(bf)
        da = d_act[r]
        d_ffn[r, :, :ff] = (da * up_lin * slope).astype(bf)
        d_ffn[r, :, ff:] = (da * act).astype(bf)

    ffn_block(s)
    act_block(s)
    ffn_all.wait_sib()
    ffn_block(p.s1)
    ffn_all.forward()
    act_block(p.s1)
    ffn_block(p.s2)
    act_block(p.s2)
    ffn_all.wait_diag()
    ffn_block(p.s3)
    act_block(p.s3)
    back = reducer(1)
    back.send_diag(dot_t(d_ffn[p.s3], w_gu[...]))
    back.send_sib(dot_t(d_ffn[p.s1], w_gu[...]))
    back.send_across(dot_t(d_ffn[p.s2], w_gu[...]))
    out = reducer(2)
    d_ffn_own = dot_t(d_ffn[s], w_gu[...])
    d_ffn_in = back.total(d_ffn_own)
    g_ffn_gain[...] = jnp.sum(d_ffn_in * norm2[...], axis=0, keepdims=True)
    d_second = d_ffn_in * second_gain
    d_mixed[...] = cot_all[s].astype(fl) + scale2 * (
        d_second - norm2[...] * jnp.mean(d_second * norm2[...], axis=-1, keepdims=True)
    )
    d_mixed_all[s] = d_mixed[...].astype(bf)
    back_all = SeqGather(p, d_mixed_all.at[s], d_mixed_all, seq_send.at[5], seq_recv.at[5])
    back_all.start()
    out.send_diag(dot(ffn_act[p.s3], w_dn[...]))
    out.send_sib(dot(ffn_act[p.s1], w_dn[...]))

    def mixer_block(r):
        block = d_mixed_all[r]
        d_gn[r] = dot_t(block, w_mo[...])
        d_attn[r] = dot_t(block, w_ao[...]).astype(bf)

    mixer_block(s)
    back_all.wait_sib()
    mixer_block(p.s1)
    out.send_across(dot(ffn_act[p.s2], w_dn[...]))
    back_all.forward()
    mixer_block(p.s2)
    back_all.wait_diag()
    mixer_block(p.s3)
    for r in range(seq_count):
        scale = scale_cols[r * rows : (r + 1) * rows, 0:1]
        values = d_gn[r] * gain * (gated[r] * scale)
        mean_buf[s, :, r * rows : (r + 1) * rows] = row_sums(values)
    mean_end = exchange(mean_buf, 6)
    layer_out[...] = (mixed[...] + out.total(dot(ffn_act[s], w_dn[...]))).astype(bf)
    gain_total = jnp.zeros_like(g_gated_gain[...])
    for r in range(seq_count):
        scale = scale_cols[r * rows : (r + 1) * rows, 0:1]
        gain_total = gain_total + jnp.sum(d_gn[r] * (gated[r] * scale), axis=0, keepdims=True)
    g_gated_gain[...] = gain_total
    means = (mean_end() / DI).T
    for r in range(seq_count):
        scale = scale_cols[r * rows : (r + 1) * rows, 0:1]
        mean = means[r * rows : (r + 1) * rows, 0:1]
        d_gated[r] = scale * (d_gn[r] * gain - (gated[r] * scale) * mean)
    for k in range(len(pieces)):
        sent_piece(k)
    mix.wait_sends()
    back.wait_sends()
    out.wait_sends()
    ffn_all.wait_sends()
    back_all.wait_sends()


def forward_all(seq_count, fsdp_count, widths, arrays):
    x_width, query_width, ff = widths
    hidden, cot, mamba_in, attn_in, small = arrays[:5]
    mamba_out, attn_out, down_proj, gain_in = arrays[6:10]
    fl, bf = jnp.float32, jnp.bfloat16
    rows, model = hidden.shape
    n = seq_count
    total = n * rows
    per = fsdp_count // seq_count
    L = fsdp_count // 2
    conv_width = x_width + 2 * NST
    in_width = x_width + conv_width + query_width + small.shape[1]
    v = pltpu.VMEM

    def sds(*shape, dtype=bf):
        return jax.ShapeDtypeStruct(shape, dtype)

    outs = [
        sds(rows, model),
        sds(rows, model, dtype=fl),
        sds(n, rows, model),
        sds(n, rows, ff),
        sds(n, rows, 2 * ff),
        sds(n, rows, model),
        sds(n, rows, x_width),
        sds(n, rows, x_width, dtype=fl),
        sds(n, rows, query_width),
        sds(1, model, dtype=fl),
        sds(1, x_width, dtype=fl),
        sds(n, rows, model),
        sds(model, in_width),
        sds(total, model),
        sds(total, x_width, dtype=fl),
        sds(total, in_width - x_width),
        sds(total, conv_width, dtype=fl),
        sds(total, x_width),
        sds(total, x_width, dtype=fl),
        sds(total, 128, dtype=fl),
        sds(total, 128, dtype=fl),
        sds(n, rows, query_width),
        sds(16, model, dtype=fl),
    ]
    vm = pl.BlockSpec(memory_space=v)
    hbm = pl.BlockSpec(memory_space=pl.ANY)
    return pl.pallas_call(
        partial(forward_kernel, seq_count, fsdp_count),
        out_shape=outs,
        in_specs=[hbm] * 10 + [vm] * (len(arrays) - 10),
        out_specs=[vm] * len(outs),
        scratch_shapes=[
            v((n, rows, model), bf),
            v((model, 2 * ff), bf),
            v((x_width, model), bf),
            v((query_width, model), bf),
            v((ff, model), bf),
            v((x_width, 128), bf),
            v((total + 8, conv_width), fl),
            v((total, x_width), fl),
            v((total, NST), bf),
            v((total, NST), bf),
            v((total, x_width), bf),
            v((total, total), fl),
            v((total, total), fl),
            v((n, rows, x_width), fl),
            v((n, rows, model), fl),
            v((n, rows, 2 * ff), fl),
            v((n, rows, ff), fl),
            v((n, rows, x_width), fl),
            v((rows, model), fl),
            v((rows, model), fl),
            v((n, 8, total), fl),
            v((n, 8, total), fl),
            v((3, 3, rows, model), bf),
            v((3, 3, rows, model), bf),
            dma(16),
            dma(3, L),
            dma(fsdp_count),
            dma(3, L),
            dma(fsdp_count),
            dma(3, per // 2, 6),
            dma(2, per // 2, 6),
            dma(9, 3),
            dma(9, 3),
        ],
        compiler_params=pltpu.CompilerParams(
            collective_id=3, has_side_effects=True, vmem_limit_bytes=VMEM_LIMIT
        ),
        name="forward_fused",
    )(*arrays)


SMALL_ROWS = 48


def backward_kernel(
    seq_count,
    fsdp_count,
    hidden,
    d_mixed,
    d_mixed_all,
    cot_all,
    ffn_in,
    ffn_act,
    d_ffn,
    gated_b,
    attn_mix,
    d_gated,
    d_attn,
    g_ffn_gain,
    g_gated_gain,
    in_all,
    normed,
    gate_raw,
    inputs_b,
    accum_in,
    scan_bf,
    scan_y,
    steps,
    cum,
    gain_rows,
    seg_col,
    seg_row,
    place,
    cosine,
    sine,
    taps,
    heads,
    in_got,
    gu_got,
    out_got,
    small_got,
    grad_tok,
    g_in,
    g_gu,
    g_out,
    small,
    d_norm,
    d_in,
    dy,
    x_act,
    b_mat,
    c_mat,
    x_step,
    inner,
    inner_t,
    bias,
    bias_t,
    d_inner,
    d_x_step,
    d_acc,
    shifted,
    d_kv,
    d_x_conv,
    in_pair,
    in_side,
    in_acc,
    gu_pair,
    gu_side,
    gu_acc,
    out_pair,
    out_side,
    out_acc,
    small_pair,
    small_line,
    stage,
    got,
    in_send,
    in_recv,
    gu_send,
    gu_recv,
    out_send,
    out_recv,
    cast_send,
    cast_recv,
    small_send,
    small_recv,
    sp_send,
    sp_recv,
    seq_send,
    seq_recv,
):
    p = Place(seq_count, fsdp_count)
    s, f, z, y, L = p.s, p.f, p.z, p.y, p.L
    fl, bf = jnp.float32, jnp.bfloat16
    per = fsdp_count // seq_count
    half = per // 2
    chunk = g_out.shape[1] // CHUNKS
    total = normed.shape[0]
    rows = total // seq_count
    model = normed.shape[1]
    own_rows = model // fsdp_count
    x_width = gate_raw.shape[1]
    query_width = attn_mix.shape[1]
    conv_width = accum_in.shape[1]
    head_share = x_width // HD
    ff = ffn_act.shape[1]
    gain_own, attn_own, ff_own = DI // fsdp_count, QH * HD // fsdp_count, FF // fsdp_count
    p.greet()

    def rows_of(c):
        return pl.ds(pl.multiple_of(c * chunk, 16), chunk)

    def out_pair_copy(i, c):
        return rcopy(
            g_out.at[2 * i + 1 - y, rows_of(c)],
            out_pair.at[i, rows_of(c)],
            out_send.at[0, i, c],
            out_recv.at[0, i, c],
            p.pair,
        )

    def side_copy(i, c, right):
        at = 0 if right else 1
        return rcopy(
            out_pair.at[i, rows_of(c)],
            out_side.at[at, i, rows_of(c)],
            out_send.at[1, i, c],
            out_recv.at[1 + at, i, c],
            p.right if right else p.left,
        )

    def cast(c, way):
        ref = out_got.at[rows_of(c)]
        return rcopy(ref, ref, cast_send.at[way, c], cast_recv.at[c], p.across if way else p.sib)

    def out_step(index):
        i, c = index // CHUNKS, index % CHUNKS
        zs = s * half + i
        out_pair_copy(i, c).wait_recv()
        mine = g_out.at[2 * i + y, rows_of(c)]
        other = out_pair.at[i, rows_of(c)]
        add_rows(out_acc, mine, other)

        @pl.when(p.has_left & (z <= zs))
        def _():
            side_copy(i, c, True).wait_recv()
            add_rows(out_acc, out_acc, out_side.at[0, i, rows_of(c)])

        @pl.when(p.has_right & (z >= zs))
        def _():
            side_copy(i, c, False).wait_recv()
            add_rows(out_acc, out_acc, out_side.at[1, i, rows_of(c)])

        @pl.when(z == zs)
        def _():
            add_rows(out_got.at[rows_of(c)], out_acc)
            cast(c, 1).start()
            cast(c, 0).start()

        @pl.when(z < zs)
        def _():
            add_rows(other, out_acc)
            side_copy(i, c, True).start()

        @pl.when(z > zs)
        def _():
            add_rows(other, out_acc)
            side_copy(i, c, False).start()

    ins = LineReduce(p, g_in, in_pair, in_side, in_acc, in_send, in_recv)
    gus = LineReduce(p, g_gu, gu_pair, gu_side, gu_acc, gu_send, gu_recv)

    for fi in range(fsdp_count):
        at = slice(fi * own_rows, (fi + 1) * own_rows)
        g_gu[fi] = t_dot(ffn_in[:, at], d_ffn[...]).astype(bf)
    gus.start()
    g_mo = t_dot(gated_b[...], d_mixed_all[...]).astype(bf)
    g_ao = t_dot(attn_mix[...], d_mixed_all[...]).astype(bf)
    for j in range(per):
        g_out[j, :gain_own] = g_mo[j * gain_own : (j + 1) * gain_own]
        g_out[j, gain_own : gain_own + attn_own] = g_ao[j * attn_own : (j + 1) * attn_own]
        act = ffn_act[:, j * ff_own : (j + 1) * ff_own]
        g_out[j, gain_own + attn_own :] = t_dot(act, cot_all[...]).astype(bf)
    loop(half * CHUNKS, lambda index: out_pair_copy(index // CHUNKS, index % CHUNKS).start())

    fill_mask(bias, seg_col, seg_row, False)
    fill_mask(bias_t, seg_col, seg_row, True)
    spread_heads = head_matrix(x_width)
    steps_wide = dot_t(steps[...], spread_heads, precision=HIGHEST)
    skip = heads[2:3, :x_width]
    cum_t = cum[...].T
    for r in range(seq_count):
        at = slice(r * rows, (r + 1) * rows)
        accum = accum_in[at]
        acts = accum * jax.nn.sigmoid(accum)
        x_act[at] = acts[:, :x_width]
        b_mat[at] = acts[:, x_width : x_width + NST].astype(bf)
        c_mat[at] = acts[:, x_width + NST :].astype(bf)
        x_step[at] = (acts[:, :x_width] * steps_wide[at]).astype(bf)
        gate_act, slope = silu_slope(gate_raw[at])
        cots = d_gated[at]
        dy[at] = (cots * gate_act).astype(bf)
        d_in[at, :x_width] = (cots * scan_bf[at].astype(fl) * slope).astype(bf)
    inner[...] = dot_t(c_mat[...], b_mat[...])
    inner_t[...] = dot_t(b_mat[...], c_mat[...])
    d_inner[...] = jnp.zeros_like(d_inner)
    pumps = {
        0: lambda: gus.step(0),
        1: lambda: gus.step(1),
        2: lambda: gus.step(2),
        3: lambda: gus.total(gu_got.at[s]),
        4: lambda: loop(half * CHUNKS, out_step),
    }
    gu_all = SeqGather(p, gu_got.at[s], gu_got, seq_send.at[2], seq_recv.at[2])
    for h in range(head_share):
        hs = slice(h * HD, (h + 1) * HD)
        for r in range(seq_count):
            at = slice(r * rows, (r + 1) * rows)
            K = (r + 1) * rows
            decay = jnp.exp(cum[at, h : h + 1] - cum_t[h : h + 1, :K] + bias[at, :K])
            d_inner[at, :K] += dot_t(dy[at, hs], x_step[:K, hs]) * decay
            decay = jnp.exp(cum_t[h : h + 1, r * rows :] - cum[at, h : h + 1] + bias_t[at, r * rows :])
            kernel_t = (inner_t[at, r * rows :] * decay).astype(bf)
            d_x_step[at, hs] = dot(kernel_t, dy[r * rows :, hs])
        if L == 4 and h in pumps:
            pumps[h]()
            if h == 3:
                gu_all.start()
    if L != 4:
        loop(L - 1, gus.step)
        gus.total(gu_got.at[s])
        gu_all.start()
        loop(half * CHUNKS, out_step)
    d_inner_b = d_inner[...].astype(bf)
    d_acc[:, x_width : x_width + NST] = t_dot(d_inner_b, c_mat[...])
    d_acc[:, x_width + NST :] = dot(d_inner_b, b_mat[...])
    dy_f = dy[...].astype(fl)
    xs = x_act[...]
    dxs = d_x_step[...]
    d_acc[:, :x_width] = steps_wide * dxs + skip * dy_f
    head_sums = dot(
        jnp.sum((dy_f * xs).reshape(total // 8, 8, x_width), axis=0), spread_heads, precision=HIGHEST
    )
    g_skip = jnp.sum(head_sums, axis=0, keepdims=True)
    step_direct = dot(xs * dxs, spread_heads, precision=HIGHEST)
    d_cum = dot(
        dy_f * scan_y[...] - x_step[...].astype(fl) * dxs, spread_heads, precision=HIGHEST
    )
    after = (iota2((total, total), 0) <= iota2((total, total), 1)).astype(fl)
    d_log = dot(after, d_cum, precision=HIGHEST)
    decay_row = heads[1:2, :128]
    g_decay = jnp.sum(d_log * (decay_row * steps[...]), axis=0, keepdims=True)
    raw = inputs_b[:, conv_width + query_width + 2 * HD :].astype(fl) + heads[0:1, :128]
    d_raw = (step_direct + d_log * decay_row) * jax.nn.sigmoid(raw)
    d_raw = jnp.where(iota2(d_raw.shape, 1) < head_share, d_raw, 0.0)
    g_step_bias = jnp.sum(d_raw, axis=0, keepdims=True)
    step_at = x_width + conv_width + query_width + 2 * HD
    d_in[:, step_at:] = d_raw.astype(bf)

    q_at = conv_width
    kv_at = conv_width + query_width
    q_in = inputs_b[:, q_at:kv_at].astype(fl)
    kv_in = inputs_b[:, kv_at : kv_at + 2 * HD].astype(fl)
    q_rot = q_in * cosine[...] + partner(q_in) * sine[...]
    k_rot = (kv_in * cosine[...] + partner(kv_in) * sine[...])[:, :HD]
    k_b = k_rot.astype(bf)
    v_b = inputs_b[:, kv_at + HD : kv_at + 2 * HD]
    d_kv[...] = jnp.zeros_like(d_kv)
    scale = 1.0 / math.sqrt(HD)
    for r in range(seq_count):
        at = slice(r * rows, (r + 1) * rows)
        K = (r + 1) * rows
        for h in range(query_width // HD):
            hs = slice(h * HD, (h + 1) * HD)
            scores = dot_t(q_rot[at, hs], k_rot[:K], precision=HIGHEST) * scale
            weights = jnp.exp(scores + bias[at, :K])
            weights = weights / jnp.sum(weights, axis=-1, keepdims=True)
            d_att = d_attn[at, hs]
            d_weights = dot_t(d_att, v_b[:K])
            along = jnp.sum(d_weights * weights, axis=-1, keepdims=True)
            d_scores = (weights * (d_weights - along) * scale).astype(bf)
            shifted[at, hs] = dot(d_scores, k_b[:K])
            d_kv[:K, :HD] += t_dot(d_scores, q_rot[at, hs].astype(bf))
            d_kv[:K, HD : 2 * HD] += t_dot(weights.astype(bf), d_att)
    d_q = shifted[:total, :query_width]
    d_q = d_q * cosine[...] + partner(d_q * sine[...])
    d_kv_all = d_kv[...]
    d_k = d_kv_all * cosine[...] + partner(d_kv_all * sine[...])
    d_kv_all = jnp.where(iota2(d_k.shape, 1) < HD, d_k, d_kv_all)
    d_in[:, x_width + q_at : x_width + kv_at] = d_q.astype(bf)
    d_in[:, x_width + kv_at : x_width + kv_at + 2 * HD] = d_kv_all.astype(bf)

    tap_sums = [jnp.zeros((1, conv_width), fl) for _ in range(KC + 1)]
    shifted[total:] = jnp.zeros((8, conv_width), fl)
    for r in range(seq_count):
        at = slice(r * rows, (r + 1) * rows)
        d_acc[at] = d_acc[at] * silu_slope(accum_in[at])[1]
        tap_sums[KC] = tap_sums[KC] + jnp.sum(d_acc[at], axis=0, keepdims=True)
        pre = inputs_b[at, :conv_width].astype(fl)
        tap_sums[KC - 1] = tap_sums[KC - 1] + jnp.sum(d_acc[at] * pre, axis=0, keepdims=True)
    for lag in range(1, KC):
        k = KC - 1 - lag
        shifted[:total] = jnp.where(place[...] >= lag, d_acc[...], 0.0)
        for r in range(seq_count):
            at = slice(r * rows, (r + 1) * rows)
            moved = shifted[r * rows + lag : (r + 1) * rows + lag]
            pre = inputs_b[at, :conv_width].astype(fl)
            tap_sums[k] = tap_sums[k] + jnp.sum(moved * pre, axis=0, keepdims=True)
            grads = taps[k : k + 1, :] * moved
            if lag == 1:
                grads = grads + taps[KC - 1 : KC, :] * d_acc[at]
                d_x_conv[at] = grads
            else:
                d_x_conv[at] += grads
    d_in[:, x_width : x_width + conv_width] = d_x_conv[...].astype(bf)

    for fi in range(fsdp_count):
        at = slice(fi * own_rows, (fi + 1) * own_rows)
        g_in[fi] = t_dot(normed[:, at], d_in[...]).astype(bf)
    ins.start()
    gu_all.forward()

    d_sum = SeqReduce(p, stage, got, seq_send.at[0], seq_recv.at[0])
    norm_gain_sum = jnp.zeros((1, model), fl)
    first_gain = gain_rows[head_share : head_share + 1, :]
    for r in range(seq_count):
        at = slice(r * rows, (r + 1) * rows)
        part = dot_t(d_in[at], in_all[...])
        d_norm[r] = part
        norm_gain_sum = norm_gain_sum + jnp.sum(part * normed[at].astype(fl), axis=0, keepdims=True)
    norm_gain_sum = norm_gain_sum / first_gain
    d_sum.send_diag(d_norm[p.s3])
    d_sum.send_sib(d_norm[p.s1])
    d_sum.send_across(d_norm[p.s2])

    def put(at, row):
        for c in range(row.shape[1] // 128):
            small[at + c : at + c + 1, :] = row[:, c * 128 : (c + 1) * 128]
        return at + row.shape[1] // 128

    at = 0
    for row in tap_sums + [g_gated_gain[...], norm_gain_sum, g_ffn_gain[...], g_step_bias, g_decay, g_skip]:
        at = put(at, row)
    small[at:] = jnp.zeros((SMALL_ROWS - at, 128), fl)
    pair_small = rcopy(small, small_pair, sp_send.at[0], sp_recv.at[0], p.pair)
    pair_small.start()
    pair_small.wait_recv()
    small_line[z] = small[...] + small_pair[...]
    smalls = LineGather(p, small_line, small_send, small_recv, pair=False)
    smalls.start()
    loop(L - 1, lambda d: smalls.step(d + 1))
    smalls.finish()
    small_sum = small_line[0]
    for b in range(1, L):
        small_sum = small_sum + small_line[b]
    small_got[s] = small_sum
    small_all = SeqGather(p, small_got.at[s], small_got, seq_send.at[1], seq_recv.at[1])
    small_all.start()
    holder = f // per
    is_across = (s + 4 - holder) % 4 == 2

    @pl.when(is_across)
    def _():
        def pass_cast(c):
            cast(c, 0).wait_recv()
            cast(c, 0).start()

        loop(CHUNKS, pass_cast)

    loop(L - 1, ins.step)
    small_all.forward()
    ins.total(in_got.at[s])
    in_gather = SeqGather(p, in_got.at[s], in_got, seq_send.at[3], seq_recv.at[3])
    in_gather.start()
    d_normed = d_sum.total(d_norm[s])
    residual = hidden[...].astype(fl)
    scale1 = lax.rsqrt(jnp.mean(residual * residual, axis=-1, keepdims=True) + EPS)
    first_norm = residual * scale1
    d_first = d_normed * first_gain
    grad_tok[...] = d_mixed[...] + scale1 * (
        d_first - first_norm * jnp.mean(d_first * first_norm, axis=-1, keepdims=True)
    )

    @pl.when((s != holder) & jnp.logical_not(is_across))
    def _():
        loop(CHUNKS, lambda c: cast(c, 0).wait_recv())

    @pl.when(s == holder)
    def _():
        def sent(c):
            cast(c, 0).wait_send()
            cast(c, 1).wait_send()

        loop(CHUNKS, sent)

    @pl.when(is_across)
    def _():
        loop(CHUNKS, lambda c: cast(c, 0).wait_send())

    def out_sent(index):
        i, c = index // CHUNKS, index % CHUNKS
        out_pair_copy(i, c).wait_send()

        @pl.when(z != s * half + i)
        def _():
            side_copy(i, c, True).wait_send()

    loop(half * CHUNKS, out_sent)
    in_gather.forward()
    pair_small.wait_send()
    gus.wait_sends()
    ins.wait_sends()
    d_sum.wait_sends()
    small_all.finish()
    gu_all.finish()
    in_gather.finish()


def backward_all(seq_count, fsdp_count, arrays):
    hidden = arrays[0]
    fl, bf = jnp.float32, jnp.bfloat16
    L = fsdp_count // 2
    per = fsdp_count // seq_count
    n = seq_count
    rows, model = hidden.shape
    total = n * rows
    ff = FF // n
    x_width = DI // n
    conv_width = x_width + 2 * NST
    in_w = arrays[13].shape[1]
    gu_w = 2 * ff
    own = model // fsdp_count
    out_rows = (DI + QH * HD + FF) // fsdp_count
    v = pltpu.VMEM
    vm = pl.BlockSpec(memory_space=v)
    return pl.pallas_call(
        partial(backward_kernel, seq_count, fsdp_count),
        out_shape=[
            jax.ShapeDtypeStruct((n, own, in_w), bf),
            jax.ShapeDtypeStruct((n, own, gu_w), bf),
            jax.ShapeDtypeStruct((out_rows, model), bf),
            jax.ShapeDtypeStruct((n, SMALL_ROWS, 128), fl),
            jax.ShapeDtypeStruct((rows, model), fl),
        ],
        in_specs=[vm] * len(arrays),
        out_specs=[vm] * 5,
        scratch_shapes=[
            v((fsdp_count, own, in_w), bf),
            v((fsdp_count, own, gu_w), bf),
            v((per, out_rows, model), bf),
            v((SMALL_ROWS, 128), fl),
            v((n, rows, model), fl),
            v((total, in_w), bf),
            v((total, x_width), bf),
            v((total, x_width), fl),
            v((total, NST), bf),
            v((total, NST), bf),
            v((total, x_width), bf),
            v((total, total), fl),
            v((total, total), fl),
            v((total, total), fl),
            v((total, total), fl),
            v((total, total), fl),
            v((total, x_width), fl),
            v((total, conv_width), fl),
            v((total + 8, conv_width), fl),
            v((total, 128), fl),
            v((total, conv_width), fl),
            v((L, own, in_w), bf),
            v((2 * L, own, in_w), bf),
            v((own, in_w), fl),
            v((L, own, gu_w), bf),
            v((2 * L, own, gu_w), bf),
            v((own, gu_w), fl),
            v((per // 2, out_rows, model), bf),
            v((2, per // 2, out_rows, model), bf),
            v((out_rows // CHUNKS, model), fl),
            v((SMALL_ROWS, 128), fl),
            v((L, SMALL_ROWS, 128), fl),
            v((3, rows, model), bf),
            v((3, rows, model), bf),
            dma(2, L),
            dma(2, 2 * L),
            dma(2, L),
            dma(2, 2 * L),
            dma(2, per // 2, CHUNKS),
            dma(3, per // 2, CHUNKS),
            dma(2, CHUNKS),
            dma(CHUNKS),
            dma(3, L),
            dma(L),
            dma(1),
            dma(1),
            dma(4, 3),
            dma(4, 3),
        ],
        compiler_params=pltpu.CompilerParams(
            collective_id=4, has_side_effects=True, vmem_limit_bytes=VMEM_LIMIT
        ),
        name="backward_fused",
    )(*arrays)


def core_inputs(seg_ids, inputs, params):
    pre_conv, step_raw, query_in, key_in = inputs
    taps, tap_bias, step_bias, log_decay = params
    row_count = pre_conv.shape[0]
    tap_count = taps.shape[0]
    accum = tap_bias[None, :] + taps[tap_count - 1][None, :] * pre_conv
    for lag_step in range(1, tap_count):
        moved = jnp.concatenate(
            [
                jnp.zeros((lag_step, pre_conv.shape[1]), pre_conv.dtype),
                pre_conv[: row_count - lag_step],
            ],
            axis=0,
        )
        prior = jnp.concatenate(
            [jnp.full((lag_step,), -1, jnp.int32), seg_ids[: row_count - lag_step]]
        )
        same_seq = (prior == seg_ids)[:, None]
        accum = accum + taps[tap_count - 1 - lag_step][None, :] * jnp.where(same_seq, moved, 0.0)
    activated = jax.nn.silu(accum)
    step = jax.nn.softplus(step_raw + step_bias[None, :])
    log_step = -jnp.exp(log_decay)[None, :] * step
    positions = jnp.arange(row_count, dtype=jnp.int32)
    first_count = jnp.sum((seg_ids == 0).astype(jnp.int32))
    place = (positions - jnp.where(seg_ids == 0, 0, first_count)).astype(jnp.float32)
    half = HD // 2
    freqs = jnp.exp(-math.log(ROPE_THETA) * 2.0 * jnp.arange(half, dtype=jnp.float32) / HD)
    angles = place[:, None] * freqs[None, :]
    cosine = jnp.cos(angles)[:, None, :]
    sine = jnp.sin(angles)[:, None, :]

    def rotate(tensor):
        heads = tensor.reshape(row_count, -1, HD)
        first_half = heads[..., :half]
        second_half = heads[..., half:]
        return jnp.concatenate(
            [first_half * cosine - second_half * sine, second_half * cosine + first_half * sine],
            axis=-1,
        ).reshape(tensor.shape)

    return activated, step, log_step, rotate(query_in), rotate(key_in)


def shards(
    hidden_in,
    grad_out,
    segments,
    norm_gain,
    mamba_in,
    step_in,
    attn_in,
    conv_taps,
    conv_bias,
    step_bias,
    log_decay,
    skip_gain,
    gated_gain,
    mamba_out,
    attn_out,
    ffn_gain,
    gate_up,
    down_proj,
):
    bf_type = jnp.bfloat16
    fl_type = jnp.float32
    seq_count = lax.axis_size("seq")
    seq_index = lax.axis_index("seq")
    fsdp_count = lax.axis_size("fsdp")
    block_rows = hidden_in.shape[1]
    model = hidden_in.shape[2]
    rows = block_rows * seq_count
    own_rows = model // fsdp_count
    x_width = DI // seq_count
    head_share = MH // seq_count
    query_width = QH * HD // seq_count
    query_share = QH // seq_count
    ff_width = FF // seq_count
    owners = [group * KVH // seq_count for group in range(seq_count)]
    owner = seq_index * KVH // seq_count
    gain_own = DI // fsdp_count
    gain_cols = -(-gain_own // own_rows)

    def cols(array, start, size):
        return lax.dynamic_slice_in_dim(array, start, size, 1)

    gain_pad = jnp.pad(gated_gain, (0, gain_cols * own_rows - gain_own))
    main_width = 2 * x_width + 2 * NST + query_width + 2 * HD
    pad_width = 128 - head_share - 2 - gain_cols
    small_pack = jnp.concatenate(
        [
            cols(attn_in, QH * HD + owner * HD, HD),
            cols(attn_in, (QH + KVH) * HD + owner * HD, HD),
            cols(step_in, seq_index * head_share, head_share),
            norm_gain[:, None],
            ffn_gain[:, None],
            gain_pad.reshape(gain_cols, own_rows).T,
            jnp.zeros((own_rows, pad_width), bf_type),
        ],
        axis=1,
    )
    out_pack = jnp.concatenate([mamba_out, attn_out, down_proj], axis=0)
    w_in, w_gate_up, w_out, hidden_all, cot_all = gather_all(
        seq_count,
        fsdp_count,
        (x_width, query_width, ff_width),
        (hidden_in[0], grad_out[0], mamba_in, attn_in, small_pack, gate_up, out_pack),
    )
    per = fsdp_count // seq_count
    in_all = w_in.reshape(model, -1)
    w_gate_up = w_gate_up.reshape(model, -1)
    hidden_all = hidden_all.reshape(rows, model)
    attn_own = QH * HD // fsdp_count
    ff_own = FF // fsdp_count
    w_mamba_out = w_out[:, :gain_own].reshape(x_width, model)
    w_attn_out = w_out[:, gain_own : gain_own + attn_own].reshape(query_width, model)
    w_down = w_out[:, gain_own + attn_own :].reshape(ff_width, model)
    gain_at = main_width + head_share
    first_gain = in_all[:, gain_at].astype(fl_type)
    second_gain = in_all[:, gain_at + 1].astype(fl_type)
    gated_gains = (
        in_all[:, gain_at + 2 : gain_at + 2 + gain_cols]
        .reshape(fsdp_count, own_rows, gain_cols)
        .transpose(0, 2, 1)
        .reshape(fsdp_count, gain_cols * own_rows)[:, :gain_own]
        .reshape(DI)
    )
    mixer_gain = lax.dynamic_slice_in_dim(gated_gains, seq_index * x_width, x_width, 0).astype(
        fl_type
    )

    res_all = hidden_all.astype(fl_type)
    normed = (res_all * rms_scale(res_all) * first_gain).astype(bf_type)
    projected = jnp.dot(normed, in_all, preferred_element_type=fl_type)
    gate_raw = projected[:, :x_width]
    inputs_b = projected[:, x_width:].astype(bf_type).astype(fl_type)
    conv_width = x_width + 2 * NST
    conv_in = inputs_b[:, :conv_width]
    query_in = inputs_b[:, conv_width : conv_width + query_width]
    key_in = inputs_b[:, conv_width + query_width : conv_width + query_width + HD]
    value_b = inputs_b[:, conv_width + query_width + HD : conv_width + query_width + 2 * HD].astype(
        bf_type
    )
    step_at = conv_width + query_width + 2 * HD
    step_raw = inputs_b[:, step_at : step_at + head_share]
    seg_ids = segments[0]
    taps = jnp.concatenate(
        [cols(conv_taps, seq_index * x_width, x_width), conv_taps[:, DI:]], axis=1
    )
    tap_bias = jnp.concatenate(
        [lax.dynamic_slice_in_dim(conv_bias, seq_index * x_width, x_width, 0), conv_bias[DI:]]
    )
    params = (
        taps,
        tap_bias,
        lax.dynamic_slice_in_dim(step_bias, seq_index * head_share, head_share, 0),
        lax.dynamic_slice_in_dim(log_decay, seq_index * head_share, head_share, 0),
    )
    skip = lax.dynamic_slice_in_dim(skip_gain, seq_index * head_share, head_share, 0)
    (activated, step, log_step, queries, keys), pull_back = jax.vjp(
        partial(core_inputs, seg_ids), (conv_in, step_raw, query_in, key_in), params
    )
    positions = jnp.arange(rows, dtype=jnp.int32)
    causal = positions[:, None] >= positions[None, :]
    mask = causal & (seg_ids[:, None] == seg_ids[None, :])
    highest = lax.Precision.HIGHEST
    x_all = activated[:, :x_width]
    b_mat = activated[:, x_width : x_width + NST].astype(bf_type)
    c_mat = activated[:, x_width + NST :].astype(bf_type)
    x_heads = x_all.reshape(rows, head_share, HD).transpose(1, 0, 2)
    step_t = step.T
    cum_t = jnp.dot(log_step.T, causal.T.astype(fl_type), precision=highest)
    inner = jnp.einsum("tn,pn->tp", c_mat, b_mat, preferred_element_type=fl_type)
    decay = jnp.exp(jnp.where(mask[None], cum_t[:, :, None] - cum_t[:, None, :], -1e30))
    kernel_b = (inner[None] * decay).astype(bf_type)
    x_step = (x_heads * step_t[:, :, None]).astype(bf_type)
    scan_y = jnp.einsum("htp,hpd->htd", kernel_b, x_step, preferred_element_type=fl_type)
    ssm = scan_y + skip[:, None, None] * x_heads
    scan_float = (
        ssm.astype(bf_type).transpose(1, 0, 2).reshape(rows, x_width).astype(fl_type)
    )
    key_b = keys.astype(bf_type)
    q_heads = queries.reshape(rows, query_share, HD).transpose(1, 0, 2)
    scores = jnp.einsum("hid,jd->hij", q_heads, keys, precision=highest) * (1.0 / math.sqrt(HD))
    weights = jnp.exp(jnp.where(mask[None], scores, -1e30))
    weights = weights / jnp.sum(weights, axis=-1, keepdims=True)
    weights_b = weights.astype(bf_type)
    attended = jnp.einsum("hij,jd->hid", weights_b, value_b, preferred_element_type=fl_type)
    attn_mix = attended.astype(bf_type).transpose(1, 0, 2).reshape(rows, query_width)

    gate_act = jax.nn.silu(gate_raw)
    gated = scan_float * gate_act
    (
        layer_out,
        d_mixed,
        ffn_in,
        ffn_act,
        d_ffn,
        d_mixed_b,
        gated_b,
        d_gated,
        d_attn,
        g_ffn_gain,
        g_gated_gain,
    ) = middle(
        seq_count,
        fsdp_count,
        (
            gated.reshape(seq_count, block_rows, x_width),
            attn_mix.reshape(seq_count, block_rows, query_width),
            w_mamba_out,
            w_attn_out,
            w_down,
            w_gate_up,
            hidden_in[0],
            grad_out[0],
            cot_all,
            mixer_gain[None],
            second_gain[None],
        ),
    )
    ffn_in = ffn_in.reshape(rows, model)
    ffn_act = ffn_act.reshape(rows, ff_width)
    d_ffn = d_ffn.reshape(rows, 2 * ff_width)
    d_mixed_b = d_mixed_b.reshape(rows, model)
    gated_b = gated_b.reshape(rows, x_width)
    d_gated = d_gated.reshape(rows, x_width)
    d_attn = d_attn.reshape(rows, query_width)
    cot_rows = cot_all.reshape(rows, model)
    g_down = jnp.einsum("tf,td->fd", ffn_act, cot_rows, preferred_element_type=fl_type)
    g_gate_up = jnp.einsum("td,tf->df", ffn_in, d_ffn, preferred_element_type=fl_type)
    g_attn_out = jnp.einsum("tq,td->qd", attn_mix, d_mixed_b, preferred_element_type=fl_type)
    g_mamba_out = jnp.einsum("ti,td->id", gated_b, d_mixed_b, preferred_element_type=fl_type)
    d_scan = (d_gated * gate_act).astype(bf_type)
    d_gate_raw = d_gated * scan_float * swish_slope(gate_raw)
    g_out = jnp.concatenate(
        [
            g_mamba_out.astype(bf_type).reshape(per, gain_own, model),
            g_attn_out.astype(bf_type).reshape(per, attn_own, model),
            g_down.astype(bf_type).reshape(per, ff_own, model),
        ],
        axis=1,
    )

    d_att = d_attn.astype(bf_type).reshape(rows, query_share, HD).transpose(1, 0, 2)
    d_weights = jnp.einsum("hid,jd->hij", d_att, value_b, preferred_element_type=fl_type)
    inner_sum = jnp.sum(d_att.astype(fl_type) * attended, axis=-1, keepdims=True)
    d_scores = (weights * (d_weights - inner_sum) * (1.0 / math.sqrt(HD))).astype(bf_type)
    d_queries = jnp.einsum("hij,jd->hid", d_scores, key_b, preferred_element_type=fl_type)
    d_keys = jnp.einsum(
        "hij,hid->jd", d_scores, q_heads.astype(bf_type), preferred_element_type=fl_type
    )
    d_value = jnp.einsum("hij,hid->jd", weights_b, d_att, preferred_element_type=fl_type)
    d_y = d_scan.reshape(rows, head_share, HD).transpose(1, 0, 2)
    d_y_float = d_y.astype(fl_type)
    d_kernel = jnp.einsum("htd,hpd->htp", d_y, x_step, preferred_element_type=fl_type)
    d_inner = jnp.sum(d_kernel * decay, axis=0).astype(bf_type)
    d_x_step = jnp.einsum("htp,htd->hpd", kernel_b, d_y, preferred_element_type=fl_type)
    d_c = jnp.dot(d_inner, b_mat, preferred_element_type=fl_type)
    d_b = jnp.einsum("tp,tn->pn", d_inner, c_mat, preferred_element_type=fl_type)
    d_x = step_t[:, :, None] * d_x_step + skip[:, None, None] * d_y_float
    g_skip = jnp.sum(d_y_float * x_heads, axis=(1, 2))
    d_step_direct = jnp.sum(x_heads * d_x_step, axis=-1)
    d_cum = jnp.sum(d_y_float * scan_y, axis=-1) - jnp.sum(
        x_step.astype(fl_type) * d_x_step, axis=-1
    )
    d_log_step = jnp.dot(d_cum, causal.astype(fl_type), precision=highest)
    (d_conv, d_step, d_query, d_key), grad_params = pull_back(
        (
            jnp.concatenate([d_x.transpose(1, 0, 2).reshape(rows, x_width), d_b, d_c], axis=1),
            d_step_direct.T,
            d_log_step.T,
            d_queries.transpose(1, 0, 2).reshape(rows, query_width),
            d_keys,
        )
    )
    d_in = jnp.concatenate(
        [
            d_gate_raw,
            d_conv,
            d_query,
            d_key,
            d_value,
            d_step,
            jnp.zeros((rows, 128 - head_share), fl_type),
        ],
        axis=1,
    ).astype(bf_type)
    g_in = jnp.einsum("td,tc->dc", normed, d_in, preferred_element_type=fl_type)
    d_normed_part = jnp.einsum("tc,dc->td", d_in, in_all, preferred_element_type=fl_type)
    first_norm_all = res_all * rms_scale(res_all)
    g_norm_gain = jnp.sum(d_normed_part * first_norm_all, axis=0)
    taps_bias = jnp.concatenate([grad_params[0], grad_params[1][None]], axis=0)
    small_parts = [
        taps_bias.reshape(-1),
        g_gated_gain.reshape(-1),
        g_norm_gain,
        g_ffn_gain.reshape(-1),
        grad_params[2],
        grad_params[3],
        g_skip,
    ]
    small_size = sum(part.shape[0] for part in small_parts)
    small_rows = -(-small_size // 1024) * 8
    small = jnp.concatenate(
        small_parts + [jnp.zeros((small_rows * 128 - small_size,), fl_type)]
    ).reshape(small_rows, 128)
    in_grads, gu_grads, out_grads, small_all, d_normed = reduce_all(
        seq_count,
        fsdp_count,
        (
            g_in.astype(bf_type).reshape(fsdp_count, own_rows, -1),
            g_gate_up.astype(bf_type).reshape(fsdp_count, own_rows, -1),
            g_out,
            small,
            d_normed_part.astype(bf_type).reshape(seq_count, block_rows, model),
        ),
    )
    in_grads = in_grads.astype(fl_type)
    gu_grads = gu_grads.astype(fl_type)
    out_grads = out_grads.astype(fl_type)
    residual = hidden_in[0].astype(fl_type)
    first_scale = rms_scale(residual)
    first_norm = residual * first_scale
    d_first = d_normed * first_gain
    grad_tok = d_mixed + first_scale * (
        d_first - first_norm * jnp.mean(d_first * first_norm, axis=-1, keepdims=True)
    )

    conv_width = x_width + 2 * NST
    small_all = small_all.reshape(seq_count, -1)
    at = (KC + 1) * conv_width
    taps_all = small_all[:, :at].reshape(seq_count, KC + 1, conv_width)
    taps_sum = jnp.concatenate(
        [taps_all[group, :, :x_width] for group in range(seq_count)]
        + [jnp.sum(taps_all[:, :, x_width:], axis=0)],
        axis=1,
    )
    fsdp_index = lax.axis_index("fsdp")
    gated_sum = lax.dynamic_slice_in_dim(
        small_all[:, at : at + x_width].reshape(-1), fsdp_index * gain_own, gain_own, 0
    )
    at = at + x_width
    gains_sum = jnp.sum(small_all[:, at : at + 2 * model], axis=0)
    norm_sum = lax.dynamic_slice_in_dim(gains_sum, fsdp_index * own_rows, own_rows, 0)
    ffn_gain_sum = lax.dynamic_slice_in_dim(gains_sum, model + fsdp_index * own_rows, own_rows, 0)
    at = at + 2 * model
    heads_sum = (
        small_all[:, at : at + 3 * head_share]
        .reshape(seq_count, 3, head_share)
        .transpose(1, 0, 2)
        .reshape(3, MH)
    )

    def side(array):
        return jnp.concatenate([array[group] for group in range(seq_count)], axis=1)

    def owned(start):
        slots = []
        for kv_head in range(KVH):
            users = [group for group in range(seq_count) if owners[group] == kv_head]
            total = in_grads[users[0]][:, start : start + HD]
            for group in users[1:]:
                total = total + in_grads[group][:, start : start + HD]
            slots.append(total)
        return slots

    q_at = 2 * x_width + 2 * NST
    grad_mamba_in = jnp.concatenate(
        [
            side(in_grads[:, :, :x_width]),
            side(in_grads[:, :, x_width : 2 * x_width]),
            jnp.sum(in_grads[:, :, 2 * x_width : q_at], axis=0),
        ],
        axis=1,
    )
    k_at = q_at + query_width
    grad_attn_in = jnp.concatenate(
        [side(in_grads[:, :, q_at:k_at])] + owned(k_at) + owned(k_at + HD), axis=1
    )
    grad_step_in = side(in_grads[:, :, main_width : main_width + head_share])
    grad_gate_up = jnp.concatenate(
        [side(gu_grads[:, :, :ff_width]), side(gu_grads[:, :, ff_width:])], axis=1
    )
    return (
        layer_out[None],
        grad_tok[None],
        norm_sum,
        grad_mamba_in,
        grad_step_in,
        grad_attn_in,
        taps_sum[:KC],
        taps_sum[KC],
        heads_sum[0],
        heads_sum[1],
        heads_sum[2],
        gated_sum,
        out_grads[:gain_own],
        out_grads[gain_own : gain_own + attn_own],
        ffn_gain_sum,
        grad_gate_up,
        out_grads[gain_own + attn_own :],
    )


def fused_shards(
    hidden_in,
    grad_out,
    segments,
    norm_gain,
    mamba_in,
    step_in,
    attn_in,
    conv_taps,
    conv_bias,
    step_bias,
    log_decay,
    skip_gain,
    gated_gain,
    mamba_out,
    attn_out,
    ffn_gain,
    gate_up,
    down_proj,
):
    bf_type = jnp.bfloat16
    fl_type = jnp.float32
    seq_count = lax.axis_size("seq")
    seq_index = lax.axis_index("seq")
    fsdp_count = lax.axis_size("fsdp")
    block_rows = hidden_in.shape[1]
    model = hidden_in.shape[2]
    rows = block_rows * seq_count
    own_rows = model // fsdp_count
    x_width = DI // seq_count
    head_share = MH // seq_count
    query_width = QH * HD // seq_count
    ff_width = FF // seq_count
    owners = [group * KVH // seq_count for group in range(seq_count)]
    owner = seq_index * KVH // seq_count
    gain_own = DI // fsdp_count
    attn_own = QH * HD // fsdp_count

    def cols(array, start, size):
        return lax.dynamic_slice_in_dim(array, start, size, 1)

    small_pack = jnp.concatenate(
        [
            cols(attn_in, QH * HD + owner * HD, HD),
            cols(attn_in, (QH + KVH) * HD + owner * HD, HD),
            cols(step_in, seq_index * head_share, head_share),
            norm_gain[:, None],
            ffn_gain[:, None],
            jnp.zeros((own_rows, 126 - head_share), bf_type),
        ],
        axis=1,
    )
    gain_in = jnp.pad(gated_gain[:, None], ((0, 0), (0, 127)))
    seg_ids = segments[0]
    seg_col = seg_ids[:, None]
    seg_row = jnp.broadcast_to(seg_ids[None, :], (8, rows))
    positions = jnp.arange(rows, dtype=jnp.int32)
    first_count = jnp.sum((seg_ids == 0).astype(jnp.int32))
    place = (positions - jnp.where(seg_ids == 0, 0, first_count)).astype(fl_type)[:, None]
    half = HD // 2
    lane = jnp.arange(2 * HD, dtype=jnp.int32)
    freqs = jnp.exp(-math.log(ROPE_THETA) * 2.0 * (lane % half).astype(fl_type) / HD)
    angles = place * freqs[None, :]
    cosine = jnp.cos(angles)
    sine = jnp.sin(angles) * jnp.where(lane % HD < half, -1.0, 1.0)[None, :]
    taps = jnp.concatenate(
        [
            jnp.concatenate(
                [cols(conv_taps, seq_index * x_width, x_width), conv_taps[:, DI:]], axis=1
            ),
            jnp.concatenate(
                [
                    lax.dynamic_slice_in_dim(conv_bias, seq_index * x_width, x_width, 0),
                    conv_bias[DI:],
                ]
            )[None],
            jnp.zeros((7 - KC, x_width + 2 * NST), fl_type),
        ],
        axis=0,
    )

    def of_heads(array):
        return lax.dynamic_slice_in_dim(array, seq_index * head_share, head_share, 0)

    def wide(array):
        return jnp.pad(array, (0, x_width - array.shape[0]))[None]

    heads = jnp.concatenate(
        [
            wide(of_heads(step_bias)),
            wide(-jnp.exp(of_heads(log_decay))),
            jnp.repeat(of_heads(skip_gain), HD)[None],
            jnp.zeros((5, x_width), fl_type),
        ],
        axis=0,
    )
    tables = (seg_col, seg_row, place, cosine, sine, taps, heads)
    (
        layer_out,
        d_mixed,
        ffn_in,
        ffn_act,
        d_ffn,
        d_mixed_all,
        gated_b,
        d_gated,
        d_attn,
        g_ffn_gain,
        g_gated_gain,
        cot_all,
        in_all,
        normed,
        gate_raw,
        inputs_b,
        accum,
        scan_bf,
        scan_y,
        steps,
        cum,
        attn_mix,
        gain_rows,
    ) = forward_all(
        seq_count,
        fsdp_count,
        (x_width, query_width, ff_width),
        (
            hidden_in[0],
            grad_out[0],
            mamba_in,
            attn_in,
            small_pack,
            gate_up,
            mamba_out,
            attn_out,
            down_proj,
            gain_in,
        )
        + tables,
    )

    def flat(array):
        return array.reshape(rows, -1)

    in_grads, gu_grads, out_grads, small_all, grad_tok = backward_all(
        seq_count,
        fsdp_count,
        (
            hidden_in[0],
            d_mixed,
            flat(d_mixed_all),
            flat(cot_all),
            flat(ffn_in),
            flat(ffn_act),
            flat(d_ffn),
            flat(gated_b),
            flat(attn_mix),
            flat(d_gated),
            flat(d_attn),
            g_ffn_gain,
            g_gated_gain,
            in_all,
            normed,
            gate_raw,
            inputs_b,
            accum,
            scan_bf,
            scan_y,
            steps,
            cum,
            gain_rows,
        )
        + tables,
    )
    in_grads = in_grads.astype(fl_type)
    gu_grads = gu_grads.astype(fl_type)
    out_grads = out_grads.astype(fl_type)
    conv_width = x_width + 2 * NST
    at = (KC + 1) * conv_width // 128
    taps_all = small_all[:, :at].reshape(seq_count, KC + 1, conv_width)
    taps_sum = jnp.concatenate(
        [taps_all[group, :, :x_width] for group in range(seq_count)]
        + [jnp.sum(taps_all[:, :, x_width:], axis=0)],
        axis=1,
    )
    fsdp_index = lax.axis_index("fsdp")
    gated_sum = lax.dynamic_slice_in_dim(
        small_all[:, at : at + x_width // 128].reshape(-1), fsdp_index * gain_own, gain_own, 0
    )
    at = at + x_width // 128
    gains_sum = jnp.sum(small_all[:, at : at + 2 * model // 128], axis=0).reshape(-1)
    norm_sum = lax.dynamic_slice_in_dim(gains_sum, fsdp_index * own_rows, own_rows, 0)
    at = at + model // 128
    ffn_gain_sum = lax.dynamic_slice_in_dim(
        gains_sum, model + fsdp_index * own_rows, own_rows, 0
    )
    at = at + model // 128
    heads_sum = small_all[:, at : at + 3, :head_share].transpose(1, 0, 2).reshape(3, MH)
    q_at = 2 * x_width + 2 * NST
    k_at = q_at + query_width

    def side(array):
        return jnp.concatenate([array[group] for group in range(seq_count)], axis=1)

    def owned(start):
        slots = []
        for kv_head in range(KVH):
            users = [group for group in range(seq_count) if owners[group] == kv_head]
            total = in_grads[users[0]][:, start : start + HD]
            for group in users[1:]:
                total = total + in_grads[group][:, start : start + HD]
            slots.append(total)
        return slots

    grad_mamba_in = jnp.concatenate(
        [
            side(in_grads[:, :, :x_width]),
            side(in_grads[:, :, x_width : 2 * x_width]),
            jnp.sum(in_grads[:, :, 2 * x_width : q_at], axis=0),
        ],
        axis=1,
    )
    grad_attn_in = jnp.concatenate(
        [side(in_grads[:, :, q_at:k_at])] + owned(k_at) + owned(k_at + HD), axis=1
    )
    grad_step_in = side(in_grads[:, :, k_at + 2 * HD : k_at + 2 * HD + head_share])
    grad_gate_up = jnp.concatenate(
        [side(gu_grads[:, :, :ff_width]), side(gu_grads[:, :, ff_width:])], axis=1
    )
    return (
        layer_out[None],
        grad_tok[None],
        norm_sum,
        grad_mamba_in,
        grad_step_in,
        grad_attn_in,
        taps_sum[:KC],
        taps_sum[KC],
        heads_sum[0],
        heads_sum[1],
        heads_sum[2],
        gated_sum,
        out_grads[:gain_own],
        out_grads[gain_own : gain_own + attn_own],
        ffn_gain_sum,
        grad_gate_up,
        out_grads[gain_own + attn_own :],
    )


def solution(mesh):
    placed = (
        P("fsdp", "seq", None),
        P("fsdp", "seq", None),
        P("fsdp", None),
        P("fsdp"),
        P("fsdp", None),
        P("fsdp", None),
        P("fsdp", None),
        P(),
        P(),
        P(),
        P(),
        P(),
        P("fsdp"),
        P("fsdp", None),
        P("fsdp", None),
        P("fsdp"),
        P("fsdp", None),
        P("fsdp", None),
    )
    fsdp_count = mesh.shape["fsdp"]
    whole_tiles = all(
        width % (16 * fsdp_count) == 0 for width in (DI // 2, QH * HD // 2, FF // 2)
    )
    return jax.shard_map(
        fused_shards if whole_tiles else shards,
        mesh=mesh,
        in_specs=placed,
        out_specs=(
            P("fsdp", "seq", None),
            P("fsdp", "seq", None),
            P("fsdp"),
            P("fsdp", None),
            P("fsdp", None),
            P("fsdp", None),
            P(),
            P(),
            P(),
            P(),
            P(),
            P("fsdp"),
            P("fsdp", None),
            P("fsdp", None),
            P("fsdp"),
            P("fsdp", None),
            P("fsdp", None),
        ),
        check_vma=False,
    )
```

```python
from functools import partial
import math

import jax
import jax.numpy as jnp
from jax import lax
from jax.experimental import pallas as pl
from jax.experimental.pallas import tpu as pltpu
from jax.sharding import PartitionSpec as P

MH = 24
HD = 64
NST = 128
KC = 4
QH = 8
KVH = 2
FF = 2048
DI = 1536


EPS = 1e-05
ROPE_THETA = 10000.0

MESH = pl.DeviceIdType.MESH
VMEM_LIMIT = 62 * 2**20
HIGHEST = lax.Precision.HIGHEST


def rcopy(src, dst, send, recv, device):
    return pltpu.make_async_remote_copy(
        src_ref=src,
        dst_ref=dst,
        send_sem=send,
        recv_sem=recv,
        device_id=device,
        device_id_type=MESH,
    )


class Place:
    def __init__(self, seq_count, fsdp_count):
        self.s = lax.axis_index("seq")
        self.f = lax.axis_index("fsdp")
        self.count = fsdp_count
        self.L = fsdp_count // 2
        self.z = self.f // 2
        self.y = self.f % 2
        self.has_right = self.z < self.L - 1
        self.has_left = self.z > 0
        self.right = (self.s, jnp.minimum(self.f + 2, fsdp_count - 1))
        self.left = (self.s, jnp.maximum(self.f - 2, 0))
        self.pair = (self.s, self.f + 1 - 2 * self.y)
        self.s1 = self.s + 1 - 2 * (self.s % 2)
        self.s2 = (self.s + 2) % 4
        self.s3 = 3 - self.s
        self.sib = (self.s1, self.f)
        self.across = (self.s2, self.f)
        self.diag = (self.s3, self.f)

    def greet(self, line=True, pair=True, diag=False):
        barrier = pltpu.get_barrier_semaphore()

        def hello(device):
            pl.semaphore_signal(barrier, inc=1, device_id=device, device_id_type=MESH)

        amount = 2
        hello(self.sib)
        hello(self.across)
        if diag:
            hello(self.diag)
            amount = amount + 1
        if pair:
            hello(self.pair)
            amount = amount + 1
        if line:

            @pl.when(self.has_right)
            def _():
                hello(self.right)

            @pl.when(self.has_left)
            def _():
                hello(self.left)

            amount = amount + jnp.where(self.has_right, 1, 0) + jnp.where(self.has_left, 1, 0)
        pl.semaphore_wait(barrier, amount)


class SeqGather:
    def __init__(self, place, src, out, send, recv):
        p = place
        self.own_sib = rcopy(src, out.at[p.s], send.at[0], recv.at[0], p.sib)
        self.own_across = rcopy(src, out.at[p.s], send.at[1], recv.at[1], p.across)
        self.forward_copy = rcopy(out.at[p.s2], out.at[p.s2], send.at[2], recv.at[2], p.sib)
        self.got_sib = rcopy(src, out.at[p.s1], send.at[0], recv.at[0], p.sib)
        self.got_across = rcopy(src, out.at[p.s2], send.at[1], recv.at[1], p.across)
        self.got_diag = rcopy(src, out.at[p.s3], send.at[2], recv.at[2], p.sib)

    def start(self):
        self.own_across.start()
        self.own_sib.start()

    def wait_sib(self):
        self.got_sib.wait_recv()

    def forward(self):
        self.got_across.wait_recv()
        self.forward_copy.start()

    def wait_diag(self):
        self.got_diag.wait_recv()

    def wait_sends(self):
        self.own_sib.wait_send()
        self.own_across.wait_send()
        self.forward_copy.wait_send()

    def finish(self):
        self.wait_sib()
        self.wait_diag()
        self.wait_sends()


class SeqReduce:
    def __init__(self, place, stage, got, send, recv):
        p = place
        self.stage, self.got = stage, got
        self.copies = [
            rcopy(stage.at[0], got.at[0], send.at[0], recv.at[0], p.sib),
            rcopy(stage.at[1], got.at[1], send.at[1], recv.at[1], p.sib),
            rcopy(stage.at[2], got.at[2], send.at[2], recv.at[2], p.across),
        ]

    def send_diag(self, value):
        self.stage[0] = value.astype(self.stage.dtype)
        self.copies[0].start()

    def send_sib(self, value):
        self.stage[1] = value.astype(self.stage.dtype)
        self.copies[1].start()

    def send_across(self, value):
        self.copies[0].wait_recv()
        self.stage[2] = (value + self.got[0].astype(jnp.float32)).astype(self.stage.dtype)
        self.copies[2].start()

    def total(self, value):
        self.copies[1].wait_recv()
        self.copies[2].wait_recv()
        return value + self.got[1].astype(jnp.float32) + self.got[2].astype(jnp.float32)

    def wait_sends(self):
        for copy in self.copies:
            copy.wait_send()


class LineGather:
    def __init__(self, place, out, send, recv, pair=True, size=0):
        self.p, self.out, self.send, self.recv, self.pair = place, out, send, recv, pair
        self.size = size

    def block(self, index):
        if self.size:
            return self.out.at[pl.ds(pl.multiple_of(index * self.size, self.size), self.size)]
        return self.out.at[index]

    def at(self, b, other=0):
        p = self.p
        if not self.pair:
            return b
        return 2 * b + (1 - p.y if other else p.y)

    def copy(self, b, way):
        p = self.p
        ref = self.block(self.at(b))
        device = (p.right, p.left, p.pair)[way]
        return rcopy(ref, ref, self.send.at[way, b], self.recv.at[self.at(b)], device)

    def push(self, b, right, left):
        if right:

            @pl.when(self.p.has_right)
            def _():
                self.copy(b, 0).start()

        if left:

            @pl.when(self.p.has_left)
            def _():
                self.copy(b, 1).start()

        if self.pair:
            self.copy(b, 2).start()

    def start(self):
        self.push(self.p.z, True, True)

    def step(self, d):
        p = self.p

        @pl.when(p.z - d >= 0)
        def _():
            self.copy(p.z - d, 0).wait_recv()
            self.push(p.z - d, True, False)

        @pl.when(p.z + d <= p.L - 1)
        def _():
            self.copy(p.z + d, 0).wait_recv()
            self.push(p.z + d, False, True)

    def finish(self):
        p = self.p

        def each(b, carry):
            if self.pair:
                ref = self.block(self.at(b, 1))
                rcopy(ref, ref, self.send.at[2, b], self.recv.at[self.at(b, 1)], p.pair).wait_recv()
                self.copy(b, 2).wait_send()

            @pl.when(p.has_right & (b <= p.z))
            def _():
                self.copy(b, 0).wait_send()

            @pl.when(p.has_left & (b >= p.z))
            def _():
                self.copy(b, 1).wait_send()

            return carry

        lax.fori_loop(0, p.L, each, 0)


def loop(count, body):
    def step(index, carry):
        body(index)
        return carry

    lax.fori_loop(0, count, step, 0)


def add_rows(target, *parts):
    def some(index):
        at = pl.ds(pl.multiple_of(index * 16, 16), 16)
        total = parts[0][at].astype(jnp.float32)
        for part in parts[1:]:
            total = total + part[at].astype(jnp.float32)
        target[at] = total.astype(target.dtype)

    loop(target.shape[0] // 16, some)


CHUNKS = 4


def gather_kernel(
    seq_count,
    fsdp_count,
    x_width,
    query_width,
    ff_width,
    hidden,
    cot,
    mamba_in,
    attn_in,
    small,
    gate_up,
    out_pack,
    w_in,
    w_gu,
    w_out,
    hidden_all,
    cot_all,
    local,
    in_send,
    in_recv,
    gu_send,
    gu_recv,
    out_send,
    out_recv,
    hid_send,
    hid_recv,
    cot_send,
    cot_recv,
):
    p = Place(seq_count, fsdp_count)
    s, f, z, y, L = p.s, p.f, p.z, p.y, p.L
    per = fsdp_count // seq_count
    half = per // 2

    def part(ref, start, size, unit):
        return ref.at[:, pl.ds(pl.multiple_of(start, unit), size)]

    bc = mamba_in.shape[1] - 2 * DI
    copies = []

    def bring(src, dst):
        copy = pltpu.make_async_copy(src, dst, local.at[len(copies)])
        copy.start()
        copies.append(copy)

    own = w_in.at[f]
    c0 = 0
    bring(part(mamba_in, s * x_width, x_width, 128), own.at[:, pl.ds(c0, x_width)])
    c0 += x_width
    bring(part(mamba_in, DI + s * x_width, x_width, 128), own.at[:, pl.ds(c0, x_width)])
    c0 += x_width
    bring(mamba_in.at[:, pl.ds(2 * DI, bc)], own.at[:, pl.ds(c0, bc)])
    c0 += bc
    bring(part(attn_in, s * query_width, query_width, 128), own.at[:, pl.ds(c0, query_width)])
    c0 += query_width
    bring(small, own.at[:, pl.ds(c0, small.shape[1])])
    own = w_gu.at[f]
    bring(part(gate_up, s * ff_width, ff_width, 128), own.at[:, pl.ds(0, ff_width)])
    bring(part(gate_up, FF + s * ff_width, ff_width, 128), own.at[:, pl.ds(ff_width, ff_width)])
    bring(hidden, hidden_all.at[s])
    bring(cot, cot_all.at[s])
    holder = f // per == s
    chunk = w_out.shape[1] // CHUNKS
    out_local = local.at[len(copies)]

    @pl.when(holder)
    def _():
        pltpu.make_async_copy(out_pack, w_out.at[f - s * per], out_local).start()

    p.greet()
    hid = SeqGather(p, hidden, hidden_all, hid_send, hid_recv)
    cots = SeqGather(p, cot, cot_all, cot_send, cot_recv)
    hid.start()
    cots.start()
    for copy in copies:
        copy.wait()

    @pl.when(holder)
    def _():
        pltpu.make_async_copy(out_pack, w_out.at[f - s * per], out_local).wait()

    ins = LineGather(p, w_in, in_send, in_recv)
    gus = LineGather(p, w_gu, gu_send, gu_recv)
    ins.start()
    gus.start()
    hid.forward()
    cots.forward()

    def hop(d):
        ins.step(d + 1)
        gus.step(d + 1)

    loop(L - 1, hop)

    def out_copy(i, c, other, way):
        ref = w_out.at[2 * i + (1 - y if other else y), pl.ds(pl.multiple_of(c * chunk, 16), chunk)]
        device = (p.right, p.left, p.pair)[way]
        return rcopy(ref, ref, out_send.at[way, i, c], out_recv.at[way // 2, i, c], device)

    def spread(index):
        i, c = index // CHUNKS, index % CHUNKS
        zs = s * half + i

        @pl.when(z != zs)
        def _():
            out_copy(i, c, 0, 0).wait_recv()

        @pl.when((z >= zs) & p.has_right)
        def _():
            out_copy(i, c, 0, 0).start()

        @pl.when((z <= zs) & p.has_left)
        def _():
            out_copy(i, c, 0, 1).start()

        out_copy(i, c, 0, 2).start()

    loop(half * CHUNKS, spread)

    def spread_end(index):
        i, c = index // CHUNKS, index % CHUNKS
        zs = s * half + i
        out_copy(i, c, 1, 2).wait_recv()
        out_copy(i, c, 0, 2).wait_send()

        @pl.when((z >= zs) & p.has_right)
        def _():
            out_copy(i, c, 0, 0).wait_send()

        @pl.when((z <= zs) & p.has_left)
        def _():
            out_copy(i, c, 0, 1).wait_send()

    loop(half * CHUNKS, spread_end)
    ins.finish()
    gus.finish()
    hid.finish()
    cots.finish()


def dma(*shape):
    return pltpu.SemaphoreType.DMA(shape)


def gather_all(seq_count, fsdp_count, widths, arrays):
    hidden, cot, mamba_in, attn_in, small, gate_up, out_pack = arrays
    x_width, query_width, ff_width = widths
    own_rows = mamba_in.shape[0]
    per = fsdp_count // seq_count
    bc = mamba_in.shape[1] - 2 * DI
    in_width = 2 * x_width + bc + query_width + small.shape[1]
    bf = jnp.bfloat16
    L = fsdp_count // 2
    return pl.pallas_call(
        partial(gather_kernel, seq_count, fsdp_count, x_width, query_width, ff_width),
        out_shape=[
            jax.ShapeDtypeStruct((fsdp_count, own_rows, in_width), bf),
            jax.ShapeDtypeStruct((fsdp_count, own_rows, 2 * ff_width), bf),
            jax.ShapeDtypeStruct((per,) + out_pack.shape, bf),
            jax.ShapeDtypeStruct((seq_count,) + hidden.shape, bf),
            jax.ShapeDtypeStruct((seq_count,) + cot.shape, bf),
        ],
        in_specs=[pl.BlockSpec(memory_space=pl.ANY)] * 7,
        out_specs=[pl.BlockSpec(memory_space=pl.ANY)] * 5,
        scratch_shapes=[
            dma(10),
            dma(3, L),
            dma(fsdp_count),
            dma(3, L),
            dma(fsdp_count),
            dma(3, per // 2, CHUNKS),
            dma(2, per // 2, CHUNKS),
            dma(3),
            dma(3),
            dma(3),
            dma(3),
        ],
        compiler_params=pltpu.CompilerParams(collective_id=0, has_side_effects=True),
        name="gather_weights",
    )(*arrays)


def mid_kernel(
    seq_count,
    fsdp_count,
    gated,
    attn_mix,
    w_mo,
    w_ao,
    w_dn,
    w_gu,
    hidden,
    cot_own,
    cot_all,
    mixer_gain,
    ffn_gain,
    layer_out,
    d_mixed,
    ffn_in,
    ffn_act,
    d_ffn,
    d_mixed_all,
    gated_b,
    d_gated,
    d_attn,
    g_ffn_gain,
    g_gated_gain,
    part_mix,
    gate_vals,
    d_act,
    d_gn,
    mixed,
    norm2,
    sq_buf,
    mean_buf,
    stage,
    got,
    seq_send,
    seq_recv,
):
    p = Place(seq_count, fsdp_count)
    s = p.s
    fl, bf = jnp.float32, jnp.bfloat16
    rows = cot_own.shape[0]
    model = cot_own.shape[1]
    ff = w_dn.shape[0]
    peers = (p.sib, p.across, p.diag)
    peer_at = (p.s1, p.s2, p.s3)

    def dot(a, b):
        return jnp.dot(a, b, preferred_element_type=fl)

    def dot_t(a, b):
        return lax.dot_general(a, b, (((1,), (1,)), ((), ())), preferred_element_type=fl)

    def row_sums(values):
        ones = jnp.ones((8, values.shape[1]), fl)
        return lax.dot_general(
            ones, values, (((1,), (1,)), ((), ())), preferred_element_type=fl, precision=HIGHEST
        )

    def exchange(buf, at):
        copies = []
        for k in range(3):
            copy = rcopy(buf.at[s], buf.at[s], seq_send.at[at, k], seq_recv.at[at, k], peers[k])
            copy.start()
            got_it = rcopy(
                buf.at[peer_at[k]], buf.at[peer_at[k]], seq_send.at[at, k], seq_recv.at[at, k], peers[k]
            )
            copies.append((copy, got_it))

        def end():
            for copy, got_it in copies:
                got_it.wait_recv()
                copy.wait_send()
            total = buf[0] + buf[1] + buf[2] + buf[3]
            return total

        return end

    for r in range(4):
        values = gated[r]
        sq_buf[s, :, r * rows : (r + 1) * rows] = row_sums(values * values)
    p.greet(line=False, pair=False, diag=True)
    sq_end = exchange(sq_buf, 0)
    gain = mixer_gain[...]
    for r in range(4):
        part_mix[r] = dot((gated[r] * gain).astype(bf), w_mo[...])
    sq_total = sq_end()
    scale_cols = lax.rsqrt(sq_total / DI + EPS).T

    for r in range(4):
        scale = scale_cols[r * rows : (r + 1) * rows, 0:1]
        part_mix[r] = part_mix[r] * scale + dot(attn_mix[r], w_ao[...])
        gated_norm = gated[r] * scale
        gated_b[r] = (gated_norm * gain).astype(bf)

    def reducer(at):
        return SeqReduce(p, stage.at[at], got.at[at], seq_send.at[at + 1], seq_recv.at[at + 1])

    mix = reducer(0)
    mix.send_diag(part_mix[p.s3])
    mix.send_sib(part_mix[p.s1])
    mix.send_across(part_mix[p.s2])
    d_act[0] = dot_t(cot_all[0], w_dn[...])
    d_act[1] = dot_t(cot_all[1], w_dn[...])
    residual = hidden[...].astype(fl)
    mixed[...] = residual + mix.total(part_mix[s])
    scale2 = lax.rsqrt(jnp.mean(mixed[...] * mixed[...], axis=-1, keepdims=True) + EPS)
    norm2[...] = mixed[...] * scale2
    ffn_in[s] = (norm2[...] * ffn_gain[...]).astype(bf)
    ffn_all = SeqGather(p, ffn_in.at[s], ffn_in, seq_send.at[4], seq_recv.at[4])
    ffn_all.start()

    def ffn_block(r):
        gate_vals[r] = dot(ffn_in[r], w_gu[...])

    def act_block(r):
        gate_lin = gate_vals[r, :, :ff]
        up_lin = gate_vals[r, :, ff:]
        sigma = jax.nn.sigmoid(gate_lin)
        act = gate_lin * sigma
        ffn_act[r] = (act * up_lin).astype(bf)
        slope = sigma * (1.0 + gate_lin * (1.0 - sigma))
        da = d_act[r]
        d_ffn[r, :, :ff] = (da * up_lin * slope).astype(bf)
        d_ffn[r, :, ff:] = (da * act).astype(bf)

    d_act[2] = dot_t(cot_all[2], w_dn[...])
    d_act[3] = dot_t(cot_all[3], w_dn[...])
    ffn_block(s)
    act_block(s)
    ffn_all.wait_sib()
    ffn_block(p.s1)
    ffn_all.forward()
    act_block(p.s1)
    ffn_block(p.s2)
    act_block(p.s2)
    ffn_all.wait_diag()
    ffn_block(p.s3)
    act_block(p.s3)
    back = reducer(1)
    back.send_diag(dot_t(d_ffn[p.s3], w_gu[...]))
    back.send_sib(dot_t(d_ffn[p.s1], w_gu[...]))
    back.send_across(dot_t(d_ffn[p.s2], w_gu[...]))
    out = reducer(2)
    d_ffn_own = dot_t(d_ffn[s], w_gu[...])
    d_ffn_in = back.total(d_ffn_own)
    g_ffn_gain[...] = jnp.sum(d_ffn_in * norm2[...], axis=0, keepdims=True)
    d_second = d_ffn_in * ffn_gain[...]
    d_mixed[...] = cot_own[...].astype(fl) + scale2 * (
        d_second - norm2[...] * jnp.mean(d_second * norm2[...], axis=-1, keepdims=True)
    )
    d_mixed_all[s] = d_mixed[...].astype(bf)
    back_all = SeqGather(p, d_mixed_all.at[s], d_mixed_all, seq_send.at[5], seq_recv.at[5])
    back_all.start()
    out.send_diag(dot(ffn_act[p.s3], w_dn[...]))
    out.send_sib(dot(ffn_act[p.s1], w_dn[...]))

    def mixer_block(r):
        block = d_mixed_all[r]
        d_gated_b = dot_t(block, w_mo[...])
        d_gn[r] = d_gated_b
        d_attn[r] = dot_t(block, w_ao[...]).astype(bf)

    mixer_block(s)
    back_all.wait_sib()
    mixer_block(p.s1)
    out.send_across(dot(ffn_act[p.s2], w_dn[...]))
    back_all.forward()
    mixer_block(p.s2)
    back_all.wait_diag()
    mixer_block(p.s3)
    for r in range(4):
        scale = scale_cols[r * rows : (r + 1) * rows, 0:1]
        values = d_gn[r] * gain * (gated[r] * scale)
        mean_buf[s, :, r * rows : (r + 1) * rows] = row_sums(values)
    mean_end = exchange(mean_buf, 6)
    layer_out[...] = (mixed[...] + out.total(dot(ffn_act[s], w_dn[...]))).astype(bf)
    gain_total = jnp.zeros_like(g_gated_gain[...])
    for r in range(4):
        scale = scale_cols[r * rows : (r + 1) * rows, 0:1]
        gain_total = gain_total + jnp.sum(d_gn[r] * (gated[r] * scale), axis=0, keepdims=True)
    g_gated_gain[...] = gain_total
    means = (mean_end() / DI).T
    for r in range(4):
        scale = scale_cols[r * rows : (r + 1) * rows, 0:1]
        mean = means[r * rows : (r + 1) * rows, 0:1]
        d_gated[r] = scale * (d_gn[r] * gain - (gated[r] * scale) * mean)
    mix.wait_sends()
    back.wait_sends()
    out.wait_sends()
    ffn_all.wait_sends()
    back_all.wait_sends()


def middle(seq_count, fsdp_count, arrays):
    gated, attn_mix, w_mo, w_ao, w_dn, w_gu, hidden = arrays[:7]
    fl, bf = jnp.float32, jnp.bfloat16
    rows, model = hidden.shape
    ff = w_dn.shape[0]
    n = seq_count
    total = n * rows

    def sds(*shape, dtype=bf):
        return jax.ShapeDtypeStruct(shape, dtype)

    return pl.pallas_call(
        partial(mid_kernel, seq_count, fsdp_count),
        out_shape=[
            sds(rows, model),
            sds(rows, model, dtype=fl),
            sds(n, rows, model),
            sds(n, rows, ff),
            sds(n, rows, 2 * ff),
            sds(n, rows, model),
            sds(*gated.shape),
            sds(*gated.shape, dtype=fl),
            sds(*attn_mix.shape),
            sds(1, model, dtype=fl),
            sds(1, gated.shape[2], dtype=fl),
        ],
        in_specs=[pl.BlockSpec(memory_space=pltpu.VMEM)] * len(arrays),
        out_specs=[pl.BlockSpec(memory_space=pltpu.VMEM)] * 11,
        scratch_shapes=[
            pltpu.VMEM((n, rows, model), fl),
            pltpu.VMEM((n, rows, 2 * ff), fl),
            pltpu.VMEM((n, rows, ff), fl),
            pltpu.VMEM(gated.shape, fl),
            pltpu.VMEM((rows, model), fl),
            pltpu.VMEM((rows, model), fl),
            pltpu.VMEM((n, 8, total), fl),
            pltpu.VMEM((n, 8, total), fl),
            pltpu.VMEM((3, 3, rows, model), bf),
            pltpu.VMEM((3, 3, rows, model), bf),
            dma(7, 3),
            dma(7, 3),
        ],
        compiler_params=pltpu.CompilerParams(
            collective_id=1, has_side_effects=True, vmem_limit_bytes=VMEM_LIMIT
        ),
        name="ffn_middle",
    )(*arrays)


class LineReduce:
    def __init__(self, place, g, pair_got, side_got, acc, send, recv):
        self.p, self.g, self.pair_got, self.side_got, self.acc = place, g, pair_got, side_got, acc
        self.send, self.recv = send, recv

    def pair_copy(self, b):
        p = self.p
        return rcopy(
            self.g.at[2 * b + 1 - p.y],
            self.pair_got.at[b],
            self.send.at[0, b],
            self.recv.at[0, b],
            p.pair,
        )

    def each_from_far(self, body):
        p = self.p

        def step(k):
            d = p.L - 1 - k

            @pl.when(p.z + d <= p.L - 1)
            def _():
                body(p.z + d)

            @pl.when((d > 0) & (p.z - d >= 0))
            def _():
                body(p.z - d)

        loop(p.L, step)

    def start(self):
        self.each_from_far(lambda b: self.pair_copy(b).start())

    def got_from(self, b, right):
        p = self.p
        slot = b if right else b + p.L
        ref = self.side_got.at[slot]
        rcopy(ref, ref, self.send.at[1, b], self.recv.at[1, slot], p.right).wait_recv()
        return ref

    def pass_on(self, b, right):
        p = self.p
        self.pair_copy(b).wait_recv()
        mine, other = self.g.at[2 * b + p.y], self.pair_got.at[b]
        inner = p.has_left if right else p.has_right

        @pl.when(inner)
        def _():
            add_rows(other, mine, other, self.got_from(b, right))

        @pl.when(jnp.logical_not(inner))
        def _():
            add_rows(other, mine, other)

        slot = b if right else b + p.L
        rcopy(
            other,
            self.side_got.at[slot],
            self.send.at[1, b],
            self.recv.at[1, slot],
            p.right if right else p.left,
        ).start()

    def step(self, k):
        p = self.p
        d = p.L - 1 - k

        @pl.when(p.z + d <= p.L - 1)
        def _():
            self.pass_on(p.z + d, True)

        @pl.when(p.z - d >= 0)
        def _():
            self.pass_on(p.z - d, False)

    def total(self, target):
        p = self.p
        b = p.z
        self.pair_copy(b).wait_recv()
        add_rows(self.acc, self.g.at[2 * b + p.y], self.pair_got.at[b])

        @pl.when(p.has_left)
        def _():
            add_rows(self.acc, self.acc, self.got_from(b, True))

        @pl.when(p.has_right)
        def _():
            add_rows(self.acc, self.acc, self.got_from(b, False))

        add_rows(target, self.acc)

    def wait_sends(self):
        p = self.p

        def each(b):
            self.pair_copy(b).wait_send()

            @pl.when(b != p.z)
            def _():
                ref = self.pair_got.at[b]
                rcopy(ref, ref, self.send.at[1, b], self.recv.at[1, b], p.right).wait_send()

        loop(p.L, each)


def reduce_kernel(
    seq_count,
    fsdp_count,
    g_in,
    g_gu,
    g_out,
    small,
    d_norm,
    in_got,
    gu_got,
    out_got,
    small_got,
    d_norm_sum,
    in_pair,
    in_side,
    in_acc,
    gu_pair,
    gu_side,
    gu_acc,
    out_pair,
    out_side,
    out_acc,
    small_pair,
    small_line,
    stage,
    got,
    in_send,
    in_recv,
    gu_send,
    gu_recv,
    out_send,
    out_recv,
    cast_send,
    cast_recv,
    small_send,
    small_recv,
    sp_send,
    sp_recv,
    seq_send,
    seq_recv,
):
    p = Place(seq_count, fsdp_count)
    s, f, z, y, L = p.s, p.f, p.z, p.y, p.L
    per = fsdp_count // seq_count
    half = per // 2
    fl = jnp.float32
    chunk = g_out.shape[1] // CHUNKS
    p.greet()
    pair_small = rcopy(small, small_pair, sp_send.at[0], sp_recv.at[0], p.pair)
    pair_small.start()

    def rows_of(c):
        return pl.ds(pl.multiple_of(c * chunk, 16), chunk)

    def out_pair_copy(i, c):
        return rcopy(
            g_out.at[2 * i + 1 - y, rows_of(c)],
            out_pair.at[i, rows_of(c)],
            out_send.at[0, i, c],
            out_recv.at[0, i, c],
            p.pair,
        )

    def side_copy(i, c, right):
        at = 0 if right else 1
        return rcopy(
            out_pair.at[i, rows_of(c)],
            out_side.at[at, i, rows_of(c)],
            out_send.at[1, i, c],
            out_recv.at[1 + at, i, c],
            p.right if right else p.left,
        )

    ins = LineReduce(p, g_in, in_pair, in_side, in_acc, in_send, in_recv)
    gus = LineReduce(p, g_gu, gu_pair, gu_side, gu_acc, gu_send, gu_recv)
    d_sum = SeqReduce(p, stage, got, seq_send.at[0], seq_recv.at[0])
    loop(half * CHUNKS, lambda index: out_pair_copy(index // CHUNKS, index % CHUNKS).start())
    gus.start()
    ins.start()
    d_sum.send_diag(d_norm[p.s3])
    d_sum.send_sib(d_norm[p.s1])
    d_sum.send_across(d_norm[p.s2].astype(fl))
    pair_small.wait_recv()
    small_line[z] = small[...] + small_pair[...]
    smalls = LineGather(p, small_line, small_send, small_recv, pair=False)
    smalls.start()
    loop(L - 1, lambda d: smalls.step(d + 1))
    smalls.finish()
    pair_small.wait_send()
    small_sum = small_line[0]
    for b in range(1, L):
        small_sum = small_sum + small_line[b]
    small_got[s] = small_sum
    small_all = SeqGather(p, small_got.at[s], small_got, seq_send.at[1], seq_recv.at[1])
    small_all.start()
    d_norm_sum[...] = d_sum.total(d_norm[s].astype(fl))

    def cast(c, way):
        ref = out_got.at[rows_of(c)]
        return rcopy(ref, ref, cast_send.at[way, c], cast_recv.at[c], p.across if way else p.sib)

    def out_step(index):
        i, c = index // CHUNKS, index % CHUNKS
        zs = s * half + i
        out_pair_copy(i, c).wait_recv()
        mine = g_out.at[2 * i + y, rows_of(c)]
        other = out_pair.at[i, rows_of(c)]
        add_rows(out_acc, mine, other)

        @pl.when(p.has_left & (z <= zs))
        def _():
            side_copy(i, c, True).wait_recv()
            add_rows(out_acc, out_acc, out_side.at[0, i, rows_of(c)])

        @pl.when(p.has_right & (z >= zs))
        def _():
            side_copy(i, c, False).wait_recv()
            add_rows(out_acc, out_acc, out_side.at[1, i, rows_of(c)])

        @pl.when(z == zs)
        def _():
            add_rows(out_got.at[rows_of(c)], out_acc)
            cast(c, 1).start()
            cast(c, 0).start()

        @pl.when(z < zs)
        def _():
            add_rows(other, out_acc)
            side_copy(i, c, True).start()

        @pl.when(z > zs)
        def _():
            add_rows(other, out_acc)
            side_copy(i, c, False).start()

    loop(half * CHUNKS, out_step)
    small_all.forward()
    loop(L - 1, gus.step)
    gus.total(gu_got.at[s])
    gu_all = SeqGather(p, gu_got.at[s], gu_got, seq_send.at[2], seq_recv.at[2])
    gu_all.start()
    holder = f // per
    moved = (s + 4 - holder) % 4
    is_across = moved == 2

    @pl.when(is_across)
    def _():
        def pass_cast(c):
            cast(c, 0).wait_recv()
            cast(c, 0).start()

        loop(CHUNKS, pass_cast)

    loop(L - 1, ins.step)
    gu_all.forward()
    ins.total(in_got.at[s])
    in_all = SeqGather(p, in_got.at[s], in_got, seq_send.at[3], seq_recv.at[3])
    in_all.start()

    @pl.when((s != holder) & jnp.logical_not(is_across))
    def _():
        loop(CHUNKS, lambda c: cast(c, 0).wait_recv())

    @pl.when(s == holder)
    def _():
        def sent(c):
            cast(c, 0).wait_send()
            cast(c, 1).wait_send()

        loop(CHUNKS, sent)

    @pl.when(is_across)
    def _():
        loop(CHUNKS, lambda c: cast(c, 0).wait_send())

    def out_sent(index):
        i, c = index // CHUNKS, index % CHUNKS
        out_pair_copy(i, c).wait_send()

        @pl.when(z != s * half + i)
        def _():
            side_copy(i, c, True).wait_send()

    loop(half * CHUNKS, out_sent)
    gus.wait_sends()
    ins.wait_sends()
    d_sum.wait_sends()
    small_all.finish()
    gu_all.finish()
    in_all.forward()
    in_all.finish()


def reduce_all(seq_count, fsdp_count, arrays):
    g_in, g_gu, g_out, small, d_norm = arrays
    fl, bf = jnp.float32, jnp.bfloat16
    L = fsdp_count // 2
    per = fsdp_count // seq_count
    n = seq_count
    own, in_w = g_in.shape[1:]
    gu_w = g_gu.shape[2]
    out_rows, model = g_out.shape[1:]
    rows = d_norm.shape[1]
    v = pltpu.VMEM
    return pl.pallas_call(
        partial(reduce_kernel, seq_count, fsdp_count),
        out_shape=[
            jax.ShapeDtypeStruct((n, own, in_w), bf),
            jax.ShapeDtypeStruct((n, own, gu_w), bf),
            jax.ShapeDtypeStruct((out_rows, model), bf),
            jax.ShapeDtypeStruct((n,) + small.shape, fl),
            jax.ShapeDtypeStruct((rows, model), fl),
        ],
        in_specs=[pl.BlockSpec(memory_space=v)] * 5,
        out_specs=[pl.BlockSpec(memory_space=v)] * 5,
        scratch_shapes=[
            v((L, own, in_w), bf),
            v((2 * L, own, in_w), bf),
            v((own, in_w), fl),
            v((L, own, gu_w), bf),
            v((2 * L, own, gu_w), bf),
            v((own, gu_w), fl),
            v((per // 2, out_rows, model), bf),
            v((2, per // 2, out_rows, model), bf),
            v((out_rows // CHUNKS, model), fl),
            v(small.shape, fl),
            v((L,) + small.shape, fl),
            v((3, rows, model), bf),
            v((3, rows, model), bf),
            dma(2, L),
            dma(2, 2 * L),
            dma(2, L),
            dma(2, 2 * L),
            dma(2, per // 2, CHUNKS),
            dma(3, per // 2, CHUNKS),
            dma(2, CHUNKS),
            dma(CHUNKS),
            dma(3, L),
            dma(L),
            dma(1),
            dma(1),
            dma(4, 3),
            dma(4, 3),
        ],
        compiler_params=pltpu.CompilerParams(
            collective_id=2, has_side_effects=True, vmem_limit_bytes=VMEM_LIMIT
        ),
        name="reduce_grads",
    )(*arrays)


def rms_scale(values):
    return lax.rsqrt(jnp.mean(values * values, axis=-1, keepdims=True) + EPS)


def swish_slope(values):
    sigma = jax.nn.sigmoid(values)
    return sigma * (1.0 + values * (1.0 - sigma))


def silu_slope(values):
    sigma = jax.nn.sigmoid(values)
    return values * sigma, sigma * (1.0 + values * (1.0 - sigma))


def rows_at(r, size=128):
    return pl.ds(pl.multiple_of(r * size, size), size)


def dot(a, b, **kw):
    return jnp.dot(a, b, preferred_element_type=jnp.float32, **kw)


def dot_t(a, b, **kw):
    return lax.dot_general(a, b, (((1,), (1,)), ((), ())), preferred_element_type=jnp.float32, **kw)


def t_dot(a, b, **kw):
    return lax.dot_general(a, b, (((0,), (0,)), ((), ())), preferred_element_type=jnp.float32, **kw)


def row_sums(values):
    ones = jnp.ones((8, values.shape[1]), jnp.float32)
    return dot_t(ones, values, precision=HIGHEST)


def iota2(shape, axis):
    return lax.broadcasted_iota(jnp.int32, shape, axis)


def head_matrix(width):
    return (iota2((width, 128), 0) // HD == iota2((width, 128), 1)).astype(jnp.float32)


def partner(values):
    lane = iota2(values.shape, 1)
    return jnp.where(lane % HD < HD // 2, pltpu.roll(values, 96, 1), pltpu.roll(values, 32, 1))


def fill_mask(bias, seg_col, seg_row, transposed):
    total = bias.shape[0]

    def some(r):
        t = iota2((128, total), 0) + r * 128
        other = iota2((128, total), 1)
        order = t <= other if transposed else t >= other
        same = seg_col[rows_at(r)] == seg_row[0:1, :]
        bias[rows_at(r)] = jnp.where(order & same, 0.0, -1e30)

    loop(total // 128, some)


def forward_kernel(
    seq_count,
    fsdp_count,
    hidden,
    cot,
    mamba_in,
    attn_in,
    small,
    gate_up,
    mamba_out,
    attn_out,
    down_proj,
    gain_in,
    seg_col,
    seg_row,
    place,
    cosine,
    sine,
    taps,
    heads,
    layer_out,
    d_mixed,
    ffn_in,
    ffn_act,
    d_ffn,
    d_mixed_all,
    gated_b,
    d_gated,
    d_attn,
    g_ffn_gain,
    g_gated_gain,
    cot_all,
    in_all,
    normed,
    gate_raw,
    inputs_b,
    accum_out,
    scan_bf,
    scan_y,
    steps,
    cum,
    attn_mix,
    gain_rows,
    hid_all,
    w_gu,
    w_mo,
    w_ao,
    w_dn,
    w_gg,
    pre_pad,
    x_act,
    b_mat,
    c_mat,
    x_step,
    inner,
    bias,
    gated,
    part_mix,
    gate_vals,
    d_act,
    d_gn,
    mixed,
    norm2,
    sq_buf,
    mean_buf,
    stage,
    got,
    local,
    in_send,
    in_recv,
    gu_send,
    gu_recv,
    out_send,
    out_recv,
    seq_send,
    seq_recv,
):
    p = Place(seq_count, fsdp_count)
    s, f, z, y, L = p.s, p.f, p.z, p.y, p.L
    fl, bf = jnp.float32, jnp.bfloat16
    per = fsdp_count // seq_count
    half = per // 2
    own_rows = mamba_in.shape[0]
    x_width = gate_raw.shape[1]
    query_width = attn_mix.shape[2]
    ff = w_dn.shape[0]
    rows = hidden.shape[0]
    total = seq_count * rows
    head_share = x_width // HD
    bc = mamba_in.shape[1] - 2 * DI
    conv_width = x_width + bc

    copies = []

    def bring(src, dst):
        copy = pltpu.make_async_copy(src, dst, local.at[len(copies)])
        copy.start()
        copies.append(copy)

    def part(ref, start, size):
        return ref.at[:, pl.ds(pl.multiple_of(start, 128), size)]

    def own_cols(ref, start, size):
        return ref.at[rows_at(f, own_rows), pl.ds(start, size)]

    c0 = 0
    for src, start, size in (
        (mamba_in, s * x_width, x_width),
        (mamba_in, DI + s * x_width, x_width),
        (mamba_in, 2 * DI, bc),
        (attn_in, s * query_width, query_width),
        (small, 0, small.shape[1]),
    ):
        bring(part(src, start, size), own_cols(in_all, c0, size))
        c0 += size
    in_copies = len(copies)
    bring(hidden, hid_all.at[s])
    bring(cot, cot_all.at[s])
    bring(part(gate_up, s * ff, ff), own_cols(w_gu, 0, ff))
    bring(part(gate_up, FF + s * ff, ff), own_cols(w_gu, ff, ff))
    holder = f // per == s
    spread_arrays = ((gain_in, w_gg, 1), (mamba_out, w_mo, 2), (attn_out, w_ao, 1), (down_proj, w_dn, 2))

    def own_spread(act):
        @pl.when(holder)
        def _():
            for k, (src, dst, _) in enumerate(spread_arrays):
                size = src.shape[0]
                act(pltpu.make_async_copy(src, dst.at[rows_at(f - s * per, size)], local.at[12 + k]))

    own_spread(lambda copy: copy.start())
    p.greet(diag=True)
    for copy in copies[:in_copies]:
        copy.wait()
    ins = LineGather(p, in_all, in_send, in_recv, size=own_rows)
    gus = LineGather(p, w_gu, gu_send, gu_recv, size=own_rows)
    hid = SeqGather(p, hidden, hid_all, seq_send.at[7], seq_recv.at[7])
    cots = SeqGather(p, cot, cot_all, seq_send.at[8], seq_recv.at[8])
    hid.start()
    ins.start()
    fill_mask(bias, seg_col, seg_row, False)
    hid.forward()
    loop(L - 1, lambda d: ins.step(d + 1))
    cots.start()
    for copy in copies[in_copies:]:
        copy.wait()
    own_spread(lambda copy: copy.wait())

    pieces = []
    for k, (src, dst, count) in enumerate(spread_arrays):
        size = src.shape[0]
        for c in range(count):
            pieces.append((dst, size, c * (size // count), size // count))

    def piece_copy(i, k, way, other=0):
        dst, size, offset, count = pieces[k]
        j = 2 * i + (1 - y if other else y)
        ref = dst.at[pl.ds(pl.multiple_of(j * size + offset, 16), count)]
        device = (p.right, p.left, p.pair)[way]
        return rcopy(ref, ref, out_send.at[way, i, k], out_recv.at[way // 2, i, k], device)

    def push_piece(i, k):
        zs = s * half + i

        @pl.when((z >= zs) & p.has_right)
        def _():
            piece_copy(i, k, 0).start()

        @pl.when((z <= zs) & p.has_left)
        def _():
            piece_copy(i, k, 1).start()

        piece_copy(i, k, 2).start()

    def hold_piece(k):
        for i in range(half):

            @pl.when(z == s * half + i)
            def _():
                push_piece(i, k)

    def pass_piece(k):
        for i in range(half):

            @pl.when(z != s * half + i)
            def _():
                piece_copy(i, k, 0).wait_recv()
                push_piece(i, k)

    def end_piece(k):
        for i in range(half):
            piece_copy(i, k, 2, 1).wait_recv()

    def sent_piece(k):
        for i in range(half):
            zs = s * half + i
            piece_copy(i, k, 2).wait_send()

            @pl.when((z >= zs) & p.has_right)
            def _():
                piece_copy(i, k, 0).wait_send()

            @pl.when((z <= zs) & p.has_left)
            def _():
                piece_copy(i, k, 1).wait_send()

    early = range(4)
    late = range(4, len(pieces))
    for k in early:
        hold_piece(k)
    gus.start()
    for k in late:
        hold_piece(k)
    ins.finish()
    hid.finish()
    cots.forward()

    gain_t = in_all[:, in_all.shape[1] - 128 :].astype(fl).T
    gain_rows[...] = gain_t[0:16]
    first_gain = gain_rows[head_share : head_share + 1, :]

    def norm_block(r):
        values = hid_all[r].astype(fl)
        scale = lax.rsqrt(jnp.mean(values * values, axis=-1, keepdims=True) + EPS)
        normed[rows_at(r)] = (values * scale * first_gain).astype(bf)

    loop(seq_count, norm_block)
    pass_piece(0)
    gate_raw[...] = dot(normed[...], in_all[:, :x_width])
    inputs_b[:, :conv_width] = dot(normed[...], in_all[:, x_width : x_width + conv_width]).astype(bf)
    inputs_b[:, conv_width:] = dot(normed[...], in_all[:, x_width + conv_width :]).astype(bf)
    pass_piece(1)
    pre_pad[0:8] = jnp.zeros((8, conv_width), fl)
    pre_pad[8 : 8 + total] = inputs_b[:, :conv_width].astype(fl)
    for r in range(seq_count):
        at = slice(r * rows, (r + 1) * rows)
        accum = taps[KC : KC + 1, :] + taps[KC - 1 : KC, :] * pre_pad[8 + r * rows : 8 + (r + 1) * rows]
        for lag in range(1, KC):
            moved = pre_pad[8 + r * rows - lag : 8 + (r + 1) * rows - lag]
            accum = accum + taps[KC - 1 - lag : KC - lag, :] * jnp.where(
                place[at] >= lag, moved, 0.0
            )
        accum_out[at] = accum
        acts = accum * jax.nn.sigmoid(accum)
        x_act[at] = acts[:, :x_width]
        b_mat[at] = acts[:, x_width : x_width + NST].astype(bf)
        c_mat[at] = acts[:, x_width + NST :].astype(bf)
    pass_piece(2)
    raw = inputs_b[:, conv_width + query_width + 2 * HD :].astype(fl) + heads[0:1, :128]
    steps[...] = jnp.maximum(raw, 0.0) + jnp.log1p(jnp.exp(-jnp.abs(raw)))
    causal = (iota2((total, total), 0) >= iota2((total, total), 1)).astype(fl)
    cum[...] = dot(causal, heads[1:2, :128] * steps[...], precision=HIGHEST)
    cum_t = cum[...].T
    spread_heads = head_matrix(x_width)
    x_step[...] = (x_act[...] * dot_t(steps[...], spread_heads, precision=HIGHEST)).astype(bf)
    inner[...] = dot_t(c_mat[...], b_mat[...])
    pass_piece(3)
    pumps = {0: lambda: gus.step(1), 2: lambda: gus.step(2), 4: lambda: gus.step(3)}
    for h in range(head_share):
        hs = slice(h * HD, (h + 1) * HD)
        for r in range(seq_count):
            at = slice(r * rows, (r + 1) * rows)
            K = (r + 1) * rows
            decay = jnp.exp(cum[at, h : h + 1] - cum_t[h : h + 1, :K] + bias[at, :K])
            kernel_b = (inner[at, :K] * decay).astype(bf)
            scan_y[at, hs] = dot(kernel_b, x_step[:K, hs])
        if h in pumps and L == 4:
            pumps[h]()
    for r in range(seq_count):
        at = slice(r * rows, (r + 1) * rows)
        scan = (scan_y[at] + heads[2:3, :x_width] * x_act[at]).astype(bf)
        scan_bf[at] = scan
        gate = gate_raw[at]
        gated[r] = scan.astype(fl) * (gate * jax.nn.sigmoid(gate))
    for r in range(seq_count):
        values = gated[r]
        sq_buf[s, :, r * rows : (r + 1) * rows] = row_sums(values * values)
    peers = (p.sib, p.across, p.diag)
    peer_at = (p.s1, p.s2, p.s3)

    def exchange(buf, at):
        pairs = []
        for k in range(3):
            copy = rcopy(buf.at[s], buf.at[s], seq_send.at[at, k], seq_recv.at[at, k], peers[k])
            copy.start()
            other = buf.at[peer_at[k]]
            pairs.append((copy, rcopy(other, other, seq_send.at[at, k], seq_recv.at[at, k], peers[k])))

        def end():
            for copy, arrived in pairs:
                arrived.wait_recv()
                copy.wait_send()
            return buf[0] + buf[1] + buf[2] + buf[3]

        return end

    sq_end = exchange(sq_buf, 0)
    q_in = inputs_b[:, conv_width : conv_width + query_width].astype(fl)
    kv_in = inputs_b[:, conv_width + query_width : conv_width + query_width + 2 * HD].astype(fl)
    q_rot = q_in * cosine[...] + partner(q_in) * sine[...]
    k_rot = (kv_in * cosine[...] + partner(kv_in) * sine[...])[:, :HD]
    v_b = inputs_b[:, conv_width + query_width + HD : conv_width + query_width + 2 * HD]
    for r in range(seq_count):
        at = slice(r * rows, (r + 1) * rows)
        K = (r + 1) * rows
        for h in range(query_width // HD):
            hs = slice(h * HD, (h + 1) * HD)
            scores = dot_t(q_rot[at, hs], k_rot[:K], precision=HIGHEST) * (1.0 / math.sqrt(HD))
            weights = jnp.exp(scores + bias[at, :K])
            weights = weights / jnp.sum(weights, axis=-1, keepdims=True)
            attn_mix[r, :, hs] = dot(weights.astype(bf), v_b[:K]).astype(bf)
    cots.finish()
    for k in early:
        end_piece(k)
    gain = w_gg[...].astype(fl).T[0:1, :]
    for r in range(seq_count):
        part_mix[r] = dot((gated[r] * gain).astype(bf), w_mo[...])
    scale_cols = lax.rsqrt(sq_end() / DI + EPS).T
    for r in range(seq_count):
        scale = scale_cols[r * rows : (r + 1) * rows, 0:1]
        part_mix[r] = part_mix[r] * scale + dot(attn_mix[r], w_ao[...])
        gated_b[r] = (gated[r] * scale * gain).astype(bf)

    def reducer(at):
        return SeqReduce(p, stage.at[at], got.at[at], seq_send.at[at + 1], seq_recv.at[at + 1])

    mix = reducer(0)
    mix.send_diag(part_mix[p.s3])
    mix.send_sib(part_mix[p.s1])
    mix.send_across(part_mix[p.s2])
    for k in late:
        pass_piece(k)
    second_gain = gain_rows[head_share + 1 : head_share + 2, :]
    residual = hid_all[s].astype(fl)
    mixed[...] = residual + mix.total(part_mix[s])
    scale2 = lax.rsqrt(jnp.mean(mixed[...] * mixed[...], axis=-1, keepdims=True) + EPS)
    norm2[...] = mixed[...] * scale2
    ffn_in[s] = (norm2[...] * second_gain).astype(bf)
    ffn_all = SeqGather(p, ffn_in.at[s], ffn_in, seq_send.at[4], seq_recv.at[4])
    ffn_all.start()
    if L != 4:
        loop(L - 1, lambda d: gus.step(d + 1))
    for k in late:
        end_piece(k)
    gus.finish()

    def ffn_block(r):
        d_act[r] = dot_t(cot_all[r], w_dn[...])
        gate_vals[r] = dot(ffn_in[r], w_gu[...])

    def act_block(r):
        gate_lin = gate_vals[r, :, :ff]
        up_lin = gate_vals[r, :, ff:]
        act, slope = silu_slope(gate_lin)
        ffn_act[r] = (act * up_lin).astype(bf)
        da = d_act[r]
        d_ffn[r, :, :ff] = (da * up_lin * slope).astype(bf)
        d_ffn[r, :, ff:] = (da * act).astype(bf)

    ffn_block(s)
    act_block(s)
    ffn_all.wait_sib()
    ffn_block(p.s1)
    ffn_all.forward()
    act_block(p.s1)
    ffn_block(p.s2)
    act_block(p.s2)
    ffn_all.wait_diag()
    ffn_block(p.s3)
    act_block(p.s3)
    back = reducer(1)
    back.send_diag(dot_t(d_ffn[p.s3], w_gu[...]))
    back.send_sib(dot_t(d_ffn[p.s1], w_gu[...]))
    back.send_across(dot_t(d_ffn[p.s2], w_gu[...]))
    out = reducer(2)
    d_ffn_own = dot_t(d_ffn[s], w_gu[...])
    d_ffn_in = back.total(d_ffn_own)
    g_ffn_gain[...] = jnp.sum(d_ffn_in * norm2[...], axis=0, keepdims=True)
    d_second = d_ffn_in * second_gain
    d_mixed[...] = cot_all[s].astype(fl) + scale2 * (
        d_second - norm2[...] * jnp.mean(d_second * norm2[...], axis=-1, keepdims=True)
    )
    d_mixed_all[s] = d_mixed[...].astype(bf)
    back_all = SeqGather(p, d_mixed_all.at[s], d_mixed_all, seq_send.at[5], seq_recv.at[5])
    back_all.start()
    out.send_diag(dot(ffn_act[p.s3], w_dn[...]))
    out.send_sib(dot(ffn_act[p.s1], w_dn[...]))

    def mixer_block(r):
        block = d_mixed_all[r]
        d_gn[r] = dot_t(block, w_mo[...])
        d_attn[r] = dot_t(block, w_ao[...]).astype(bf)

    mixer_block(s)
    back_all.wait_sib()
    mixer_block(p.s1)
    out.send_across(dot(ffn_act[p.s2], w_dn[...]))
    back_all.forward()
    mixer_block(p.s2)
    back_all.wait_diag()
    mixer_block(p.s3)
    for r in range(seq_count):
        scale = scale_cols[r * rows : (r + 1) * rows, 0:1]
        values = d_gn[r] * gain * (gated[r] * scale)
        mean_buf[s, :, r * rows : (r + 1) * rows] = row_sums(values)
    mean_end = exchange(mean_buf, 6)
    layer_out[...] = (mixed[...] + out.total(dot(ffn_act[s], w_dn[...]))).astype(bf)
    gain_total = jnp.zeros_like(g_gated_gain[...])
    for r in range(seq_count):
        scale = scale_cols[r * rows : (r + 1) * rows, 0:1]
        gain_total = gain_total + jnp.sum(d_gn[r] * (gated[r] * scale), axis=0, keepdims=True)
    g_gated_gain[...] = gain_total
    means = (mean_end() / DI).T
    for r in range(seq_count):
        scale = scale_cols[r * rows : (r + 1) * rows, 0:1]
        mean = means[r * rows : (r + 1) * rows, 0:1]
        d_gated[r] = scale * (d_gn[r] * gain - (gated[r] * scale) * mean)
    for k in range(len(pieces)):
        sent_piece(k)
    mix.wait_sends()
    back.wait_sends()
    out.wait_sends()
    ffn_all.wait_sends()
    back_all.wait_sends()


def forward_all(seq_count, fsdp_count, widths, arrays):
    x_width, query_width, ff = widths
    hidden, cot, mamba_in, attn_in, small = arrays[:5]
    mamba_out, attn_out, down_proj, gain_in = arrays[6:10]
    fl, bf = jnp.float32, jnp.bfloat16
    rows, model = hidden.shape
    n = seq_count
    total = n * rows
    per = fsdp_count // seq_count
    L = fsdp_count // 2
    conv_width = x_width + 2 * NST
    in_width = x_width + conv_width + query_width + small.shape[1]
    v = pltpu.VMEM

    def sds(*shape, dtype=bf):
        return jax.ShapeDtypeStruct(shape, dtype)

    outs = [
        sds(rows, model),
        sds(rows, model, dtype=fl),
        sds(n, rows, model),
        sds(n, rows, ff),
        sds(n, rows, 2 * ff),
        sds(n, rows, model),
        sds(n, rows, x_width),
        sds(n, rows, x_width, dtype=fl),
        sds(n, rows, query_width),
        sds(1, model, dtype=fl),
        sds(1, x_width, dtype=fl),
        sds(n, rows, model),
        sds(model, in_width),
        sds(total, model),
        sds(total, x_width, dtype=fl),
        sds(total, in_width - x_width),
        sds(total, conv_width, dtype=fl),
        sds(total, x_width),
        sds(total, x_width, dtype=fl),
        sds(total, 128, dtype=fl),
        sds(total, 128, dtype=fl),
        sds(n, rows, query_width),
        sds(16, model, dtype=fl),
    ]
    vm = pl.BlockSpec(memory_space=v)
    hbm = pl.BlockSpec(memory_space=pl.ANY)
    return pl.pallas_call(
        partial(forward_kernel, seq_count, fsdp_count),
        out_shape=outs,
        in_specs=[hbm] * 10 + [vm] * (len(arrays) - 10),
        out_specs=[vm] * len(outs),
        scratch_shapes=[
            v((n, rows, model), bf),
            v((model, 2 * ff), bf),
            v((x_width, model), bf),
            v((query_width, model), bf),
            v((ff, model), bf),
            v((x_width, 128), bf),
            v((total + 8, conv_width), fl),
            v((total, x_width), fl),
            v((total, NST), bf),
            v((total, NST), bf),
            v((total, x_width), bf),
            v((total, total), fl),
            v((total, total), fl),
            v((n, rows, x_width), fl),
            v((n, rows, model), fl),
            v((n, rows, 2 * ff), fl),
            v((n, rows, ff), fl),
            v((n, rows, x_width), fl),
            v((rows, model), fl),
            v((rows, model), fl),
            v((n, 8, total), fl),
            v((n, 8, total), fl),
            v((3, 3, rows, model), bf),
            v((3, 3, rows, model), bf),
            dma(16),
            dma(3, L),
            dma(fsdp_count),
            dma(3, L),
            dma(fsdp_count),
            dma(3, per // 2, 6),
            dma(2, per // 2, 6),
            dma(9, 3),
            dma(9, 3),
        ],
        compiler_params=pltpu.CompilerParams(
            collective_id=3, has_side_effects=True, vmem_limit_bytes=VMEM_LIMIT
        ),
        name="forward_fused",
    )(*arrays)


SMALL_ROWS = 48


def backward_kernel(
    seq_count,
    fsdp_count,
    hidden,
    d_mixed,
    d_mixed_all,
    cot_all,
    ffn_in,
    ffn_act,
    d_ffn,
    gated_b,
    attn_mix,
    d_gated,
    d_attn,
    g_ffn_gain,
    g_gated_gain,
    in_all,
    normed,
    gate_raw,
    inputs_b,
    accum_in,
    scan_bf,
    scan_y,
    steps,
    cum,
    gain_rows,
    seg_col,
    seg_row,
    place,
    cosine,
    sine,
    taps,
    heads,
    in_got,
    gu_got,
    out_got,
    small_got,
    grad_tok,
    g_in,
    g_gu,
    g_out,
    small,
    d_norm,
    d_in,
    dy,
    x_act,
    b_mat,
    c_mat,
    x_step,
    inner,
    inner_t,
    bias,
    bias_t,
    d_inner,
    d_x_step,
    d_acc,
    shifted,
    d_kv,
    d_x_conv,
    in_pair,
    in_side,
    in_acc,
    gu_pair,
    gu_side,
    gu_acc,
    out_pair,
    out_side,
    out_acc,
    small_pair,
    small_line,
    stage,
    got,
    in_send,
    in_recv,
    gu_send,
    gu_recv,
    out_send,
    out_recv,
    cast_send,
    cast_recv,
    small_send,
    small_recv,
    sp_send,
    sp_recv,
    seq_send,
    seq_recv,
):
    p = Place(seq_count, fsdp_count)
    s, f, z, y, L = p.s, p.f, p.z, p.y, p.L
    fl, bf = jnp.float32, jnp.bfloat16
    per = fsdp_count // seq_count
    half = per // 2
    chunk = g_out.shape[1] // CHUNKS
    total = normed.shape[0]
    rows = total // seq_count
    model = normed.shape[1]
    own_rows = model // fsdp_count
    x_width = gate_raw.shape[1]
    query_width = attn_mix.shape[1]
    conv_width = accum_in.shape[1]
    head_share = x_width // HD
    ff = ffn_act.shape[1]
    gain_own, attn_own, ff_own = DI // fsdp_count, QH * HD // fsdp_count, FF // fsdp_count
    p.greet()

    def rows_of(c):
        return pl.ds(pl.multiple_of(c * chunk, 16), chunk)

    def out_pair_copy(i, c):
        return rcopy(
            g_out.at[2 * i + 1 - y, rows_of(c)],
            out_pair.at[i, rows_of(c)],
            out_send.at[0, i, c],
            out_recv.at[0, i, c],
            p.pair,
        )

    def side_copy(i, c, right):
        at = 0 if right else 1
        return rcopy(
            out_pair.at[i, rows_of(c)],
            out_side.at[at, i, rows_of(c)],
            out_send.at[1, i, c],
            out_recv.at[1 + at, i, c],
            p.right if right else p.left,
        )

    def cast(c, way):
        ref = out_got.at[rows_of(c)]
        return rcopy(ref, ref, cast_send.at[way, c], cast_recv.at[c], p.across if way else p.sib)

    def out_step(index):
        i, c = index // CHUNKS, index % CHUNKS
        zs = s * half + i
        out_pair_copy(i, c).wait_recv()
        mine = g_out.at[2 * i + y, rows_of(c)]
        other = out_pair.at[i, rows_of(c)]
        add_rows(out_acc, mine, other)

        @pl.when(p.has_left & (z <= zs))
        def _():
            side_copy(i, c, True).wait_recv()
            add_rows(out_acc, out_acc, out_side.at[0, i, rows_of(c)])

        @pl.when(p.has_right & (z >= zs))
        def _():
            side_copy(i, c, False).wait_recv()
            add_rows(out_acc, out_acc, out_side.at[1, i, rows_of(c)])

        @pl.when(z == zs)
        def _():
            add_rows(out_got.at[rows_of(c)], out_acc)
            cast(c, 1).start()
            cast(c, 0).start()

        @pl.when(z < zs)
        def _():
            add_rows(other, out_acc)
            side_copy(i, c, True).start()

        @pl.when(z > zs)
        def _():
            add_rows(other, out_acc)
            side_copy(i, c, False).start()

    ins = LineReduce(p, g_in, in_pair, in_side, in_acc, in_send, in_recv)
    gus = LineReduce(p, g_gu, gu_pair, gu_side, gu_acc, gu_send, gu_recv)

    for fi in range(fsdp_count):
        at = slice(fi * own_rows, (fi + 1) * own_rows)
        g_gu[fi] = t_dot(ffn_in[:, at], d_ffn[...]).astype(bf)
    gus.start()
    g_mo = t_dot(gated_b[...], d_mixed_all[...]).astype(bf)
    g_ao = t_dot(attn_mix[...], d_mixed_all[...]).astype(bf)
    for j in range(per):
        g_out[j, :gain_own] = g_mo[j * gain_own : (j + 1) * gain_own]
        g_out[j, gain_own : gain_own + attn_own] = g_ao[j * attn_own : (j + 1) * attn_own]
        act = ffn_act[:, j * ff_own : (j + 1) * ff_own]
        g_out[j, gain_own + attn_own :] = t_dot(act, cot_all[...]).astype(bf)
    loop(half * CHUNKS, lambda index: out_pair_copy(index // CHUNKS, index % CHUNKS).start())

    fill_mask(bias, seg_col, seg_row, False)
    fill_mask(bias_t, seg_col, seg_row, True)
    spread_heads = head_matrix(x_width)
    steps_wide = dot_t(steps[...], spread_heads, precision=HIGHEST)
    skip = heads[2:3, :x_width]
    cum_t = cum[...].T
    for r in range(seq_count):
        at = slice(r * rows, (r + 1) * rows)
        accum = accum_in[at]
        acts = accum * jax.nn.sigmoid(accum)
        x_act[at] = acts[:, :x_width]
        b_mat[at] = acts[:, x_width : x_width + NST].astype(bf)
        c_mat[at] = acts[:, x_width + NST :].astype(bf)
        x_step[at] = (acts[:, :x_width] * steps_wide[at]).astype(bf)
        gate_act, slope = silu_slope(gate_raw[at])
        cots = d_gated[at]
        dy[at] = (cots * gate_act).astype(bf)
        d_in[at, :x_width] = (cots * scan_bf[at].astype(fl) * slope).astype(bf)
    inner[...] = dot_t(c_mat[...], b_mat[...])
    inner_t[...] = dot_t(b_mat[...], c_mat[...])
    d_inner[...] = jnp.zeros_like(d_inner)
    gu_all = SeqGather(p, gu_got.at[s], gu_got, seq_send.at[2], seq_recv.at[2])
    for h in range(head_share):
        hs = slice(h * HD, (h + 1) * HD)
        for r in range(seq_count):
            at = slice(r * rows, (r + 1) * rows)
            K = (r + 1) * rows
            decay = jnp.exp(cum[at, h : h + 1] - cum_t[h : h + 1, :K] + bias[at, :K])
            d_inner[at, :K] += dot_t(dy[at, hs], x_step[:K, hs]) * decay
            decay = jnp.exp(cum_t[h : h + 1, r * rows :] - cum[at, h : h + 1] + bias_t[at, r * rows :])
            kernel_t = (inner_t[at, r * rows :] * decay).astype(bf)
            d_x_step[at, hs] = dot(kernel_t, dy[r * rows :, hs])
    gus.step(0)
    d_inner_b = d_inner[...].astype(bf)
    d_acc[:, x_width : x_width + NST] = t_dot(d_inner_b, c_mat[...])
    d_acc[:, x_width + NST :] = dot(d_inner_b, b_mat[...])
    dy_f = dy[...].astype(fl)
    xs = x_act[...]
    dxs = d_x_step[...]
    d_acc[:, :x_width] = steps_wide * dxs + skip * dy_f
    head_sums = dot(
        jnp.sum((dy_f * xs).reshape(total // 8, 8, x_width), axis=0), spread_heads, precision=HIGHEST
    )
    g_skip = jnp.sum(head_sums, axis=0, keepdims=True)
    step_direct = dot(xs * dxs, spread_heads, precision=HIGHEST)
    d_cum = dot(
        dy_f * scan_y[...] - x_step[...].astype(fl) * dxs, spread_heads, precision=HIGHEST
    )
    after = (iota2((total, total), 0) <= iota2((total, total), 1)).astype(fl)
    d_log = dot(after, d_cum, precision=HIGHEST)
    decay_row = heads[1:2, :128]
    g_decay = jnp.sum(d_log * (decay_row * steps[...]), axis=0, keepdims=True)
    raw = inputs_b[:, conv_width + query_width + 2 * HD :].astype(fl) + heads[0:1, :128]
    d_raw = (step_direct + d_log * decay_row) * jax.nn.sigmoid(raw)
    d_raw = jnp.where(iota2(d_raw.shape, 1) < head_share, d_raw, 0.0)
    g_step_bias = jnp.sum(d_raw, axis=0, keepdims=True)
    step_at = x_width + conv_width + query_width + 2 * HD
    d_in[:, step_at:] = d_raw.astype(bf)

    q_at = conv_width
    kv_at = conv_width + query_width
    q_in = inputs_b[:, q_at:kv_at].astype(fl)
    kv_in = inputs_b[:, kv_at : kv_at + 2 * HD].astype(fl)
    q_rot = q_in * cosine[...] + partner(q_in) * sine[...]
    k_rot = (kv_in * cosine[...] + partner(kv_in) * sine[...])[:, :HD]
    k_b = k_rot.astype(bf)
    v_b = inputs_b[:, kv_at + HD : kv_at + 2 * HD]
    d_kv[...] = jnp.zeros_like(d_kv)
    scale = 1.0 / math.sqrt(HD)
    for r in range(seq_count):
        at = slice(r * rows, (r + 1) * rows)
        K = (r + 1) * rows
        for h in range(query_width // HD):
            hs = slice(h * HD, (h + 1) * HD)
            scores = dot_t(q_rot[at, hs], k_rot[:K], precision=HIGHEST) * scale
            weights = jnp.exp(scores + bias[at, :K])
            weights = weights / jnp.sum(weights, axis=-1, keepdims=True)
            d_att = d_attn[at, hs]
            d_weights = dot_t(d_att, v_b[:K])
            along = jnp.sum(d_weights * weights, axis=-1, keepdims=True)
            d_scores = (weights * (d_weights - along) * scale).astype(bf)
            shifted[at, hs] = dot(d_scores, k_b[:K])
            d_kv[:K, :HD] += t_dot(d_scores, q_rot[at, hs].astype(bf))
            d_kv[:K, HD : 2 * HD] += t_dot(weights.astype(bf), d_att)
    d_q = shifted[:total, :query_width]
    d_q = d_q * cosine[...] + partner(d_q * sine[...])
    d_kv_all = d_kv[...]
    d_k = d_kv_all * cosine[...] + partner(d_kv_all * sine[...])
    d_kv_all = jnp.where(iota2(d_k.shape, 1) < HD, d_k, d_kv_all)
    d_in[:, x_width + q_at : x_width + kv_at] = d_q.astype(bf)
    d_in[:, x_width + kv_at : x_width + kv_at + 2 * HD] = d_kv_all.astype(bf)

    gus.step(1)

    tap_sums = [jnp.zeros((1, conv_width), fl) for _ in range(KC + 1)]
    shifted[total:] = jnp.zeros((8, conv_width), fl)
    for r in range(seq_count):
        at = slice(r * rows, (r + 1) * rows)
        d_acc[at] = d_acc[at] * silu_slope(accum_in[at])[1]
        tap_sums[KC] = tap_sums[KC] + jnp.sum(d_acc[at], axis=0, keepdims=True)
        pre = inputs_b[at, :conv_width].astype(fl)
        tap_sums[KC - 1] = tap_sums[KC - 1] + jnp.sum(d_acc[at] * pre, axis=0, keepdims=True)
    for lag in range(1, KC):
        k = KC - 1 - lag
        shifted[:total] = jnp.where(place[...] >= lag, d_acc[...], 0.0)
        for r in range(seq_count):
            at = slice(r * rows, (r + 1) * rows)
            moved = shifted[r * rows + lag : (r + 1) * rows + lag]
            pre = inputs_b[at, :conv_width].astype(fl)
            tap_sums[k] = tap_sums[k] + jnp.sum(moved * pre, axis=0, keepdims=True)
            grads = taps[k : k + 1, :] * moved
            if lag == 1:
                grads = grads + taps[KC - 1 : KC, :] * d_acc[at]
                d_x_conv[at] = grads
            else:
                d_x_conv[at] += grads
    d_in[:, x_width : x_width + conv_width] = d_x_conv[...].astype(bf)

    loop(L - 3, lambda k: gus.step(k + 2))

    d_sum = SeqReduce(p, stage, got, seq_send.at[0], seq_recv.at[0])
    norm_gain_sum = jnp.zeros((1, model), fl)
    first_gain = gain_rows[head_share : head_share + 1, :]
    for r in range(seq_count):
        at = slice(r * rows, (r + 1) * rows)
        part = dot_t(d_in[at], in_all[...])
        d_norm[r] = part
        norm_gain_sum = norm_gain_sum + jnp.sum(part * normed[at].astype(fl), axis=0, keepdims=True)
    norm_gain_sum = norm_gain_sum / first_gain
    d_sum.send_diag(d_norm[p.s3])
    d_sum.send_sib(d_norm[p.s1])
    d_sum.send_across(d_norm[p.s2])

    def put(at, row):
        for c in range(row.shape[1] // 128):
            small[at + c : at + c + 1, :] = row[:, c * 128 : (c + 1) * 128]
        return at + row.shape[1] // 128

    at = 0
    for row in tap_sums + [g_gated_gain[...], norm_gain_sum, g_ffn_gain[...], g_step_bias, g_decay, g_skip]:
        at = put(at, row)
    small[at:] = jnp.zeros((SMALL_ROWS - at, 128), fl)
    pair_small = rcopy(small, small_pair, sp_send.at[0], sp_recv.at[0], p.pair)
    pair_small.start()
    for fi in range(fsdp_count):
        at = slice(fi * own_rows, (fi + 1) * own_rows)
        g_in[fi] = t_dot(normed[:, at], d_in[...]).astype(bf)
    ins.start()
    gus.total(gu_got.at[s])
    gu_all.start()
    loop(half * CHUNKS, out_step)
    pair_small.wait_recv()
    small_line[z] = small[...] + small_pair[...]
    smalls = LineGather(p, small_line, small_send, small_recv, pair=False)
    smalls.start()
    gu_all.forward()
    holder = f // per
    is_across = (s + 4 - holder) % 4 == 2

    def hop(k):
        ins.step(k)
        smalls.step(k + 1)

    loop(L - 1, hop)

    @pl.when(is_across)
    def _():
        def pass_cast(c):
            cast(c, 0).wait_recv()
            cast(c, 0).start()

        loop(CHUNKS, pass_cast)

    smalls.finish()
    small_sum = small_line[0]
    for b in range(1, L):
        small_sum = small_sum + small_line[b]
    small_got[s] = small_sum
    small_all = SeqGather(p, small_got.at[s], small_got, seq_send.at[1], seq_recv.at[1])
    small_all.start()
    ins.total(in_got.at[s])
    in_gather = SeqGather(p, in_got.at[s], in_got, seq_send.at[3], seq_recv.at[3])
    in_gather.start()
    small_all.forward()
    d_normed = d_sum.total(d_norm[s])
    residual = hidden[...].astype(fl)
    scale1 = lax.rsqrt(jnp.mean(residual * residual, axis=-1, keepdims=True) + EPS)
    first_norm = residual * scale1
    d_first = d_normed * first_gain
    grad_tok[...] = d_mixed[...] + scale1 * (
        d_first - first_norm * jnp.mean(d_first * first_norm, axis=-1, keepdims=True)
    )

    @pl.when((s != holder) & jnp.logical_not(is_across))
    def _():
        loop(CHUNKS, lambda c: cast(c, 0).wait_recv())

    @pl.when(s == holder)
    def _():
        def sent(c):
            cast(c, 0).wait_send()
            cast(c, 1).wait_send()

        loop(CHUNKS, sent)

    @pl.when(is_across)
    def _():
        loop(CHUNKS, lambda c: cast(c, 0).wait_send())

    def out_sent(index):
        i, c = index // CHUNKS, index % CHUNKS
        out_pair_copy(i, c).wait_send()

        @pl.when(z != s * half + i)
        def _():
            side_copy(i, c, True).wait_send()

    loop(half * CHUNKS, out_sent)
    in_gather.forward()
    pair_small.wait_send()
    gus.wait_sends()
    ins.wait_sends()
    d_sum.wait_sends()
    small_all.finish()
    gu_all.finish()
    in_gather.finish()


def backward_all(seq_count, fsdp_count, arrays):
    hidden = arrays[0]
    fl, bf = jnp.float32, jnp.bfloat16
    L = fsdp_count // 2
    per = fsdp_count // seq_count
    n = seq_count
    rows, model = hidden.shape
    total = n * rows
    ff = FF // n
    x_width = DI // n
    conv_width = x_width + 2 * NST
    in_w = arrays[13].shape[1]
    gu_w = 2 * ff
    own = model // fsdp_count
    out_rows = (DI + QH * HD + FF) // fsdp_count
    v = pltpu.VMEM
    vm = pl.BlockSpec(memory_space=v)
    return pl.pallas_call(
        partial(backward_kernel, seq_count, fsdp_count),
        out_shape=[
            jax.ShapeDtypeStruct((n, own, in_w), bf),
            jax.ShapeDtypeStruct((n, own, gu_w), bf),
            jax.ShapeDtypeStruct((out_rows, model), bf),
            jax.ShapeDtypeStruct((n, SMALL_ROWS, 128), fl),
            jax.ShapeDtypeStruct((rows, model), fl),
        ],
        in_specs=[vm] * len(arrays),
        out_specs=[vm] * 5,
        scratch_shapes=[
            v((fsdp_count, own, in_w), bf),
            v((fsdp_count, own, gu_w), bf),
            v((per, out_rows, model), bf),
            v((SMALL_ROWS, 128), fl),
            v((n, rows, model), fl),
            v((total, in_w), bf),
            v((total, x_width), bf),
            v((total, x_width), fl),
            v((total, NST), bf),
            v((total, NST), bf),
            v((total, x_width), bf),
            v((total, total), fl),
            v((total, total), fl),
            v((total, total), fl),
            v((total, total), fl),
            v((total, total), fl),
            v((total, x_width), fl),
            v((total, conv_width), fl),
            v((total + 8, conv_width), fl),
            v((total, 128), fl),
            v((total, conv_width), fl),
            v((L, own, in_w), bf),
            v((2 * L, own, in_w), bf),
            v((own, in_w), fl),
            v((L, own, gu_w), bf),
            v((2 * L, own, gu_w), bf),
            v((own, gu_w), fl),
            v((per // 2, out_rows, model), bf),
            v((2, per // 2, out_rows, model), bf),
            v((out_rows // CHUNKS, model), fl),
            v((SMALL_ROWS, 128), fl),
            v((L, SMALL_ROWS, 128), fl),
            v((3, rows, model), bf),
            v((3, rows, model), bf),
            dma(2, L),
            dma(2, 2 * L),
            dma(2, L),
            dma(2, 2 * L),
            dma(2, per // 2, CHUNKS),
            dma(3, per // 2, CHUNKS),
            dma(2, CHUNKS),
            dma(CHUNKS),
            dma(3, L),
            dma(L),
            dma(1),
            dma(1),
            dma(4, 3),
            dma(4, 3),
        ],
        compiler_params=pltpu.CompilerParams(
            collective_id=4, has_side_effects=True, vmem_limit_bytes=VMEM_LIMIT
        ),
        name="backward_fused",
    )(*arrays)


def core_inputs(seg_ids, inputs, params):
    pre_conv, step_raw, query_in, key_in = inputs
    taps, tap_bias, step_bias, log_decay = params
    row_count = pre_conv.shape[0]
    tap_count = taps.shape[0]
    accum = tap_bias[None, :] + taps[tap_count - 1][None, :] * pre_conv
    for lag_step in range(1, tap_count):
        moved = jnp.concatenate(
            [
                jnp.zeros((lag_step, pre_conv.shape[1]), pre_conv.dtype),
                pre_conv[: row_count - lag_step],
            ],
            axis=0,
        )
        prior = jnp.concatenate(
            [jnp.full((lag_step,), -1, jnp.int32), seg_ids[: row_count - lag_step]]
        )
        same_seq = (prior == seg_ids)[:, None]
        accum = accum + taps[tap_count - 1 - lag_step][None, :] * jnp.where(same_seq, moved, 0.0)
    activated = jax.nn.silu(accum)
    step = jax.nn.softplus(step_raw + step_bias[None, :])
    log_step = -jnp.exp(log_decay)[None, :] * step
    positions = jnp.arange(row_count, dtype=jnp.int32)
    first_count = jnp.sum((seg_ids == 0).astype(jnp.int32))
    place = (positions - jnp.where(seg_ids == 0, 0, first_count)).astype(jnp.float32)
    half = HD // 2
    freqs = jnp.exp(-math.log(ROPE_THETA) * 2.0 * jnp.arange(half, dtype=jnp.float32) / HD)
    angles = place[:, None] * freqs[None, :]
    cosine = jnp.cos(angles)[:, None, :]
    sine = jnp.sin(angles)[:, None, :]

    def rotate(tensor):
        heads = tensor.reshape(row_count, -1, HD)
        first_half = heads[..., :half]
        second_half = heads[..., half:]
        return jnp.concatenate(
            [first_half * cosine - second_half * sine, second_half * cosine + first_half * sine],
            axis=-1,
        ).reshape(tensor.shape)

    return activated, step, log_step, rotate(query_in), rotate(key_in)


def shards(
    hidden_in,
    grad_out,
    segments,
    norm_gain,
    mamba_in,
    step_in,
    attn_in,
    conv_taps,
    conv_bias,
    step_bias,
    log_decay,
    skip_gain,
    gated_gain,
    mamba_out,
    attn_out,
    ffn_gain,
    gate_up,
    down_proj,
):
    bf_type = jnp.bfloat16
    fl_type = jnp.float32
    seq_count = lax.axis_size("seq")
    seq_index = lax.axis_index("seq")
    fsdp_count = lax.axis_size("fsdp")
    block_rows = hidden_in.shape[1]
    model = hidden_in.shape[2]
    rows = block_rows * seq_count
    own_rows = model // fsdp_count
    x_width = DI // seq_count
    head_share = MH // seq_count
    query_width = QH * HD // seq_count
    query_share = QH // seq_count
    ff_width = FF // seq_count
    owners = [group * KVH // seq_count for group in range(seq_count)]
    owner = seq_index * KVH // seq_count
    gain_own = DI // fsdp_count
    gain_cols = -(-gain_own // own_rows)

    def cols(array, start, size):
        return lax.dynamic_slice_in_dim(array, start, size, 1)

    gain_pad = jnp.pad(gated_gain, (0, gain_cols * own_rows - gain_own))
    main_width = 2 * x_width + 2 * NST + query_width + 2 * HD
    pad_width = 128 - head_share - 2 - gain_cols
    small_pack = jnp.concatenate(
        [
            cols(attn_in, QH * HD + owner * HD, HD),
            cols(attn_in, (QH + KVH) * HD + owner * HD, HD),
            cols(step_in, seq_index * head_share, head_share),
            norm_gain[:, None],
            ffn_gain[:, None],
            gain_pad.reshape(gain_cols, own_rows).T,
            jnp.zeros((own_rows, pad_width), bf_type),
        ],
        axis=1,
    )
    out_pack = jnp.concatenate([mamba_out, attn_out, down_proj], axis=0)
    w_in, w_gate_up, w_out, hidden_all, cot_all = gather_all(
        seq_count,
        fsdp_count,
        (x_width, query_width, ff_width),
        (hidden_in[0], grad_out[0], mamba_in, attn_in, small_pack, gate_up, out_pack),
    )
    per = fsdp_count // seq_count
    in_all = w_in.reshape(model, -1)
    w_gate_up = w_gate_up.reshape(model, -1)
    hidden_all = hidden_all.reshape(rows, model)
    attn_own = QH * HD // fsdp_count
    ff_own = FF // fsdp_count
    w_mamba_out = w_out[:, :gain_own].reshape(x_width, model)
    w_attn_out = w_out[:, gain_own : gain_own + attn_own].reshape(query_width, model)
    w_down = w_out[:, gain_own + attn_own :].reshape(ff_width, model)
    gain_at = main_width + head_share
    first_gain = in_all[:, gain_at].astype(fl_type)
    second_gain = in_all[:, gain_at + 1].astype(fl_type)
    gated_gains = (
        in_all[:, gain_at + 2 : gain_at + 2 + gain_cols]
        .reshape(fsdp_count, own_rows, gain_cols)
        .transpose(0, 2, 1)
        .reshape(fsdp_count, gain_cols * own_rows)[:, :gain_own]
        .reshape(DI)
    )
    mixer_gain = lax.dynamic_slice_in_dim(gated_gains, seq_index * x_width, x_width, 0).astype(
        fl_type
    )

    res_all = hidden_all.astype(fl_type)
    normed = (res_all * rms_scale(res_all) * first_gain).astype(bf_type)
    projected = jnp.dot(normed, in_all, preferred_element_type=fl_type)
    gate_raw = projected[:, :x_width]
    inputs_b = projected[:, x_width:].astype(bf_type).astype(fl_type)
    conv_width = x_width + 2 * NST
    conv_in = inputs_b[:, :conv_width]
    query_in = inputs_b[:, conv_width : conv_width + query_width]
    key_in = inputs_b[:, conv_width + query_width : conv_width + query_width + HD]
    value_b = inputs_b[:, conv_width + query_width + HD : conv_width + query_width + 2 * HD].astype(
        bf_type
    )
    step_at = conv_width + query_width + 2 * HD
    step_raw = inputs_b[:, step_at : step_at + head_share]
    seg_ids = segments[0]
    taps = jnp.concatenate(
        [cols(conv_taps, seq_index * x_width, x_width), conv_taps[:, DI:]], axis=1
    )
    tap_bias = jnp.concatenate(
        [lax.dynamic_slice_in_dim(conv_bias, seq_index * x_width, x_width, 0), conv_bias[DI:]]
    )
    params = (
        taps,
        tap_bias,
        lax.dynamic_slice_in_dim(step_bias, seq_index * head_share, head_share, 0),
        lax.dynamic_slice_in_dim(log_decay, seq_index * head_share, head_share, 0),
    )
    skip = lax.dynamic_slice_in_dim(skip_gain, seq_index * head_share, head_share, 0)
    (activated, step, log_step, queries, keys), pull_back = jax.vjp(
        partial(core_inputs, seg_ids), (conv_in, step_raw, query_in, key_in), params
    )
    positions = jnp.arange(rows, dtype=jnp.int32)
    causal = positions[:, None] >= positions[None, :]
    mask = causal & (seg_ids[:, None] == seg_ids[None, :])
    highest = lax.Precision.HIGHEST
    x_all = activated[:, :x_width]
    b_mat = activated[:, x_width : x_width + NST].astype(bf_type)
    c_mat = activated[:, x_width + NST :].astype(bf_type)
    x_heads = x_all.reshape(rows, head_share, HD).transpose(1, 0, 2)
    step_t = step.T
    cum_t = jnp.dot(log_step.T, causal.T.astype(fl_type), precision=highest)
    inner = jnp.einsum("tn,pn->tp", c_mat, b_mat, preferred_element_type=fl_type)
    decay = jnp.exp(jnp.where(mask[None], cum_t[:, :, None] - cum_t[:, None, :], -1e30))
    kernel_b = (inner[None] * decay).astype(bf_type)
    x_step = (x_heads * step_t[:, :, None]).astype(bf_type)
    scan_y = jnp.einsum("htp,hpd->htd", kernel_b, x_step, preferred_element_type=fl_type)
    ssm = scan_y + skip[:, None, None] * x_heads
    scan_float = (
        ssm.astype(bf_type).transpose(1, 0, 2).reshape(rows, x_width).astype(fl_type)
    )
    key_b = keys.astype(bf_type)
    q_heads = queries.reshape(rows, query_share, HD).transpose(1, 0, 2)
    scores = jnp.einsum("hid,jd->hij", q_heads, keys, precision=highest) * (1.0 / math.sqrt(HD))
    weights = jnp.exp(jnp.where(mask[None], scores, -1e30))
    weights = weights / jnp.sum(weights, axis=-1, keepdims=True)
    weights_b = weights.astype(bf_type)
    attended = jnp.einsum("hij,jd->hid", weights_b, value_b, preferred_element_type=fl_type)
    attn_mix = attended.astype(bf_type).transpose(1, 0, 2).reshape(rows, query_width)

    gate_act = jax.nn.silu(gate_raw)
    gated = scan_float * gate_act
    (
        layer_out,
        d_mixed,
        ffn_in,
        ffn_act,
        d_ffn,
        d_mixed_b,
        gated_b,
        d_gated,
        d_attn,
        g_ffn_gain,
        g_gated_gain,
    ) = middle(
        seq_count,
        fsdp_count,
        (
            gated.reshape(seq_count, block_rows, x_width),
            attn_mix.reshape(seq_count, block_rows, query_width),
            w_mamba_out,
            w_attn_out,
            w_down,
            w_gate_up,
            hidden_in[0],
            grad_out[0],
            cot_all,
            mixer_gain[None],
            second_gain[None],
        ),
    )
    ffn_in = ffn_in.reshape(rows, model)
    ffn_act = ffn_act.reshape(rows, ff_width)
    d_ffn = d_ffn.reshape(rows, 2 * ff_width)
    d_mixed_b = d_mixed_b.reshape(rows, model)
    gated_b = gated_b.reshape(rows, x_width)
    d_gated = d_gated.reshape(rows, x_width)
    d_attn = d_attn.reshape(rows, query_width)
    cot_rows = cot_all.reshape(rows, model)
    g_down = jnp.einsum("tf,td->fd", ffn_act, cot_rows, preferred_element_type=fl_type)
    g_gate_up = jnp.einsum("td,tf->df", ffn_in, d_ffn, preferred_element_type=fl_type)
    g_attn_out = jnp.einsum("tq,td->qd", attn_mix, d_mixed_b, preferred_element_type=fl_type)
    g_mamba_out = jnp.einsum("ti,td->id", gated_b, d_mixed_b, preferred_element_type=fl_type)
    d_scan = (d_gated * gate_act).astype(bf_type)
    d_gate_raw = d_gated * scan_float * swish_slope(gate_raw)
    g_out = jnp.concatenate(
        [
            g_mamba_out.astype(bf_type).reshape(per, gain_own, model),
            g_attn_out.astype(bf_type).reshape(per, attn_own, model),
            g_down.astype(bf_type).reshape(per, ff_own, model),
        ],
        axis=1,
    )

    d_att = d_attn.astype(bf_type).reshape(rows, query_share, HD).transpose(1, 0, 2)
    d_weights = jnp.einsum("hid,jd->hij", d_att, value_b, preferred_element_type=fl_type)
    inner_sum = jnp.sum(d_att.astype(fl_type) * attended, axis=-1, keepdims=True)
    d_scores = (weights * (d_weights - inner_sum) * (1.0 / math.sqrt(HD))).astype(bf_type)
    d_queries = jnp.einsum("hij,jd->hid", d_scores, key_b, preferred_element_type=fl_type)
    d_keys = jnp.einsum(
        "hij,hid->jd", d_scores, q_heads.astype(bf_type), preferred_element_type=fl_type
    )
    d_value = jnp.einsum("hij,hid->jd", weights_b, d_att, preferred_element_type=fl_type)
    d_y = d_scan.reshape(rows, head_share, HD).transpose(1, 0, 2)
    d_y_float = d_y.astype(fl_type)
    d_kernel = jnp.einsum("htd,hpd->htp", d_y, x_step, preferred_element_type=fl_type)
    d_inner = jnp.sum(d_kernel * decay, axis=0).astype(bf_type)
    d_x_step = jnp.einsum("htp,htd->hpd", kernel_b, d_y, preferred_element_type=fl_type)
    d_c = jnp.dot(d_inner, b_mat, preferred_element_type=fl_type)
    d_b = jnp.einsum("tp,tn->pn", d_inner, c_mat, preferred_element_type=fl_type)
    d_x = step_t[:, :, None] * d_x_step + skip[:, None, None] * d_y_float
    g_skip = jnp.sum(d_y_float * x_heads, axis=(1, 2))
    d_step_direct = jnp.sum(x_heads * d_x_step, axis=-1)
    d_cum = jnp.sum(d_y_float * scan_y, axis=-1) - jnp.sum(
        x_step.astype(fl_type) * d_x_step, axis=-1
    )
    d_log_step = jnp.dot(d_cum, causal.astype(fl_type), precision=highest)
    (d_conv, d_step, d_query, d_key), grad_params = pull_back(
        (
            jnp.concatenate([d_x.transpose(1, 0, 2).reshape(rows, x_width), d_b, d_c], axis=1),
            d_step_direct.T,
            d_log_step.T,
            d_queries.transpose(1, 0, 2).reshape(rows, query_width),
            d_keys,
        )
    )
    d_in = jnp.concatenate(
        [
            d_gate_raw,
            d_conv,
            d_query,
            d_key,
            d_value,
            d_step,
            jnp.zeros((rows, 128 - head_share), fl_type),
        ],
        axis=1,
    ).astype(bf_type)
    g_in = jnp.einsum("td,tc->dc", normed, d_in, preferred_element_type=fl_type)
    d_normed_part = jnp.einsum("tc,dc->td", d_in, in_all, preferred_element_type=fl_type)
    first_norm_all = res_all * rms_scale(res_all)
    g_norm_gain = jnp.sum(d_normed_part * first_norm_all, axis=0)
    taps_bias = jnp.concatenate([grad_params[0], grad_params[1][None]], axis=0)
    small_parts = [
        taps_bias.reshape(-1),
        g_gated_gain.reshape(-1),
        g_norm_gain,
        g_ffn_gain.reshape(-1),
        grad_params[2],
        grad_params[3],
        g_skip,
    ]
    small_size = sum(part.shape[0] for part in small_parts)
    small_rows = -(-small_size // 1024) * 8
    small = jnp.concatenate(
        small_parts + [jnp.zeros((small_rows * 128 - small_size,), fl_type)]
    ).reshape(small_rows, 128)
    in_grads, gu_grads, out_grads, small_all, d_normed = reduce_all(
        seq_count,
        fsdp_count,
        (
            g_in.astype(bf_type).reshape(fsdp_count, own_rows, -1),
            g_gate_up.astype(bf_type).reshape(fsdp_count, own_rows, -1),
            g_out,
            small,
            d_normed_part.astype(bf_type).reshape(seq_count, block_rows, model),
        ),
    )
    in_grads = in_grads.astype(fl_type)
    gu_grads = gu_grads.astype(fl_type)
    out_grads = out_grads.astype(fl_type)
    residual = hidden_in[0].astype(fl_type)
    first_scale = rms_scale(residual)
    first_norm = residual * first_scale
    d_first = d_normed * first_gain
    grad_tok = d_mixed + first_scale * (
        d_first - first_norm * jnp.mean(d_first * first_norm, axis=-1, keepdims=True)
    )

    conv_width = x_width + 2 * NST
    small_all = small_all.reshape(seq_count, -1)
    at = (KC + 1) * conv_width
    taps_all = small_all[:, :at].reshape(seq_count, KC + 1, conv_width)
    taps_sum = jnp.concatenate(
        [taps_all[group, :, :x_width] for group in range(seq_count)]
        + [jnp.sum(taps_all[:, :, x_width:], axis=0)],
        axis=1,
    )
    fsdp_index = lax.axis_index("fsdp")
    gated_sum = lax.dynamic_slice_in_dim(
        small_all[:, at : at + x_width].reshape(-1), fsdp_index * gain_own, gain_own, 0
    )
    at = at + x_width
    gains_sum = jnp.sum(small_all[:, at : at + 2 * model], axis=0)
    norm_sum = lax.dynamic_slice_in_dim(gains_sum, fsdp_index * own_rows, own_rows, 0)
    ffn_gain_sum = lax.dynamic_slice_in_dim(gains_sum, model + fsdp_index * own_rows, own_rows, 0)
    at = at + 2 * model
    heads_sum = (
        small_all[:, at : at + 3 * head_share]
        .reshape(seq_count, 3, head_share)
        .transpose(1, 0, 2)
        .reshape(3, MH)
    )

    def side(array):
        return jnp.concatenate([array[group] for group in range(seq_count)], axis=1)

    def owned(start):
        slots = []
        for kv_head in range(KVH):
            users = [group for group in range(seq_count) if owners[group] == kv_head]
            total = in_grads[users[0]][:, start : start + HD]
            for group in users[1:]:
                total = total + in_grads[group][:, start : start + HD]
            slots.append(total)
        return slots

    q_at = 2 * x_width + 2 * NST
    grad_mamba_in = jnp.concatenate(
        [
            side(in_grads[:, :, :x_width]),
            side(in_grads[:, :, x_width : 2 * x_width]),
            jnp.sum(in_grads[:, :, 2 * x_width : q_at], axis=0),
        ],
        axis=1,
    )
    k_at = q_at + query_width
    grad_attn_in = jnp.concatenate(
        [side(in_grads[:, :, q_at:k_at])] + owned(k_at) + owned(k_at + HD), axis=1
    )
    grad_step_in = side(in_grads[:, :, main_width : main_width + head_share])
    grad_gate_up = jnp.concatenate(
        [side(gu_grads[:, :, :ff_width]), side(gu_grads[:, :, ff_width:])], axis=1
    )
    return (
        layer_out[None],
        grad_tok[None],
        norm_sum,
        grad_mamba_in,
        grad_step_in,
        grad_attn_in,
        taps_sum[:KC],
        taps_sum[KC],
        heads_sum[0],
        heads_sum[1],
        heads_sum[2],
        gated_sum,
        out_grads[:gain_own],
        out_grads[gain_own : gain_own + attn_own],
        ffn_gain_sum,
        grad_gate_up,
        out_grads[gain_own + attn_own :],
    )


def unpack_kernel(
    x_width, query_width, ff, gain_own, attn_own, in_got, gu_got, out_got, g_mi, g_si, g_ai, g_gu, g_mo, g_ao, g_dn
):
    fl = jnp.float32
    bc_at, q_at = 2 * x_width, 2 * x_width + 2 * NST
    kv_at = q_at + query_width
    count = in_got.shape[0]
    users = count // KVH
    head_share = x_width // HD
    for g in range(count):
        g_mi[:, g * x_width : (g + 1) * x_width] = in_got[g, :, :x_width].astype(fl)
        g_mi[:, DI + g * x_width : DI + (g + 1) * x_width] = in_got[g, :, x_width:bc_at].astype(fl)
        g_ai[:, g * query_width : (g + 1) * query_width] = in_got[g, :, q_at:kv_at].astype(fl)
        g_gu[:, g * ff : (g + 1) * ff] = gu_got[g, :, :ff].astype(fl)
        g_gu[:, FF + g * ff : FF + (g + 1) * ff] = gu_got[g, :, ff:].astype(fl)
    g_mi[:, 2 * DI :] = sum(in_got[g, :, bc_at:q_at].astype(fl) for g in range(count))
    pairs = [
        sum(in_got[g, :, kv_at : kv_at + 2 * HD].astype(fl) for g in range(k * users, (k + 1) * users))
        for k in range(KVH)
    ]
    lane = iota2(pairs[0].shape, 1)
    keys = jnp.where(lane < HD, pairs[0], pltpu.roll(pairs[1], HD, 1))
    values = jnp.where(lane < HD, pltpu.roll(pairs[0], HD, 1), pairs[1])
    g_ai[:, QH * HD : (QH + KVH) * HD] = keys
    g_ai[:, (QH + KVH) * HD :] = values
    steps = in_got[0, :, kv_at + 2 * HD :].astype(fl)
    for g in range(1, count):
        moved = pltpu.roll(in_got[g, :, kv_at + 2 * HD :].astype(fl), g * head_share, 1)
        steps = jnp.where(lane >= g * head_share, moved, steps)
    g_si[...] = steps[:, :MH]
    g_mo[...] = out_got[:gain_own].astype(fl)
    g_ao[...] = out_got[gain_own : gain_own + attn_own].astype(fl)
    g_dn[...] = out_got[gain_own + attn_own :].astype(fl)


def unpack(widths, owns, arrays):
    own, model = arrays[0].shape[1], arrays[2].shape[1]
    gain_own, attn_own, ff_own = owns
    vm = pl.BlockSpec(memory_space=pltpu.VMEM)
    shapes = [
        (own, 2 * DI + 2 * NST),
        (own, MH),
        (own, (QH + 2 * KVH) * HD),
        (own, 2 * FF),
        (gain_own, model),
        (attn_own, model),
        (ff_own, model),
    ]
    return pl.pallas_call(
        partial(unpack_kernel, *widths, gain_own, attn_own),
        out_shape=[jax.ShapeDtypeStruct(shape, jnp.float32) for shape in shapes],
        in_specs=[vm] * 3,
        out_specs=[vm] * 7,
        compiler_params=pltpu.CompilerParams(vmem_limit_bytes=VMEM_LIMIT),
        name="unpack_grads",
    )(*arrays)


def fused_shards(
    hidden_in,
    grad_out,
    segments,
    norm_gain,
    mamba_in,
    step_in,
    attn_in,
    conv_taps,
    conv_bias,
    step_bias,
    log_decay,
    skip_gain,
    gated_gain,
    mamba_out,
    attn_out,
    ffn_gain,
    gate_up,
    down_proj,
):
    bf_type = jnp.bfloat16
    fl_type = jnp.float32
    seq_count = lax.axis_size("seq")
    seq_index = lax.axis_index("seq")
    fsdp_count = lax.axis_size("fsdp")
    block_rows = hidden_in.shape[1]
    model = hidden_in.shape[2]
    rows = block_rows * seq_count
    own_rows = model // fsdp_count
    x_width = DI // seq_count
    head_share = MH // seq_count
    query_width = QH * HD // seq_count
    ff_width = FF // seq_count
    owner = seq_index * KVH // seq_count
    gain_own = DI // fsdp_count
    attn_own = QH * HD // fsdp_count

    def cols(array, start, size):
        return lax.dynamic_slice_in_dim(array, start, size, 1)

    small_pack = jnp.concatenate(
        [
            cols(attn_in, QH * HD + owner * HD, HD),
            cols(attn_in, (QH + KVH) * HD + owner * HD, HD),
            cols(step_in, seq_index * head_share, head_share),
            norm_gain[:, None],
            ffn_gain[:, None],
            jnp.zeros((own_rows, 126 - head_share), bf_type),
        ],
        axis=1,
    )
    gain_in = jnp.pad(gated_gain[:, None], ((0, 0), (0, 127)))
    seg_ids = segments[0]
    seg_col = seg_ids[:, None]
    seg_row = jnp.broadcast_to(seg_ids[None, :], (8, rows))
    positions = jnp.arange(rows, dtype=jnp.int32)
    first_count = jnp.sum((seg_ids == 0).astype(jnp.int32))
    place = (positions - jnp.where(seg_ids == 0, 0, first_count)).astype(fl_type)[:, None]
    half = HD // 2
    lane = jnp.arange(2 * HD, dtype=jnp.int32)
    freqs = jnp.exp(-math.log(ROPE_THETA) * 2.0 * (lane % half).astype(fl_type) / HD)
    angles = place * freqs[None, :]
    cosine = jnp.cos(angles)
    sine = jnp.sin(angles) * jnp.where(lane % HD < half, -1.0, 1.0)[None, :]
    taps = jnp.concatenate(
        [
            jnp.concatenate(
                [cols(conv_taps, seq_index * x_width, x_width), conv_taps[:, DI:]], axis=1
            ),
            jnp.concatenate(
                [
                    lax.dynamic_slice_in_dim(conv_bias, seq_index * x_width, x_width, 0),
                    conv_bias[DI:],
                ]
            )[None],
            jnp.zeros((7 - KC, x_width + 2 * NST), fl_type),
        ],
        axis=0,
    )

    def of_heads(array):
        return lax.dynamic_slice_in_dim(array, seq_index * head_share, head_share, 0)

    def wide(array):
        return jnp.pad(array, (0, x_width - array.shape[0]))[None]

    heads = jnp.concatenate(
        [
            wide(of_heads(step_bias)),
            wide(-jnp.exp(of_heads(log_decay))),
            jnp.repeat(of_heads(skip_gain), HD)[None],
            jnp.zeros((5, x_width), fl_type),
        ],
        axis=0,
    )
    tables = (seg_col, seg_row, place, cosine, sine, taps, heads)
    (
        layer_out,
        d_mixed,
        ffn_in,
        ffn_act,
        d_ffn,
        d_mixed_all,
        gated_b,
        d_gated,
        d_attn,
        g_ffn_gain,
        g_gated_gain,
        cot_all,
        in_all,
        normed,
        gate_raw,
        inputs_b,
        accum,
        scan_bf,
        scan_y,
        steps,
        cum,
        attn_mix,
        gain_rows,
    ) = forward_all(
        seq_count,
        fsdp_count,
        (x_width, query_width, ff_width),
        (
            hidden_in[0],
            grad_out[0],
            mamba_in,
            attn_in,
            small_pack,
            gate_up,
            mamba_out,
            attn_out,
            down_proj,
            gain_in,
        )
        + tables,
    )

    def flat(array):
        return array.reshape(rows, -1)

    in_grads, gu_grads, out_grads, small_all, grad_tok = backward_all(
        seq_count,
        fsdp_count,
        (
            hidden_in[0],
            d_mixed,
            flat(d_mixed_all),
            flat(cot_all),
            flat(ffn_in),
            flat(ffn_act),
            flat(d_ffn),
            flat(gated_b),
            flat(attn_mix),
            flat(d_gated),
            flat(d_attn),
            g_ffn_gain,
            g_gated_gain,
            in_all,
            normed,
            gate_raw,
            inputs_b,
            accum,
            scan_bf,
            scan_y,
            steps,
            cum,
            gain_rows,
        )
        + tables,
    )
    grad_mamba_in, grad_step_in, grad_attn_in, grad_gate_up, grad_mo, grad_ao, grad_dn = unpack(
        (x_width, query_width, ff_width),
        (gain_own, attn_own, FF // fsdp_count),
        (in_grads, gu_grads, out_grads),
    )
    conv_width = x_width + 2 * NST
    at = (KC + 1) * conv_width // 128
    taps_all = small_all[:, :at].reshape(seq_count, KC + 1, conv_width)
    taps_sum = jnp.concatenate(
        [taps_all[group, :, :x_width] for group in range(seq_count)]
        + [jnp.sum(taps_all[:, :, x_width:], axis=0)],
        axis=1,
    )
    fsdp_index = lax.axis_index("fsdp")
    gated_sum = lax.dynamic_slice_in_dim(
        small_all[:, at : at + x_width // 128].reshape(-1), fsdp_index * gain_own, gain_own, 0
    )
    at = at + x_width // 128
    gains_sum = jnp.sum(small_all[:, at : at + 2 * model // 128], axis=0).reshape(-1)
    norm_sum = lax.dynamic_slice_in_dim(gains_sum, fsdp_index * own_rows, own_rows, 0)
    at = at + model // 128
    ffn_gain_sum = lax.dynamic_slice_in_dim(
        gains_sum, model + fsdp_index * own_rows, own_rows, 0
    )
    at = at + model // 128
    heads_sum = small_all[:, at : at + 3, :head_share].transpose(1, 0, 2).reshape(3, MH)
    return (
        layer_out[None],
        grad_tok[None],
        norm_sum,
        grad_mamba_in,
        grad_step_in,
        grad_attn_in,
        taps_sum[:KC],
        taps_sum[KC],
        heads_sum[0],
        heads_sum[1],
        heads_sum[2],
        gated_sum,
        grad_mo,
        grad_ao,
        ffn_gain_sum,
        grad_gate_up,
        grad_dn,
    )


def solution(mesh):
    placed = (
        P("fsdp", "seq", None),
        P("fsdp", "seq", None),
        P("fsdp", None),
        P("fsdp"),
        P("fsdp", None),
        P("fsdp", None),
        P("fsdp", None),
        P(),
        P(),
        P(),
        P(),
        P(),
        P("fsdp"),
        P("fsdp", None),
        P("fsdp", None),
        P("fsdp"),
        P("fsdp", None),
        P("fsdp", None),
    )
    fsdp_count = mesh.shape["fsdp"]
    whole_tiles = all(
        width % (16 * fsdp_count) == 0 for width in (DI // 2, QH * HD // 2, FF // 2)
    )
    return jax.shard_map(
        fused_shards if whole_tiles else shards,
        mesh=mesh,
        in_specs=placed,
        out_specs=(
            P("fsdp", "seq", None),
            P("fsdp", "seq", None),
            P("fsdp"),
            P("fsdp", None),
            P("fsdp", None),
            P("fsdp", None),
            P(),
            P(),
            P(),
            P(),
            P(),
            P("fsdp"),
            P("fsdp", None),
            P("fsdp", None),
            P("fsdp"),
            P("fsdp", None),
            P("fsdp", None),
        ),
        check_vma=False,
    )
```

```python
from functools import partial
import math

import jax
import jax.numpy as jnp
from jax import lax
from jax.experimental import pallas as pl
from jax.experimental.pallas import tpu as pltpu
from jax.sharding import PartitionSpec as P

MH = 24
HD = 64
NST = 128
KC = 4
QH = 8
KVH = 2
FF = 2048
DI = 1536


EPS = 1e-05
ROPE_THETA = 10000.0

MESH = pl.DeviceIdType.MESH
VMEM_LIMIT = 62 * 2**20
HIGHEST = lax.Precision.HIGHEST


def rcopy(src, dst, send, recv, device):
    return pltpu.make_async_remote_copy(
        src_ref=src,
        dst_ref=dst,
        send_sem=send,
        recv_sem=recv,
        device_id=device,
        device_id_type=MESH,
    )


class Place:
    def __init__(self, seq_count, fsdp_count):
        self.s = lax.axis_index("seq")
        self.f = lax.axis_index("fsdp")
        self.count = fsdp_count
        self.L = fsdp_count // 2
        self.z = self.f // 2
        self.y = self.f % 2
        self.has_right = self.z < self.L - 1
        self.has_left = self.z > 0
        self.right = (self.s, jnp.minimum(self.f + 2, fsdp_count - 1))
        self.left = (self.s, jnp.maximum(self.f - 2, 0))
        self.pair = (self.s, self.f + 1 - 2 * self.y)
        self.s1 = self.s + 1 - 2 * (self.s % 2)
        self.s2 = (self.s + 2) % 4
        self.s3 = 3 - self.s
        self.sib = (self.s1, self.f)
        self.across = (self.s2, self.f)
        self.diag = (self.s3, self.f)

    def greet(self, line=True, pair=True, diag=False):
        barrier = pltpu.get_barrier_semaphore()

        def hello(device):
            pl.semaphore_signal(barrier, inc=1, device_id=device, device_id_type=MESH)

        amount = 2
        hello(self.sib)
        hello(self.across)
        if diag:
            hello(self.diag)
            amount = amount + 1
        if pair:
            hello(self.pair)
            amount = amount + 1
        if line:

            @pl.when(self.has_right)
            def _():
                hello(self.right)

            @pl.when(self.has_left)
            def _():
                hello(self.left)

            amount = amount + jnp.where(self.has_right, 1, 0) + jnp.where(self.has_left, 1, 0)
        pl.semaphore_wait(barrier, amount)


class SeqGather:
    def __init__(self, place, src, out, send, recv):
        p = place
        self.own_sib = rcopy(src, out.at[p.s], send.at[0], recv.at[0], p.sib)
        self.own_across = rcopy(src, out.at[p.s], send.at[1], recv.at[1], p.across)
        self.forward_copy = rcopy(out.at[p.s2], out.at[p.s2], send.at[2], recv.at[2], p.sib)
        self.got_sib = rcopy(src, out.at[p.s1], send.at[0], recv.at[0], p.sib)
        self.got_across = rcopy(src, out.at[p.s2], send.at[1], recv.at[1], p.across)
        self.got_diag = rcopy(src, out.at[p.s3], send.at[2], recv.at[2], p.sib)

    def start(self):
        self.own_across.start()
        self.own_sib.start()

    def wait_sib(self):
        self.got_sib.wait_recv()

    def forward(self):
        self.got_across.wait_recv()
        self.forward_copy.start()

    def wait_diag(self):
        self.got_diag.wait_recv()

    def wait_sends(self):
        self.own_sib.wait_send()
        self.own_across.wait_send()
        self.forward_copy.wait_send()

    def finish(self):
        self.wait_sib()
        self.wait_diag()
        self.wait_sends()


class SeqReduce:
    def __init__(self, place, stage, got, send, recv):
        p = place
        self.stage, self.got = stage, got
        self.copies = [
            rcopy(stage.at[0], got.at[0], send.at[0], recv.at[0], p.sib),
            rcopy(stage.at[1], got.at[1], send.at[1], recv.at[1], p.sib),
            rcopy(stage.at[2], got.at[2], send.at[2], recv.at[2], p.across),
        ]

    def send_diag(self, value):
        self.stage[0] = value.astype(self.stage.dtype)
        self.copies[0].start()

    def send_sib(self, value):
        self.stage[1] = value.astype(self.stage.dtype)
        self.copies[1].start()

    def send_across(self, value):
        self.copies[0].wait_recv()
        self.stage[2] = (value + self.got[0].astype(jnp.float32)).astype(self.stage.dtype)
        self.copies[2].start()

    def total(self, value):
        self.copies[1].wait_recv()
        self.copies[2].wait_recv()
        return value + self.got[1].astype(jnp.float32) + self.got[2].astype(jnp.float32)

    def wait_sends(self):
        for copy in self.copies:
            copy.wait_send()


class LineGather:
    def __init__(self, place, out, send, recv, pair=True, size=0):
        self.p, self.out, self.send, self.recv, self.pair = place, out, send, recv, pair
        self.size = size

    def block(self, index):
        if self.size:
            return self.out.at[pl.ds(pl.multiple_of(index * self.size, self.size), self.size)]
        return self.out.at[index]

    def at(self, b, other=0):
        p = self.p
        if not self.pair:
            return b
        return 2 * b + (1 - p.y if other else p.y)

    def copy(self, b, way):
        p = self.p
        ref = self.block(self.at(b))
        device = (p.right, p.left, p.pair)[way]
        return rcopy(ref, ref, self.send.at[way, b], self.recv.at[self.at(b)], device)

    def push(self, b, right, left):
        if right:

            @pl.when(self.p.has_right)
            def _():
                self.copy(b, 0).start()

        if left:

            @pl.when(self.p.has_left)
            def _():
                self.copy(b, 1).start()

        if self.pair:
            self.copy(b, 2).start()

    def start(self):
        self.push(self.p.z, True, True)

    def step(self, d):
        p = self.p

        @pl.when(p.z - d >= 0)
        def _():
            self.copy(p.z - d, 0).wait_recv()
            self.push(p.z - d, True, False)

        @pl.when(p.z + d <= p.L - 1)
        def _():
            self.copy(p.z + d, 0).wait_recv()
            self.push(p.z + d, False, True)

    def finish(self):
        p = self.p

        def each(b, carry):
            if self.pair:
                ref = self.block(self.at(b, 1))
                rcopy(ref, ref, self.send.at[2, b], self.recv.at[self.at(b, 1)], p.pair).wait_recv()
                self.copy(b, 2).wait_send()

            @pl.when(p.has_right & (b <= p.z))
            def _():
                self.copy(b, 0).wait_send()

            @pl.when(p.has_left & (b >= p.z))
            def _():
                self.copy(b, 1).wait_send()

            return carry

        lax.fori_loop(0, p.L, each, 0)


def loop(count, body):
    def step(index, carry):
        body(index)
        return carry

    lax.fori_loop(0, count, step, 0)


def add_rows(target, *parts):
    def some(index):
        at = pl.ds(pl.multiple_of(index * 16, 16), 16)
        total = parts[0][at].astype(jnp.float32)
        for part in parts[1:]:
            total = total + part[at].astype(jnp.float32)
        target[at] = total.astype(target.dtype)

    loop(target.shape[0] // 16, some)


CHUNKS = 4


def gather_kernel(
    seq_count,
    fsdp_count,
    x_width,
    query_width,
    ff_width,
    hidden,
    cot,
    mamba_in,
    attn_in,
    small,
    gate_up,
    out_pack,
    w_in,
    w_gu,
    w_out,
    hidden_all,
    cot_all,
    local,
    in_send,
    in_recv,
    gu_send,
    gu_recv,
    out_send,
    out_recv,
    hid_send,
    hid_recv,
    cot_send,
    cot_recv,
):
    p = Place(seq_count, fsdp_count)
    s, f, z, y, L = p.s, p.f, p.z, p.y, p.L
    per = fsdp_count // seq_count
    half = per // 2

    def part(ref, start, size, unit):
        return ref.at[:, pl.ds(pl.multiple_of(start, unit), size)]

    bc = mamba_in.shape[1] - 2 * DI
    copies = []

    def bring(src, dst):
        copy = pltpu.make_async_copy(src, dst, local.at[len(copies)])
        copy.start()
        copies.append(copy)

    own = w_in.at[f]
    c0 = 0
    bring(part(mamba_in, s * x_width, x_width, 128), own.at[:, pl.ds(c0, x_width)])
    c0 += x_width
    bring(part(mamba_in, DI + s * x_width, x_width, 128), own.at[:, pl.ds(c0, x_width)])
    c0 += x_width
    bring(mamba_in.at[:, pl.ds(2 * DI, bc)], own.at[:, pl.ds(c0, bc)])
    c0 += bc
    bring(part(attn_in, s * query_width, query_width, 128), own.at[:, pl.ds(c0, query_width)])
    c0 += query_width
    bring(small, own.at[:, pl.ds(c0, small.shape[1])])
    own = w_gu.at[f]
    bring(part(gate_up, s * ff_width, ff_width, 128), own.at[:, pl.ds(0, ff_width)])
    bring(part(gate_up, FF + s * ff_width, ff_width, 128), own.at[:, pl.ds(ff_width, ff_width)])
    bring(hidden, hidden_all.at[s])
    bring(cot, cot_all.at[s])
    holder = f // per == s
    chunk = w_out.shape[1] // CHUNKS
    out_local = local.at[len(copies)]

    @pl.when(holder)
    def _():
        pltpu.make_async_copy(out_pack, w_out.at[f - s * per], out_local).start()

    p.greet()
    hid = SeqGather(p, hidden, hidden_all, hid_send, hid_recv)
    cots = SeqGather(p, cot, cot_all, cot_send, cot_recv)
    hid.start()
    cots.start()
    for copy in copies:
        copy.wait()

    @pl.when(holder)
    def _():
        pltpu.make_async_copy(out_pack, w_out.at[f - s * per], out_local).wait()

    ins = LineGather(p, w_in, in_send, in_recv)
    gus = LineGather(p, w_gu, gu_send, gu_recv)
    ins.start()
    gus.start()
    hid.forward()
    cots.forward()

    def hop(d):
        ins.step(d + 1)
        gus.step(d + 1)

    loop(L - 1, hop)

    def out_copy(i, c, other, way):
        ref = w_out.at[2 * i + (1 - y if other else y), pl.ds(pl.multiple_of(c * chunk, 16), chunk)]
        device = (p.right, p.left, p.pair)[way]
        return rcopy(ref, ref, out_send.at[way, i, c], out_recv.at[way // 2, i, c], device)

    def spread(index):
        i, c = index // CHUNKS, index % CHUNKS
        zs = s * half + i

        @pl.when(z != zs)
        def _():
            out_copy(i, c, 0, 0).wait_recv()

        @pl.when((z >= zs) & p.has_right)
        def _():
            out_copy(i, c, 0, 0).start()

        @pl.when((z <= zs) & p.has_left)
        def _():
            out_copy(i, c, 0, 1).start()

        out_copy(i, c, 0, 2).start()

    loop(half * CHUNKS, spread)

    def spread_end(index):
        i, c = index // CHUNKS, index % CHUNKS
        zs = s * half + i
        out_copy(i, c, 1, 2).wait_recv()
        out_copy(i, c, 0, 2).wait_send()

        @pl.when((z >= zs) & p.has_right)
        def _():
            out_copy(i, c, 0, 0).wait_send()

        @pl.when((z <= zs) & p.has_left)
        def _():
            out_copy(i, c, 0, 1).wait_send()

    loop(half * CHUNKS, spread_end)
    ins.finish()
    gus.finish()
    hid.finish()
    cots.finish()


def dma(*shape):
    return pltpu.SemaphoreType.DMA(shape)


def gather_all(seq_count, fsdp_count, widths, arrays):
    hidden, cot, mamba_in, attn_in, small, gate_up, out_pack = arrays
    x_width, query_width, ff_width = widths
    own_rows = mamba_in.shape[0]
    per = fsdp_count // seq_count
    bc = mamba_in.shape[1] - 2 * DI
    in_width = 2 * x_width + bc + query_width + small.shape[1]
    bf = jnp.bfloat16
    L = fsdp_count // 2
    return pl.pallas_call(
        partial(gather_kernel, seq_count, fsdp_count, x_width, query_width, ff_width),
        out_shape=[
            jax.ShapeDtypeStruct((fsdp_count, own_rows, in_width), bf),
            jax.ShapeDtypeStruct((fsdp_count, own_rows, 2 * ff_width), bf),
            jax.ShapeDtypeStruct((per,) + out_pack.shape, bf),
            jax.ShapeDtypeStruct((seq_count,) + hidden.shape, bf),
            jax.ShapeDtypeStruct((seq_count,) + cot.shape, bf),
        ],
        in_specs=[pl.BlockSpec(memory_space=pl.ANY)] * 7,
        out_specs=[pl.BlockSpec(memory_space=pl.ANY)] * 5,
        scratch_shapes=[
            dma(10),
            dma(3, L),
            dma(fsdp_count),
            dma(3, L),
            dma(fsdp_count),
            dma(3, per // 2, CHUNKS),
            dma(2, per // 2, CHUNKS),
            dma(3),
            dma(3),
            dma(3),
            dma(3),
        ],
        compiler_params=pltpu.CompilerParams(collective_id=0, has_side_effects=True),
        name="gather_weights",
    )(*arrays)


def mid_kernel(
    seq_count,
    fsdp_count,
    gated,
    attn_mix,
    w_mo,
    w_ao,
    w_dn,
    w_gu,
    hidden,
    cot_own,
    cot_all,
    mixer_gain,
    ffn_gain,
    layer_out,
    d_mixed,
    ffn_in,
    ffn_act,
    d_ffn,
    d_mixed_all,
    gated_b,
    d_gated,
    d_attn,
    g_ffn_gain,
    g_gated_gain,
    part_mix,
    gate_vals,
    d_act,
    d_gn,
    mixed,
    norm2,
    sq_buf,
    mean_buf,
    stage,
    got,
    seq_send,
    seq_recv,
):
    p = Place(seq_count, fsdp_count)
    s = p.s
    fl, bf = jnp.float32, jnp.bfloat16
    rows = cot_own.shape[0]
    model = cot_own.shape[1]
    ff = w_dn.shape[0]
    peers = (p.sib, p.across, p.diag)
    peer_at = (p.s1, p.s2, p.s3)

    def dot(a, b):
        return jnp.dot(a, b, preferred_element_type=fl)

    def dot_t(a, b):
        return lax.dot_general(a, b, (((1,), (1,)), ((), ())), preferred_element_type=fl)

    def row_sums(values):
        ones = jnp.ones((8, values.shape[1]), fl)
        return lax.dot_general(
            ones, values, (((1,), (1,)), ((), ())), preferred_element_type=fl, precision=HIGHEST
        )

    def exchange(buf, at):
        copies = []
        for k in range(3):
            copy = rcopy(buf.at[s], buf.at[s], seq_send.at[at, k], seq_recv.at[at, k], peers[k])
            copy.start()
            got_it = rcopy(
                buf.at[peer_at[k]], buf.at[peer_at[k]], seq_send.at[at, k], seq_recv.at[at, k], peers[k]
            )
            copies.append((copy, got_it))

        def end():
            for copy, got_it in copies:
                got_it.wait_recv()
                copy.wait_send()
            total = buf[0] + buf[1] + buf[2] + buf[3]
            return total

        return end

    for r in range(4):
        values = gated[r]
        sq_buf[s, :, r * rows : (r + 1) * rows] = row_sums(values * values)
    p.greet(line=False, pair=False, diag=True)
    sq_end = exchange(sq_buf, 0)
    gain = mixer_gain[...]
    for r in range(4):
        part_mix[r] = dot((gated[r] * gain).astype(bf), w_mo[...])
    sq_total = sq_end()
    scale_cols = lax.rsqrt(sq_total / DI + EPS).T

    for r in range(4):
        scale = scale_cols[r * rows : (r + 1) * rows, 0:1]
        part_mix[r] = part_mix[r] * scale + dot(attn_mix[r], w_ao[...])
        gated_norm = gated[r] * scale
        gated_b[r] = (gated_norm * gain).astype(bf)

    def reducer(at):
        return SeqReduce(p, stage.at[at], got.at[at], seq_send.at[at + 1], seq_recv.at[at + 1])

    mix = reducer(0)
    mix.send_diag(part_mix[p.s3])
    mix.send_sib(part_mix[p.s1])
    mix.send_across(part_mix[p.s2])
    d_act[0] = dot_t(cot_all[0], w_dn[...])
    d_act[1] = dot_t(cot_all[1], w_dn[...])
    residual = hidden[...].astype(fl)
    mixed[...] = residual + mix.total(part_mix[s])
    scale2 = lax.rsqrt(jnp.mean(mixed[...] * mixed[...], axis=-1, keepdims=True) + EPS)
    norm2[...] = mixed[...] * scale2
    ffn_in[s] = (norm2[...] * ffn_gain[...]).astype(bf)
    ffn_all = SeqGather(p, ffn_in.at[s], ffn_in, seq_send.at[4], seq_recv.at[4])
    ffn_all.start()

    def ffn_block(r):
        gate_vals[r] = dot(ffn_in[r], w_gu[...])

    def act_block(r):
        gate_lin = gate_vals[r, :, :ff]
        up_lin = gate_vals[r, :, ff:]
        sigma = jax.nn.sigmoid(gate_lin)
        act = gate_lin * sigma
        ffn_act[r] = (act * up_lin).astype(bf)
        slope = sigma * (1.0 + gate_lin * (1.0 - sigma))
        da = d_act[r]
        d_ffn[r, :, :ff] = (da * up_lin * slope).astype(bf)
        d_ffn[r, :, ff:] = (da * act).astype(bf)

    d_act[2] = dot_t(cot_all[2], w_dn[...])
    d_act[3] = dot_t(cot_all[3], w_dn[...])
    ffn_block(s)
    act_block(s)
    ffn_all.wait_sib()
    ffn_block(p.s1)
    ffn_all.forward()
    act_block(p.s1)
    ffn_block(p.s2)
    act_block(p.s2)
    ffn_all.wait_diag()
    ffn_block(p.s3)
    act_block(p.s3)
    back = reducer(1)
    back.send_diag(dot_t(d_ffn[p.s3], w_gu[...]))
    back.send_sib(dot_t(d_ffn[p.s1], w_gu[...]))
    back.send_across(dot_t(d_ffn[p.s2], w_gu[...]))
    out = reducer(2)
    d_ffn_own = dot_t(d_ffn[s], w_gu[...])
    d_ffn_in = back.total(d_ffn_own)
    g_ffn_gain[...] = jnp.sum(d_ffn_in * norm2[...], axis=0, keepdims=True)
    d_second = d_ffn_in * ffn_gain[...]
    d_mixed[...] = cot_own[...].astype(fl) + scale2 * (
        d_second - norm2[...] * jnp.mean(d_second * norm2[...], axis=-1, keepdims=True)
    )
    d_mixed_all[s] = d_mixed[...].astype(bf)
    back_all = SeqGather(p, d_mixed_all.at[s], d_mixed_all, seq_send.at[5], seq_recv.at[5])
    back_all.start()
    out.send_diag(dot(ffn_act[p.s3], w_dn[...]))
    out.send_sib(dot(ffn_act[p.s1], w_dn[...]))

    def mixer_block(r):
        block = d_mixed_all[r]
        d_gated_b = dot_t(block, w_mo[...])
        d_gn[r] = d_gated_b
        d_attn[r] = dot_t(block, w_ao[...]).astype(bf)

    mixer_block(s)
    back_all.wait_sib()
    mixer_block(p.s1)
    out.send_across(dot(ffn_act[p.s2], w_dn[...]))
    back_all.forward()
    mixer_block(p.s2)
    back_all.wait_diag()
    mixer_block(p.s3)
    for r in range(4):
        scale = scale_cols[r * rows : (r + 1) * rows, 0:1]
        values = d_gn[r] * gain * (gated[r] * scale)
        mean_buf[s, :, r * rows : (r + 1) * rows] = row_sums(values)
    mean_end = exchange(mean_buf, 6)
    layer_out[...] = (mixed[...] + out.total(dot(ffn_act[s], w_dn[...]))).astype(bf)
    gain_total = jnp.zeros_like(g_gated_gain[...])
    for r in range(4):
        scale = scale_cols[r * rows : (r + 1) * rows, 0:1]
        gain_total = gain_total + jnp.sum(d_gn[r] * (gated[r] * scale), axis=0, keepdims=True)
    g_gated_gain[...] = gain_total
    means = (mean_end() / DI).T
    for r in range(4):
        scale = scale_cols[r * rows : (r + 1) * rows, 0:1]
        mean = means[r * rows : (r + 1) * rows, 0:1]
        d_gated[r] = scale * (d_gn[r] * gain - (gated[r] * scale) * mean)
    mix.wait_sends()
    back.wait_sends()
    out.wait_sends()
    ffn_all.wait_sends()
    back_all.wait_sends()


def middle(seq_count, fsdp_count, arrays):
    gated, attn_mix, w_mo, w_ao, w_dn, w_gu, hidden = arrays[:7]
    fl, bf = jnp.float32, jnp.bfloat16
    rows, model = hidden.shape
    ff = w_dn.shape[0]
    n = seq_count
    total = n * rows

    def sds(*shape, dtype=bf):
        return jax.ShapeDtypeStruct(shape, dtype)

    return pl.pallas_call(
        partial(mid_kernel, seq_count, fsdp_count),
        out_shape=[
            sds(rows, model),
            sds(rows, model, dtype=fl),
            sds(n, rows, model),
            sds(n, rows, ff),
            sds(n, rows, 2 * ff),
            sds(n, rows, model),
            sds(*gated.shape),
            sds(*gated.shape, dtype=fl),
            sds(*attn_mix.shape),
            sds(1, model, dtype=fl),
            sds(1, gated.shape[2], dtype=fl),
        ],
        in_specs=[pl.BlockSpec(memory_space=pltpu.VMEM)] * len(arrays),
        out_specs=[pl.BlockSpec(memory_space=pltpu.VMEM)] * 11,
        scratch_shapes=[
            pltpu.VMEM((n, rows, model), fl),
            pltpu.VMEM((n, rows, 2 * ff), fl),
            pltpu.VMEM((n, rows, ff), fl),
            pltpu.VMEM(gated.shape, fl),
            pltpu.VMEM((rows, model), fl),
            pltpu.VMEM((rows, model), fl),
            pltpu.VMEM((n, 8, total), fl),
            pltpu.VMEM((n, 8, total), fl),
            pltpu.VMEM((3, 3, rows, model), bf),
            pltpu.VMEM((3, 3, rows, model), bf),
            dma(7, 3),
            dma(7, 3),
        ],
        compiler_params=pltpu.CompilerParams(
            collective_id=1, has_side_effects=True, vmem_limit_bytes=VMEM_LIMIT
        ),
        name="ffn_middle",
    )(*arrays)


class LineReduce:
    def __init__(self, place, g, pair_got, side_got, acc, send, recv):
        self.p, self.g, self.pair_got, self.side_got, self.acc = place, g, pair_got, side_got, acc
        self.send, self.recv = send, recv

    def pair_copy(self, b):
        p = self.p
        return rcopy(
            self.g.at[2 * b + 1 - p.y],
            self.pair_got.at[b],
            self.send.at[0, b],
            self.recv.at[0, b],
            p.pair,
        )

    def each_from_far(self, body):
        p = self.p

        def step(k):
            d = p.L - 1 - k

            @pl.when(p.z + d <= p.L - 1)
            def _():
                body(p.z + d)

            @pl.when((d > 0) & (p.z - d >= 0))
            def _():
                body(p.z - d)

        loop(p.L, step)

    def start(self):
        self.each_from_far(lambda b: self.pair_copy(b).start())

    def got_from(self, b, right):
        p = self.p
        slot = b if right else b + p.L
        ref = self.side_got.at[slot]
        rcopy(ref, ref, self.send.at[1, b], self.recv.at[1, slot], p.right).wait_recv()
        return ref

    def pass_on(self, b, right):
        p = self.p
        self.pair_copy(b).wait_recv()
        mine, other = self.g.at[2 * b + p.y], self.pair_got.at[b]
        inner = p.has_left if right else p.has_right

        @pl.when(inner)
        def _():
            add_rows(other, mine, other, self.got_from(b, right))

        @pl.when(jnp.logical_not(inner))
        def _():
            add_rows(other, mine, other)

        slot = b if right else b + p.L
        rcopy(
            other,
            self.side_got.at[slot],
            self.send.at[1, b],
            self.recv.at[1, slot],
            p.right if right else p.left,
        ).start()

    def step(self, k):
        p = self.p
        d = p.L - 1 - k

        @pl.when(p.z + d <= p.L - 1)
        def _():
            self.pass_on(p.z + d, True)

        @pl.when(p.z - d >= 0)
        def _():
            self.pass_on(p.z - d, False)

    def total(self, target):
        p = self.p
        b = p.z
        self.pair_copy(b).wait_recv()
        add_rows(self.acc, self.g.at[2 * b + p.y], self.pair_got.at[b])

        @pl.when(p.has_left)
        def _():
            add_rows(self.acc, self.acc, self.got_from(b, True))

        @pl.when(p.has_right)
        def _():
            add_rows(self.acc, self.acc, self.got_from(b, False))

        add_rows(target, self.acc)

    def wait_sends(self):
        p = self.p

        def each(b):
            self.pair_copy(b).wait_send()

            @pl.when(b != p.z)
            def _():
                ref = self.pair_got.at[b]
                rcopy(ref, ref, self.send.at[1, b], self.recv.at[1, b], p.right).wait_send()

        loop(p.L, each)


def reduce_kernel(
    seq_count,
    fsdp_count,
    g_in,
    g_gu,
    g_out,
    small,
    d_norm,
    in_got,
    gu_got,
    out_got,
    small_got,
    d_norm_sum,
    in_pair,
    in_side,
    in_acc,
    gu_pair,
    gu_side,
    gu_acc,
    out_pair,
    out_side,
    out_acc,
    small_pair,
    small_line,
    stage,
    got,
    in_send,
    in_recv,
    gu_send,
    gu_recv,
    out_send,
    out_recv,
    cast_send,
    cast_recv,
    small_send,
    small_recv,
    sp_send,
    sp_recv,
    seq_send,
    seq_recv,
):
    p = Place(seq_count, fsdp_count)
    s, f, z, y, L = p.s, p.f, p.z, p.y, p.L
    per = fsdp_count // seq_count
    half = per // 2
    fl = jnp.float32
    chunk = g_out.shape[1] // CHUNKS
    p.greet()
    pair_small = rcopy(small, small_pair, sp_send.at[0], sp_recv.at[0], p.pair)
    pair_small.start()

    def rows_of(c):
        return pl.ds(pl.multiple_of(c * chunk, 16), chunk)

    def out_pair_copy(i, c):
        return rcopy(
            g_out.at[2 * i + 1 - y, rows_of(c)],
            out_pair.at[i, rows_of(c)],
            out_send.at[0, i, c],
            out_recv.at[0, i, c],
            p.pair,
        )

    def side_copy(i, c, right):
        at = 0 if right else 1
        return rcopy(
            out_pair.at[i, rows_of(c)],
            out_side.at[at, i, rows_of(c)],
            out_send.at[1, i, c],
            out_recv.at[1 + at, i, c],
            p.right if right else p.left,
        )

    ins = LineReduce(p, g_in, in_pair, in_side, in_acc, in_send, in_recv)
    gus = LineReduce(p, g_gu, gu_pair, gu_side, gu_acc, gu_send, gu_recv)
    d_sum = SeqReduce(p, stage, got, seq_send.at[0], seq_recv.at[0])
    loop(half * CHUNKS, lambda index: out_pair_copy(index // CHUNKS, index % CHUNKS).start())
    gus.start()
    ins.start()
    d_sum.send_diag(d_norm[p.s3])
    d_sum.send_sib(d_norm[p.s1])
    d_sum.send_across(d_norm[p.s2].astype(fl))
    pair_small.wait_recv()
    small_line[z] = small[...] + small_pair[...]
    smalls = LineGather(p, small_line, small_send, small_recv, pair=False)
    smalls.start()
    loop(L - 1, lambda d: smalls.step(d + 1))
    smalls.finish()
    pair_small.wait_send()
    small_sum = small_line[0]
    for b in range(1, L):
        small_sum = small_sum + small_line[b]
    small_got[s] = small_sum
    small_all = SeqGather(p, small_got.at[s], small_got, seq_send.at[1], seq_recv.at[1])
    small_all.start()
    d_norm_sum[...] = d_sum.total(d_norm[s].astype(fl))

    def cast(c, way):
        ref = out_got.at[rows_of(c)]
        return rcopy(ref, ref, cast_send.at[way, c], cast_recv.at[c], p.across if way else p.sib)

    def out_step(index):
        i, c = index // CHUNKS, index % CHUNKS
        zs = s * half + i
        out_pair_copy(i, c).wait_recv()
        mine = g_out.at[2 * i + y, rows_of(c)]
        other = out_pair.at[i, rows_of(c)]
        add_rows(out_acc, mine, other)

        @pl.when(p.has_left & (z <= zs))
        def _():
            side_copy(i, c, True).wait_recv()
            add_rows(out_acc, out_acc, out_side.at[0, i, rows_of(c)])

        @pl.when(p.has_right & (z >= zs))
        def _():
            side_copy(i, c, False).wait_recv()
            add_rows(out_acc, out_acc, out_side.at[1, i, rows_of(c)])

        @pl.when(z == zs)
        def _():
            add_rows(out_got.at[rows_of(c)], out_acc)
            cast(c, 1).start()
            cast(c, 0).start()

        @pl.when(z < zs)
        def _():
            add_rows(other, out_acc)
            side_copy(i, c, True).start()

        @pl.when(z > zs)
        def _():
            add_rows(other, out_acc)
            side_copy(i, c, False).start()

    loop(half * CHUNKS, out_step)
    small_all.forward()
    loop(L - 1, gus.step)
    gus.total(gu_got.at[s])
    gu_all = SeqGather(p, gu_got.at[s], gu_got, seq_send.at[2], seq_recv.at[2])
    gu_all.start()
    holder = f // per
    moved = (s + 4 - holder) % 4
    is_across = moved == 2

    @pl.when(is_across)
    def _():
        def pass_cast(c):
            cast(c, 0).wait_recv()
            cast(c, 0).start()

        loop(CHUNKS, pass_cast)

    loop(L - 1, ins.step)
    gu_all.forward()
    ins.total(in_got.at[s])
    in_all = SeqGather(p, in_got.at[s], in_got, seq_send.at[3], seq_recv.at[3])
    in_all.start()

    @pl.when((s != holder) & jnp.logical_not(is_across))
    def _():
        loop(CHUNKS, lambda c: cast(c, 0).wait_recv())

    @pl.when(s == holder)
    def _():
        def sent(c):
            cast(c, 0).wait_send()
            cast(c, 1).wait_send()

        loop(CHUNKS, sent)

    @pl.when(is_across)
    def _():
        loop(CHUNKS, lambda c: cast(c, 0).wait_send())

    def out_sent(index):
        i, c = index // CHUNKS, index % CHUNKS
        out_pair_copy(i, c).wait_send()

        @pl.when(z != s * half + i)
        def _():
            side_copy(i, c, True).wait_send()

    loop(half * CHUNKS, out_sent)
    gus.wait_sends()
    ins.wait_sends()
    d_sum.wait_sends()
    small_all.finish()
    gu_all.finish()
    in_all.forward()
    in_all.finish()


def reduce_all(seq_count, fsdp_count, arrays):
    g_in, g_gu, g_out, small, d_norm = arrays
    fl, bf = jnp.float32, jnp.bfloat16
    L = fsdp_count // 2
    per = fsdp_count // seq_count
    n = seq_count
    own, in_w = g_in.shape[1:]
    gu_w = g_gu.shape[2]
    out_rows, model = g_out.shape[1:]
    rows = d_norm.shape[1]
    v = pltpu.VMEM
    return pl.pallas_call(
        partial(reduce_kernel, seq_count, fsdp_count),
        out_shape=[
            jax.ShapeDtypeStruct((n, own, in_w), bf),
            jax.ShapeDtypeStruct((n, own, gu_w), bf),
            jax.ShapeDtypeStruct((out_rows, model), bf),
            jax.ShapeDtypeStruct((n,) + small.shape, fl),
            jax.ShapeDtypeStruct((rows, model), fl),
        ],
        in_specs=[pl.BlockSpec(memory_space=v)] * 5,
        out_specs=[pl.BlockSpec(memory_space=v)] * 5,
        scratch_shapes=[
            v((L, own, in_w), bf),
            v((2 * L, own, in_w), bf),
            v((own, in_w), fl),
            v((L, own, gu_w), bf),
            v((2 * L, own, gu_w), bf),
            v((own, gu_w), fl),
            v((per // 2, out_rows, model), bf),
            v((2, per // 2, out_rows, model), bf),
            v((out_rows // CHUNKS, model), fl),
            v(small.shape, fl),
            v((L,) + small.shape, fl),
            v((3, rows, model), bf),
            v((3, rows, model), bf),
            dma(2, L),
            dma(2, 2 * L),
            dma(2, L),
            dma(2, 2 * L),
            dma(2, per // 2, CHUNKS),
            dma(3, per // 2, CHUNKS),
            dma(2, CHUNKS),
            dma(CHUNKS),
            dma(3, L),
            dma(L),
            dma(1),
            dma(1),
            dma(4, 3),
            dma(4, 3),
        ],
        compiler_params=pltpu.CompilerParams(
            collective_id=2, has_side_effects=True, vmem_limit_bytes=VMEM_LIMIT
        ),
        name="reduce_grads",
    )(*arrays)


def rms_scale(values):
    return lax.rsqrt(jnp.mean(values * values, axis=-1, keepdims=True) + EPS)


def swish_slope(values):
    sigma = jax.nn.sigmoid(values)
    return sigma * (1.0 + values * (1.0 - sigma))


def silu_slope(values):
    sigma = jax.nn.sigmoid(values)
    return values * sigma, sigma * (1.0 + values * (1.0 - sigma))


def rows_at(r, size=128):
    return pl.ds(pl.multiple_of(r * size, size), size)


def dot(a, b, **kw):
    return jnp.dot(a, b, preferred_element_type=jnp.float32, **kw)


def dot_t(a, b, **kw):
    return lax.dot_general(a, b, (((1,), (1,)), ((), ())), preferred_element_type=jnp.float32, **kw)


def t_dot(a, b, **kw):
    return lax.dot_general(a, b, (((0,), (0,)), ((), ())), preferred_element_type=jnp.float32, **kw)


def row_sums(values):
    ones = jnp.ones((8, values.shape[1]), jnp.float32)
    return dot_t(ones, values, precision=HIGHEST)


def iota2(shape, axis):
    return lax.broadcasted_iota(jnp.int32, shape, axis)


def head_matrix(width):
    return (iota2((width, 128), 0) // HD == iota2((width, 128), 1)).astype(jnp.float32)


def partner(values):
    lane = iota2(values.shape, 1)
    return jnp.where(lane % HD < HD // 2, pltpu.roll(values, 96, 1), pltpu.roll(values, 32, 1))


def fill_mask(bias, seg_col, seg_row, transposed):
    total = bias.shape[0]

    def some(r):
        t = iota2((128, total), 0) + r * 128
        other = iota2((128, total), 1)
        order = t <= other if transposed else t >= other
        same = seg_col[rows_at(r)] == seg_row[0:1, :].astype(jnp.float32)
        bias[rows_at(r)] = jnp.where(order & same, 0.0, -1e30)

    loop(total // 128, some)


def forward_kernel(
    seq_count,
    fsdp_count,
    hidden,
    cot,
    mamba_in,
    attn_in,
    small,
    gate_up,
    mamba_out,
    attn_out,
    down_proj,
    gain_in,
    seg_row,
    all_taps,
    all_bias,
    all_heads,
    layer_out,
    d_mixed,
    ffn_in,
    ffn_act,
    d_ffn,
    d_mixed_all,
    gated_b,
    d_gated,
    d_attn,
    g_ffn_gain,
    g_gated_gain,
    cot_all,
    in_all,
    normed,
    gate_raw,
    inputs_b,
    accum_out,
    scan_bf,
    scan_y,
    steps,
    cum,
    attn_mix,
    gain_rows,
    seg_col,
    place,
    cosine,
    sine,
    taps,
    heads,
    hid_all,
    w_gu,
    w_mo,
    w_ao,
    w_dn,
    w_gg,
    pre_pad,
    x_act,
    b_mat,
    c_mat,
    x_step,
    inner,
    bias,
    gated,
    part_mix,
    gate_vals,
    d_gn,
    mixed,
    norm2,
    sq_buf,
    mean_buf,
    stage,
    got,
    local,
    in_send,
    in_recv,
    gu_send,
    gu_recv,
    out_send,
    out_recv,
    seq_send,
    seq_recv,
):
    p = Place(seq_count, fsdp_count)
    s, f, z, y, L = p.s, p.f, p.z, p.y, p.L
    fl, bf = jnp.float32, jnp.bfloat16
    per = fsdp_count // seq_count
    half = per // 2
    own_rows = mamba_in.shape[0]
    x_width = gate_raw.shape[1]
    query_width = attn_mix.shape[2]
    ff = w_dn.shape[0]
    rows = hidden.shape[0]
    total = seq_count * rows
    head_share = x_width // HD
    bc = mamba_in.shape[1] - 2 * DI
    conv_width = x_width + bc

    copies = []

    def bring(src, dst):
        copy = pltpu.make_async_copy(src, dst, local.at[len(copies)])
        copy.start()
        copies.append(copy)

    def part(ref, start, size):
        return ref.at[:, pl.ds(pl.multiple_of(start, 128), size)]

    def own_cols(ref, start, size):
        return ref.at[rows_at(f, own_rows), pl.ds(start, size)]

    c0 = 0
    for src, start, size in (
        (mamba_in, s * x_width, x_width),
        (mamba_in, DI + s * x_width, x_width),
        (mamba_in, 2 * DI, bc),
        (attn_in, s * query_width, query_width),
        (small, 0, small.shape[1]),
    ):
        bring(part(src, start, size), own_cols(in_all, c0, size))
        c0 += size
    in_copies = len(copies)
    bring(hidden, hid_all.at[s])
    bring(cot, cot_all.at[s])
    bring(part(gate_up, s * ff, ff), own_cols(w_gu, 0, ff))
    bring(part(gate_up, FF + s * ff, ff), own_cols(w_gu, ff, ff))
    holder = f // per == s
    spread_arrays = ((gain_in, w_gg, 1), (mamba_out, w_mo, 2), (attn_out, w_ao, 1), (down_proj, w_dn, 2))

    def own_spread(act):
        @pl.when(holder)
        def _():
            for k, (src, dst, _) in enumerate(spread_arrays):
                size = src.shape[0]
                act(pltpu.make_async_copy(src, dst.at[rows_at(f - s * per, size)], local.at[12 + k]))

    own_spread(lambda copy: copy.start())
    p.greet(diag=True)
    for copy in copies[:in_copies]:
        copy.wait()
    ins = LineGather(p, in_all, in_send, in_recv, size=own_rows)
    gus = LineGather(p, w_gu, gu_send, gu_recv, size=own_rows)
    hid = SeqGather(p, hidden, hid_all, seq_send.at[7], seq_recv.at[7])
    cots = SeqGather(p, cot, cot_all, seq_send.at[8], seq_recv.at[8])
    hid.start()
    ins.start()
    seg_float = seg_row[...].astype(fl)
    seg_col[...] = jnp.broadcast_to(seg_float, (8, total)).T[:, 0:1]
    first_count = jnp.sum(1.0 - seg_float, axis=1, keepdims=True)
    position = iota2((total, 1), 0).astype(fl)
    place[...] = position - jnp.where(seg_col[...] == 0.0, 0.0, first_count)
    lane = iota2((1, 128), 1)
    turn = (lane % (HD // 2)).astype(fl)
    angles = place[...] * jnp.exp(-math.log(ROPE_THETA) * 2.0 * turn / HD)
    cosine[...] = jnp.cos(angles)
    sine[...] = jnp.sin(angles) * jnp.where(lane % HD < HD // 2, -1.0, 1.0)
    fill_mask(bias, seg_col, seg_row, False)
    own_x = pl.ds(pl.multiple_of(s * x_width, 128), x_width)
    taps[0:KC, :x_width] = all_taps[:, own_x]
    taps[0:KC, x_width:] = all_taps[:, DI:]
    taps[KC : KC + 1, :x_width] = all_bias[:, own_x]
    taps[KC : KC + 1, x_width:] = all_bias[:, DI:]
    mine = pltpu.roll(all_heads[...], (128 - s * head_share) % 128, 1)
    mine = jnp.where(iota2(mine.shape, 1) < head_share, mine, 0.0)
    heads[0:1, :128] = mine[0:1]
    heads[1:2, :128] = jnp.where(iota2((1, 128), 1) < head_share, -jnp.exp(mine[1:2]), 0.0)
    heads[2:3, :] = dot_t(mine, head_matrix(x_width), precision=HIGHEST)[2:3]
    hid.forward()
    loop(L - 1, lambda d: ins.step(d + 1))
    cots.start()
    for copy in copies[in_copies:]:
        copy.wait()
    own_spread(lambda copy: copy.wait())

    pieces = []
    for k, (src, dst, count) in enumerate(spread_arrays):
        size = src.shape[0]
        for c in range(count):
            pieces.append((dst, size, c * (size // count), size // count))

    def piece_copy(i, k, way, other=0):
        dst, size, offset, count = pieces[k]
        j = 2 * i + (1 - y if other else y)
        ref = dst.at[pl.ds(pl.multiple_of(j * size + offset, 16), count)]
        device = (p.right, p.left, p.pair)[way]
        return rcopy(ref, ref, out_send.at[way, i, k], out_recv.at[way // 2, i, k], device)

    def push_piece(i, k):
        zs = s * half + i

        @pl.when((z >= zs) & p.has_right)
        def _():
            piece_copy(i, k, 0).start()

        @pl.when((z <= zs) & p.has_left)
        def _():
            piece_copy(i, k, 1).start()

        piece_copy(i, k, 2).start()

    def hold_piece(k):
        for i in range(half):

            @pl.when(z == s * half + i)
            def _():
                push_piece(i, k)

    def pass_pieces(group, far):
        for k in group:
            pass_piece(k, far)

    def pass_piece(k, far):
        for i in range(half):
            zs = s * half + i

            @pl.when((z - zs == far) | (zs - z == far))
            def _():
                piece_copy(i, k, 0).wait_recv()
                push_piece(i, k)

    def end_piece(k):
        for i in range(half):
            piece_copy(i, k, 2, 1).wait_recv()

    def sent_piece(k):
        for i in range(half):
            zs = s * half + i
            piece_copy(i, k, 2).wait_send()

            @pl.when((z >= zs) & p.has_right)
            def _():
                piece_copy(i, k, 0).wait_send()

            @pl.when((z <= zs) & p.has_left)
            def _():
                piece_copy(i, k, 1).wait_send()

    early = range(4)
    late = range(4, len(pieces))
    for k in early:
        hold_piece(k)
    gus.start()
    for k in late:
        hold_piece(k)
    ins.finish()
    hid.finish()
    cots.forward()

    gain_t = in_all[:, in_all.shape[1] - 128 :].astype(fl).T
    gain_rows[...] = gain_t[0:16]
    first_gain = gain_rows[head_share : head_share + 1, :]

    def norm_block(r):
        values = hid_all[r].astype(fl)
        scale = lax.rsqrt(jnp.mean(values * values, axis=-1, keepdims=True) + EPS)
        normed[rows_at(r)] = (values * scale * first_gain).astype(bf)

    loop(seq_count, norm_block)
    pass_pieces(early, 1)
    gate_raw[...] = dot(normed[...], in_all[:, :x_width])
    inputs_b[:, :conv_width] = dot(normed[...], in_all[:, x_width : x_width + conv_width]).astype(bf)
    inputs_b[:, conv_width:] = dot(normed[...], in_all[:, x_width + conv_width :]).astype(bf)
    pass_pieces(late, 1)
    gus.step(1)
    pre_pad[0:8] = jnp.zeros((8, conv_width), fl)
    pre_pad[8 : 8 + total] = inputs_b[:, :conv_width].astype(fl)
    for r in range(seq_count):
        at = slice(r * rows, (r + 1) * rows)
        accum = taps[KC : KC + 1, :] + taps[KC - 1 : KC, :] * pre_pad[8 + r * rows : 8 + (r + 1) * rows]
        for lag in range(1, KC):
            moved = pre_pad[8 + r * rows - lag : 8 + (r + 1) * rows - lag]
            accum = accum + taps[KC - 1 - lag : KC - lag, :] * jnp.where(
                place[at] >= lag, moved, 0.0
            )
        accum_out[at] = accum
        acts = accum * jax.nn.sigmoid(accum)
        x_act[at] = acts[:, :x_width]
        b_mat[at] = acts[:, x_width : x_width + NST].astype(bf)
        c_mat[at] = acts[:, x_width + NST :].astype(bf)
    pass_pieces(early, 2)
    raw = inputs_b[:, conv_width + query_width + 2 * HD :].astype(fl) + heads[0:1, :128]
    steps[...] = jnp.maximum(raw, 0.0) + jnp.log1p(jnp.exp(-jnp.abs(raw)))
    causal = (iota2((total, total), 0) >= iota2((total, total), 1)).astype(fl)
    cum[...] = dot(causal, heads[1:2, :128] * steps[...], precision=HIGHEST)
    cum_t = cum[...].T
    spread_heads = head_matrix(x_width)
    x_step[...] = (x_act[...] * dot_t(steps[...], spread_heads, precision=HIGHEST)).astype(bf)
    inner[...] = dot_t(c_mat[...], b_mat[...])
    gus.step(2)
    pumps = {
        0: lambda: pass_pieces(late, 2),
        1: lambda: pass_pieces(early, 3),
        3: lambda: gus.step(3),
        5: lambda: pass_pieces(late, 3),
    }
    for h in range(head_share):
        hs = slice(h * HD, (h + 1) * HD)
        for r in range(seq_count):
            at = slice(r * rows, (r + 1) * rows)
            K = (r + 1) * rows
            decay = jnp.exp(cum[at, h : h + 1] - cum_t[h : h + 1, :K] + bias[at, :K])
            kernel_b = (inner[at, :K] * decay).astype(bf)
            scan_y[at, hs] = dot(kernel_b, x_step[:K, hs])
        if h in pumps:
            pumps[h]()
    for r in range(seq_count):
        at = slice(r * rows, (r + 1) * rows)
        scan = (scan_y[at] + heads[2:3, :x_width] * x_act[at]).astype(bf)
        scan_bf[at] = scan
        gate = gate_raw[at]
        gated[r] = scan.astype(fl) * (gate * jax.nn.sigmoid(gate))
    for r in range(seq_count):
        values = gated[r]
        sq_buf[s, :, r * rows : (r + 1) * rows] = row_sums(values * values)
    peers = (p.sib, p.across, p.diag)
    peer_at = (p.s1, p.s2, p.s3)

    def exchange(buf, at):
        pairs = []
        for k in range(3):
            copy = rcopy(buf.at[s], buf.at[s], seq_send.at[at, k], seq_recv.at[at, k], peers[k])
            copy.start()
            other = buf.at[peer_at[k]]
            pairs.append((copy, rcopy(other, other, seq_send.at[at, k], seq_recv.at[at, k], peers[k])))

        def end():
            for copy, arrived in pairs:
                arrived.wait_recv()
                copy.wait_send()
            return buf[0] + buf[1] + buf[2] + buf[3]

        return end

    sq_end = exchange(sq_buf, 0)
    q_in = inputs_b[:, conv_width : conv_width + query_width].astype(fl)
    kv_in = inputs_b[:, conv_width + query_width : conv_width + query_width + 2 * HD].astype(fl)
    q_rot = q_in * cosine[...] + partner(q_in) * sine[...]
    k_rot = (kv_in * cosine[...] + partner(kv_in) * sine[...])[:, :HD]
    v_b = inputs_b[:, conv_width + query_width + HD : conv_width + query_width + 2 * HD]
    for r in range(seq_count):
        at = slice(r * rows, (r + 1) * rows)
        K = (r + 1) * rows
        for h in range(query_width // HD):
            hs = slice(h * HD, (h + 1) * HD)
            scores = dot_t(q_rot[at, hs], k_rot[:K], precision=HIGHEST) * (1.0 / math.sqrt(HD))
            weights = jnp.exp(scores + bias[at, :K])
            weights = weights / jnp.sum(weights, axis=-1, keepdims=True)
            attn_mix[r, :, hs] = dot(weights.astype(bf), v_b[:K]).astype(bf)
    cots.finish()
    for k in early:
        end_piece(k)
    gain = w_gg[...].astype(fl).T[0:1, :]
    for r in range(seq_count):
        part_mix[r] = dot((gated[r] * gain).astype(bf), w_mo[...])
    scale_cols = lax.rsqrt(sq_end() / DI + EPS).T
    for r in range(seq_count):
        scale = scale_cols[r * rows : (r + 1) * rows, 0:1]
        part_mix[r] = part_mix[r] * scale + dot(attn_mix[r], w_ao[...])
        gated_b[r] = (gated[r] * scale * gain).astype(bf)

    def reducer(at):
        return SeqReduce(p, stage.at[at], got.at[at], seq_send.at[at + 1], seq_recv.at[at + 1])

    mix = reducer(0)
    mix.send_diag(part_mix[p.s3])
    mix.send_sib(part_mix[p.s1])
    mix.send_across(part_mix[p.s2])
    second_gain = gain_rows[head_share + 1 : head_share + 2, :]
    residual = hid_all[s].astype(fl)
    mixed[...] = residual + mix.total(part_mix[s])
    scale2 = lax.rsqrt(jnp.mean(mixed[...] * mixed[...], axis=-1, keepdims=True) + EPS)
    norm2[...] = mixed[...] * scale2
    ffn_in[s] = (norm2[...] * second_gain).astype(bf)
    ffn_all = SeqGather(p, ffn_in.at[s], ffn_in, seq_send.at[4], seq_recv.at[4])
    ffn_all.start()
    gus.finish()

    def ffn_block(r):
        gate_vals[r] = dot(ffn_in[r], w_gu[...])

    def act_block(r):
        gate_lin = gate_vals[r, :, :ff]
        up_lin = gate_vals[r, :, ff:]
        act, slope = silu_slope(gate_lin)
        ffn_act[r] = (act * up_lin).astype(bf)
        da = dot_t(cot_all[r], w_dn[...])
        d_ffn[r, :, :ff] = (da * up_lin * slope).astype(bf)
        d_ffn[r, :, ff:] = (da * act).astype(bf)

    ffn_block(s)
    for k in late:
        end_piece(k)
    act_block(s)
    ffn_all.wait_sib()
    ffn_block(p.s1)
    ffn_all.forward()
    act_block(p.s1)
    ffn_block(p.s2)
    act_block(p.s2)
    ffn_all.wait_diag()
    ffn_block(p.s3)
    act_block(p.s3)
    back = reducer(1)
    back.send_diag(dot_t(d_ffn[p.s3], w_gu[...]))
    back.send_sib(dot_t(d_ffn[p.s1], w_gu[...]))
    back.send_across(dot_t(d_ffn[p.s2], w_gu[...]))
    out = reducer(2)
    d_ffn_own = dot_t(d_ffn[s], w_gu[...])
    d_ffn_in = back.total(d_ffn_own)
    g_ffn_gain[...] = jnp.sum(d_ffn_in * norm2[...], axis=0, keepdims=True)
    d_second = d_ffn_in * second_gain
    d_mixed[...] = cot_all[s].astype(fl) + scale2 * (
        d_second - norm2[...] * jnp.mean(d_second * norm2[...], axis=-1, keepdims=True)
    )
    d_mixed_all[s] = d_mixed[...].astype(bf)
    back_all = SeqGather(p, d_mixed_all.at[s], d_mixed_all, seq_send.at[5], seq_recv.at[5])
    back_all.start()
    out.send_diag(dot(ffn_act[p.s3], w_dn[...]))
    out.send_sib(dot(ffn_act[p.s1], w_dn[...]))

    def mixer_block(r):
        block = d_mixed_all[r]
        d_gn[r] = dot_t(block, w_mo[...])
        d_attn[r] = dot_t(block, w_ao[...]).astype(bf)

    mixer_block(s)
    back_all.wait_sib()
    mixer_block(p.s1)
    out.send_across(dot(ffn_act[p.s2], w_dn[...]))
    back_all.forward()
    mixer_block(p.s2)
    back_all.wait_diag()
    mixer_block(p.s3)
    for r in range(seq_count):
        scale = scale_cols[r * rows : (r + 1) * rows, 0:1]
        values = d_gn[r] * gain * (gated[r] * scale)
        mean_buf[s, :, r * rows : (r + 1) * rows] = row_sums(values)
    mean_end = exchange(mean_buf, 6)
    layer_out[...] = (mixed[...] + out.total(dot(ffn_act[s], w_dn[...]))).astype(bf)
    gain_total = jnp.zeros_like(g_gated_gain[...])
    for r in range(seq_count):
        scale = scale_cols[r * rows : (r + 1) * rows, 0:1]
        gain_total = gain_total + jnp.sum(d_gn[r] * (gated[r] * scale), axis=0, keepdims=True)
    g_gated_gain[...] = gain_total
    means = (mean_end() / DI).T
    for r in range(seq_count):
        scale = scale_cols[r * rows : (r + 1) * rows, 0:1]
        mean = means[r * rows : (r + 1) * rows, 0:1]
        d_gated[r] = scale * (d_gn[r] * gain - (gated[r] * scale) * mean)
    for k in range(len(pieces)):
        sent_piece(k)
    mix.wait_sends()
    back.wait_sends()
    out.wait_sends()
    ffn_all.wait_sends()
    back_all.wait_sends()


def forward_all(seq_count, fsdp_count, widths, arrays):
    x_width, query_width, ff = widths
    hidden, cot, mamba_in, attn_in, small = arrays[:5]
    mamba_out, attn_out, down_proj, gain_in = arrays[6:10]
    fl, bf = jnp.float32, jnp.bfloat16
    rows, model = hidden.shape
    n = seq_count
    total = n * rows
    per = fsdp_count // seq_count
    L = fsdp_count // 2
    conv_width = x_width + 2 * NST
    in_width = x_width + conv_width + query_width + small.shape[1]
    v = pltpu.VMEM

    def sds(*shape, dtype=bf):
        return jax.ShapeDtypeStruct(shape, dtype)

    outs = [
        sds(rows, model),
        sds(rows, model, dtype=fl),
        sds(n, rows, model),
        sds(n, rows, ff),
        sds(n, rows, 2 * ff),
        sds(n, rows, model),
        sds(n, rows, x_width),
        sds(n, rows, x_width, dtype=fl),
        sds(n, rows, query_width),
        sds(1, model, dtype=fl),
        sds(1, x_width, dtype=fl),
        sds(n, rows, model),
        sds(model, in_width),
        sds(total, model),
        sds(total, x_width, dtype=fl),
        sds(total, in_width - x_width),
        sds(total, conv_width, dtype=fl),
        sds(total, x_width),
        sds(total, x_width, dtype=fl),
        sds(total, 128, dtype=fl),
        sds(total, 128, dtype=fl),
        sds(n, rows, query_width),
        sds(16, model, dtype=fl),
        sds(total, 1, dtype=fl),
        sds(total, 1, dtype=fl),
        sds(total, 128, dtype=fl),
        sds(total, 128, dtype=fl),
        sds(8, conv_width, dtype=fl),
        sds(8, x_width, dtype=fl),
    ]
    vm = pl.BlockSpec(memory_space=v)
    hbm = pl.BlockSpec(memory_space=pl.ANY)
    return pl.pallas_call(
        partial(forward_kernel, seq_count, fsdp_count),
        out_shape=outs,
        in_specs=[hbm] * 10 + [vm] * (len(arrays) - 10),
        out_specs=[vm] * len(outs),
        scratch_shapes=[
            v((n, rows, model), bf),
            v((model, 2 * ff), bf),
            v((x_width, model), bf),
            v((query_width, model), bf),
            v((ff, model), bf),
            v((x_width, 128), bf),
            v((total + 8, conv_width), fl),
            v((total, x_width), fl),
            v((total, NST), bf),
            v((total, NST), bf),
            v((total, x_width), bf),
            v((total, total), fl),
            v((total, total), fl),
            v((n, rows, x_width), fl),
            v((n, rows, model), fl),
            v((n, rows, 2 * ff), fl),
            v((n, rows, x_width), fl),
            v((rows, model), fl),
            v((rows, model), fl),
            v((n, 8, total), fl),
            v((n, 8, total), fl),
            v((3, 3, rows, model), bf),
            v((3, 3, rows, model), bf),
            dma(16),
            dma(3, L),
            dma(fsdp_count),
            dma(3, L),
            dma(fsdp_count),
            dma(3, per // 2, 6),
            dma(2, per // 2, 6),
            dma(9, 3),
            dma(9, 3),
        ],
        compiler_params=pltpu.CompilerParams(
            collective_id=3, has_side_effects=True, vmem_limit_bytes=VMEM_LIMIT
        ),
        name="forward_fused",
    )(*arrays)


SMALL_ROWS = 48


def backward_kernel(
    seq_count,
    fsdp_count,
    hidden,
    d_mixed,
    d_mixed_all,
    cot_all,
    ffn_in,
    ffn_act,
    d_ffn,
    gated_b,
    attn_mix,
    d_gated,
    d_attn,
    g_ffn_gain,
    g_gated_gain,
    in_all,
    normed,
    gate_raw,
    inputs_b,
    accum_in,
    scan_bf,
    scan_y,
    steps,
    cum,
    gain_rows,
    seg_col,
    seg_row,
    place,
    cosine,
    sine,
    taps,
    heads,
    in_got,
    gu_got,
    out_got,
    small_got,
    grad_tok,
    g_in,
    g_gu,
    g_out,
    small,
    d_norm,
    d_in,
    dy,
    x_act,
    b_mat,
    c_mat,
    x_step,
    inner,
    inner_t,
    bias,
    bias_t,
    d_inner,
    d_x_step,
    d_acc,
    shifted,
    d_kv,
    d_x_conv,
    in_pair,
    in_side,
    in_acc,
    gu_pair,
    gu_side,
    gu_acc,
    out_pair,
    out_side,
    out_acc,
    small_pair,
    small_line,
    stage,
    got,
    in_send,
    in_recv,
    gu_send,
    gu_recv,
    out_send,
    out_recv,
    cast_send,
    cast_recv,
    small_send,
    small_recv,
    sp_send,
    sp_recv,
    seq_send,
    seq_recv,
):
    p = Place(seq_count, fsdp_count)
    s, f, z, y, L = p.s, p.f, p.z, p.y, p.L
    fl, bf = jnp.float32, jnp.bfloat16
    per = fsdp_count // seq_count
    half = per // 2
    chunk = g_out.shape[1] // CHUNKS
    total = normed.shape[0]
    rows = total // seq_count
    model = normed.shape[1]
    own_rows = model // fsdp_count
    x_width = gate_raw.shape[1]
    query_width = attn_mix.shape[1]
    conv_width = accum_in.shape[1]
    head_share = x_width // HD
    ff = ffn_act.shape[1]
    gain_own, attn_own, ff_own = DI // fsdp_count, QH * HD // fsdp_count, FF // fsdp_count
    p.greet()

    def rows_of(c):
        return pl.ds(pl.multiple_of(c * chunk, 16), chunk)

    def out_pair_copy(i, c):
        return rcopy(
            g_out.at[2 * i + 1 - y, rows_of(c)],
            out_pair.at[i, rows_of(c)],
            out_send.at[0, i, c],
            out_recv.at[0, i, c],
            p.pair,
        )

    def side_copy(i, c, right):
        at = 0 if right else 1
        return rcopy(
            out_pair.at[i, rows_of(c)],
            out_side.at[at, i, rows_of(c)],
            out_send.at[1, i, c],
            out_recv.at[1 + at, i, c],
            p.right if right else p.left,
        )

    def cast(c, way):
        ref = out_got.at[rows_of(c)]
        return rcopy(ref, ref, cast_send.at[way, c], cast_recv.at[c], p.across if way else p.sib)

    def out_step(index):
        i, c = index // CHUNKS, index % CHUNKS
        zs = s * half + i
        out_pair_copy(i, c).wait_recv()
        mine = g_out.at[2 * i + y, rows_of(c)]
        other = out_pair.at[i, rows_of(c)]
        add_rows(out_acc, mine, other)

        @pl.when(p.has_left & (z <= zs))
        def _():
            side_copy(i, c, True).wait_recv()
            add_rows(out_acc, out_acc, out_side.at[0, i, rows_of(c)])

        @pl.when(p.has_right & (z >= zs))
        def _():
            side_copy(i, c, False).wait_recv()
            add_rows(out_acc, out_acc, out_side.at[1, i, rows_of(c)])

        @pl.when(z == zs)
        def _():
            add_rows(out_got.at[rows_of(c)], out_acc)
            cast(c, 1).start()
            cast(c, 0).start()

        @pl.when(z < zs)
        def _():
            add_rows(other, out_acc)
            side_copy(i, c, True).start()

        @pl.when(z > zs)
        def _():
            add_rows(other, out_acc)
            side_copy(i, c, False).start()

    ins = LineReduce(p, g_in, in_pair, in_side, in_acc, in_send, in_recv)
    gus = LineReduce(p, g_gu, gu_pair, gu_side, gu_acc, gu_send, gu_recv)

    for fi in range(fsdp_count):
        at = slice(fi * own_rows, (fi + 1) * own_rows)
        g_gu[fi] = t_dot(ffn_in[:, at], d_ffn[...]).astype(bf)
    gus.start()
    g_mo = t_dot(gated_b[...], d_mixed_all[...]).astype(bf)
    g_ao = t_dot(attn_mix[...], d_mixed_all[...]).astype(bf)
    for j in range(per):
        g_out[j, :gain_own] = g_mo[j * gain_own : (j + 1) * gain_own]
        g_out[j, gain_own : gain_own + attn_own] = g_ao[j * attn_own : (j + 1) * attn_own]
        act = ffn_act[:, j * ff_own : (j + 1) * ff_own]
        g_out[j, gain_own + attn_own :] = t_dot(act, cot_all[...]).astype(bf)
    loop(half * CHUNKS, lambda index: out_pair_copy(index // CHUNKS, index % CHUNKS).start())

    fill_mask(bias, seg_col, seg_row, False)
    fill_mask(bias_t, seg_col, seg_row, True)
    spread_heads = head_matrix(x_width)
    steps_wide = dot_t(steps[...], spread_heads, precision=HIGHEST)
    skip = heads[2:3, :x_width]
    cum_t = cum[...].T
    for r in range(seq_count):
        at = slice(r * rows, (r + 1) * rows)
        accum = accum_in[at]
        acts = accum * jax.nn.sigmoid(accum)
        x_act[at] = acts[:, :x_width]
        b_mat[at] = acts[:, x_width : x_width + NST].astype(bf)
        c_mat[at] = acts[:, x_width + NST :].astype(bf)
        x_step[at] = (acts[:, :x_width] * steps_wide[at]).astype(bf)
        gate_act, slope = silu_slope(gate_raw[at])
        cots = d_gated[at]
        dy[at] = (cots * gate_act).astype(bf)
        d_in[at, :x_width] = (cots * scan_bf[at].astype(fl) * slope).astype(bf)
    inner[...] = dot_t(c_mat[...], b_mat[...])
    inner_t[...] = dot_t(b_mat[...], c_mat[...])
    d_inner[...] = jnp.zeros_like(d_inner)
    gu_all = SeqGather(p, gu_got.at[s], gu_got, seq_send.at[2], seq_recv.at[2])
    for h in range(head_share):
        hs = slice(h * HD, (h + 1) * HD)
        for r in range(seq_count):
            at = slice(r * rows, (r + 1) * rows)
            K = (r + 1) * rows
            decay = jnp.exp(cum[at, h : h + 1] - cum_t[h : h + 1, :K] + bias[at, :K])
            d_inner[at, :K] += dot_t(dy[at, hs], x_step[:K, hs]) * decay
            decay = jnp.exp(cum_t[h : h + 1, r * rows :] - cum[at, h : h + 1] + bias_t[at, r * rows :])
            kernel_t = (inner_t[at, r * rows :] * decay).astype(bf)
            d_x_step[at, hs] = dot(kernel_t, dy[r * rows :, hs])
    gus.step(0)
    d_inner_b = d_inner[...].astype(bf)
    d_acc[:, x_width : x_width + NST] = t_dot(d_inner_b, c_mat[...])
    d_acc[:, x_width + NST :] = dot(d_inner_b, b_mat[...])
    dy_f = dy[...].astype(fl)
    xs = x_act[...]
    dxs = d_x_step[...]
    d_acc[:, :x_width] = steps_wide * dxs + skip * dy_f
    head_sums = dot(
        jnp.sum((dy_f * xs).reshape(total // 8, 8, x_width), axis=0), spread_heads, precision=HIGHEST
    )
    g_skip = jnp.sum(head_sums, axis=0, keepdims=True)
    step_direct = dot(xs * dxs, spread_heads, precision=HIGHEST)
    d_cum = dot(
        dy_f * scan_y[...] - x_step[...].astype(fl) * dxs, spread_heads, precision=HIGHEST
    )
    after = (iota2((total, total), 0) <= iota2((total, total), 1)).astype(fl)
    d_log = dot(after, d_cum, precision=HIGHEST)
    decay_row = heads[1:2, :128]
    g_decay = jnp.sum(d_log * (decay_row * steps[...]), axis=0, keepdims=True)
    raw = inputs_b[:, conv_width + query_width + 2 * HD :].astype(fl) + heads[0:1, :128]
    d_raw = (step_direct + d_log * decay_row) * jax.nn.sigmoid(raw)
    d_raw = jnp.where(iota2(d_raw.shape, 1) < head_share, d_raw, 0.0)
    g_step_bias = jnp.sum(d_raw, axis=0, keepdims=True)
    step_at = x_width + conv_width + query_width + 2 * HD
    d_in[:, step_at:] = d_raw.astype(bf)

    q_at = conv_width
    kv_at = conv_width + query_width
    q_in = inputs_b[:, q_at:kv_at].astype(fl)
    kv_in = inputs_b[:, kv_at : kv_at + 2 * HD].astype(fl)
    q_rot = q_in * cosine[...] + partner(q_in) * sine[...]
    k_rot = (kv_in * cosine[...] + partner(kv_in) * sine[...])[:, :HD]
    k_b = k_rot.astype(bf)
    v_b = inputs_b[:, kv_at + HD : kv_at + 2 * HD]
    d_kv[...] = jnp.zeros_like(d_kv)
    scale = 1.0 / math.sqrt(HD)
    for r in range(seq_count):
        at = slice(r * rows, (r + 1) * rows)
        K = (r + 1) * rows
        for h in range(query_width // HD):
            hs = slice(h * HD, (h + 1) * HD)
            scores = dot_t(q_rot[at, hs], k_rot[:K], precision=HIGHEST) * scale
            weights = jnp.exp(scores + bias[at, :K])
            weights = weights / jnp.sum(weights, axis=-1, keepdims=True)
            d_att = d_attn[at, hs]
            d_weights = dot_t(d_att, v_b[:K])
            along = jnp.sum(d_weights * weights, axis=-1, keepdims=True)
            d_scores = (weights * (d_weights - along) * scale).astype(bf)
            shifted[at, hs] = dot(d_scores, k_b[:K])
            d_kv[:K, :HD] += t_dot(d_scores, q_rot[at, hs].astype(bf))
            d_kv[:K, HD : 2 * HD] += t_dot(weights.astype(bf), d_att)
    d_q = shifted[:total, :query_width]
    d_q = d_q * cosine[...] + partner(d_q * sine[...])
    d_kv_all = d_kv[...]
    d_k = d_kv_all * cosine[...] + partner(d_kv_all * sine[...])
    d_kv_all = jnp.where(iota2(d_k.shape, 1) < HD, d_k, d_kv_all)
    d_in[:, x_width + q_at : x_width + kv_at] = d_q.astype(bf)
    d_in[:, x_width + kv_at : x_width + kv_at + 2 * HD] = d_kv_all.astype(bf)

    gus.step(1)

    tap_sums = [jnp.zeros((1, conv_width), fl) for _ in range(KC + 1)]
    shifted[total:] = jnp.zeros((8, conv_width), fl)
    for r in range(seq_count):
        at = slice(r * rows, (r + 1) * rows)
        d_acc[at] = d_acc[at] * silu_slope(accum_in[at])[1]
        tap_sums[KC] = tap_sums[KC] + jnp.sum(d_acc[at], axis=0, keepdims=True)
        pre = inputs_b[at, :conv_width].astype(fl)
        tap_sums[KC - 1] = tap_sums[KC - 1] + jnp.sum(d_acc[at] * pre, axis=0, keepdims=True)
    for lag in range(1, KC):
        k = KC - 1 - lag
        shifted[:total] = jnp.where(place[...] >= lag, d_acc[...], 0.0)
        for r in range(seq_count):
            at = slice(r * rows, (r + 1) * rows)
            moved = shifted[r * rows + lag : (r + 1) * rows + lag]
            pre = inputs_b[at, :conv_width].astype(fl)
            tap_sums[k] = tap_sums[k] + jnp.sum(moved * pre, axis=0, keepdims=True)
            grads = taps[k : k + 1, :] * moved
            if lag == 1:
                grads = grads + taps[KC - 1 : KC, :] * d_acc[at]
                d_x_conv[at] = grads
            else:
                d_x_conv[at] += grads
    d_in[:, x_width : x_width + conv_width] = d_x_conv[...].astype(bf)

    loop(L - 3, lambda k: gus.step(k + 2))

    d_sum = SeqReduce(p, stage, got, seq_send.at[0], seq_recv.at[0])
    norm_gain_sum = jnp.zeros((1, model), fl)
    first_gain = gain_rows[head_share : head_share + 1, :]
    for r in range(seq_count):
        at = slice(r * rows, (r + 1) * rows)
        part = dot_t(d_in[at], in_all[...])
        d_norm[r] = part
        norm_gain_sum = norm_gain_sum + jnp.sum(part * normed[at].astype(fl), axis=0, keepdims=True)
    norm_gain_sum = norm_gain_sum / first_gain
    d_sum.send_diag(d_norm[p.s3])
    d_sum.send_sib(d_norm[p.s1])
    d_sum.send_across(d_norm[p.s2])

    def put(at, row):
        for c in range(row.shape[1] // 128):
            small[at + c : at + c + 1, :] = row[:, c * 128 : (c + 1) * 128]
        return at + row.shape[1] // 128

    at = 0
    for row in tap_sums + [g_gated_gain[...], norm_gain_sum, g_ffn_gain[...], g_step_bias, g_decay, g_skip]:
        at = put(at, row)
    small[at:] = jnp.zeros((SMALL_ROWS - at, 128), fl)
    pair_small = rcopy(small, small_pair, sp_send.at[0], sp_recv.at[0], p.pair)
    pair_small.start()
    for fi in range(fsdp_count):
        at = slice(fi * own_rows, (fi + 1) * own_rows)
        g_in[fi] = t_dot(normed[:, at], d_in[...]).astype(bf)
    ins.start()
    gus.total(gu_got.at[s])
    gu_all.start()
    loop(half * CHUNKS, out_step)
    pair_small.wait_recv()
    small_line[z] = small[...] + small_pair[...]
    smalls = LineGather(p, small_line, small_send, small_recv, pair=False)
    smalls.start()
    gu_all.forward()
    holder = f // per
    is_across = (s + 4 - holder) % 4 == 2

    def hop(k):
        ins.step(k)
        smalls.step(k + 1)

    loop(L - 1, hop)

    @pl.when(is_across)
    def _():
        def pass_cast(c):
            cast(c, 0).wait_recv()
            cast(c, 0).start()

        loop(CHUNKS, pass_cast)

    smalls.finish()
    small_sum = small_line[0]
    for b in range(1, L):
        small_sum = small_sum + small_line[b]
    small_got[s] = small_sum
    small_all = SeqGather(p, small_got.at[s], small_got, seq_send.at[1], seq_recv.at[1])
    small_all.start()
    ins.total(in_got.at[s])
    in_gather = SeqGather(p, in_got.at[s], in_got, seq_send.at[3], seq_recv.at[3])
    in_gather.start()
    small_all.forward()
    d_normed = d_sum.total(d_norm[s])
    residual = hidden[...].astype(fl)
    scale1 = lax.rsqrt(jnp.mean(residual * residual, axis=-1, keepdims=True) + EPS)
    first_norm = residual * scale1
    d_first = d_normed * first_gain
    grad_tok[...] = d_mixed[...] + scale1 * (
        d_first - first_norm * jnp.mean(d_first * first_norm, axis=-1, keepdims=True)
    )

    @pl.when((s != holder) & jnp.logical_not(is_across))
    def _():
        loop(CHUNKS, lambda c: cast(c, 0).wait_recv())

    @pl.when(s == holder)
    def _():
        def sent(c):
            cast(c, 0).wait_send()
            cast(c, 1).wait_send()

        loop(CHUNKS, sent)

    @pl.when(is_across)
    def _():
        loop(CHUNKS, lambda c: cast(c, 0).wait_send())

    def out_sent(index):
        i, c = index // CHUNKS, index % CHUNKS
        out_pair_copy(i, c).wait_send()

        @pl.when(z != s * half + i)
        def _():
            side_copy(i, c, True).wait_send()

    loop(half * CHUNKS, out_sent)
    in_gather.forward()
    pair_small.wait_send()
    gus.wait_sends()
    ins.wait_sends()
    d_sum.wait_sends()
    small_all.finish()
    gu_all.finish()
    in_gather.finish()


def backward_all(seq_count, fsdp_count, arrays):
    hidden = arrays[0]
    fl, bf = jnp.float32, jnp.bfloat16
    L = fsdp_count // 2
    per = fsdp_count // seq_count
    n = seq_count
    rows, model = hidden.shape
    total = n * rows
    ff = FF // n
    x_width = DI // n
    conv_width = x_width + 2 * NST
    in_w = arrays[13].shape[1]
    gu_w = 2 * ff
    own = model // fsdp_count
    out_rows = (DI + QH * HD + FF) // fsdp_count
    v = pltpu.VMEM
    vm = pl.BlockSpec(memory_space=v)
    return pl.pallas_call(
        partial(backward_kernel, seq_count, fsdp_count),
        out_shape=[
            jax.ShapeDtypeStruct((n, own, in_w), bf),
            jax.ShapeDtypeStruct((n, own, gu_w), bf),
            jax.ShapeDtypeStruct((out_rows, model), bf),
            jax.ShapeDtypeStruct((n, SMALL_ROWS, 128), fl),
            jax.ShapeDtypeStruct((rows, model), fl),
        ],
        in_specs=[vm] * len(arrays),
        out_specs=[vm] * 5,
        scratch_shapes=[
            v((fsdp_count, own, in_w), bf),
            v((fsdp_count, own, gu_w), bf),
            v((per, out_rows, model), bf),
            v((SMALL_ROWS, 128), fl),
            v((n, rows, model), fl),
            v((total, in_w), bf),
            v((total, x_width), bf),
            v((total, x_width), fl),
            v((total, NST), bf),
            v((total, NST), bf),
            v((total, x_width), bf),
            v((total, total), fl),
            v((total, total), fl),
            v((total, total), fl),
            v((total, total), fl),
            v((total, total), fl),
            v((total, x_width), fl),
            v((total, conv_width), fl),
            v((total + 8, conv_width), fl),
            v((total, 128), fl),
            v((total, conv_width), fl),
            v((L, own, in_w), bf),
            v((2 * L, own, in_w), bf),
            v((own, in_w), fl),
            v((L, own, gu_w), bf),
            v((2 * L, own, gu_w), bf),
            v((own, gu_w), fl),
            v((per // 2, out_rows, model), bf),
            v((2, per // 2, out_rows, model), bf),
            v((out_rows // CHUNKS, model), fl),
            v((SMALL_ROWS, 128), fl),
            v((L, SMALL_ROWS, 128), fl),
            v((3, rows, model), bf),
            v((3, rows, model), bf),
            dma(2, L),
            dma(2, 2 * L),
            dma(2, L),
            dma(2, 2 * L),
            dma(2, per // 2, CHUNKS),
            dma(3, per // 2, CHUNKS),
            dma(2, CHUNKS),
            dma(CHUNKS),
            dma(3, L),
            dma(L),
            dma(1),
            dma(1),
            dma(4, 3),
            dma(4, 3),
        ],
        compiler_params=pltpu.CompilerParams(
            collective_id=4, has_side_effects=True, vmem_limit_bytes=VMEM_LIMIT
        ),
        name="backward_fused",
    )(*arrays)


def core_inputs(seg_ids, inputs, params):
    pre_conv, step_raw, query_in, key_in = inputs
    taps, tap_bias, step_bias, log_decay = params
    row_count = pre_conv.shape[0]
    tap_count = taps.shape[0]
    accum = tap_bias[None, :] + taps[tap_count - 1][None, :] * pre_conv
    for lag_step in range(1, tap_count):
        moved = jnp.concatenate(
            [
                jnp.zeros((lag_step, pre_conv.shape[1]), pre_conv.dtype),
                pre_conv[: row_count - lag_step],
            ],
            axis=0,
        )
        prior = jnp.concatenate(
            [jnp.full((lag_step,), -1, jnp.int32), seg_ids[: row_count - lag_step]]
        )
        same_seq = (prior == seg_ids)[:, None]
        accum = accum + taps[tap_count - 1 - lag_step][None, :] * jnp.where(same_seq, moved, 0.0)
    activated = jax.nn.silu(accum)
    step = jax.nn.softplus(step_raw + step_bias[None, :])
    log_step = -jnp.exp(log_decay)[None, :] * step
    positions = jnp.arange(row_count, dtype=jnp.int32)
    first_count = jnp.sum((seg_ids == 0).astype(jnp.int32))
    place = (positions - jnp.where(seg_ids == 0, 0, first_count)).astype(jnp.float32)
    half = HD // 2
    freqs = jnp.exp(-math.log(ROPE_THETA) * 2.0 * jnp.arange(half, dtype=jnp.float32) / HD)
    angles = place[:, None] * freqs[None, :]
    cosine = jnp.cos(angles)[:, None, :]
    sine = jnp.sin(angles)[:, None, :]

    def rotate(tensor):
        heads = tensor.reshape(row_count, -1, HD)
        first_half = heads[..., :half]
        second_half = heads[..., half:]
        return jnp.concatenate(
            [first_half * cosine - second_half * sine, second_half * cosine + first_half * sine],
            axis=-1,
        ).reshape(tensor.shape)

    return activated, step, log_step, rotate(query_in), rotate(key_in)


def shards(
    hidden_in,
    grad_out,
    segments,
    norm_gain,
    mamba_in,
    step_in,
    attn_in,
    conv_taps,
    conv_bias,
    step_bias,
    log_decay,
    skip_gain,
    gated_gain,
    mamba_out,
    attn_out,
    ffn_gain,
    gate_up,
    down_proj,
):
    bf_type = jnp.bfloat16
    fl_type = jnp.float32
    seq_count = lax.axis_size("seq")
    seq_index = lax.axis_index("seq")
    fsdp_count = lax.axis_size("fsdp")
    block_rows = hidden_in.shape[1]
    model = hidden_in.shape[2]
    rows = block_rows * seq_count
    own_rows = model // fsdp_count
    x_width = DI // seq_count
    head_share = MH // seq_count
    query_width = QH * HD // seq_count
    query_share = QH // seq_count
    ff_width = FF // seq_count
    owners = [group * KVH // seq_count for group in range(seq_count)]
    owner = seq_index * KVH // seq_count
    gain_own = DI // fsdp_count
    gain_cols = -(-gain_own // own_rows)

    def cols(array, start, size):
        return lax.dynamic_slice_in_dim(array, start, size, 1)

    gain_pad = jnp.pad(gated_gain, (0, gain_cols * own_rows - gain_own))
    main_width = 2 * x_width + 2 * NST + query_width + 2 * HD
    pad_width = 128 - head_share - 2 - gain_cols
    small_pack = jnp.concatenate(
        [
            cols(attn_in, QH * HD + owner * HD, HD),
            cols(attn_in, (QH + KVH) * HD + owner * HD, HD),
            cols(step_in, seq_index * head_share, head_share),
            norm_gain[:, None],
            ffn_gain[:, None],
            gain_pad.reshape(gain_cols, own_rows).T,
            jnp.zeros((own_rows, pad_width), bf_type),
        ],
        axis=1,
    )
    out_pack = jnp.concatenate([mamba_out, attn_out, down_proj], axis=0)
    w_in, w_gate_up, w_out, hidden_all, cot_all = gather_all(
        seq_count,
        fsdp_count,
        (x_width, query_width, ff_width),
        (hidden_in[0], grad_out[0], mamba_in, attn_in, small_pack, gate_up, out_pack),
    )
    per = fsdp_count // seq_count
    in_all = w_in.reshape(model, -1)
    w_gate_up = w_gate_up.reshape(model, -1)
    hidden_all = hidden_all.reshape(rows, model)
    attn_own = QH * HD // fsdp_count
    ff_own = FF // fsdp_count
    w_mamba_out = w_out[:, :gain_own].reshape(x_width, model)
    w_attn_out = w_out[:, gain_own : gain_own + attn_own].reshape(query_width, model)
    w_down = w_out[:, gain_own + attn_own :].reshape(ff_width, model)
    gain_at = main_width + head_share
    first_gain = in_all[:, gain_at].astype(fl_type)
    second_gain = in_all[:, gain_at + 1].astype(fl_type)
    gated_gains = (
        in_all[:, gain_at + 2 : gain_at + 2 + gain_cols]
        .reshape(fsdp_count, own_rows, gain_cols)
        .transpose(0, 2, 1)
        .reshape(fsdp_count, gain_cols * own_rows)[:, :gain_own]
        .reshape(DI)
    )
    mixer_gain = lax.dynamic_slice_in_dim(gated_gains, seq_index * x_width, x_width, 0).astype(
        fl_type
    )

    res_all = hidden_all.astype(fl_type)
    normed = (res_all * rms_scale(res_all) * first_gain).astype(bf_type)
    projected = jnp.dot(normed, in_all, preferred_element_type=fl_type)
    gate_raw = projected[:, :x_width]
    inputs_b = projected[:, x_width:].astype(bf_type).astype(fl_type)
    conv_width = x_width + 2 * NST
    conv_in = inputs_b[:, :conv_width]
    query_in = inputs_b[:, conv_width : conv_width + query_width]
    key_in = inputs_b[:, conv_width + query_width : conv_width + query_width + HD]
    value_b = inputs_b[:, conv_width + query_width + HD : conv_width + query_width + 2 * HD].astype(
        bf_type
    )
    step_at = conv_width + query_width + 2 * HD
    step_raw = inputs_b[:, step_at : step_at + head_share]
    seg_ids = segments[0]
    taps = jnp.concatenate(
        [cols(conv_taps, seq_index * x_width, x_width), conv_taps[:, DI:]], axis=1
    )
    tap_bias = jnp.concatenate(
        [lax.dynamic_slice_in_dim(conv_bias, seq_index * x_width, x_width, 0), conv_bias[DI:]]
    )
    params = (
        taps,
        tap_bias,
        lax.dynamic_slice_in_dim(step_bias, seq_index * head_share, head_share, 0),
        lax.dynamic_slice_in_dim(log_decay, seq_index * head_share, head_share, 0),
    )
    skip = lax.dynamic_slice_in_dim(skip_gain, seq_index * head_share, head_share, 0)
    (activated, step, log_step, queries, keys), pull_back = jax.vjp(
        partial(core_inputs, seg_ids), (conv_in, step_raw, query_in, key_in), params
    )
    positions = jnp.arange(rows, dtype=jnp.int32)
    causal = positions[:, None] >= positions[None, :]
    mask = causal & (seg_ids[:, None] == seg_ids[None, :])
    highest = lax.Precision.HIGHEST
    x_all = activated[:, :x_width]
    b_mat = activated[:, x_width : x_width + NST].astype(bf_type)
    c_mat = activated[:, x_width + NST :].astype(bf_type)
    x_heads = x_all.reshape(rows, head_share, HD).transpose(1, 0, 2)
    step_t = step.T
    cum_t = jnp.dot(log_step.T, causal.T.astype(fl_type), precision=highest)
    inner = jnp.einsum("tn,pn->tp", c_mat, b_mat, preferred_element_type=fl_type)
    decay = jnp.exp(jnp.where(mask[None], cum_t[:, :, None] - cum_t[:, None, :], -1e30))
    kernel_b = (inner[None] * decay).astype(bf_type)
    x_step = (x_heads * step_t[:, :, None]).astype(bf_type)
    scan_y = jnp.einsum("htp,hpd->htd", kernel_b, x_step, preferred_element_type=fl_type)
    ssm = scan_y + skip[:, None, None] * x_heads
    scan_float = (
        ssm.astype(bf_type).transpose(1, 0, 2).reshape(rows, x_width).astype(fl_type)
    )
    key_b = keys.astype(bf_type)
    q_heads = queries.reshape(rows, query_share, HD).transpose(1, 0, 2)
    scores = jnp.einsum("hid,jd->hij", q_heads, keys, precision=highest) * (1.0 / math.sqrt(HD))
    weights = jnp.exp(jnp.where(mask[None], scores, -1e30))
    weights = weights / jnp.sum(weights, axis=-1, keepdims=True)
    weights_b = weights.astype(bf_type)
    attended = jnp.einsum("hij,jd->hid", weights_b, value_b, preferred_element_type=fl_type)
    attn_mix = attended.astype(bf_type).transpose(1, 0, 2).reshape(rows, query_width)

    gate_act = jax.nn.silu(gate_raw)
    gated = scan_float * gate_act
    (
        layer_out,
        d_mixed,
        ffn_in,
        ffn_act,
        d_ffn,
        d_mixed_b,
        gated_b,
        d_gated,
        d_attn,
        g_ffn_gain,
        g_gated_gain,
    ) = middle(
        seq_count,
        fsdp_count,
        (
            gated.reshape(seq_count, block_rows, x_width),
            attn_mix.reshape(seq_count, block_rows, query_width),
            w_mamba_out,
            w_attn_out,
            w_down,
            w_gate_up,
            hidden_in[0],
            grad_out[0],
            cot_all,
            mixer_gain[None],
            second_gain[None],
        ),
    )
    ffn_in = ffn_in.reshape(rows, model)
    ffn_act = ffn_act.reshape(rows, ff_width)
    d_ffn = d_ffn.reshape(rows, 2 * ff_width)
    d_mixed_b = d_mixed_b.reshape(rows, model)
    gated_b = gated_b.reshape(rows, x_width)
    d_gated = d_gated.reshape(rows, x_width)
    d_attn = d_attn.reshape(rows, query_width)
    cot_rows = cot_all.reshape(rows, model)
    g_down = jnp.einsum("tf,td->fd", ffn_act, cot_rows, preferred_element_type=fl_type)
    g_gate_up = jnp.einsum("td,tf->df", ffn_in, d_ffn, preferred_element_type=fl_type)
    g_attn_out = jnp.einsum("tq,td->qd", attn_mix, d_mixed_b, preferred_element_type=fl_type)
    g_mamba_out = jnp.einsum("ti,td->id", gated_b, d_mixed_b, preferred_element_type=fl_type)
    d_scan = (d_gated * gate_act).astype(bf_type)
    d_gate_raw = d_gated * scan_float * swish_slope(gate_raw)
    g_out = jnp.concatenate(
        [
            g_mamba_out.astype(bf_type).reshape(per, gain_own, model),
            g_attn_out.astype(bf_type).reshape(per, attn_own, model),
            g_down.astype(bf_type).reshape(per, ff_own, model),
        ],
        axis=1,
    )

    d_att = d_attn.astype(bf_type).reshape(rows, query_share, HD).transpose(1, 0, 2)
    d_weights = jnp.einsum("hid,jd->hij", d_att, value_b, preferred_element_type=fl_type)
    inner_sum = jnp.sum(d_att.astype(fl_type) * attended, axis=-1, keepdims=True)
    d_scores = (weights * (d_weights - inner_sum) * (1.0 / math.sqrt(HD))).astype(bf_type)
    d_queries = jnp.einsum("hij,jd->hid", d_scores, key_b, preferred_element_type=fl_type)
    d_keys = jnp.einsum(
        "hij,hid->jd", d_scores, q_heads.astype(bf_type), preferred_element_type=fl_type
    )
    d_value = jnp.einsum("hij,hid->jd", weights_b, d_att, preferred_element_type=fl_type)
    d_y = d_scan.reshape(rows, head_share, HD).transpose(1, 0, 2)
    d_y_float = d_y.astype(fl_type)
    d_kernel = jnp.einsum("htd,hpd->htp", d_y, x_step, preferred_element_type=fl_type)
    d_inner = jnp.sum(d_kernel * decay, axis=0).astype(bf_type)
    d_x_step = jnp.einsum("htp,htd->hpd", kernel_b, d_y, preferred_element_type=fl_type)
    d_c = jnp.dot(d_inner, b_mat, preferred_element_type=fl_type)
    d_b = jnp.einsum("tp,tn->pn", d_inner, c_mat, preferred_element_type=fl_type)
    d_x = step_t[:, :, None] * d_x_step + skip[:, None, None] * d_y_float
    g_skip = jnp.sum(d_y_float * x_heads, axis=(1, 2))
    d_step_direct = jnp.sum(x_heads * d_x_step, axis=-1)
    d_cum = jnp.sum(d_y_float * scan_y, axis=-1) - jnp.sum(
        x_step.astype(fl_type) * d_x_step, axis=-1
    )
    d_log_step = jnp.dot(d_cum, causal.astype(fl_type), precision=highest)
    (d_conv, d_step, d_query, d_key), grad_params = pull_back(
        (
            jnp.concatenate([d_x.transpose(1, 0, 2).reshape(rows, x_width), d_b, d_c], axis=1),
            d_step_direct.T,
            d_log_step.T,
            d_queries.transpose(1, 0, 2).reshape(rows, query_width),
            d_keys,
        )
    )
    d_in = jnp.concatenate(
        [
            d_gate_raw,
            d_conv,
            d_query,
            d_key,
            d_value,
            d_step,
            jnp.zeros((rows, 128 - head_share), fl_type),
        ],
        axis=1,
    ).astype(bf_type)
    g_in = jnp.einsum("td,tc->dc", normed, d_in, preferred_element_type=fl_type)
    d_normed_part = jnp.einsum("tc,dc->td", d_in, in_all, preferred_element_type=fl_type)
    first_norm_all = res_all * rms_scale(res_all)
    g_norm_gain = jnp.sum(d_normed_part * first_norm_all, axis=0)
    taps_bias = jnp.concatenate([grad_params[0], grad_params[1][None]], axis=0)
    small_parts = [
        taps_bias.reshape(-1),
        g_gated_gain.reshape(-1),
        g_norm_gain,
        g_ffn_gain.reshape(-1),
        grad_params[2],
        grad_params[3],
        g_skip,
    ]
    small_size = sum(part.shape[0] for part in small_parts)
    small_rows = -(-small_size // 1024) * 8
    small = jnp.concatenate(
        small_parts + [jnp.zeros((small_rows * 128 - small_size,), fl_type)]
    ).reshape(small_rows, 128)
    in_grads, gu_grads, out_grads, small_all, d_normed = reduce_all(
        seq_count,
        fsdp_count,
        (
            g_in.astype(bf_type).reshape(fsdp_count, own_rows, -1),
            g_gate_up.astype(bf_type).reshape(fsdp_count, own_rows, -1),
            g_out,
            small,
            d_normed_part.astype(bf_type).reshape(seq_count, block_rows, model),
        ),
    )
    in_grads = in_grads.astype(fl_type)
    gu_grads = gu_grads.astype(fl_type)
    out_grads = out_grads.astype(fl_type)
    residual = hidden_in[0].astype(fl_type)
    first_scale = rms_scale(residual)
    first_norm = residual * first_scale
    d_first = d_normed * first_gain
    grad_tok = d_mixed + first_scale * (
        d_first - first_norm * jnp.mean(d_first * first_norm, axis=-1, keepdims=True)
    )

    conv_width = x_width + 2 * NST
    small_all = small_all.reshape(seq_count, -1)
    at = (KC + 1) * conv_width
    taps_all = small_all[:, :at].reshape(seq_count, KC + 1, conv_width)
    taps_sum = jnp.concatenate(
        [taps_all[group, :, :x_width] for group in range(seq_count)]
        + [jnp.sum(taps_all[:, :, x_width:], axis=0)],
        axis=1,
    )
    fsdp_index = lax.axis_index("fsdp")
    gated_sum = lax.dynamic_slice_in_dim(
        small_all[:, at : at + x_width].reshape(-1), fsdp_index * gain_own, gain_own, 0
    )
    at = at + x_width
    gains_sum = jnp.sum(small_all[:, at : at + 2 * model], axis=0)
    norm_sum = lax.dynamic_slice_in_dim(gains_sum, fsdp_index * own_rows, own_rows, 0)
    ffn_gain_sum = lax.dynamic_slice_in_dim(gains_sum, model + fsdp_index * own_rows, own_rows, 0)
    at = at + 2 * model
    heads_sum = (
        small_all[:, at : at + 3 * head_share]
        .reshape(seq_count, 3, head_share)
        .transpose(1, 0, 2)
        .reshape(3, MH)
    )

    def side(array):
        return jnp.concatenate([array[group] for group in range(seq_count)], axis=1)

    def owned(start):
        slots = []
        for kv_head in range(KVH):
            users = [group for group in range(seq_count) if owners[group] == kv_head]
            total = in_grads[users[0]][:, start : start + HD]
            for group in users[1:]:
                total = total + in_grads[group][:, start : start + HD]
            slots.append(total)
        return slots

    q_at = 2 * x_width + 2 * NST
    grad_mamba_in = jnp.concatenate(
        [
            side(in_grads[:, :, :x_width]),
            side(in_grads[:, :, x_width : 2 * x_width]),
            jnp.sum(in_grads[:, :, 2 * x_width : q_at], axis=0),
        ],
        axis=1,
    )
    k_at = q_at + query_width
    grad_attn_in = jnp.concatenate(
        [side(in_grads[:, :, q_at:k_at])] + owned(k_at) + owned(k_at + HD), axis=1
    )
    grad_step_in = side(in_grads[:, :, main_width : main_width + head_share])
    grad_gate_up = jnp.concatenate(
        [side(gu_grads[:, :, :ff_width]), side(gu_grads[:, :, ff_width:])], axis=1
    )
    return (
        layer_out[None],
        grad_tok[None],
        norm_sum,
        grad_mamba_in,
        grad_step_in,
        grad_attn_in,
        taps_sum[:KC],
        taps_sum[KC],
        heads_sum[0],
        heads_sum[1],
        heads_sum[2],
        gated_sum,
        out_grads[:gain_own],
        out_grads[gain_own : gain_own + attn_own],
        ffn_gain_sum,
        grad_gate_up,
        out_grads[gain_own + attn_own :],
    )


def unpack_kernel(
    x_width, query_width, ff, gain_own, attn_own, in_got, gu_got, out_got, tok, layer, g_mi, g_si, g_ai, g_gu, g_mo, g_ao, g_dn, tok_out, layer_out
):
    tok_out[...] = tok[...]
    layer_out[...] = layer[...]
    fl = jnp.float32
    bc_at, q_at = 2 * x_width, 2 * x_width + 2 * NST
    kv_at = q_at + query_width
    count = in_got.shape[0]
    users = count // KVH
    head_share = x_width // HD
    for g in range(count):
        g_mi[:, g * x_width : (g + 1) * x_width] = in_got[g, :, :x_width].astype(fl)
        g_mi[:, DI + g * x_width : DI + (g + 1) * x_width] = in_got[g, :, x_width:bc_at].astype(fl)
        g_ai[:, g * query_width : (g + 1) * query_width] = in_got[g, :, q_at:kv_at].astype(fl)
        g_gu[:, g * ff : (g + 1) * ff] = gu_got[g, :, :ff].astype(fl)
        g_gu[:, FF + g * ff : FF + (g + 1) * ff] = gu_got[g, :, ff:].astype(fl)
    g_mi[:, 2 * DI :] = sum(in_got[g, :, bc_at:q_at].astype(fl) for g in range(count))
    pairs = [
        sum(in_got[g, :, kv_at : kv_at + 2 * HD].astype(fl) for g in range(k * users, (k + 1) * users))
        for k in range(KVH)
    ]
    lane = iota2(pairs[0].shape, 1)
    keys = jnp.where(lane < HD, pairs[0], pltpu.roll(pairs[1], HD, 1))
    values = jnp.where(lane < HD, pltpu.roll(pairs[0], HD, 1), pairs[1])
    g_ai[:, QH * HD : (QH + KVH) * HD] = keys
    g_ai[:, (QH + KVH) * HD :] = values
    steps = in_got[0, :, kv_at + 2 * HD :].astype(fl)
    for g in range(1, count):
        moved = pltpu.roll(in_got[g, :, kv_at + 2 * HD :].astype(fl), g * head_share, 1)
        steps = jnp.where(lane >= g * head_share, moved, steps)
    g_si[...] = steps[:, :MH]
    g_mo[...] = out_got[:gain_own].astype(fl)
    g_ao[...] = out_got[gain_own : gain_own + attn_own].astype(fl)
    g_dn[...] = out_got[gain_own + attn_own :].astype(fl)


def unpack(widths, owns, arrays):
    own, model = arrays[0].shape[1], arrays[2].shape[1]
    gain_own, attn_own, ff_own = owns
    vm = pl.BlockSpec(memory_space=pltpu.VMEM)
    shapes = [
        (own, 2 * DI + 2 * NST),
        (own, MH),
        (own, (QH + 2 * KVH) * HD),
        (own, 2 * FF),
        (gain_own, model),
        (attn_own, model),
        (ff_own, model),
    ]
    return pl.pallas_call(
        partial(unpack_kernel, *widths, gain_own, attn_own),
        out_shape=[jax.ShapeDtypeStruct(shape, jnp.float32) for shape in shapes]
        + [jax.ShapeDtypeStruct(array.shape, array.dtype) for array in arrays[3:]],
        in_specs=[vm] * 5,
        out_specs=[vm] * 9,
        compiler_params=pltpu.CompilerParams(vmem_limit_bytes=VMEM_LIMIT),
        name="unpack_grads",
    )(*arrays)


def fused_shards(
    hidden_in,
    grad_out,
    segments,
    norm_gain,
    mamba_in,
    step_in,
    attn_in,
    conv_taps,
    conv_bias,
    step_bias,
    log_decay,
    skip_gain,
    gated_gain,
    mamba_out,
    attn_out,
    ffn_gain,
    gate_up,
    down_proj,
):
    bf_type = jnp.bfloat16
    fl_type = jnp.float32
    seq_count = lax.axis_size("seq")
    seq_index = lax.axis_index("seq")
    fsdp_count = lax.axis_size("fsdp")
    block_rows = hidden_in.shape[1]
    model = hidden_in.shape[2]
    rows = block_rows * seq_count
    own_rows = model // fsdp_count
    x_width = DI // seq_count
    head_share = MH // seq_count
    query_width = QH * HD // seq_count
    ff_width = FF // seq_count
    owner = seq_index * KVH // seq_count
    gain_own = DI // fsdp_count
    attn_own = QH * HD // fsdp_count

    def cols(array, start, size):
        return lax.dynamic_slice_in_dim(array, start, size, 1)

    small_pack = jnp.concatenate(
        [
            cols(attn_in, QH * HD + owner * HD, HD),
            cols(attn_in, (QH + KVH) * HD + owner * HD, HD),
            cols(step_in, seq_index * head_share, head_share),
            norm_gain[:, None],
            ffn_gain[:, None],
            jnp.zeros((own_rows, 126 - head_share), bf_type),
        ],
        axis=1,
    )
    gain_in = jnp.pad(gated_gain[:, None], ((0, 0), (0, 127)))
    all_heads = jnp.pad(jnp.stack([step_bias, log_decay, skip_gain]), ((0, 5), (0, 128 - MH)))
    (
        layer_out,
        d_mixed,
        ffn_in,
        ffn_act,
        d_ffn,
        d_mixed_all,
        gated_b,
        d_gated,
        d_attn,
        g_ffn_gain,
        g_gated_gain,
        cot_all,
        in_all,
        normed,
        gate_raw,
        inputs_b,
        accum,
        scan_bf,
        scan_y,
        steps,
        cum,
        attn_mix,
        gain_rows,
        seg_col,
        place,
        cosine,
        sine,
        taps,
        heads,
    ) = forward_all(
        seq_count,
        fsdp_count,
        (x_width, query_width, ff_width),
        (
            hidden_in[0],
            grad_out[0],
            mamba_in,
            attn_in,
            small_pack,
            gate_up,
            mamba_out,
            attn_out,
            down_proj,
            gain_in,
            segments,
            conv_taps,
            conv_bias[None],
            all_heads,
        ),
    )

    def flat(array):
        return array.reshape(rows, -1)

    in_grads, gu_grads, out_grads, small_all, grad_tok = backward_all(
        seq_count,
        fsdp_count,
        (
            hidden_in[0],
            d_mixed,
            flat(d_mixed_all),
            flat(cot_all),
            flat(ffn_in),
            flat(ffn_act),
            flat(d_ffn),
            flat(gated_b),
            flat(attn_mix),
            flat(d_gated),
            flat(d_attn),
            g_ffn_gain,
            g_gated_gain,
            in_all,
            normed,
            gate_raw,
            inputs_b,
            accum,
            scan_bf,
            scan_y,
            steps,
            cum,
            gain_rows,
            seg_col,
            segments,
            place,
            cosine,
            sine,
            taps,
            heads,
        ),
    )
    (
        grad_mamba_in,
        grad_step_in,
        grad_attn_in,
        grad_gate_up,
        grad_mo,
        grad_ao,
        grad_dn,
        grad_tok,
        layer_out,
    ) = unpack(
        (x_width, query_width, ff_width),
        (gain_own, attn_own, FF // fsdp_count),
        (in_grads, gu_grads, out_grads, grad_tok, layer_out),
    )
    conv_width = x_width + 2 * NST
    at = (KC + 1) * conv_width // 128
    taps_all = small_all[:, :at].reshape(seq_count, KC + 1, conv_width)
    taps_sum = jnp.concatenate(
        [taps_all[group, :, :x_width] for group in range(seq_count)]
        + [jnp.sum(taps_all[:, :, x_width:], axis=0)],
        axis=1,
    )
    fsdp_index = lax.axis_index("fsdp")
    gated_sum = lax.dynamic_slice_in_dim(
        small_all[:, at : at + x_width // 128].reshape(-1), fsdp_index * gain_own, gain_own, 0
    )
    at = at + x_width // 128
    gains_sum = jnp.sum(small_all[:, at : at + 2 * model // 128], axis=0).reshape(-1)
    norm_sum = lax.dynamic_slice_in_dim(gains_sum, fsdp_index * own_rows, own_rows, 0)
    at = at + model // 128
    ffn_gain_sum = lax.dynamic_slice_in_dim(
        gains_sum, model + fsdp_index * own_rows, own_rows, 0
    )
    at = at + model // 128
    heads_sum = small_all[:, at : at + 3, :head_share].transpose(1, 0, 2).reshape(3, MH)
    return (
        layer_out[None],
        grad_tok[None],
        norm_sum,
        grad_mamba_in,
        grad_step_in,
        grad_attn_in,
        taps_sum[:KC],
        taps_sum[KC],
        heads_sum[0],
        heads_sum[1],
        heads_sum[2],
        gated_sum,
        grad_mo,
        grad_ao,
        ffn_gain_sum,
        grad_gate_up,
        grad_dn,
    )


def solution(mesh):
    placed = (
        P("fsdp", "seq", None),
        P("fsdp", "seq", None),
        P("fsdp", None),
        P("fsdp"),
        P("fsdp", None),
        P("fsdp", None),
        P("fsdp", None),
        P(),
        P(),
        P(),
        P(),
        P(),
        P("fsdp"),
        P("fsdp", None),
        P("fsdp", None),
        P("fsdp"),
        P("fsdp", None),
        P("fsdp", None),
    )
    fsdp_count = mesh.shape["fsdp"]
    whole_tiles = all(
        width % (16 * fsdp_count) == 0 for width in (DI // 2, QH * HD // 2, FF // 2)
    )
    return jax.shard_map(
        fused_shards if whole_tiles else shards,
        mesh=mesh,
        in_specs=placed,
        out_specs=(
            P("fsdp", "seq", None),
            P("fsdp", "seq", None),
            P("fsdp"),
            P("fsdp", None),
            P("fsdp", None),
            P("fsdp", None),
            P(),
            P(),
            P(),
            P(),
            P(),
            P("fsdp"),
            P("fsdp", None),
            P("fsdp", None),
            P("fsdp"),
            P("fsdp", None),
            P("fsdp", None),
        ),
        check_vma=False,
    )
```

```python
from functools import partial
import math

import jax
import jax.numpy as jnp
from jax import lax
from jax.experimental import pallas as pl
from jax.experimental.pallas import tpu as pltpu
from jax.sharding import PartitionSpec as P

MH = 24
HD = 64
NST = 128
KC = 4
QH = 8
KVH = 2
FF = 2048
DI = 1536


EPS = 1e-05
ROPE_THETA = 10000.0

MESH = pl.DeviceIdType.MESH
VMEM_LIMIT = 62 * 2**20
HIGHEST = lax.Precision.HIGHEST


def rcopy(src, dst, send, recv, device):
    return pltpu.make_async_remote_copy(
        src_ref=src,
        dst_ref=dst,
        send_sem=send,
        recv_sem=recv,
        device_id=device,
        device_id_type=MESH,
    )


class Place:
    def __init__(self, seq_count, fsdp_count):
        self.s = lax.axis_index("seq")
        self.f = lax.axis_index("fsdp")
        self.count = fsdp_count
        self.L = fsdp_count // 2
        self.z = self.f // 2
        self.y = self.f % 2
        self.has_right = self.z < self.L - 1
        self.has_left = self.z > 0
        self.right = (self.s, jnp.minimum(self.f + 2, fsdp_count - 1))
        self.left = (self.s, jnp.maximum(self.f - 2, 0))
        self.pair = (self.s, self.f + 1 - 2 * self.y)
        self.s1 = self.s + 1 - 2 * (self.s % 2)
        self.s2 = (self.s + 2) % 4
        self.s3 = 3 - self.s
        self.sib = (self.s1, self.f)
        self.across = (self.s2, self.f)
        self.diag = (self.s3, self.f)

    def greet(self, line=True, pair=True, diag=False):
        barrier = pltpu.get_barrier_semaphore()

        def hello(device):
            pl.semaphore_signal(barrier, inc=1, device_id=device, device_id_type=MESH)

        amount = 2
        hello(self.sib)
        hello(self.across)
        if diag:
            hello(self.diag)
            amount = amount + 1
        if pair:
            hello(self.pair)
            amount = amount + 1
        if line:

            @pl.when(self.has_right)
            def _():
                hello(self.right)

            @pl.when(self.has_left)
            def _():
                hello(self.left)

            amount = amount + jnp.where(self.has_right, 1, 0) + jnp.where(self.has_left, 1, 0)
        pl.semaphore_wait(barrier, amount)


class SeqGather:
    def __init__(self, place, src, out, send, recv):
        p = place
        self.own_sib = rcopy(src, out.at[p.s], send.at[0], recv.at[0], p.sib)
        self.own_across = rcopy(src, out.at[p.s], send.at[1], recv.at[1], p.across)
        self.forward_copy = rcopy(out.at[p.s2], out.at[p.s2], send.at[2], recv.at[2], p.sib)
        self.got_sib = rcopy(src, out.at[p.s1], send.at[0], recv.at[0], p.sib)
        self.got_across = rcopy(src, out.at[p.s2], send.at[1], recv.at[1], p.across)
        self.got_diag = rcopy(src, out.at[p.s3], send.at[2], recv.at[2], p.sib)

    def start(self):
        self.own_across.start()
        self.own_sib.start()

    def wait_sib(self):
        self.got_sib.wait_recv()

    def forward(self):
        self.got_across.wait_recv()
        self.forward_copy.start()

    def wait_diag(self):
        self.got_diag.wait_recv()

    def wait_sends(self):
        self.own_sib.wait_send()
        self.own_across.wait_send()
        self.forward_copy.wait_send()

    def finish(self):
        self.wait_sib()
        self.wait_diag()
        self.wait_sends()


class SeqReduce:
    def __init__(self, place, stage, got, send, recv):
        p = place
        self.stage, self.got = stage, got
        self.copies = [
            rcopy(stage.at[0], got.at[0], send.at[0], recv.at[0], p.sib),
            rcopy(stage.at[1], got.at[1], send.at[1], recv.at[1], p.sib),
            rcopy(stage.at[2], got.at[2], send.at[2], recv.at[2], p.across),
        ]

    def send_diag(self, value):
        self.stage[0] = value.astype(self.stage.dtype)
        self.copies[0].start()

    def send_sib(self, value):
        self.stage[1] = value.astype(self.stage.dtype)
        self.copies[1].start()

    def send_across(self, value):
        self.copies[0].wait_recv()
        self.stage[2] = (value + self.got[0].astype(jnp.float32)).astype(self.stage.dtype)
        self.copies[2].start()

    def total(self, value):
        self.copies[1].wait_recv()
        self.copies[2].wait_recv()
        return value + self.got[1].astype(jnp.float32) + self.got[2].astype(jnp.float32)

    def wait_sends(self):
        for copy in self.copies:
            copy.wait_send()


class LineGather:
    def __init__(self, place, out, send, recv, pair=True, size=0):
        self.p, self.out, self.send, self.recv, self.pair = place, out, send, recv, pair
        self.size = size

    def block(self, index):
        if self.size:
            return self.out.at[pl.ds(pl.multiple_of(index * self.size, self.size), self.size)]
        return self.out.at[index]

    def at(self, b, other=0):
        p = self.p
        if not self.pair:
            return b
        return 2 * b + (1 - p.y if other else p.y)

    def copy(self, b, way):
        p = self.p
        ref = self.block(self.at(b))
        device = (p.right, p.left, p.pair)[way]
        return rcopy(ref, ref, self.send.at[way, b], self.recv.at[self.at(b)], device)

    def push(self, b, right, left):
        if right:

            @pl.when(self.p.has_right)
            def _():
                self.copy(b, 0).start()

        if left:

            @pl.when(self.p.has_left)
            def _():
                self.copy(b, 1).start()

        if self.pair:
            self.copy(b, 2).start()

    def start(self):
        self.push(self.p.z, True, True)

    def step(self, d):
        p = self.p

        @pl.when(p.z - d >= 0)
        def _():
            self.copy(p.z - d, 0).wait_recv()
            self.push(p.z - d, True, False)

        @pl.when(p.z + d <= p.L - 1)
        def _():
            self.copy(p.z + d, 0).wait_recv()
            self.push(p.z + d, False, True)

    def finish(self):
        p = self.p

        def each(b, carry):
            if self.pair:
                ref = self.block(self.at(b, 1))
                rcopy(ref, ref, self.send.at[2, b], self.recv.at[self.at(b, 1)], p.pair).wait_recv()
                self.copy(b, 2).wait_send()

            @pl.when(p.has_right & (b <= p.z))
            def _():
                self.copy(b, 0).wait_send()

            @pl.when(p.has_left & (b >= p.z))
            def _():
                self.copy(b, 1).wait_send()

            return carry

        lax.fori_loop(0, p.L, each, 0)


def loop(count, body):
    def step(index, carry):
        body(index)
        return carry

    lax.fori_loop(0, count, step, 0)


def add_rows(target, *parts):
    def some(index):
        at = pl.ds(pl.multiple_of(index * 16, 16), 16)
        total = parts[0][at].astype(jnp.float32)
        for part in parts[1:]:
            total = total + part[at].astype(jnp.float32)
        target[at] = total.astype(target.dtype)

    loop(target.shape[0] // 16, some)


CHUNKS = 4


def gather_kernel(
    seq_count,
    fsdp_count,
    x_width,
    query_width,
    ff_width,
    hidden,
    cot,
    mamba_in,
    attn_in,
    small,
    gate_up,
    out_pack,
    w_in,
    w_gu,
    w_out,
    hidden_all,
    cot_all,
    local,
    in_send,
    in_recv,
    gu_send,
    gu_recv,
    out_send,
    out_recv,
    hid_send,
    hid_recv,
    cot_send,
    cot_recv,
):
    p = Place(seq_count, fsdp_count)
    s, f, z, y, L = p.s, p.f, p.z, p.y, p.L
    per = fsdp_count // seq_count
    half = per // 2

    def part(ref, start, size, unit):
        return ref.at[:, pl.ds(pl.multiple_of(start, unit), size)]

    bc = mamba_in.shape[1] - 2 * DI
    copies = []

    def bring(src, dst):
        copy = pltpu.make_async_copy(src, dst, local.at[len(copies)])
        copy.start()
        copies.append(copy)

    own = w_in.at[f]
    c0 = 0
    bring(part(mamba_in, s * x_width, x_width, 128), own.at[:, pl.ds(c0, x_width)])
    c0 += x_width
    bring(part(mamba_in, DI + s * x_width, x_width, 128), own.at[:, pl.ds(c0, x_width)])
    c0 += x_width
    bring(mamba_in.at[:, pl.ds(2 * DI, bc)], own.at[:, pl.ds(c0, bc)])
    c0 += bc
    bring(part(attn_in, s * query_width, query_width, 128), own.at[:, pl.ds(c0, query_width)])
    c0 += query_width
    bring(small, own.at[:, pl.ds(c0, small.shape[1])])
    own = w_gu.at[f]
    bring(part(gate_up, s * ff_width, ff_width, 128), own.at[:, pl.ds(0, ff_width)])
    bring(part(gate_up, FF + s * ff_width, ff_width, 128), own.at[:, pl.ds(ff_width, ff_width)])
    bring(hidden, hidden_all.at[s])
    bring(cot, cot_all.at[s])
    holder = f // per == s
    chunk = w_out.shape[1] // CHUNKS
    out_local = local.at[len(copies)]

    @pl.when(holder)
    def _():
        pltpu.make_async_copy(out_pack, w_out.at[f - s * per], out_local).start()

    p.greet()
    hid = SeqGather(p, hidden, hidden_all, hid_send, hid_recv)
    cots = SeqGather(p, cot, cot_all, cot_send, cot_recv)
    hid.start()
    cots.start()
    for copy in copies:
        copy.wait()

    @pl.when(holder)
    def _():
        pltpu.make_async_copy(out_pack, w_out.at[f - s * per], out_local).wait()

    ins = LineGather(p, w_in, in_send, in_recv)
    gus = LineGather(p, w_gu, gu_send, gu_recv)
    ins.start()
    gus.start()
    hid.forward()
    cots.forward()

    def hop(d):
        ins.step(d + 1)
        gus.step(d + 1)

    loop(L - 1, hop)

    def out_copy(i, c, other, way):
        ref = w_out.at[2 * i + (1 - y if other else y), pl.ds(pl.multiple_of(c * chunk, 16), chunk)]
        device = (p.right, p.left, p.pair)[way]
        return rcopy(ref, ref, out_send.at[way, i, c], out_recv.at[way // 2, i, c], device)

    def spread(index):
        i, c = index // CHUNKS, index % CHUNKS
        zs = s * half + i

        @pl.when(z != zs)
        def _():
            out_copy(i, c, 0, 0).wait_recv()

        @pl.when((z >= zs) & p.has_right)
        def _():
            out_copy(i, c, 0, 0).start()

        @pl.when((z <= zs) & p.has_left)
        def _():
            out_copy(i, c, 0, 1).start()

        out_copy(i, c, 0, 2).start()

    loop(half * CHUNKS, spread)

    def spread_end(index):
        i, c = index // CHUNKS, index % CHUNKS
        zs = s * half + i
        out_copy(i, c, 1, 2).wait_recv()
        out_copy(i, c, 0, 2).wait_send()

        @pl.when((z >= zs) & p.has_right)
        def _():
            out_copy(i, c, 0, 0).wait_send()

        @pl.when((z <= zs) & p.has_left)
        def _():
            out_copy(i, c, 0, 1).wait_send()

    loop(half * CHUNKS, spread_end)
    ins.finish()
    gus.finish()
    hid.finish()
    cots.finish()


def dma(*shape):
    return pltpu.SemaphoreType.DMA(shape)


def gather_all(seq_count, fsdp_count, widths, arrays):
    hidden, cot, mamba_in, attn_in, small, gate_up, out_pack = arrays
    x_width, query_width, ff_width = widths
    own_rows = mamba_in.shape[0]
    per = fsdp_count // seq_count
    bc = mamba_in.shape[1] - 2 * DI
    in_width = 2 * x_width + bc + query_width + small.shape[1]
    bf = jnp.bfloat16
    L = fsdp_count // 2
    return pl.pallas_call(
        partial(gather_kernel, seq_count, fsdp_count, x_width, query_width, ff_width),
        out_shape=[
            jax.ShapeDtypeStruct((fsdp_count, own_rows, in_width), bf),
            jax.ShapeDtypeStruct((fsdp_count, own_rows, 2 * ff_width), bf),
            jax.ShapeDtypeStruct((per,) + out_pack.shape, bf),
            jax.ShapeDtypeStruct((seq_count,) + hidden.shape, bf),
            jax.ShapeDtypeStruct((seq_count,) + cot.shape, bf),
        ],
        in_specs=[pl.BlockSpec(memory_space=pl.ANY)] * 7,
        out_specs=[pl.BlockSpec(memory_space=pl.ANY)] * 5,
        scratch_shapes=[
            dma(10),
            dma(3, L),
            dma(fsdp_count),
            dma(3, L),
            dma(fsdp_count),
            dma(3, per // 2, CHUNKS),
            dma(2, per // 2, CHUNKS),
            dma(3),
            dma(3),
            dma(3),
            dma(3),
        ],
        compiler_params=pltpu.CompilerParams(collective_id=0, has_side_effects=True),
        name="gather_weights",
    )(*arrays)


def mid_kernel(
    seq_count,
    fsdp_count,
    gated,
    attn_mix,
    w_mo,
    w_ao,
    w_dn,
    w_gu,
    hidden,
    cot_own,
    cot_all,
    mixer_gain,
    ffn_gain,
    layer_out,
    d_mixed,
    ffn_in,
    ffn_act,
    d_ffn,
    d_mixed_all,
    gated_b,
    d_gated,
    d_attn,
    g_ffn_gain,
    g_gated_gain,
    part_mix,
    gate_vals,
    d_act,
    d_gn,
    mixed,
    norm2,
    sq_buf,
    mean_buf,
    stage,
    got,
    seq_send,
    seq_recv,
):
    p = Place(seq_count, fsdp_count)
    s = p.s
    fl, bf = jnp.float32, jnp.bfloat16
    rows = cot_own.shape[0]
    model = cot_own.shape[1]
    ff = w_dn.shape[0]
    peers = (p.sib, p.across, p.diag)
    peer_at = (p.s1, p.s2, p.s3)

    def dot(a, b):
        return jnp.dot(a, b, preferred_element_type=fl)

    def dot_t(a, b):
        return lax.dot_general(a, b, (((1,), (1,)), ((), ())), preferred_element_type=fl)

    def row_sums(values):
        ones = jnp.ones((8, values.shape[1]), fl)
        return lax.dot_general(
            ones, values, (((1,), (1,)), ((), ())), preferred_element_type=fl, precision=HIGHEST
        )

    def exchange(buf, at):
        copies = []
        for k in range(3):
            copy = rcopy(buf.at[s], buf.at[s], seq_send.at[at, k], seq_recv.at[at, k], peers[k])
            copy.start()
            got_it = rcopy(
                buf.at[peer_at[k]], buf.at[peer_at[k]], seq_send.at[at, k], seq_recv.at[at, k], peers[k]
            )
            copies.append((copy, got_it))

        def end():
            for copy, got_it in copies:
                got_it.wait_recv()
                copy.wait_send()
            total = buf[0] + buf[1] + buf[2] + buf[3]
            return total

        return end

    for r in range(4):
        values = gated[r]
        sq_buf[s, :, r * rows : (r + 1) * rows] = row_sums(values * values)
    p.greet(line=False, pair=False, diag=True)
    sq_end = exchange(sq_buf, 0)
    gain = mixer_gain[...]
    for r in range(4):
        part_mix[r] = dot((gated[r] * gain).astype(bf), w_mo[...])
    sq_total = sq_end()
    scale_cols = lax.rsqrt(sq_total / DI + EPS).T

    for r in range(4):
        scale = scale_cols[r * rows : (r + 1) * rows, 0:1]
        part_mix[r] = part_mix[r] * scale + dot(attn_mix[r], w_ao[...])
        gated_norm = gated[r] * scale
        gated_b[r] = (gated_norm * gain).astype(bf)

    def reducer(at):
        return SeqReduce(p, stage.at[at], got.at[at], seq_send.at[at + 1], seq_recv.at[at + 1])

    mix = reducer(0)
    mix.send_diag(part_mix[p.s3])
    mix.send_sib(part_mix[p.s1])
    mix.send_across(part_mix[p.s2])
    d_act[0] = dot_t(cot_all[0], w_dn[...])
    d_act[1] = dot_t(cot_all[1], w_dn[...])
    residual = hidden[...].astype(fl)
    mixed[...] = residual + mix.total(part_mix[s])
    scale2 = lax.rsqrt(jnp.mean(mixed[...] * mixed[...], axis=-1, keepdims=True) + EPS)
    norm2[...] = mixed[...] * scale2
    ffn_in[s] = (norm2[...] * ffn_gain[...]).astype(bf)
    ffn_all = SeqGather(p, ffn_in.at[s], ffn_in, seq_send.at[4], seq_recv.at[4])
    ffn_all.start()

    def ffn_block(r):
        gate_vals[r] = dot(ffn_in[r], w_gu[...])

    def act_block(r):
        gate_lin = gate_vals[r, :, :ff]
        up_lin = gate_vals[r, :, ff:]
        sigma = jax.nn.sigmoid(gate_lin)
        act = gate_lin * sigma
        ffn_act[r] = (act * up_lin).astype(bf)
        slope = sigma * (1.0 + gate_lin * (1.0 - sigma))
        da = d_act[r]
        d_ffn[r, :, :ff] = (da * up_lin * slope).astype(bf)
        d_ffn[r, :, ff:] = (da * act).astype(bf)

    d_act[2] = dot_t(cot_all[2], w_dn[...])
    d_act[3] = dot_t(cot_all[3], w_dn[...])
    ffn_block(s)
    act_block(s)
    ffn_all.wait_sib()
    ffn_block(p.s1)
    ffn_all.forward()
    act_block(p.s1)
    ffn_block(p.s2)
    act_block(p.s2)
    ffn_all.wait_diag()
    ffn_block(p.s3)
    act_block(p.s3)
    back = reducer(1)
    back.send_diag(dot_t(d_ffn[p.s3], w_gu[...]))
    back.send_sib(dot_t(d_ffn[p.s1], w_gu[...]))
    back.send_across(dot_t(d_ffn[p.s2], w_gu[...]))
    out = reducer(2)
    d_ffn_own = dot_t(d_ffn[s], w_gu[...])
    d_ffn_in = back.total(d_ffn_own)
    g_ffn_gain[...] = jnp.sum(d_ffn_in * norm2[...], axis=0, keepdims=True)
    d_second = d_ffn_in * ffn_gain[...]
    d_mixed[...] = cot_own[...].astype(fl) + scale2 * (
        d_second - norm2[...] * jnp.mean(d_second * norm2[...], axis=-1, keepdims=True)
    )
    d_mixed_all[s] = d_mixed[...].astype(bf)
    back_all = SeqGather(p, d_mixed_all.at[s], d_mixed_all, seq_send.at[5], seq_recv.at[5])
    back_all.start()
    out.send_diag(dot(ffn_act[p.s3], w_dn[...]))
    out.send_sib(dot(ffn_act[p.s1], w_dn[...]))

    def mixer_block(r):
        block = d_mixed_all[r]
        d_gated_b = dot_t(block, w_mo[...])
        d_gn[r] = d_gated_b
        d_attn[r] = dot_t(block, w_ao[...]).astype(bf)

    mixer_block(s)
    back_all.wait_sib()
    mixer_block(p.s1)
    out.send_across(dot(ffn_act[p.s2], w_dn[...]))
    back_all.forward()
    mixer_block(p.s2)
    back_all.wait_diag()
    mixer_block(p.s3)
    for r in range(4):
        scale = scale_cols[r * rows : (r + 1) * rows, 0:1]
        values = d_gn[r] * gain * (gated[r] * scale)
        mean_buf[s, :, r * rows : (r + 1) * rows] = row_sums(values)
    mean_end = exchange(mean_buf, 6)
    layer_out[...] = (mixed[...] + out.total(dot(ffn_act[s], w_dn[...]))).astype(bf)
    gain_total = jnp.zeros_like(g_gated_gain[...])
    for r in range(4):
        scale = scale_cols[r * rows : (r + 1) * rows, 0:1]
        gain_total = gain_total + jnp.sum(d_gn[r] * (gated[r] * scale), axis=0, keepdims=True)
    g_gated_gain[...] = gain_total
    means = (mean_end() / DI).T
    for r in range(4):
        scale = scale_cols[r * rows : (r + 1) * rows, 0:1]
        mean = means[r * rows : (r + 1) * rows, 0:1]
        d_gated[r] = scale * (d_gn[r] * gain - (gated[r] * scale) * mean)
    mix.wait_sends()
    back.wait_sends()
    out.wait_sends()
    ffn_all.wait_sends()
    back_all.wait_sends()


def middle(seq_count, fsdp_count, arrays):
    gated, attn_mix, w_mo, w_ao, w_dn, w_gu, hidden = arrays[:7]
    fl, bf = jnp.float32, jnp.bfloat16
    rows, model = hidden.shape
    ff = w_dn.shape[0]
    n = seq_count
    total = n * rows

    def sds(*shape, dtype=bf):
        return jax.ShapeDtypeStruct(shape, dtype)

    return pl.pallas_call(
        partial(mid_kernel, seq_count, fsdp_count),
        out_shape=[
            sds(rows, model),
            sds(rows, model, dtype=fl),
            sds(n, rows, model),
            sds(n, rows, ff),
            sds(n, rows, 2 * ff),
            sds(n, rows, model),
            sds(*gated.shape),
            sds(*gated.shape, dtype=fl),
            sds(*attn_mix.shape),
            sds(1, model, dtype=fl),
            sds(1, gated.shape[2], dtype=fl),
        ],
        in_specs=[pl.BlockSpec(memory_space=pltpu.VMEM)] * len(arrays),
        out_specs=[pl.BlockSpec(memory_space=pltpu.VMEM)] * 11,
        scratch_shapes=[
            pltpu.VMEM((n, rows, model), fl),
            pltpu.VMEM((n, rows, 2 * ff), fl),
            pltpu.VMEM((n, rows, ff), fl),
            pltpu.VMEM(gated.shape, fl),
            pltpu.VMEM((rows, model), fl),
            pltpu.VMEM((rows, model), fl),
            pltpu.VMEM((n, 8, total), fl),
            pltpu.VMEM((n, 8, total), fl),
            pltpu.VMEM((3, 3, rows, model), bf),
            pltpu.VMEM((3, 3, rows, model), bf),
            dma(7, 3),
            dma(7, 3),
        ],
        compiler_params=pltpu.CompilerParams(
            collective_id=1, has_side_effects=True, vmem_limit_bytes=VMEM_LIMIT
        ),
        name="ffn_middle",
    )(*arrays)


class LineReduce:
    def __init__(self, place, g, pair_got, side_got, acc, send, recv):
        self.p, self.g, self.pair_got, self.side_got, self.acc = place, g, pair_got, side_got, acc
        self.send, self.recv = send, recv

    def pair_copy(self, b):
        p = self.p
        return rcopy(
            self.g.at[2 * b + 1 - p.y],
            self.pair_got.at[b],
            self.send.at[0, b],
            self.recv.at[0, b],
            p.pair,
        )

    def each_from_far(self, body):
        p = self.p

        def step(k):
            d = p.L - 1 - k

            @pl.when(p.z + d <= p.L - 1)
            def _():
                body(p.z + d)

            @pl.when((d > 0) & (p.z - d >= 0))
            def _():
                body(p.z - d)

        loop(p.L, step)

    def start(self):
        self.each_from_far(lambda b: self.pair_copy(b).start())

    def got_from(self, b, right):
        p = self.p
        slot = b if right else b + p.L
        ref = self.side_got.at[slot]
        rcopy(ref, ref, self.send.at[1, b], self.recv.at[1, slot], p.right).wait_recv()
        return ref

    def pass_on(self, b, right):
        p = self.p
        self.pair_copy(b).wait_recv()
        mine, other = self.g.at[2 * b + p.y], self.pair_got.at[b]
        inner = p.has_left if right else p.has_right

        @pl.when(inner)
        def _():
            add_rows(other, mine, other, self.got_from(b, right))

        @pl.when(jnp.logical_not(inner))
        def _():
            add_rows(other, mine, other)

        slot = b if right else b + p.L
        rcopy(
            other,
            self.side_got.at[slot],
            self.send.at[1, b],
            self.recv.at[1, slot],
            p.right if right else p.left,
        ).start()

    def step(self, k):
        p = self.p
        d = p.L - 1 - k

        @pl.when(p.z + d <= p.L - 1)
        def _():
            self.pass_on(p.z + d, True)

        @pl.when(p.z - d >= 0)
        def _():
            self.pass_on(p.z - d, False)

    def total(self, target):
        p = self.p
        b = p.z
        self.pair_copy(b).wait_recv()
        add_rows(self.acc, self.g.at[2 * b + p.y], self.pair_got.at[b])

        @pl.when(p.has_left)
        def _():
            add_rows(self.acc, self.acc, self.got_from(b, True))

        @pl.when(p.has_right)
        def _():
            add_rows(self.acc, self.acc, self.got_from(b, False))

        add_rows(target, self.acc)

    def wait_sends(self):
        p = self.p

        def each(b):
            self.pair_copy(b).wait_send()

            @pl.when(b != p.z)
            def _():
                ref = self.pair_got.at[b]
                rcopy(ref, ref, self.send.at[1, b], self.recv.at[1, b], p.right).wait_send()

        loop(p.L, each)


def reduce_kernel(
    seq_count,
    fsdp_count,
    g_in,
    g_gu,
    g_out,
    small,
    d_norm,
    in_got,
    gu_got,
    out_got,
    small_got,
    d_norm_sum,
    in_pair,
    in_side,
    in_acc,
    gu_pair,
    gu_side,
    gu_acc,
    out_pair,
    out_side,
    out_acc,
    small_pair,
    small_line,
    stage,
    got,
    in_send,
    in_recv,
    gu_send,
    gu_recv,
    out_send,
    out_recv,
    cast_send,
    cast_recv,
    small_send,
    small_recv,
    sp_send,
    sp_recv,
    seq_send,
    seq_recv,
):
    p = Place(seq_count, fsdp_count)
    s, f, z, y, L = p.s, p.f, p.z, p.y, p.L
    per = fsdp_count // seq_count
    half = per // 2
    fl = jnp.float32
    chunk = g_out.shape[1] // CHUNKS
    p.greet()
    pair_small = rcopy(small, small_pair, sp_send.at[0], sp_recv.at[0], p.pair)
    pair_small.start()

    def rows_of(c):
        return pl.ds(pl.multiple_of(c * chunk, 16), chunk)

    def out_pair_copy(i, c):
        return rcopy(
            g_out.at[2 * i + 1 - y, rows_of(c)],
            out_pair.at[i, rows_of(c)],
            out_send.at[0, i, c],
            out_recv.at[0, i, c],
            p.pair,
        )

    def side_copy(i, c, right):
        at = 0 if right else 1
        return rcopy(
            out_pair.at[i, rows_of(c)],
            out_side.at[at, i, rows_of(c)],
            out_send.at[1, i, c],
            out_recv.at[1 + at, i, c],
            p.right if right else p.left,
        )

    ins = LineReduce(p, g_in, in_pair, in_side, in_acc, in_send, in_recv)
    gus = LineReduce(p, g_gu, gu_pair, gu_side, gu_acc, gu_send, gu_recv)
    d_sum = SeqReduce(p, stage, got, seq_send.at[0], seq_recv.at[0])
    loop(half * CHUNKS, lambda index: out_pair_copy(index // CHUNKS, index % CHUNKS).start())
    gus.start()
    ins.start()
    d_sum.send_diag(d_norm[p.s3])
    d_sum.send_sib(d_norm[p.s1])
    d_sum.send_across(d_norm[p.s2].astype(fl))
    pair_small.wait_recv()
    small_line[z] = small[...] + small_pair[...]
    smalls = LineGather(p, small_line, small_send, small_recv, pair=False)
    smalls.start()
    loop(L - 1, lambda d: smalls.step(d + 1))
    smalls.finish()
    pair_small.wait_send()
    small_sum = small_line[0]
    for b in range(1, L):
        small_sum = small_sum + small_line[b]
    small_got[s] = small_sum
    small_all = SeqGather(p, small_got.at[s], small_got, seq_send.at[1], seq_recv.at[1])
    small_all.start()
    d_norm_sum[...] = d_sum.total(d_norm[s].astype(fl))

    def cast(c, way):
        ref = out_got.at[rows_of(c)]
        return rcopy(ref, ref, cast_send.at[way, c], cast_recv.at[c], p.across if way else p.sib)

    def out_step(index):
        i, c = index // CHUNKS, index % CHUNKS
        zs = s * half + i
        out_pair_copy(i, c).wait_recv()
        mine = g_out.at[2 * i + y, rows_of(c)]
        other = out_pair.at[i, rows_of(c)]
        add_rows(out_acc, mine, other)

        @pl.when(p.has_left & (z <= zs))
        def _():
            side_copy(i, c, True).wait_recv()
            add_rows(out_acc, out_acc, out_side.at[0, i, rows_of(c)])

        @pl.when(p.has_right & (z >= zs))
        def _():
            side_copy(i, c, False).wait_recv()
            add_rows(out_acc, out_acc, out_side.at[1, i, rows_of(c)])

        @pl.when(z == zs)
        def _():
            add_rows(out_got.at[rows_of(c)], out_acc)
            cast(c, 1).start()
            cast(c, 0).start()

        @pl.when(z < zs)
        def _():
            add_rows(other, out_acc)
            side_copy(i, c, True).start()

        @pl.when(z > zs)
        def _():
            add_rows(other, out_acc)
            side_copy(i, c, False).start()

    loop(half * CHUNKS, out_step)
    small_all.forward()
    loop(L - 1, gus.step)
    gus.total(gu_got.at[s])
    gu_all = SeqGather(p, gu_got.at[s], gu_got, seq_send.at[2], seq_recv.at[2])
    gu_all.start()
    holder = f // per
    moved = (s + 4 - holder) % 4
    is_across = moved == 2

    @pl.when(is_across)
    def _():
        def pass_cast(c):
            cast(c, 0).wait_recv()
            cast(c, 0).start()

        loop(CHUNKS, pass_cast)

    loop(L - 1, ins.step)
    gu_all.forward()
    ins.total(in_got.at[s])
    in_all = SeqGather(p, in_got.at[s], in_got, seq_send.at[3], seq_recv.at[3])
    in_all.start()

    @pl.when((s != holder) & jnp.logical_not(is_across))
    def _():
        loop(CHUNKS, lambda c: cast(c, 0).wait_recv())

    @pl.when(s == holder)
    def _():
        def sent(c):
            cast(c, 0).wait_send()
            cast(c, 1).wait_send()

        loop(CHUNKS, sent)

    @pl.when(is_across)
    def _():
        loop(CHUNKS, lambda c: cast(c, 0).wait_send())

    def out_sent(index):
        i, c = index // CHUNKS, index % CHUNKS
        out_pair_copy(i, c).wait_send()

        @pl.when(z != s * half + i)
        def _():
            side_copy(i, c, True).wait_send()

    loop(half * CHUNKS, out_sent)
    gus.wait_sends()
    ins.wait_sends()
    d_sum.wait_sends()
    small_all.finish()
    gu_all.finish()
    in_all.forward()
    in_all.finish()


def reduce_all(seq_count, fsdp_count, arrays):
    g_in, g_gu, g_out, small, d_norm = arrays
    fl, bf = jnp.float32, jnp.bfloat16
    L = fsdp_count // 2
    per = fsdp_count // seq_count
    n = seq_count
    own, in_w = g_in.shape[1:]
    gu_w = g_gu.shape[2]
    out_rows, model = g_out.shape[1:]
    rows = d_norm.shape[1]
    v = pltpu.VMEM
    return pl.pallas_call(
        partial(reduce_kernel, seq_count, fsdp_count),
        out_shape=[
            jax.ShapeDtypeStruct((n, own, in_w), bf),
            jax.ShapeDtypeStruct((n, own, gu_w), bf),
            jax.ShapeDtypeStruct((out_rows, model), bf),
            jax.ShapeDtypeStruct((n,) + small.shape, fl),
            jax.ShapeDtypeStruct((rows, model), fl),
        ],
        in_specs=[pl.BlockSpec(memory_space=v)] * 5,
        out_specs=[pl.BlockSpec(memory_space=v)] * 5,
        scratch_shapes=[
            v((L, own, in_w), bf),
            v((2 * L, own, in_w), bf),
            v((own, in_w), fl),
            v((L, own, gu_w), bf),
            v((2 * L, own, gu_w), bf),
            v((own, gu_w), fl),
            v((per // 2, out_rows, model), bf),
            v((2, per // 2, out_rows, model), bf),
            v((out_rows // CHUNKS, model), fl),
            v(small.shape, fl),
            v((L,) + small.shape, fl),
            v((3, rows, model), bf),
            v((3, rows, model), bf),
            dma(2, L),
            dma(2, 2 * L),
            dma(2, L),
            dma(2, 2 * L),
            dma(2, per // 2, CHUNKS),
            dma(3, per // 2, CHUNKS),
            dma(2, CHUNKS),
            dma(CHUNKS),
            dma(3, L),
            dma(L),
            dma(1),
            dma(1),
            dma(4, 3),
            dma(4, 3),
        ],
        compiler_params=pltpu.CompilerParams(
            collective_id=2, has_side_effects=True, vmem_limit_bytes=VMEM_LIMIT
        ),
        name="reduce_grads",
    )(*arrays)


def rms_scale(values):
    return lax.rsqrt(jnp.mean(values * values, axis=-1, keepdims=True) + EPS)


def swish_slope(values):
    sigma = jax.nn.sigmoid(values)
    return sigma * (1.0 + values * (1.0 - sigma))


def silu_slope(values):
    sigma = jax.nn.sigmoid(values)
    return values * sigma, sigma * (1.0 + values * (1.0 - sigma))


def rows_at(r, size=128):
    return pl.ds(pl.multiple_of(r * size, size), size)


def dot(a, b, **kw):
    return jnp.dot(a, b, preferred_element_type=jnp.float32, **kw)


def dot_t(a, b, **kw):
    return lax.dot_general(a, b, (((1,), (1,)), ((), ())), preferred_element_type=jnp.float32, **kw)


def t_dot(a, b, **kw):
    return lax.dot_general(a, b, (((0,), (0,)), ((), ())), preferred_element_type=jnp.float32, **kw)


def row_sums(values):
    ones = jnp.ones((8, values.shape[1]), jnp.float32)
    return dot_t(ones, values, precision=HIGHEST)


def iota2(shape, axis):
    return lax.broadcasted_iota(jnp.int32, shape, axis)


def head_matrix(width):
    return (iota2((width, 128), 0) // HD == iota2((width, 128), 1)).astype(jnp.float32)


def partner(values):
    lane = iota2(values.shape, 1)
    return jnp.where(lane % HD < HD // 2, pltpu.roll(values, 96, 1), pltpu.roll(values, 32, 1))


def fill_mask(bias, seg_col, seg_row, transposed):
    total = bias.shape[0]

    def some(r):
        t = iota2((128, total), 0) + r * 128
        other = iota2((128, total), 1)
        order = t <= other if transposed else t >= other
        same = seg_col[rows_at(r)] == seg_row[0:1, :].astype(jnp.float32)
        bias[rows_at(r)] = jnp.where(order & same, 0.0, -1e30)

    loop(total // 128, some)


def forward_kernel(
    seq_count,
    fsdp_count,
    hidden,
    cot,
    mamba_in,
    attn_in,
    small,
    gate_up,
    mamba_out,
    attn_out,
    down_proj,
    gain_in,
    seg_row,
    all_taps,
    all_bias,
    all_heads,
    layer_out,
    d_mixed,
    ffn_in,
    ffn_act,
    d_ffn,
    d_mixed_all,
    gated_b,
    d_gated,
    d_attn,
    g_ffn_gain,
    g_gated_gain,
    cot_all,
    in_all,
    normed,
    gate_raw,
    inputs_b,
    accum_out,
    scan_bf,
    scan_y,
    steps,
    cum,
    attn_mix,
    gain_rows,
    seg_col,
    place,
    cosine,
    sine,
    taps,
    heads,
    hid_all,
    w_gu,
    w_mo,
    w_ao,
    w_dn,
    w_gg,
    pre_pad,
    x_act,
    b_mat,
    c_mat,
    x_step,
    inner,
    bias,
    gated,
    part_mix,
    gate_vals,
    d_gn,
    mixed,
    norm2,
    sq_buf,
    mean_buf,
    stage,
    got,
    local,
    in_send,
    in_recv,
    gu_send,
    gu_recv,
    out_send,
    out_recv,
    seq_send,
    seq_recv,
):
    p = Place(seq_count, fsdp_count)
    s, f, z, y, L = p.s, p.f, p.z, p.y, p.L
    fl, bf = jnp.float32, jnp.bfloat16
    per = fsdp_count // seq_count
    half = per // 2
    own_rows = mamba_in.shape[0]
    x_width = gate_raw.shape[1]
    query_width = attn_mix.shape[2]
    ff = w_dn.shape[0]
    rows = hidden.shape[0]
    total = seq_count * rows
    head_share = x_width // HD
    bc = mamba_in.shape[1] - 2 * DI
    conv_width = x_width + bc

    copies = []

    def bring(src, dst):
        copy = pltpu.make_async_copy(src, dst, local.at[len(copies)])
        copy.start()
        copies.append(copy)

    def part(ref, start, size):
        return ref.at[:, pl.ds(pl.multiple_of(start, 128), size)]

    def own_cols(ref, start, size):
        return ref.at[rows_at(f, own_rows), pl.ds(start, size)]

    c0 = 0
    for src, start, size in (
        (mamba_in, s * x_width, x_width),
        (mamba_in, DI + s * x_width, x_width),
        (mamba_in, 2 * DI, bc),
        (attn_in, s * query_width, query_width),
        (small, 0, small.shape[1]),
    ):
        bring(part(src, start, size), own_cols(in_all, c0, size))
        c0 += size
    in_copies = len(copies)
    bring(hidden, hid_all.at[s])
    bring(cot, cot_all.at[s])
    bring(part(gate_up, s * ff, ff), own_cols(w_gu, 0, ff))
    bring(part(gate_up, FF + s * ff, ff), own_cols(w_gu, ff, ff))
    holder = f // per == s
    spread_arrays = ((gain_in, w_gg, 1), (mamba_out, w_mo, 2), (attn_out, w_ao, 1), (down_proj, w_dn, 2))

    def own_spread(act):
        @pl.when(holder)
        def _():
            for k, (src, dst, _) in enumerate(spread_arrays):
                size = src.shape[0]
                act(pltpu.make_async_copy(src, dst.at[rows_at(f - s * per, size)], local.at[12 + k]))

    own_spread(lambda copy: copy.start())
    p.greet(diag=True)
    for copy in copies[:in_copies]:
        copy.wait()
    ins = LineGather(p, in_all, in_send, in_recv, size=own_rows)
    gus = LineGather(p, w_gu, gu_send, gu_recv, size=own_rows)
    hid = SeqGather(p, hidden, hid_all, seq_send.at[7], seq_recv.at[7])
    cots = SeqGather(p, cot, cot_all, seq_send.at[8], seq_recv.at[8])
    hid.start()
    ins.start()
    seg_float = seg_row[...].astype(fl)
    seg_col[...] = jnp.broadcast_to(seg_float, (8, total)).T[:, 0:1]
    first_count = jnp.sum(1.0 - seg_float, axis=1, keepdims=True)
    position = iota2((total, 1), 0).astype(fl)
    place[...] = position - jnp.where(seg_col[...] == 0.0, 0.0, first_count)
    lane = iota2((1, 128), 1)
    turn = (lane % (HD // 2)).astype(fl)
    angles = place[...] * jnp.exp(-math.log(ROPE_THETA) * 2.0 * turn / HD)
    cosine[...] = jnp.cos(angles)
    sine[...] = jnp.sin(angles) * jnp.where(lane % HD < HD // 2, -1.0, 1.0)
    fill_mask(bias, seg_col, seg_row, False)
    own_x = pl.ds(pl.multiple_of(s * x_width, 128), x_width)
    taps[0:KC, :x_width] = all_taps[:, own_x]
    taps[0:KC, x_width:] = all_taps[:, DI:]
    taps[KC : KC + 1, :x_width] = all_bias[:, own_x]
    taps[KC : KC + 1, x_width:] = all_bias[:, DI:]
    mine = pltpu.roll(all_heads[...], (128 - s * head_share) % 128, 1)
    mine = jnp.where(iota2(mine.shape, 1) < head_share, mine, 0.0)
    heads[0:1, :128] = mine[0:1]
    heads[1:2, :128] = jnp.where(iota2((1, 128), 1) < head_share, -jnp.exp(mine[1:2]), 0.0)
    heads[2:3, :] = dot_t(mine, head_matrix(x_width), precision=HIGHEST)[2:3]
    hid.forward()
    loop(L - 1, lambda d: ins.step(d + 1))
    cots.start()
    for copy in copies[in_copies:]:
        copy.wait()
    own_spread(lambda copy: copy.wait())

    pieces = []
    for k, (src, dst, count) in enumerate(spread_arrays):
        size = src.shape[0]
        for c in range(count):
            pieces.append((dst, size, c * (size // count), size // count))

    def piece_copy(i, k, way, other=0):
        dst, size, offset, count = pieces[k]
        j = 2 * i + (1 - y if other else y)
        ref = dst.at[pl.ds(pl.multiple_of(j * size + offset, 16), count)]
        device = (p.right, p.left, p.pair)[way]
        return rcopy(ref, ref, out_send.at[way, i, k], out_recv.at[way // 2, i, k], device)

    def push_piece(i, k):
        zs = s * half + i

        @pl.when((z >= zs) & p.has_right)
        def _():
            piece_copy(i, k, 0).start()

        @pl.when((z <= zs) & p.has_left)
        def _():
            piece_copy(i, k, 1).start()

        piece_copy(i, k, 2).start()

    def hold_piece(k):
        for i in range(half):

            @pl.when(z == s * half + i)
            def _():
                push_piece(i, k)

    def pass_pieces(group, far):
        for k in group:
            pass_piece(k, far)

    def pass_piece(k, far):
        for i in range(half):
            zs = s * half + i

            @pl.when((z - zs == far) | (zs - z == far))
            def _():
                piece_copy(i, k, 0).wait_recv()
                push_piece(i, k)

    def end_piece(k):
        for i in range(half):
            piece_copy(i, k, 2, 1).wait_recv()

    def sent_piece(k):
        for i in range(half):
            zs = s * half + i
            piece_copy(i, k, 2).wait_send()

            @pl.when((z >= zs) & p.has_right)
            def _():
                piece_copy(i, k, 0).wait_send()

            @pl.when((z <= zs) & p.has_left)
            def _():
                piece_copy(i, k, 1).wait_send()

    early = range(4)
    late = range(4, len(pieces))
    for k in early:
        hold_piece(k)
    gus.start()
    for k in late:
        hold_piece(k)
    ins.finish()
    hid.finish()
    cots.forward()

    gain_t = in_all[:, in_all.shape[1] - 128 :].astype(fl).T
    gain_rows[...] = gain_t[0:16]
    first_gain = gain_rows[head_share : head_share + 1, :]

    def norm_block(r):
        values = hid_all[r].astype(fl)
        scale = lax.rsqrt(jnp.mean(values * values, axis=-1, keepdims=True) + EPS)
        normed[rows_at(r)] = (values * scale * first_gain).astype(bf)

    loop(seq_count, norm_block)
    pass_pieces(early, 1)
    gate_raw[...] = dot(normed[...], in_all[:, :x_width])
    inputs_b[:, :conv_width] = dot(normed[...], in_all[:, x_width : x_width + conv_width]).astype(bf)
    inputs_b[:, conv_width:] = dot(normed[...], in_all[:, x_width + conv_width :]).astype(bf)
    pass_pieces(late, 1)
    gus.step(1)
    pre_pad[0:8] = jnp.zeros((8, conv_width), fl)
    pre_pad[8 : 8 + total] = inputs_b[:, :conv_width].astype(fl)
    for r in range(seq_count):
        at = slice(r * rows, (r + 1) * rows)
        accum = taps[KC : KC + 1, :] + taps[KC - 1 : KC, :] * pre_pad[8 + r * rows : 8 + (r + 1) * rows]
        for lag in range(1, KC):
            moved = pre_pad[8 + r * rows - lag : 8 + (r + 1) * rows - lag]
            accum = accum + taps[KC - 1 - lag : KC - lag, :] * jnp.where(
                place[at] >= lag, moved, 0.0
            )
        accum_out[at] = accum
        acts = accum * jax.nn.sigmoid(accum)
        x_act[at] = acts[:, :x_width]
        b_mat[at] = acts[:, x_width : x_width + NST].astype(bf)
        c_mat[at] = acts[:, x_width + NST :].astype(bf)
    pass_pieces(early, 2)
    raw = inputs_b[:, conv_width + query_width + 2 * HD :].astype(fl) + heads[0:1, :128]
    steps[...] = jnp.maximum(raw, 0.0) + jnp.log1p(jnp.exp(-jnp.abs(raw)))
    causal = (iota2((total, total), 0) >= iota2((total, total), 1)).astype(fl)
    cum[...] = dot(causal, heads[1:2, :128] * steps[...], precision=HIGHEST)
    cum_t = cum[...].T
    spread_heads = head_matrix(x_width)
    x_step[...] = (x_act[...] * dot_t(steps[...], spread_heads, precision=HIGHEST)).astype(bf)
    inner[...] = dot_t(c_mat[...], b_mat[...])
    gus.step(2)
    pumps = {
        0: lambda: pass_pieces(late, 2),
        1: lambda: pass_pieces(early, 3),
        3: lambda: gus.step(3),
        5: lambda: pass_pieces(late, 3),
    }
    for h in range(head_share):
        hs = slice(h * HD, (h + 1) * HD)
        for r in range(seq_count):
            at = slice(r * rows, (r + 1) * rows)
            K = (r + 1) * rows
            decay = jnp.exp(cum[at, h : h + 1] - cum_t[h : h + 1, :K] + bias[at, :K])
            kernel_b = (inner[at, :K] * decay).astype(bf)
            scan_y[at, hs] = dot(kernel_b, x_step[:K, hs])
        if h in pumps:
            pumps[h]()
    for r in range(seq_count):
        at = slice(r * rows, (r + 1) * rows)
        scan = (scan_y[at] + heads[2:3, :x_width] * x_act[at]).astype(bf)
        scan_bf[at] = scan
        gate = gate_raw[at]
        gated[r] = scan.astype(fl) * (gate * jax.nn.sigmoid(gate))
    for r in range(seq_count):
        values = gated[r]
        sq_buf[s, :, r * rows : (r + 1) * rows] = row_sums(values * values)
    peers = (p.sib, p.across, p.diag)
    peer_at = (p.s1, p.s2, p.s3)

    def exchange(buf, at):
        pairs = []
        for k in range(3):
            copy = rcopy(buf.at[s], buf.at[s], seq_send.at[at, k], seq_recv.at[at, k], peers[k])
            copy.start()
            other = buf.at[peer_at[k]]
            pairs.append((copy, rcopy(other, other, seq_send.at[at, k], seq_recv.at[at, k], peers[k])))

        def end():
            for copy, arrived in pairs:
                arrived.wait_recv()
                copy.wait_send()
            return buf[0] + buf[1] + buf[2] + buf[3]

        return end

    sq_end = exchange(sq_buf, 0)
    q_in = inputs_b[:, conv_width : conv_width + query_width].astype(fl)
    kv_in = inputs_b[:, conv_width + query_width : conv_width + query_width + 2 * HD].astype(fl)
    q_rot = q_in * cosine[...] + partner(q_in) * sine[...]
    k_rot = (kv_in * cosine[...] + partner(kv_in) * sine[...])[:, :HD]
    v_b = inputs_b[:, conv_width + query_width + HD : conv_width + query_width + 2 * HD]
    for r in range(seq_count):
        at = slice(r * rows, (r + 1) * rows)
        K = (r + 1) * rows
        for h in range(query_width // HD):
            hs = slice(h * HD, (h + 1) * HD)
            scores = dot_t(q_rot[at, hs], k_rot[:K], precision=HIGHEST) * (1.0 / math.sqrt(HD))
            weights = jnp.exp(scores + bias[at, :K])
            weights = weights / jnp.sum(weights, axis=-1, keepdims=True)
            attn_mix[r, :, hs] = dot(weights.astype(bf), v_b[:K]).astype(bf)
    cots.finish()
    for k in early:
        end_piece(k)
    gain = w_gg[...].astype(fl).T[0:1, :]
    for r in range(seq_count):
        part_mix[r] = dot((gated[r] * gain).astype(bf), w_mo[...])
    scale_cols = lax.rsqrt(sq_end() / DI + EPS).T
    for r in range(seq_count):
        scale = scale_cols[r * rows : (r + 1) * rows, 0:1]
        part_mix[r] = part_mix[r] * scale + dot(attn_mix[r], w_ao[...])
        gated_b[r] = (gated[r] * scale * gain).astype(bf)

    def reducer(at):
        return SeqReduce(p, stage.at[at], got.at[at], seq_send.at[at + 1], seq_recv.at[at + 1])

    mix = reducer(0)
    mix.send_diag(part_mix[p.s3])
    mix.send_sib(part_mix[p.s1])
    mix.send_across(part_mix[p.s2])
    second_gain = gain_rows[head_share + 1 : head_share + 2, :]
    residual = hid_all[s].astype(fl)
    mixed[...] = residual + mix.total(part_mix[s])
    scale2 = lax.rsqrt(jnp.mean(mixed[...] * mixed[...], axis=-1, keepdims=True) + EPS)
    norm2[...] = mixed[...] * scale2
    ffn_in[s] = (norm2[...] * second_gain).astype(bf)
    ffn_all = SeqGather(p, ffn_in.at[s], ffn_in, seq_send.at[4], seq_recv.at[4])
    ffn_all.start()
    ffn_all.wait_sib()
    ffn_all.forward()
    ffn_all.wait_diag()
    gus.finish()

    def act_block(r, da):
        gate_lin = gate_vals[r, :, :ff]
        up_lin = gate_vals[r, :, ff:]
        act, slope = silu_slope(gate_lin)
        ffn_act[r] = (act * up_lin).astype(bf)
        d_ffn[r, :, :ff] = (da * up_lin * slope).astype(bf)
        d_ffn[r, :, ff:] = (da * act).astype(bf)

    model = ffn_in.shape[2]
    vals = dot(ffn_in[...].reshape(total, model), w_gu[...])
    gate_vals[...] = vals.reshape(seq_count, rows, 2 * ff)
    for k in late:
        end_piece(k)
    d_act = dot_t(cot_all[...].reshape(total, model), w_dn[...])
    for r in range(seq_count):
        act_block(r, d_act[r * rows : (r + 1) * rows])
    back = reducer(1)
    back.send_diag(dot_t(d_ffn[p.s3], w_gu[...]))
    back.send_sib(dot_t(d_ffn[p.s1], w_gu[...]))
    back.send_across(dot_t(d_ffn[p.s2], w_gu[...]))
    out = reducer(2)
    d_ffn_own = dot_t(d_ffn[s], w_gu[...])
    d_ffn_in = back.total(d_ffn_own)
    g_ffn_gain[...] = jnp.sum(d_ffn_in * norm2[...], axis=0, keepdims=True)
    d_second = d_ffn_in * second_gain
    d_mixed[...] = cot_all[s].astype(fl) + scale2 * (
        d_second - norm2[...] * jnp.mean(d_second * norm2[...], axis=-1, keepdims=True)
    )
    d_mixed_all[s] = d_mixed[...].astype(bf)
    back_all = SeqGather(p, d_mixed_all.at[s], d_mixed_all, seq_send.at[5], seq_recv.at[5])
    back_all.start()
    out.send_diag(dot(ffn_act[p.s3], w_dn[...]))
    out.send_sib(dot(ffn_act[p.s1], w_dn[...]))

    def mixer_block(r):
        block = d_mixed_all[r]
        d_gn[r] = dot_t(block, w_mo[...])
        d_attn[r] = dot_t(block, w_ao[...]).astype(bf)

    mixer_block(s)
    back_all.wait_sib()
    mixer_block(p.s1)
    out.send_across(dot(ffn_act[p.s2], w_dn[...]))
    back_all.forward()
    mixer_block(p.s2)
    back_all.wait_diag()
    mixer_block(p.s3)
    for r in range(seq_count):
        scale = scale_cols[r * rows : (r + 1) * rows, 0:1]
        values = d_gn[r] * gain * (gated[r] * scale)
        mean_buf[s, :, r * rows : (r + 1) * rows] = row_sums(values)
    mean_end = exchange(mean_buf, 6)
    layer_out[...] = (mixed[...] + out.total(dot(ffn_act[s], w_dn[...]))).astype(bf)
    gain_total = jnp.zeros_like(g_gated_gain[...])
    for r in range(seq_count):
        scale = scale_cols[r * rows : (r + 1) * rows, 0:1]
        gain_total = gain_total + jnp.sum(d_gn[r] * (gated[r] * scale), axis=0, keepdims=True)
    g_gated_gain[...] = gain_total
    means = (mean_end() / DI).T
    for r in range(seq_count):
        scale = scale_cols[r * rows : (r + 1) * rows, 0:1]
        mean = means[r * rows : (r + 1) * rows, 0:1]
        d_gated[r] = scale * (d_gn[r] * gain - (gated[r] * scale) * mean)
    for k in range(len(pieces)):
        sent_piece(k)
    mix.wait_sends()
    back.wait_sends()
    out.wait_sends()
    ffn_all.wait_sends()
    back_all.wait_sends()


def forward_all(seq_count, fsdp_count, widths, arrays):
    x_width, query_width, ff = widths
    hidden, cot, mamba_in, attn_in, small = arrays[:5]
    mamba_out, attn_out, down_proj, gain_in = arrays[6:10]
    fl, bf = jnp.float32, jnp.bfloat16
    rows, model = hidden.shape
    n = seq_count
    total = n * rows
    per = fsdp_count // seq_count
    L = fsdp_count // 2
    conv_width = x_width + 2 * NST
    in_width = x_width + conv_width + query_width + small.shape[1]
    v = pltpu.VMEM

    def sds(*shape, dtype=bf):
        return jax.ShapeDtypeStruct(shape, dtype)

    outs = [
        sds(rows, model),
        sds(rows, model, dtype=fl),
        sds(n, rows, model),
        sds(n, rows, ff),
        sds(n, rows, 2 * ff),
        sds(n, rows, model),
        sds(n, rows, x_width),
        sds(n, rows, x_width, dtype=fl),
        sds(n, rows, query_width),
        sds(1, model, dtype=fl),
        sds(1, x_width, dtype=fl),
        sds(n, rows, model),
        sds(model, in_width),
        sds(total, model),
        sds(total, x_width, dtype=fl),
        sds(total, in_width - x_width),
        sds(total, conv_width, dtype=fl),
        sds(total, x_width),
        sds(total, x_width, dtype=fl),
        sds(total, 128, dtype=fl),
        sds(total, 128, dtype=fl),
        sds(n, rows, query_width),
        sds(16, model, dtype=fl),
        sds(total, 1, dtype=fl),
        sds(total, 1, dtype=fl),
        sds(total, 128, dtype=fl),
        sds(total, 128, dtype=fl),
        sds(8, conv_width, dtype=fl),
        sds(8, x_width, dtype=fl),
    ]
    vm = pl.BlockSpec(memory_space=v)
    hbm = pl.BlockSpec(memory_space=pl.ANY)
    return pl.pallas_call(
        partial(forward_kernel, seq_count, fsdp_count),
        out_shape=outs,
        in_specs=[hbm] * 10 + [vm] * (len(arrays) - 10),
        out_specs=[vm] * len(outs),
        scratch_shapes=[
            v((n, rows, model), bf),
            v((model, 2 * ff), bf),
            v((x_width, model), bf),
            v((query_width, model), bf),
            v((ff, model), bf),
            v((x_width, 128), bf),
            v((total + 8, conv_width), fl),
            v((total, x_width), fl),
            v((total, NST), bf),
            v((total, NST), bf),
            v((total, x_width), bf),
            v((total, total), fl),
            v((total, total), fl),
            v((n, rows, x_width), fl),
            v((n, rows, model), fl),
            v((n, rows, 2 * ff), fl),
            v((n, rows, x_width), fl),
            v((rows, model), fl),
            v((rows, model), fl),
            v((n, 8, total), fl),
            v((n, 8, total), fl),
            v((3, 3, rows, model), bf),
            v((3, 3, rows, model), bf),
            dma(16),
            dma(3, L),
            dma(fsdp_count),
            dma(3, L),
            dma(fsdp_count),
            dma(3, per // 2, 6),
            dma(2, per // 2, 6),
            dma(9, 3),
            dma(9, 3),
        ],
        compiler_params=pltpu.CompilerParams(
            collective_id=3, has_side_effects=True, vmem_limit_bytes=VMEM_LIMIT
        ),
        name="forward_fused",
    )(*arrays)


SMALL_ROWS = 48


def backward_kernel(
    seq_count,
    fsdp_count,
    hidden,
    d_mixed,
    d_mixed_all,
    cot_all,
    ffn_in,
    ffn_act,
    d_ffn,
    gated_b,
    attn_mix,
    d_gated,
    d_attn,
    g_ffn_gain,
    g_gated_gain,
    in_all,
    normed,
    gate_raw,
    inputs_b,
    accum_in,
    scan_bf,
    scan_y,
    steps,
    cum,
    gain_rows,
    seg_col,
    seg_row,
    place,
    cosine,
    sine,
    taps,
    heads,
    in_got,
    gu_got,
    out_got,
    small_got,
    grad_tok,
    g_in,
    g_gu,
    g_out,
    small,
    d_norm,
    d_in,
    dy,
    x_act,
    b_mat,
    c_mat,
    x_step,
    inner,
    inner_t,
    bias,
    bias_t,
    d_inner,
    d_x_step,
    d_acc,
    shifted,
    d_kv,
    d_x_conv,
    in_pair,
    in_side,
    in_acc,
    gu_pair,
    gu_side,
    gu_acc,
    out_pair,
    out_side,
    out_acc,
    small_pair,
    small_line,
    stage,
    got,
    in_send,
    in_recv,
    gu_send,
    gu_recv,
    out_send,
    out_recv,
    cast_send,
    cast_recv,
    small_send,
    small_recv,
    sp_send,
    sp_recv,
    seq_send,
    seq_recv,
):
    p = Place(seq_count, fsdp_count)
    s, f, z, y, L = p.s, p.f, p.z, p.y, p.L
    fl, bf = jnp.float32, jnp.bfloat16
    per = fsdp_count // seq_count
    half = per // 2
    chunk = g_out.shape[1] // CHUNKS
    total = normed.shape[0]
    rows = total // seq_count
    model = normed.shape[1]
    own_rows = model // fsdp_count
    x_width = gate_raw.shape[1]
    query_width = attn_mix.shape[1]
    conv_width = accum_in.shape[1]
    head_share = x_width // HD
    ff = ffn_act.shape[1]
    gain_own, attn_own, ff_own = DI // fsdp_count, QH * HD // fsdp_count, FF // fsdp_count
    p.greet()

    def rows_of(c):
        return pl.ds(pl.multiple_of(c * chunk, 16), chunk)

    def out_pair_copy(i, c):
        return rcopy(
            g_out.at[2 * i + 1 - y, rows_of(c)],
            out_pair.at[i, rows_of(c)],
            out_send.at[0, i, c],
            out_recv.at[0, i, c],
            p.pair,
        )

    def side_copy(i, c, right):
        at = 0 if right else 1
        return rcopy(
            out_pair.at[i, rows_of(c)],
            out_side.at[at, i, rows_of(c)],
            out_send.at[1, i, c],
            out_recv.at[1 + at, i, c],
            p.right if right else p.left,
        )

    def cast(c, way):
        ref = out_got.at[rows_of(c)]
        return rcopy(ref, ref, cast_send.at[way, c], cast_recv.at[c], p.across if way else p.sib)

    def out_step(index):
        i, c = index // CHUNKS, index % CHUNKS
        zs = s * half + i
        out_pair_copy(i, c).wait_recv()
        mine = g_out.at[2 * i + y, rows_of(c)]
        other = out_pair.at[i, rows_of(c)]
        add_rows(out_acc, mine, other)

        @pl.when(p.has_left & (z <= zs))
        def _():
            side_copy(i, c, True).wait_recv()
            add_rows(out_acc, out_acc, out_side.at[0, i, rows_of(c)])

        @pl.when(p.has_right & (z >= zs))
        def _():
            side_copy(i, c, False).wait_recv()
            add_rows(out_acc, out_acc, out_side.at[1, i, rows_of(c)])

        @pl.when(z == zs)
        def _():
            add_rows(out_got.at[rows_of(c)], out_acc)
            cast(c, 1).start()
            cast(c, 0).start()

        @pl.when(z < zs)
        def _():
            add_rows(other, out_acc)
            side_copy(i, c, True).start()

        @pl.when(z > zs)
        def _():
            add_rows(other, out_acc)
            side_copy(i, c, False).start()

    ins = LineReduce(p, g_in, in_pair, in_side, in_acc, in_send, in_recv)
    gus = LineReduce(p, g_gu, gu_pair, gu_side, gu_acc, gu_send, gu_recv)

    for fi in range(fsdp_count):
        at = slice(fi * own_rows, (fi + 1) * own_rows)
        g_gu[fi] = t_dot(ffn_in[:, at], d_ffn[...]).astype(bf)
    gus.start()
    g_mo = t_dot(gated_b[...], d_mixed_all[...]).astype(bf)
    g_ao = t_dot(attn_mix[...], d_mixed_all[...]).astype(bf)
    for j in range(per):
        g_out[j, :gain_own] = g_mo[j * gain_own : (j + 1) * gain_own]
        g_out[j, gain_own : gain_own + attn_own] = g_ao[j * attn_own : (j + 1) * attn_own]
        act = ffn_act[:, j * ff_own : (j + 1) * ff_own]
        g_out[j, gain_own + attn_own :] = t_dot(act, cot_all[...]).astype(bf)
    loop(half * CHUNKS, lambda index: out_pair_copy(index // CHUNKS, index % CHUNKS).start())

    fill_mask(bias, seg_col, seg_row, False)
    fill_mask(bias_t, seg_col, seg_row, True)
    spread_heads = head_matrix(x_width)
    steps_wide = dot_t(steps[...], spread_heads, precision=HIGHEST)
    skip = heads[2:3, :x_width]
    cum_t = cum[...].T
    for r in range(seq_count):
        at = slice(r * rows, (r + 1) * rows)
        accum = accum_in[at]
        acts = accum * jax.nn.sigmoid(accum)
        x_act[at] = acts[:, :x_width]
        b_mat[at] = acts[:, x_width : x_width + NST].astype(bf)
        c_mat[at] = acts[:, x_width + NST :].astype(bf)
        x_step[at] = (acts[:, :x_width] * steps_wide[at]).astype(bf)
        gate_act, slope = silu_slope(gate_raw[at])
        cots = d_gated[at]
        dy[at] = (cots * gate_act).astype(bf)
        d_in[at, :x_width] = (cots * scan_bf[at].astype(fl) * slope).astype(bf)
    inner[...] = dot_t(c_mat[...], b_mat[...])
    inner_t[...] = dot_t(b_mat[...], c_mat[...])
    d_inner[...] = jnp.zeros_like(d_inner)
    gu_all = SeqGather(p, gu_got.at[s], gu_got, seq_send.at[2], seq_recv.at[2])
    for h in range(head_share):
        hs = slice(h * HD, (h + 1) * HD)
        for r in range(seq_count):
            at = slice(r * rows, (r + 1) * rows)
            K = (r + 1) * rows
            decay = jnp.exp(cum[at, h : h + 1] - cum_t[h : h + 1, :K] + bias[at, :K])
            d_inner[at, :K] += dot_t(dy[at, hs], x_step[:K, hs]) * decay
            decay = jnp.exp(cum_t[h : h + 1, r * rows :] - cum[at, h : h + 1] + bias_t[at, r * rows :])
            kernel_t = (inner_t[at, r * rows :] * decay).astype(bf)
            d_x_step[at, hs] = dot(kernel_t, dy[r * rows :, hs])
    gus.step(0)
    d_inner_b = d_inner[...].astype(bf)
    d_acc[:, x_width : x_width + NST] = t_dot(d_inner_b, c_mat[...])
    d_acc[:, x_width + NST :] = dot(d_inner_b, b_mat[...])
    dy_f = dy[...].astype(fl)
    xs = x_act[...]
    dxs = d_x_step[...]
    d_acc[:, :x_width] = steps_wide * dxs + skip * dy_f
    head_sums = dot(
        jnp.sum((dy_f * xs).reshape(total // 8, 8, x_width), axis=0), spread_heads, precision=HIGHEST
    )
    g_skip = jnp.sum(head_sums, axis=0, keepdims=True)
    step_direct = dot(xs * dxs, spread_heads, precision=HIGHEST)
    d_cum = dot(
        dy_f * scan_y[...] - x_step[...].astype(fl) * dxs, spread_heads, precision=HIGHEST
    )
    after = (iota2((total, total), 0) <= iota2((total, total), 1)).astype(fl)
    d_log = dot(after, d_cum, precision=HIGHEST)
    decay_row = heads[1:2, :128]
    g_decay = jnp.sum(d_log * (decay_row * steps[...]), axis=0, keepdims=True)
    raw = inputs_b[:, conv_width + query_width + 2 * HD :].astype(fl) + heads[0:1, :128]
    d_raw = (step_direct + d_log * decay_row) * jax.nn.sigmoid(raw)
    d_raw = jnp.where(iota2(d_raw.shape, 1) < head_share, d_raw, 0.0)
    g_step_bias = jnp.sum(d_raw, axis=0, keepdims=True)
    step_at = x_width + conv_width + query_width + 2 * HD
    d_in[:, step_at:] = d_raw.astype(bf)

    q_at = conv_width
    kv_at = conv_width + query_width
    q_in = inputs_b[:, q_at:kv_at].astype(fl)
    kv_in = inputs_b[:, kv_at : kv_at + 2 * HD].astype(fl)
    q_rot = q_in * cosine[...] + partner(q_in) * sine[...]
    k_rot = (kv_in * cosine[...] + partner(kv_in) * sine[...])[:, :HD]
    k_b = k_rot.astype(bf)
    v_b = inputs_b[:, kv_at + HD : kv_at + 2 * HD]
    d_kv[...] = jnp.zeros_like(d_kv)
    scale = 1.0 / math.sqrt(HD)
    for r in range(seq_count):
        at = slice(r * rows, (r + 1) * rows)
        K = (r + 1) * rows
        for h in range(query_width // HD):
            hs = slice(h * HD, (h + 1) * HD)
            scores = dot_t(q_rot[at, hs], k_rot[:K], precision=HIGHEST) * scale
            weights = jnp.exp(scores + bias[at, :K])
            weights = weights / jnp.sum(weights, axis=-1, keepdims=True)
            d_att = d_attn[at, hs]
            d_weights = dot_t(d_att, v_b[:K])
            along = jnp.sum(d_weights * weights, axis=-1, keepdims=True)
            d_scores = (weights * (d_weights - along) * scale).astype(bf)
            shifted[at, hs] = dot(d_scores, k_b[:K])
            d_kv[:K, :HD] += t_dot(d_scores, q_rot[at, hs].astype(bf))
            d_kv[:K, HD : 2 * HD] += t_dot(weights.astype(bf), d_att)
    d_q = shifted[:total, :query_width]
    d_q = d_q * cosine[...] + partner(d_q * sine[...])
    d_kv_all = d_kv[...]
    d_k = d_kv_all * cosine[...] + partner(d_kv_all * sine[...])
    d_kv_all = jnp.where(iota2(d_k.shape, 1) < HD, d_k, d_kv_all)
    d_in[:, x_width + q_at : x_width + kv_at] = d_q.astype(bf)
    d_in[:, x_width + kv_at : x_width + kv_at + 2 * HD] = d_kv_all.astype(bf)

    gus.step(1)

    tap_sums = [jnp.zeros((1, conv_width), fl) for _ in range(KC + 1)]
    shifted[total:] = jnp.zeros((8, conv_width), fl)
    for r in range(seq_count):
        at = slice(r * rows, (r + 1) * rows)
        d_acc[at] = d_acc[at] * silu_slope(accum_in[at])[1]
        tap_sums[KC] = tap_sums[KC] + jnp.sum(d_acc[at], axis=0, keepdims=True)
        pre = inputs_b[at, :conv_width].astype(fl)
        tap_sums[KC - 1] = tap_sums[KC - 1] + jnp.sum(d_acc[at] * pre, axis=0, keepdims=True)
    for lag in range(1, KC):
        k = KC - 1 - lag
        shifted[:total] = jnp.where(place[...] >= lag, d_acc[...], 0.0)
        for r in range(seq_count):
            at = slice(r * rows, (r + 1) * rows)
            moved = shifted[r * rows + lag : (r + 1) * rows + lag]
            pre = inputs_b[at, :conv_width].astype(fl)
            tap_sums[k] = tap_sums[k] + jnp.sum(moved * pre, axis=0, keepdims=True)
            grads = taps[k : k + 1, :] * moved
            if lag == 1:
                grads = grads + taps[KC - 1 : KC, :] * d_acc[at]
                d_x_conv[at] = grads
            else:
                d_x_conv[at] += grads
    d_in[:, x_width : x_width + conv_width] = d_x_conv[...].astype(bf)

    loop(L - 3, lambda k: gus.step(k + 2))

    d_sum = SeqReduce(p, stage, got, seq_send.at[0], seq_recv.at[0])
    norm_gain_sum = jnp.zeros((1, model), fl)
    first_gain = gain_rows[head_share : head_share + 1, :]
    for r in range(seq_count):
        at = slice(r * rows, (r + 1) * rows)
        part = dot_t(d_in[at], in_all[...])
        d_norm[r] = part
        norm_gain_sum = norm_gain_sum + jnp.sum(part * normed[at].astype(fl), axis=0, keepdims=True)
    norm_gain_sum = norm_gain_sum / first_gain
    d_sum.send_diag(d_norm[p.s3])
    d_sum.send_sib(d_norm[p.s1])
    d_sum.send_across(d_norm[p.s2])

    def put(at, row):
        for c in range(row.shape[1] // 128):
            small[at + c : at + c + 1, :] = row[:, c * 128 : (c + 1) * 128]
        return at + row.shape[1] // 128

    at = 0
    for row in tap_sums + [g_gated_gain[...], norm_gain_sum, g_ffn_gain[...], g_step_bias, g_decay, g_skip]:
        at = put(at, row)
    small[at:] = jnp.zeros((SMALL_ROWS - at, 128), fl)
    pair_small = rcopy(small, small_pair, sp_send.at[0], sp_recv.at[0], p.pair)
    pair_small.start()
    for fi in range(fsdp_count):
        at = slice(fi * own_rows, (fi + 1) * own_rows)
        g_in[fi] = t_dot(normed[:, at], d_in[...]).astype(bf)
    ins.start()
    gus.total(gu_got.at[s])
    gu_all.start()
    loop(half * CHUNKS, out_step)
    pair_small.wait_recv()
    small_line[z] = small[...] + small_pair[...]
    smalls = LineGather(p, small_line, small_send, small_recv, pair=False)
    smalls.start()
    gu_all.forward()
    holder = f // per
    is_across = (s + 4 - holder) % 4 == 2

    def hop(k):
        ins.step(k)
        smalls.step(k + 1)

    loop(L - 1, hop)

    @pl.when(is_across)
    def _():
        def pass_cast(c):
            cast(c, 0).wait_recv()
            cast(c, 0).start()

        loop(CHUNKS, pass_cast)

    smalls.finish()
    small_sum = small_line[0]
    for b in range(1, L):
        small_sum = small_sum + small_line[b]
    small_got[s] = small_sum
    small_all = SeqGather(p, small_got.at[s], small_got, seq_send.at[1], seq_recv.at[1])
    small_all.start()
    ins.total(in_got.at[s])
    in_gather = SeqGather(p, in_got.at[s], in_got, seq_send.at[3], seq_recv.at[3])
    in_gather.start()
    small_all.forward()
    d_normed = d_sum.total(d_norm[s])
    residual = hidden[...].astype(fl)
    scale1 = lax.rsqrt(jnp.mean(residual * residual, axis=-1, keepdims=True) + EPS)
    first_norm = residual * scale1
    d_first = d_normed * first_gain
    grad_tok[...] = d_mixed[...] + scale1 * (
        d_first - first_norm * jnp.mean(d_first * first_norm, axis=-1, keepdims=True)
    )

    @pl.when((s != holder) & jnp.logical_not(is_across))
    def _():
        loop(CHUNKS, lambda c: cast(c, 0).wait_recv())

    @pl.when(s == holder)
    def _():
        def sent(c):
            cast(c, 0).wait_send()
            cast(c, 1).wait_send()

        loop(CHUNKS, sent)

    @pl.when(is_across)
    def _():
        loop(CHUNKS, lambda c: cast(c, 0).wait_send())

    def out_sent(index):
        i, c = index // CHUNKS, index % CHUNKS
        out_pair_copy(i, c).wait_send()

        @pl.when(z != s * half + i)
        def _():
            side_copy(i, c, True).wait_send()

    loop(half * CHUNKS, out_sent)
    in_gather.forward()
    pair_small.wait_send()
    gus.wait_sends()
    ins.wait_sends()
    d_sum.wait_sends()
    small_all.finish()
    gu_all.finish()
    in_gather.finish()


def backward_all(seq_count, fsdp_count, arrays):
    hidden = arrays[0]
    fl, bf = jnp.float32, jnp.bfloat16
    L = fsdp_count // 2
    per = fsdp_count // seq_count
    n = seq_count
    rows, model = hidden.shape
    total = n * rows
    ff = FF // n
    x_width = DI // n
    conv_width = x_width + 2 * NST
    in_w = arrays[13].shape[1]
    gu_w = 2 * ff
    own = model // fsdp_count
    out_rows = (DI + QH * HD + FF) // fsdp_count
    v = pltpu.VMEM
    vm = pl.BlockSpec(memory_space=v)
    return pl.pallas_call(
        partial(backward_kernel, seq_count, fsdp_count),
        out_shape=[
            jax.ShapeDtypeStruct((n, own, in_w), bf),
            jax.ShapeDtypeStruct((n, own, gu_w), bf),
            jax.ShapeDtypeStruct((out_rows, model), bf),
            jax.ShapeDtypeStruct((n, SMALL_ROWS, 128), fl),
            jax.ShapeDtypeStruct((rows, model), fl),
        ],
        in_specs=[vm] * len(arrays),
        out_specs=[vm] * 5,
        scratch_shapes=[
            v((fsdp_count, own, in_w), bf),
            v((fsdp_count, own, gu_w), bf),
            v((per, out_rows, model), bf),
            v((SMALL_ROWS, 128), fl),
            v((n, rows, model), fl),
            v((total, in_w), bf),
            v((total, x_width), bf),
            v((total, x_width), fl),
            v((total, NST), bf),
            v((total, NST), bf),
            v((total, x_width), bf),
            v((total, total), fl),
            v((total, total), fl),
            v((total, total), fl),
            v((total, total), fl),
            v((total, total), fl),
            v((total, x_width), fl),
            v((total, conv_width), fl),
            v((total + 8, conv_width), fl),
            v((total, 128), fl),
            v((total, conv_width), fl),
            v((L, own, in_w), bf),
            v((2 * L, own, in_w), bf),
            v((own, in_w), fl),
            v((L, own, gu_w), bf),
            v((2 * L, own, gu_w), bf),
            v((own, gu_w), fl),
            v((per // 2, out_rows, model), bf),
            v((2, per // 2, out_rows, model), bf),
            v((out_rows // CHUNKS, model), fl),
            v((SMALL_ROWS, 128), fl),
            v((L, SMALL_ROWS, 128), fl),
            v((3, rows, model), bf),
            v((3, rows, model), bf),
            dma(2, L),
            dma(2, 2 * L),
            dma(2, L),
            dma(2, 2 * L),
            dma(2, per // 2, CHUNKS),
            dma(3, per // 2, CHUNKS),
            dma(2, CHUNKS),
            dma(CHUNKS),
            dma(3, L),
            dma(L),
            dma(1),
            dma(1),
            dma(4, 3),
            dma(4, 3),
        ],
        compiler_params=pltpu.CompilerParams(
            collective_id=4, has_side_effects=True, vmem_limit_bytes=VMEM_LIMIT
        ),
        name="backward_fused",
    )(*arrays)


def core_inputs(seg_ids, inputs, params):
    pre_conv, step_raw, query_in, key_in = inputs
    taps, tap_bias, step_bias, log_decay = params
    row_count = pre_conv.shape[0]
    tap_count = taps.shape[0]
    accum = tap_bias[None, :] + taps[tap_count - 1][None, :] * pre_conv
    for lag_step in range(1, tap_count):
        moved = jnp.concatenate(
            [
                jnp.zeros((lag_step, pre_conv.shape[1]), pre_conv.dtype),
                pre_conv[: row_count - lag_step],
            ],
            axis=0,
        )
        prior = jnp.concatenate(
            [jnp.full((lag_step,), -1, jnp.int32), seg_ids[: row_count - lag_step]]
        )
        same_seq = (prior == seg_ids)[:, None]
        accum = accum + taps[tap_count - 1 - lag_step][None, :] * jnp.where(same_seq, moved, 0.0)
    activated = jax.nn.silu(accum)
    step = jax.nn.softplus(step_raw + step_bias[None, :])
    log_step = -jnp.exp(log_decay)[None, :] * step
    positions = jnp.arange(row_count, dtype=jnp.int32)
    first_count = jnp.sum((seg_ids == 0).astype(jnp.int32))
    place = (positions - jnp.where(seg_ids == 0, 0, first_count)).astype(jnp.float32)
    half = HD // 2
    freqs = jnp.exp(-math.log(ROPE_THETA) * 2.0 * jnp.arange(half, dtype=jnp.float32) / HD)
    angles = place[:, None] * freqs[None, :]
    cosine = jnp.cos(angles)[:, None, :]
    sine = jnp.sin(angles)[:, None, :]

    def rotate(tensor):
        heads = tensor.reshape(row_count, -1, HD)
        first_half = heads[..., :half]
        second_half = heads[..., half:]
        return jnp.concatenate(
            [first_half * cosine - second_half * sine, second_half * cosine + first_half * sine],
            axis=-1,
        ).reshape(tensor.shape)

    return activated, step, log_step, rotate(query_in), rotate(key_in)


def shards(
    hidden_in,
    grad_out,
    segments,
    norm_gain,
    mamba_in,
    step_in,
    attn_in,
    conv_taps,
    conv_bias,
    step_bias,
    log_decay,
    skip_gain,
    gated_gain,
    mamba_out,
    attn_out,
    ffn_gain,
    gate_up,
    down_proj,
):
    bf_type = jnp.bfloat16
    fl_type = jnp.float32
    seq_count = lax.axis_size("seq")
    seq_index = lax.axis_index("seq")
    fsdp_count = lax.axis_size("fsdp")
    block_rows = hidden_in.shape[1]
    model = hidden_in.shape[2]
    rows = block_rows * seq_count
    own_rows = model // fsdp_count
    x_width = DI // seq_count
    head_share = MH // seq_count
    query_width = QH * HD // seq_count
    query_share = QH // seq_count
    ff_width = FF // seq_count
    owners = [group * KVH // seq_count for group in range(seq_count)]
    owner = seq_index * KVH // seq_count
    gain_own = DI // fsdp_count
    gain_cols = -(-gain_own // own_rows)

    def cols(array, start, size):
        return lax.dynamic_slice_in_dim(array, start, size, 1)

    gain_pad = jnp.pad(gated_gain, (0, gain_cols * own_rows - gain_own))
    main_width = 2 * x_width + 2 * NST + query_width + 2 * HD
    pad_width = 128 - head_share - 2 - gain_cols
    small_pack = jnp.concatenate(
        [
            cols(attn_in, QH * HD + owner * HD, HD),
            cols(attn_in, (QH + KVH) * HD + owner * HD, HD),
            cols(step_in, seq_index * head_share, head_share),
            norm_gain[:, None],
            ffn_gain[:, None],
            gain_pad.reshape(gain_cols, own_rows).T,
            jnp.zeros((own_rows, pad_width), bf_type),
        ],
        axis=1,
    )
    out_pack = jnp.concatenate([mamba_out, attn_out, down_proj], axis=0)
    w_in, w_gate_up, w_out, hidden_all, cot_all = gather_all(
        seq_count,
        fsdp_count,
        (x_width, query_width, ff_width),
        (hidden_in[0], grad_out[0], mamba_in, attn_in, small_pack, gate_up, out_pack),
    )
    per = fsdp_count // seq_count
    in_all = w_in.reshape(model, -1)
    w_gate_up = w_gate_up.reshape(model, -1)
    hidden_all = hidden_all.reshape(rows, model)
    attn_own = QH * HD // fsdp_count
    ff_own = FF // fsdp_count
    w_mamba_out = w_out[:, :gain_own].reshape(x_width, model)
    w_attn_out = w_out[:, gain_own : gain_own + attn_own].reshape(query_width, model)
    w_down = w_out[:, gain_own + attn_own :].reshape(ff_width, model)
    gain_at = main_width + head_share
    first_gain = in_all[:, gain_at].astype(fl_type)
    second_gain = in_all[:, gain_at + 1].astype(fl_type)
    gated_gains = (
        in_all[:, gain_at + 2 : gain_at + 2 + gain_cols]
        .reshape(fsdp_count, own_rows, gain_cols)
        .transpose(0, 2, 1)
        .reshape(fsdp_count, gain_cols * own_rows)[:, :gain_own]
        .reshape(DI)
    )
    mixer_gain = lax.dynamic_slice_in_dim(gated_gains, seq_index * x_width, x_width, 0).astype(
        fl_type
    )

    res_all = hidden_all.astype(fl_type)
    normed = (res_all * rms_scale(res_all) * first_gain).astype(bf_type)
    projected = jnp.dot(normed, in_all, preferred_element_type=fl_type)
    gate_raw = projected[:, :x_width]
    inputs_b = projected[:, x_width:].astype(bf_type).astype(fl_type)
    conv_width = x_width + 2 * NST
    conv_in = inputs_b[:, :conv_width]
    query_in = inputs_b[:, conv_width : conv_width + query_width]
    key_in = inputs_b[:, conv_width + query_width : conv_width + query_width + HD]
    value_b = inputs_b[:, conv_width + query_width + HD : conv_width + query_width + 2 * HD].astype(
        bf_type
    )
    step_at = conv_width + query_width + 2 * HD
    step_raw = inputs_b[:, step_at : step_at + head_share]
    seg_ids = segments[0]
    taps = jnp.concatenate(
        [cols(conv_taps, seq_index * x_width, x_width), conv_taps[:, DI:]], axis=1
    )
    tap_bias = jnp.concatenate(
        [lax.dynamic_slice_in_dim(conv_bias, seq_index * x_width, x_width, 0), conv_bias[DI:]]
    )
    params = (
        taps,
        tap_bias,
        lax.dynamic_slice_in_dim(step_bias, seq_index * head_share, head_share, 0),
        lax.dynamic_slice_in_dim(log_decay, seq_index * head_share, head_share, 0),
    )
    skip = lax.dynamic_slice_in_dim(skip_gain, seq_index * head_share, head_share, 0)
    (activated, step, log_step, queries, keys), pull_back = jax.vjp(
        partial(core_inputs, seg_ids), (conv_in, step_raw, query_in, key_in), params
    )
    positions = jnp.arange(rows, dtype=jnp.int32)
    causal = positions[:, None] >= positions[None, :]
    mask = causal & (seg_ids[:, None] == seg_ids[None, :])
    highest = lax.Precision.HIGHEST
    x_all = activated[:, :x_width]
    b_mat = activated[:, x_width : x_width + NST].astype(bf_type)
    c_mat = activated[:, x_width + NST :].astype(bf_type)
    x_heads = x_all.reshape(rows, head_share, HD).transpose(1, 0, 2)
    step_t = step.T
    cum_t = jnp.dot(log_step.T, causal.T.astype(fl_type), precision=highest)
    inner = jnp.einsum("tn,pn->tp", c_mat, b_mat, preferred_element_type=fl_type)
    decay = jnp.exp(jnp.where(mask[None], cum_t[:, :, None] - cum_t[:, None, :], -1e30))
    kernel_b = (inner[None] * decay).astype(bf_type)
    x_step = (x_heads * step_t[:, :, None]).astype(bf_type)
    scan_y = jnp.einsum("htp,hpd->htd", kernel_b, x_step, preferred_element_type=fl_type)
    ssm = scan_y + skip[:, None, None] * x_heads
    scan_float = (
        ssm.astype(bf_type).transpose(1, 0, 2).reshape(rows, x_width).astype(fl_type)
    )
    key_b = keys.astype(bf_type)
    q_heads = queries.reshape(rows, query_share, HD).transpose(1, 0, 2)
    scores = jnp.einsum("hid,jd->hij", q_heads, keys, precision=highest) * (1.0 / math.sqrt(HD))
    weights = jnp.exp(jnp.where(mask[None], scores, -1e30))
    weights = weights / jnp.sum(weights, axis=-1, keepdims=True)
    weights_b = weights.astype(bf_type)
    attended = jnp.einsum("hij,jd->hid", weights_b, value_b, preferred_element_type=fl_type)
    attn_mix = attended.astype(bf_type).transpose(1, 0, 2).reshape(rows, query_width)

    gate_act = jax.nn.silu(gate_raw)
    gated = scan_float * gate_act
    (
        layer_out,
        d_mixed,
        ffn_in,
        ffn_act,
        d_ffn,
        d_mixed_b,
        gated_b,
        d_gated,
        d_attn,
        g_ffn_gain,
        g_gated_gain,
    ) = middle(
        seq_count,
        fsdp_count,
        (
            gated.reshape(seq_count, block_rows, x_width),
            attn_mix.reshape(seq_count, block_rows, query_width),
            w_mamba_out,
            w_attn_out,
            w_down,
            w_gate_up,
            hidden_in[0],
            grad_out[0],
            cot_all,
            mixer_gain[None],
            second_gain[None],
        ),
    )
    ffn_in = ffn_in.reshape(rows, model)
    ffn_act = ffn_act.reshape(rows, ff_width)
    d_ffn = d_ffn.reshape(rows, 2 * ff_width)
    d_mixed_b = d_mixed_b.reshape(rows, model)
    gated_b = gated_b.reshape(rows, x_width)
    d_gated = d_gated.reshape(rows, x_width)
    d_attn = d_attn.reshape(rows, query_width)
    cot_rows = cot_all.reshape(rows, model)
    g_down = jnp.einsum("tf,td->fd", ffn_act, cot_rows, preferred_element_type=fl_type)
    g_gate_up = jnp.einsum("td,tf->df", ffn_in, d_ffn, preferred_element_type=fl_type)
    g_attn_out = jnp.einsum("tq,td->qd", attn_mix, d_mixed_b, preferred_element_type=fl_type)
    g_mamba_out = jnp.einsum("ti,td->id", gated_b, d_mixed_b, preferred_element_type=fl_type)
    d_scan = (d_gated * gate_act).astype(bf_type)
    d_gate_raw = d_gated * scan_float * swish_slope(gate_raw)
    g_out = jnp.concatenate(
        [
            g_mamba_out.astype(bf_type).reshape(per, gain_own, model),
            g_attn_out.astype(bf_type).reshape(per, attn_own, model),
            g_down.astype(bf_type).reshape(per, ff_own, model),
        ],
        axis=1,
    )

    d_att = d_attn.astype(bf_type).reshape(rows, query_share, HD).transpose(1, 0, 2)
    d_weights = jnp.einsum("hid,jd->hij", d_att, value_b, preferred_element_type=fl_type)
    inner_sum = jnp.sum(d_att.astype(fl_type) * attended, axis=-1, keepdims=True)
    d_scores = (weights * (d_weights - inner_sum) * (1.0 / math.sqrt(HD))).astype(bf_type)
    d_queries = jnp.einsum("hij,jd->hid", d_scores, key_b, preferred_element_type=fl_type)
    d_keys = jnp.einsum(
        "hij,hid->jd", d_scores, q_heads.astype(bf_type), preferred_element_type=fl_type
    )
    d_value = jnp.einsum("hij,hid->jd", weights_b, d_att, preferred_element_type=fl_type)
    d_y = d_scan.reshape(rows, head_share, HD).transpose(1, 0, 2)
    d_y_float = d_y.astype(fl_type)
    d_kernel = jnp.einsum("htd,hpd->htp", d_y, x_step, preferred_element_type=fl_type)
    d_inner = jnp.sum(d_kernel * decay, axis=0).astype(bf_type)
    d_x_step = jnp.einsum("htp,htd->hpd", kernel_b, d_y, preferred_element_type=fl_type)
    d_c = jnp.dot(d_inner, b_mat, preferred_element_type=fl_type)
    d_b = jnp.einsum("tp,tn->pn", d_inner, c_mat, preferred_element_type=fl_type)
    d_x = step_t[:, :, None] * d_x_step + skip[:, None, None] * d_y_float
    g_skip = jnp.sum(d_y_float * x_heads, axis=(1, 2))
    d_step_direct = jnp.sum(x_heads * d_x_step, axis=-1)
    d_cum = jnp.sum(d_y_float * scan_y, axis=-1) - jnp.sum(
        x_step.astype(fl_type) * d_x_step, axis=-1
    )
    d_log_step = jnp.dot(d_cum, causal.astype(fl_type), precision=highest)
    (d_conv, d_step, d_query, d_key), grad_params = pull_back(
        (
            jnp.concatenate([d_x.transpose(1, 0, 2).reshape(rows, x_width), d_b, d_c], axis=1),
            d_step_direct.T,
            d_log_step.T,
            d_queries.transpose(1, 0, 2).reshape(rows, query_width),
            d_keys,
        )
    )
    d_in = jnp.concatenate(
        [
            d_gate_raw,
            d_conv,
            d_query,
            d_key,
            d_value,
            d_step,
            jnp.zeros((rows, 128 - head_share), fl_type),
        ],
        axis=1,
    ).astype(bf_type)
    g_in = jnp.einsum("td,tc->dc", normed, d_in, preferred_element_type=fl_type)
    d_normed_part = jnp.einsum("tc,dc->td", d_in, in_all, preferred_element_type=fl_type)
    first_norm_all = res_all * rms_scale(res_all)
    g_norm_gain = jnp.sum(d_normed_part * first_norm_all, axis=0)
    taps_bias = jnp.concatenate([grad_params[0], grad_params[1][None]], axis=0)
    small_parts = [
        taps_bias.reshape(-1),
        g_gated_gain.reshape(-1),
        g_norm_gain,
        g_ffn_gain.reshape(-1),
        grad_params[2],
        grad_params[3],
        g_skip,
    ]
    small_size = sum(part.shape[0] for part in small_parts)
    small_rows = -(-small_size // 1024) * 8
    small = jnp.concatenate(
        small_parts + [jnp.zeros((small_rows * 128 - small_size,), fl_type)]
    ).reshape(small_rows, 128)
    in_grads, gu_grads, out_grads, small_all, d_normed = reduce_all(
        seq_count,
        fsdp_count,
        (
            g_in.astype(bf_type).reshape(fsdp_count, own_rows, -1),
            g_gate_up.astype(bf_type).reshape(fsdp_count, own_rows, -1),
            g_out,
            small,
            d_normed_part.astype(bf_type).reshape(seq_count, block_rows, model),
        ),
    )
    in_grads = in_grads.astype(fl_type)
    gu_grads = gu_grads.astype(fl_type)
    out_grads = out_grads.astype(fl_type)
    residual = hidden_in[0].astype(fl_type)
    first_scale = rms_scale(residual)
    first_norm = residual * first_scale
    d_first = d_normed * first_gain
    grad_tok = d_mixed + first_scale * (
        d_first - first_norm * jnp.mean(d_first * first_norm, axis=-1, keepdims=True)
    )

    conv_width = x_width + 2 * NST
    small_all = small_all.reshape(seq_count, -1)
    at = (KC + 1) * conv_width
    taps_all = small_all[:, :at].reshape(seq_count, KC + 1, conv_width)
    taps_sum = jnp.concatenate(
        [taps_all[group, :, :x_width] for group in range(seq_count)]
        + [jnp.sum(taps_all[:, :, x_width:], axis=0)],
        axis=1,
    )
    fsdp_index = lax.axis_index("fsdp")
    gated_sum = lax.dynamic_slice_in_dim(
        small_all[:, at : at + x_width].reshape(-1), fsdp_index * gain_own, gain_own, 0
    )
    at = at + x_width
    gains_sum = jnp.sum(small_all[:, at : at + 2 * model], axis=0)
    norm_sum = lax.dynamic_slice_in_dim(gains_sum, fsdp_index * own_rows, own_rows, 0)
    ffn_gain_sum = lax.dynamic_slice_in_dim(gains_sum, model + fsdp_index * own_rows, own_rows, 0)
    at = at + 2 * model
    heads_sum = (
        small_all[:, at : at + 3 * head_share]
        .reshape(seq_count, 3, head_share)
        .transpose(1, 0, 2)
        .reshape(3, MH)
    )

    def side(array):
        return jnp.concatenate([array[group] for group in range(seq_count)], axis=1)

    def owned(start):
        slots = []
        for kv_head in range(KVH):
            users = [group for group in range(seq_count) if owners[group] == kv_head]
            total = in_grads[users[0]][:, start : start + HD]
            for group in users[1:]:
                total = total + in_grads[group][:, start : start + HD]
            slots.append(total)
        return slots

    q_at = 2 * x_width + 2 * NST
    grad_mamba_in = jnp.concatenate(
        [
            side(in_grads[:, :, :x_width]),
            side(in_grads[:, :, x_width : 2 * x_width]),
            jnp.sum(in_grads[:, :, 2 * x_width : q_at], axis=0),
        ],
        axis=1,
    )
    k_at = q_at + query_width
    grad_attn_in = jnp.concatenate(
        [side(in_grads[:, :, q_at:k_at])] + owned(k_at) + owned(k_at + HD), axis=1
    )
    grad_step_in = side(in_grads[:, :, main_width : main_width + head_share])
    grad_gate_up = jnp.concatenate(
        [side(gu_grads[:, :, :ff_width]), side(gu_grads[:, :, ff_width:])], axis=1
    )
    return (
        layer_out[None],
        grad_tok[None],
        norm_sum,
        grad_mamba_in,
        grad_step_in,
        grad_attn_in,
        taps_sum[:KC],
        taps_sum[KC],
        heads_sum[0],
        heads_sum[1],
        heads_sum[2],
        gated_sum,
        out_grads[:gain_own],
        out_grads[gain_own : gain_own + attn_own],
        ffn_gain_sum,
        grad_gate_up,
        out_grads[gain_own + attn_own :],
    )


def unpack_kernel(
    x_width, query_width, ff, gain_own, attn_own, in_got, gu_got, out_got, tok, layer, g_mi, g_si, g_ai, g_gu, g_mo, g_ao, g_dn, tok_out, layer_out
):
    tok_out[...] = tok[...]
    layer_out[...] = layer[...]
    fl = jnp.float32
    bc_at, q_at = 2 * x_width, 2 * x_width + 2 * NST
    kv_at = q_at + query_width
    count = in_got.shape[0]
    users = count // KVH
    head_share = x_width // HD
    for g in range(count):
        g_mi[:, g * x_width : (g + 1) * x_width] = in_got[g, :, :x_width].astype(fl)
        g_mi[:, DI + g * x_width : DI + (g + 1) * x_width] = in_got[g, :, x_width:bc_at].astype(fl)
        g_ai[:, g * query_width : (g + 1) * query_width] = in_got[g, :, q_at:kv_at].astype(fl)
        g_gu[:, g * ff : (g + 1) * ff] = gu_got[g, :, :ff].astype(fl)
        g_gu[:, FF + g * ff : FF + (g + 1) * ff] = gu_got[g, :, ff:].astype(fl)
    g_mi[:, 2 * DI :] = sum(in_got[g, :, bc_at:q_at].astype(fl) for g in range(count))
    pairs = [
        sum(in_got[g, :, kv_at : kv_at + 2 * HD].astype(fl) for g in range(k * users, (k + 1) * users))
        for k in range(KVH)
    ]
    lane = iota2(pairs[0].shape, 1)
    keys = jnp.where(lane < HD, pairs[0], pltpu.roll(pairs[1], HD, 1))
    values = jnp.where(lane < HD, pltpu.roll(pairs[0], HD, 1), pairs[1])
    g_ai[:, QH * HD : (QH + KVH) * HD] = keys
    g_ai[:, (QH + KVH) * HD :] = values
    steps = in_got[0, :, kv_at + 2 * HD :].astype(fl)
    for g in range(1, count):
        moved = pltpu.roll(in_got[g, :, kv_at + 2 * HD :].astype(fl), g * head_share, 1)
        steps = jnp.where(lane >= g * head_share, moved, steps)
    g_si[...] = steps[:, :MH]
    g_mo[...] = out_got[:gain_own].astype(fl)
    g_ao[...] = out_got[gain_own : gain_own + attn_own].astype(fl)
    g_dn[...] = out_got[gain_own + attn_own :].astype(fl)


def unpack(widths, owns, arrays):
    own, model = arrays[0].shape[1], arrays[2].shape[1]
    gain_own, attn_own, ff_own = owns
    vm = pl.BlockSpec(memory_space=pltpu.VMEM)
    shapes = [
        (own, 2 * DI + 2 * NST),
        (own, MH),
        (own, (QH + 2 * KVH) * HD),
        (own, 2 * FF),
        (gain_own, model),
        (attn_own, model),
        (ff_own, model),
    ]
    return pl.pallas_call(
        partial(unpack_kernel, *widths, gain_own, attn_own),
        out_shape=[jax.ShapeDtypeStruct(shape, jnp.float32) for shape in shapes]
        + [jax.ShapeDtypeStruct(array.shape, array.dtype) for array in arrays[3:]],
        in_specs=[vm] * 5,
        out_specs=[vm] * 9,
        compiler_params=pltpu.CompilerParams(vmem_limit_bytes=VMEM_LIMIT),
        name="unpack_grads",
    )(*arrays)


def fused_shards(
    hidden_in,
    grad_out,
    segments,
    norm_gain,
    mamba_in,
    step_in,
    attn_in,
    conv_taps,
    conv_bias,
    step_bias,
    log_decay,
    skip_gain,
    gated_gain,
    mamba_out,
    attn_out,
    ffn_gain,
    gate_up,
    down_proj,
):
    bf_type = jnp.bfloat16
    fl_type = jnp.float32
    seq_count = lax.axis_size("seq")
    seq_index = lax.axis_index("seq")
    fsdp_count = lax.axis_size("fsdp")
    block_rows = hidden_in.shape[1]
    model = hidden_in.shape[2]
    rows = block_rows * seq_count
    own_rows = model // fsdp_count
    x_width = DI // seq_count
    head_share = MH // seq_count
    query_width = QH * HD // seq_count
    ff_width = FF // seq_count
    owner = seq_index * KVH // seq_count
    gain_own = DI // fsdp_count
    attn_own = QH * HD // fsdp_count

    def cols(array, start, size):
        return lax.dynamic_slice_in_dim(array, start, size, 1)

    small_pack = jnp.concatenate(
        [
            cols(attn_in, QH * HD + owner * HD, HD),
            cols(attn_in, (QH + KVH) * HD + owner * HD, HD),
            cols(step_in, seq_index * head_share, head_share),
            norm_gain[:, None],
            ffn_gain[:, None],
            jnp.zeros((own_rows, 126 - head_share), bf_type),
        ],
        axis=1,
    )
    gain_in = jnp.pad(gated_gain[:, None], ((0, 0), (0, 127)))
    all_heads = jnp.pad(jnp.stack([step_bias, log_decay, skip_gain]), ((0, 5), (0, 128 - MH)))
    (
        layer_out,
        d_mixed,
        ffn_in,
        ffn_act,
        d_ffn,
        d_mixed_all,
        gated_b,
        d_gated,
        d_attn,
        g_ffn_gain,
        g_gated_gain,
        cot_all,
        in_all,
        normed,
        gate_raw,
        inputs_b,
        accum,
        scan_bf,
        scan_y,
        steps,
        cum,
        attn_mix,
        gain_rows,
        seg_col,
        place,
        cosine,
        sine,
        taps,
        heads,
    ) = forward_all(
        seq_count,
        fsdp_count,
        (x_width, query_width, ff_width),
        (
            hidden_in[0],
            grad_out[0],
            mamba_in,
            attn_in,
            small_pack,
            gate_up,
            mamba_out,
            attn_out,
            down_proj,
            gain_in,
            segments,
            conv_taps,
            conv_bias[None],
            all_heads,
        ),
    )

    def flat(array):
        return array.reshape(rows, -1)

    in_grads, gu_grads, out_grads, small_all, grad_tok = backward_all(
        seq_count,
        fsdp_count,
        (
            hidden_in[0],
            d_mixed,
            flat(d_mixed_all),
            flat(cot_all),
            flat(ffn_in),
            flat(ffn_act),
            flat(d_ffn),
            flat(gated_b),
            flat(attn_mix),
            flat(d_gated),
            flat(d_attn),
            g_ffn_gain,
            g_gated_gain,
            in_all,
            normed,
            gate_raw,
            inputs_b,
            accum,
            scan_bf,
            scan_y,
            steps,
            cum,
            gain_rows,
            seg_col,
            segments,
            place,
            cosine,
            sine,
            taps,
            heads,
        ),
    )
    (
        grad_mamba_in,
        grad_step_in,
        grad_attn_in,
        grad_gate_up,
        grad_mo,
        grad_ao,
        grad_dn,
        grad_tok,
        layer_out,
    ) = unpack(
        (x_width, query_width, ff_width),
        (gain_own, attn_own, FF // fsdp_count),
        (in_grads, gu_grads, out_grads, grad_tok, layer_out),
    )
    conv_width = x_width + 2 * NST
    at = (KC + 1) * conv_width // 128
    taps_all = small_all[:, :at].reshape(seq_count, KC + 1, conv_width)
    taps_sum = jnp.concatenate(
        [taps_all[group, :, :x_width] for group in range(seq_count)]
        + [jnp.sum(taps_all[:, :, x_width:], axis=0)],
        axis=1,
    )
    fsdp_index = lax.axis_index("fsdp")
    gated_sum = lax.dynamic_slice_in_dim(
        small_all[:, at : at + x_width // 128].reshape(-1), fsdp_index * gain_own, gain_own, 0
    )
    at = at + x_width // 128
    gains_sum = jnp.sum(small_all[:, at : at + 2 * model // 128], axis=0).reshape(-1)
    norm_sum = lax.dynamic_slice_in_dim(gains_sum, fsdp_index * own_rows, own_rows, 0)
    at = at + model // 128
    ffn_gain_sum = lax.dynamic_slice_in_dim(
        gains_sum, model + fsdp_index * own_rows, own_rows, 0
    )
    at = at + model // 128
    heads_sum = small_all[:, at : at + 3, :head_share].transpose(1, 0, 2).reshape(3, MH)
    return (
        layer_out[None],
        grad_tok[None],
        norm_sum,
        grad_mamba_in,
        grad_step_in,
        grad_attn_in,
        taps_sum[:KC],
        taps_sum[KC],
        heads_sum[0],
        heads_sum[1],
        heads_sum[2],
        gated_sum,
        grad_mo,
        grad_ao,
        ffn_gain_sum,
        grad_gate_up,
        grad_dn,
    )


def solution(mesh):
    placed = (
        P("fsdp", "seq", None),
        P("fsdp", "seq", None),
        P("fsdp", None),
        P("fsdp"),
        P("fsdp", None),
        P("fsdp", None),
        P("fsdp", None),
        P(),
        P(),
        P(),
        P(),
        P(),
        P("fsdp"),
        P("fsdp", None),
        P("fsdp", None),
        P("fsdp"),
        P("fsdp", None),
        P("fsdp", None),
    )
    fsdp_count = mesh.shape["fsdp"]
    whole_tiles = all(
        width % (16 * fsdp_count) == 0 for width in (DI // 2, QH * HD // 2, FF // 2)
    )
    return jax.shard_map(
        fused_shards if whole_tiles else shards,
        mesh=mesh,
        in_specs=placed,
        out_specs=(
            P("fsdp", "seq", None),
            P("fsdp", "seq", None),
            P("fsdp"),
            P("fsdp", None),
            P("fsdp", None),
            P("fsdp", None),
            P(),
            P(),
            P(),
            P(),
            P(),
            P("fsdp"),
            P("fsdp", None),
            P("fsdp", None),
            P("fsdp"),
            P("fsdp", None),
            P("fsdp", None),
        ),
        check_vma=False,
    )
```
